32 devices in a mesh: dp: 8 (over y, x, core), tensor: 4 (over z).
Axes of the slice: x: 2, y: 2, z: 4, core: 2. Of those that a mesh axis runs over, the one named last changes fastest.
Arguments:
- tokens_in: bfloat16 [18464, 1024], P('dp', 'tensor'), may hold values from -6 to 6
- cotangent: bfloat16 [18464, 1024], P('dp', 'tensor'), may hold values from -6 to 6
- slot_mask: int32 [32], P('dp'), may hold values 0 or 1
- norm1_gain: float32 [4, 256], P('tensor', 'dp'), may hold values from 0.1 to 1.9
- norm1_bias: float32 [4, 256], P('tensor', 'dp'), may hold values from -4 to 4
- w_qkv: float32 [1024, 3, 1024], P('dp', None, 'tensor')
- b_qkv: float32 [2, 4, 256], P(None, 'tensor', 'dp'), may hold values from -6 to 6
- w_out: float32 [1024, 1024], P('tensor', 'dp'), may hold values from -1.5 to 1.5
- b_out: float32 [4, 256], P('tensor', 'dp'), may hold values from -4 to 4
- norm2_gain: float32 [4, 256], P('tensor', 'dp'), may hold values from 0.1 to 1.9
- norm2_bias: float32 [4, 256], P('tensor', 'dp'), may hold values from -4 to 4
- w_fc1: float32 [1024, 4096], P('dp', 'tensor')
- b_fc1: float32 [4, 1024], P('tensor', 'dp'), may hold values from -6 to 6
- w_fc2: float32 [4096, 1024], P('tensor', 'dp'), may hold values from -0.09375 to 0.09375
- b_fc2: float32 [4, 256], P('tensor', 'dp'), may hold values from -4 to 4
Outputs:
- block_out: bfloat16 [18464, 1024], P('dp', 'tensor')
- grad_tokens: bfloat16 [18464, 1024], P('dp', 'tensor')
- grad_norm1_gain: float32 [4, 256], P('tensor', 'dp')
- grad_norm1_bias: float32 [4, 256], P('tensor', 'dp')
- grad_w_qkv: float32 [1024, 3, 1024], P('dp', None, 'tensor')
- grad_b_qkv: float32 [2, 4, 256], P(None, 'tensor', 'dp')
- grad_w_out: float32 [1024, 1024], P('tensor', 'dp')
- grad_b_out: float32 [4, 256], P('tensor', 'dp')
- grad_norm2_gain: float32 [4, 256], P('tensor', 'dp')
- grad_norm2_bias: float32 [4, 256], P('tensor', 'dp')
- grad_w_fc1: float32 [1024, 4096], P('dp', 'tensor')
- grad_b_fc1: float32 [4, 1024], P('tensor', 'dp')
- grad_w_fc2: float32 [4096, 1024], P('tensor', 'dp')
- grad_b_fc2: float32 [4, 256], P('tensor', 'dp')
The draws below stay inside these ranges and needn't reach their ends.
All inputs are finite; a program needn't handle non-finite values. No bound on the sum of `slot_mask` on one device may be relied on, other than what follows from the above.
Results may differ from the reference program's by a relative error of at most 0.025.
Values may be sent and summed in bfloat16 or wider, within the bound.
A program may use at most 192 MiB of HBM per device.

```python
import jax
import jax.numpy as jnp
from jax import lax

D = 1024
H = 16
HD = 64
FF = 4096
SEQ = 577
IMG_DEV = 4
IMAGES = 32
TOKENS = 18464
N_TENSOR = 4


def draw_w_qkv(key, part):
    key_rows, key_common = jax.random.split(jax.random.fold_in(key, 11))
    rows = jax.random.truncated_normal(key_rows, -6.0, 6.0, (D, 3, D), jnp.float32)
    common = jax.random.truncated_normal(key_common, -4.0, 4.0, (1, 3, D), jnp.float32)
    return (rows + 0.5 * common) * D ** (-0.5)


def draw_w_fc1(key, part):
    key_rows, key_common = jax.random.split(jax.random.fold_in(key, 13))
    rows = jax.random.truncated_normal(key_rows, -6.0, 6.0, (D, FF), jnp.float32)
    common = jax.random.truncated_normal(key_common, -4.0, 4.0, (1, FF), jnp.float32)
    return (rows + 0.5 * common) * D ** (-0.5)


def touch_ends(values, rng, low, high):
    longest = values.shape.index(max(values.shape))
    spots = []
    for shift in (0, 1):
        where = [jax.random.randint(jax.random.fold_in(rng, axis), (), 0, length) for axis, length in enumerate(values.shape)]
        where[longest] = (where[longest] + shift) % values.shape[longest]
        spots.append(tuple(where))
    return values.at[spots[0]].set(low).at[spots[1]].set(high)


def levels(stream_key, shape, cuts, low, top_value):
    level = 1.0
    for position, parts in cuts:
        draws = jax.random.uniform(jax.random.fold_in(jax.random.fold_in(stream_key, 6), position), (parts,), jnp.float32, low / len(cuts), top_value / len(cuts))
        level = level * jnp.repeat(jnp.exp(draws), shape[position] // parts).reshape((-1,) + (1,) * (len(shape) - 1 - position))
    return level


def noise(stream_key, shape, deviation, most, pieces=(), kind=jnp.bfloat16):
    factor_of = levels(stream_key, shape, pieces, -0.22, 0.18) if pieces else 1.0
    drawn = jax.random.normal(stream_key, shape, jnp.float32) * deviation * factor_of
    return jnp.minimum(jnp.maximum(drawn, -most), most).astype(kind)


def setup_inputs(seed: int = 0) -> dict:
    key_of = jax.random.split(jax.random.key(seed), 16)
    return {
        "tokens_in": noise(key_of[0], (TOKENS, D), 1.0, 6.0, ((0, 8), (1, 4))),
        "cotangent": noise(key_of[1], (TOKENS, D), 1.0, 6.0, ((0, 8), (1, 4))),
        "slot_mask": touch_ends((jax.random.randint(key_of[2], (IMAGES,), 0, 8) < 7).astype(jnp.int32), jax.random.fold_in(key_of[2], 1), 0, 1),
        "norm1_gain": jnp.clip(1.0 + 0.18 * jax.random.normal(key_of[3], (N_TENSOR, D // N_TENSOR), jnp.float32), 0.1, 1.9),
        "norm1_bias": noise(key_of[4], (N_TENSOR, D // N_TENSOR), 0.3, 4.0, ((0, 4), (1, 8)), jnp.float32),
        "w_qkv": draw_w_qkv(jax.random.fold_in(key_of[15], 71), 0),
        "b_qkv": noise(key_of[6], (2, N_TENSOR, D // N_TENSOR), 0.5, 6.0, ((1, 4), (2, 8)), jnp.float32),
        "w_out": noise(key_of[7], (D, D), (D // 64) ** -0.5, 1.5, ((0, 4), (1, 8)), jnp.float32),
        "b_out": noise(key_of[8], (N_TENSOR, D // N_TENSOR), 0.3, 4.0, ((0, 4), (1, 8)), jnp.float32),
        "norm2_gain": jnp.clip(1.0 + 0.18 * jax.random.normal(key_of[9], (N_TENSOR, D // N_TENSOR), jnp.float32), 0.1, 1.9),
        "norm2_bias": noise(key_of[10], (N_TENSOR, D // N_TENSOR), 0.3, 4.0, ((0, 4), (1, 8)), jnp.float32),
        "w_fc1": draw_w_fc1(jax.random.fold_in(key_of[15], 71), 0),
        "b_fc1": noise(key_of[12], (N_TENSOR, FF // N_TENSOR), 0.5, 6.0, ((0, 4), (1, 8)), jnp.float32),
        "w_fc2": noise(key_of[13], (FF, D), FF ** -0.5, 0.09375, ((0, 4), (1, 8)), jnp.float32),
        "b_fc2": noise(key_of[14], (N_TENSOR, D // N_TENSOR), 0.3, 4.0, ((0, 4), (1, 8)), jnp.float32),
    }


@jax.custom_vjp
def low(v):
    return lax.optimization_barrier(v.astype(jnp.bfloat16)).astype(jnp.float32)

@jax.custom_vjp
def low_back(v):
    return v

def low_keep(v):
    return (low(v), None)

def low_pass(kept, grad):
    return (grad,)

def back_keep(v):
    return (v, None)

def back_low(kept, grad):
    return (low(grad),)
low.defvjp(low_keep, low_pass)
low_back.defvjp(back_keep, back_low)

def layer_norm(values, gain, shift):
    mean_row = lax.optimization_barrier(jnp.mean(values, axis=-1, keepdims=True))
    centered = values - mean_row
    variance = lax.optimization_barrier(jnp.mean(centered * centered, axis=-1, keepdims=True))
    return centered * lax.rsqrt(variance + 1e-05) * gain + shift

def block(params, tokens, mask_rows):
    params = jax.tree.map(low, params)
    gain_one, shift_one, weight_mix, bias_mix, weight_proj, bias_proj, gain_two, shift_two, weight_up, bias_up, weight_down, bias_down = params
    highest = lax.Precision.HIGHEST
    group_images = tokens.shape[0]
    normed_in = low(layer_norm(tokens, gain_one.reshape(-1), shift_one.reshape(-1)))
    mixed = low_back(jnp.einsum('gsd,dcf->gscf', normed_in, weight_mix, precision=highest))
    bias_pair = bias_mix.reshape(2, -1)
    head_shape = (group_images, SEQ, H, HD)
    queries = low(mixed[:, :, 0] + bias_pair[0]).reshape(head_shape)
    key_rows = low(mixed[:, :, 1]).reshape(head_shape)
    value_rows = low(mixed[:, :, 2] + bias_pair[1]).reshape(head_shape)
    scores = low_back(jnp.einsum('gqhe,gkhe->ghqk', queries, key_rows, precision=highest)) * HD ** (-0.5)
    attn_probs = low(jax.nn.softmax(scores, axis=-1))
    context = low_back(low(jnp.einsum('ghqk,gkhe->gqhe', attn_probs, value_rows, precision=highest)))
    context = context.reshape(group_images, SEQ, D)
    attn_out = low_back(jnp.einsum('gsf,fd->gsd', context, weight_proj, precision=highest))
    resid_mid = tokens + attn_out + bias_proj.reshape(-1)
    normed_mid = low(layer_norm(resid_mid, gain_two.reshape(-1), shift_two.reshape(-1)))
    pre_act = low_back(jnp.einsum('gsd,df->gsf', normed_mid, weight_up, precision=highest)) + bias_up.reshape(-1)
    activation = low(pre_act * jax.nn.sigmoid(1.702 * pre_act))
    mlp_out = low_back(jnp.einsum('gsf,fd->gsd', activation, weight_down, precision=highest))
    return (resid_mid + mlp_out + bias_down.reshape(-1)) * mask_rows[:, None, None]

def reference(tokens_in, cotangent, slot_mask, norm1_gain, norm1_bias, w_qkv, b_qkv, w_out, b_out, norm2_gain, norm2_bias, w_fc1, b_fc1, w_fc2, b_fc2):
    params = (norm1_gain, norm1_bias, w_qkv, b_qkv, w_out, b_out, norm2_gain, norm2_bias, w_fc1, b_fc1, w_fc2, b_fc2)
    groups = slot_mask.shape[0] // IMG_DEV
    token_groups = tokens_in.astype(jnp.float32).reshape(groups, IMG_DEV, SEQ, D)
    cot_groups = cotangent.astype(jnp.float32).reshape(groups, IMG_DEV, SEQ, D)
    mask_groups = slot_mask.astype(jnp.float32).reshape(groups, IMG_DEV)

    def group_step(carry_sum, group_entry):
        token_block, cot_block, mask_block = group_entry

        def forward(param_set, token_set):
            return block(param_set, token_set, mask_block)
        block_value, pullback = jax.vjp(forward, params, token_block)
        param_grads, token_grads = pullback(cot_block)
        carry_sum = jax.tree.map(lambda total_sum, addend: total_sum + addend, carry_sum, param_grads)
        return (carry_sum, (block_value.astype(jnp.bfloat16), token_grads.astype(jnp.bfloat16)))
    zero_grads = jax.tree.map(jnp.zeros_like, params)
    grad_sums, (outputs, input_grads) = lax.scan(group_step, zero_grads, (token_groups, cot_groups, mask_groups))
    return (outputs.reshape(-1, D), input_grads.reshape(-1, D), grad_sums[0], grad_sums[1], grad_sums[2], grad_sums[3], grad_sums[4], grad_sums[5], grad_sums[6], grad_sums[7], grad_sums[8], grad_sums[9], grad_sums[10], grad_sums[11])
```

```python
import functools
import jax
import jax.numpy as jnp
from jax import lax
from jax.experimental import pallas as pl
from jax.experimental.pallas import tpu as pltpu
from jax.sharding import PartitionSpec as P

D = 1024
HD = 64
SEQ = 577
ROWS = 592
STEP = 16
F32 = jnp.float32
BF16 = jnp.bfloat16
LAST = (((1,), (1,)), ((), ()))
VMEM_BYTES = 66_000_000


def mm(a, b):
    return jnp.dot(a, b, preferred_element_type=F32)


def mm_t(a, b):
    return lax.dot_general(a, b, LAST, preferred_element_type=F32)


def cols(i, n):
    return pl.ds(pl.multiple_of(i * n, n), n)


def row_stats(values):
    mean = jnp.sum(values, axis=1, keepdims=True) * (1.0 / D)
    centered = values - mean
    var = jnp.sum(centered * centered, axis=1, keepdims=True) * (1.0 / D)
    inv = lax.rsqrt(var + 1e-05)
    return centered * inv, inv


def wide(ref, rows):
    return jnp.concatenate([ref[t, rows, :].astype(F32) for t in range(4)], axis=1)


def vec(vectors, row):
    return jnp.concatenate([vectors[t, row : row + 1, :] for t in range(4)], axis=1)


def norm_in(x, vectors, nin):
    gain, shift = vec(vectors, 0), vec(vectors, 1)

    @pl.loop(0, ROWS // STEP)
    def _(i):
        rows = pl.ds(pl.multiple_of(i * STEP, STEP), STEP)
        xhat, _ = row_stats(wide(x, rows))
        nin[rows, :] = (xhat * gain + shift).astype(BF16)


def flip(src, dst, n):
    @pl.loop(0, n // 256)
    def _(i):
        dst[cols(i, 256), :] = src[:, cols(i, 256)].T


def project(nin, wqkv, vectors, t, q, k, v):
    here = pl.ds(t * 256, 256)
    q[:, here] = (mm(nin[...], wqkv[t, :, 0:256]) + vectors[t, 2:3, :]).astype(BF16)
    k[:, here] = mm(nin[...], wqkv[t, :, 256:512]).astype(BF16)
    v[:, here] = (mm(nin[...], wqkv[t, :, 512:768]) + vectors[t, 3:4, :]).astype(BF16)


def attend_pair(pair, q, k, v, ctx, probs, slot):
    here = cols(pair, 128)
    lane = lax.broadcasted_iota(jnp.int32, (ROWS, 128), 1)
    row = lax.broadcasted_iota(jnp.int32, (ROWS, 128), 0)
    queries = q[:, here].astype(F32) * (HD**-0.5)
    keys = k[:, here].astype(F32)
    values = v[:, here]
    blocked = jnp.where(row >= SEQ, -1e30, 0.0)
    parts = []
    for h in range(2):
        own = (lane < 64) if h == 0 else (lane >= 64)
        spare = 64 if h == 0 else 0
        qa = jnp.where(own, queries, jnp.where(lane == spare, 1.0, 0.0)).astype(BF16)
        ka = jnp.where(lane == spare, blocked, keys).astype(BF16)
        scores = mm_t(ka, qa)
        top = jnp.max(scores, axis=0, keepdims=True)
        e = jnp.exp(scores - top)
        total = jnp.sum(e, axis=0, keepdims=True)
        p = (e * (1.0 / total)).astype(BF16)
        probs[slot, h] = p
        parts.append(
            lax.dot_general(p, values, (((0,), (0,)), ((), ())), preferred_element_type=F32)
        )
    ctx[:, here] = jnp.where(lane < 64, parts[0], parts[1]).astype(BF16)


def out_block(i, ctx, wout, x, vectors, resid):
    w = jnp.concatenate([wout[2 * i], wout[2 * i + 1]], axis=1)
    resid[:, cols(i, 256)] = x[i].astype(F32) + mm(ctx[...], w) + vectors[i, 4:5, :]


def norm_mid(resid, vectors, nmid):
    gain, shift = vec(vectors, 5), vec(vectors, 6)

    @pl.loop(0, ROWS // STEP)
    def _(i):
        rows = pl.ds(pl.multiple_of(i * STEP, STEP), STEP)
        xhat, _ = row_stats(resid[rows, :])
        nmid[rows, :] = (xhat * gain + shift).astype(BF16)


def hidden_tile(t, j, nmid, w1, b1, act, act_t, slope):
    here = pl.ds(pl.multiple_of(t * 1024 + j * 256, 256), 256)
    bias = b1[t, :, cols(j, 256)]
    pre = mm(nmid[...], w1[t, :, cols(j, 256)]) + bias
    sig = 1.0 / (1.0 + jnp.exp(-1.702 * pre))
    a = pre * sig
    slope[:, here] = (sig + 1.702 * a * (1.0 - sig)).astype(BF16)
    low = a.astype(BF16)
    act[:, here] = low
    act_t[here, :] = low.T


def down_block(i, act, w2, resid, vectors, mask, out):
    w = jnp.concatenate([w2[2 * i], w2[2 * i + 1]], axis=1)
    total = resid[:, cols(i, 256)] + mm(act[...], w) + vectors[i, 7:8, :]
    out[i] = (total * mask[...]).astype(BF16)


def grad_norm_rows(values, gain, n):
    xhat, inv = row_stats(values)
    e = n * gain
    first = jnp.sum(e, axis=1, keepdims=True) * (1.0 / D)
    second = jnp.sum(e * xhat, axis=1, keepdims=True) * (1.0 / D)
    return inv * (e - first - xhat * second), n * xhat


def fold(a):
    return a[0:8] + a[8:16]


def attend_back_pair(pair, q, k, v, ctx, gctx, probs, slot, gmix, sums):
    here = cols(pair, 128)
    lane = lax.broadcasted_iota(jnp.int32, (ROWS, 128), 1)
    queries, keys, values = q[:, here], k[:, here], v[:, here].astype(F32)
    go = gctx[:, here]
    go_f = go.astype(F32)
    dots = go_f * ctx[:, here].astype(F32)
    dq, dk, dv = [], [], []
    for h in range(2):
        own = (lane < 64) if h == 0 else (lane >= 64)
        spare = 64 if h == 0 else 0
        delta = -jnp.sum(jnp.where(own, dots, 0.0), axis=1, keepdims=True)
        high = delta.astype(BF16).astype(F32)
        rest = delta - high
        ga = jnp.where(
            own, go_f, jnp.where(lane == spare, high, jnp.where(lane == spare + 1, rest, 0.0))
        ).astype(BF16)
        marks = jnp.where((lane == spare) | (lane == spare + 1), 1.0, 0.0)
        va = jnp.where(own, values, marks).astype(BF16)
        p = probs[slot, h]
        gs = (p.astype(F32) * mm_t(va, ga)).astype(BF16)
        dv.append(mm(p, go))
        dk.append(mm(gs, queries))
        dq.append(
            lax.dot_general(gs, keys, (((0,), (0,)), ((), ())), preferred_element_type=F32)
        )
    scale = HD**-0.5
    low = lane < 64
    gq = jnp.where(low, dq[0], dq[1]) * scale
    gk = jnp.where(low, dk[0], dk[1]) * scale
    gv = jnp.where(low, dv[0], dv[1])
    t, half = pair // 2, pair % 2
    at = [pl.ds(pl.multiple_of(c * 256 + half * 128, 128), 128) for c in range(3)]
    gmix[t, :, at[0]] = gq.astype(BF16)
    gmix[t, :, at[1]] = gk.astype(BF16)
    gmix[t, :, at[2]] = gv.astype(BF16)
    sums[2:3, here] = jnp.sum(gq, axis=0, keepdims=True)
    sums[3:4, here] = jnp.sum(gv, axis=0, keepdims=True)


ACT = jax.ShapeDtypeStruct((ROWS, D), BF16)
TURNED = jax.ShapeDtypeStruct((D, ROWS), BF16)
SAVED = dict(
    nin_t=TURNED,
    q=ACT,
    k=ACT,
    v=ACT,
    ctx=ACT,
    ctx_t=TURNED,
    nmid_t=TURNED,
    resid=jax.ShapeDtypeStruct((ROWS, D), F32),
    act_t=jax.ShapeDtypeStruct((4 * D, ROWS), BF16),
    slope=jax.ShapeDtypeStruct((ROWS, 4 * D), BF16),
)
PROBS = jax.ShapeDtypeStruct((8, 2, ROWS, ROWS), BF16)
IMAGE = jax.ShapeDtypeStruct((4, ROWS, 256), BF16)
ANY = pl.BlockSpec(memory_space=pl.ANY)
VM = pl.BlockSpec(memory_space=pltpu.VMEM)


def scratch(like):
    return pltpu.VMEM(like.shape, like.dtype)


def forward_kernel(x_h, wqkv_h, wout_h, w1_h, w2_h, vectors, b1, mask, *rest):
    n = len(SAVED)
    out_h, probs_h = rest[0], rest[1]
    saved_h = dict(zip(SAVED, rest[2 : 2 + n]))
    rest = rest[2 + n :]
    saved = dict(zip(SAVED, rest[:n]))
    x, wqkv, wout, w1, w2, nin, nmid, act, probs, out, in_sem, probs_sem, out_sem = rest[n:]
    loads = [
        pltpu.make_async_copy(a, b, in_sem.at[i])
        for i, (a, b) in enumerate(((x_h, x), (wqkv_h, wqkv), (wout_h, wout), (w1_h, w1), (w2_h, w2)))
    ]
    for c in loads:
        c.start()
    loads[0].wait()
    norm_in(x, vectors, nin)
    loads[1].wait()
    for t in range(4):
        project(nin, wqkv, vectors, t, saved["q"], saved["k"], saved["v"])
    flip(nin, saved["nin_t"], D)

    def put(pair, slot):
        return pltpu.make_async_copy(probs.at[slot], probs_h.at[pair], probs_sem.at[slot])

    @pl.loop(0, 8)
    def _(pair):
        slot = pair % 2

        @pl.when(pair >= 2)
        def _():
            put(pair - 2, slot).wait()

        attend_pair(pair, saved["q"], saved["k"], saved["v"], saved["ctx"], probs, slot)
        put(pair, slot).start()

    put(6, 0).wait()
    put(7, 1).wait()
    loads[2].wait()

    @pl.loop(0, 4)
    def _(i):
        out_block(i, saved["ctx"], wout, x, vectors, saved["resid"])

    norm_mid(saved["resid"], vectors, nmid)
    loads[3].wait()

    @pl.loop(0, 16)
    def _(i):
        hidden_tile(i // 4, i % 4, nmid, w1, b1, act, saved["act_t"], saved["slope"])

    flip(saved["ctx"], saved["ctx_t"], D)
    flip(nmid, saved["nmid_t"], D)
    loads[4].wait()

    @pl.loop(0, 4)
    def _(i):
        down_block(i, act, w2, saved["resid"], vectors, mask, out)

    stores = [pltpu.make_async_copy(out, out_h, out_sem.at[n])]
    stores += [pltpu.make_async_copy(saved[a], saved_h[a], out_sem.at[i]) for i, a in enumerate(SAVED)]
    for c in stores:
        c.start()
    for c in stores:
        c.wait()


def forward(x, wqkv, wout, w1, w2, vectors, b1, mask):
    n = len(SAVED)
    outs = pl.pallas_call(
        forward_kernel,
        out_shape=[IMAGE, PROBS, *SAVED.values()],
        in_specs=[ANY] * 5 + [VM, VM, VM],
        out_specs=[ANY] * (2 + n),
        scratch_shapes=[scratch(a) for a in SAVED.values()]
        + [scratch(a) for a in (x, wqkv, wout, w1, w2)]
        + [
            scratch(ACT),
            scratch(ACT),
            pltpu.VMEM((ROWS, 4 * D), BF16),
            pltpu.VMEM((2, 2, ROWS, ROWS), BF16),
            scratch(IMAGE),
            pltpu.SemaphoreType.DMA((5,)),
            pltpu.SemaphoreType.DMA((2,)),
            pltpu.SemaphoreType.DMA((n + 1,)),
        ],
        compiler_params=pltpu.CompilerParams(vmem_limit_bytes=VMEM_BYTES),
        name="forward",
    )(x, wqkv, wout, w1, w2, vectors, b1, mask)
    return outs[0], outs[1], dict(zip(SAVED, outs[2:]))


GRADS = dict(
    wqkv=jax.ShapeDtypeStruct((4, 1024, 768), BF16),
    wout=jax.ShapeDtypeStruct((8, 1024, 128), BF16),
    w1=jax.ShapeDtypeStruct((4, 1024, 1024), BF16),
    w2=jax.ShapeDtypeStruct((8, 4096, 128), BF16),
)


def send_tile(stage, sem, i, value, targets):
    slot = lax.rem(i, 2)

    def copies(s):
        return [
            pltpu.make_async_copy(
                stage.at[s] if w == 256 else stage.at[s, :, pl.ds(c, w)], ref, sem.at[s]
            )
            for ref, c, w in targets
        ]

    @pl.when(i >= 2)
    def _():
        pltpu.make_async_copy(stage.at[slot], stage.at[slot], sem.at[slot]).wait()

    stage[slot] = value
    for c in copies(slot):
        c.start()


def drain(stage, sem):
    for slot in range(2):
        pltpu.make_async_copy(stage.at[slot], stage.at[slot], sem.at[slot]).wait()


def backward_kernel(x_h, ct_h, wqkv_h, wout_h, w1_h, w2_h, vectors, mask, probs_h, *rest):
    n = len(SAVED)
    saved_h = dict(zip(SAVED, rest[:n]))
    gtok_h, sums_o = rest[n], rest[n + 1]
    g_h = dict(zip(GRADS, rest[n + 2 : n + 6]))
    rest = rest[n + 6 :]
    saved = dict(zip(SAVED, rest[:n]))
    (x, wqkv, wout, w1, w2, b1, gmlp, gattn, gctx, gn, gmix, probs, sums, part, stage,
     in_sem, probs_sem, tile_sem, saved_sem) = rest[n:]
    gtok = x
    names = dict(ct=(ct_h, gtok), x=(x_h, x), w2=(w2_h, w2), w1=(w1_h, w1), wout=(wout_h, wout), wqkv=(wqkv_h, wqkv))
    load = {a: pltpu.make_async_copy(*names[a], in_sem.at[i]) for i, a in enumerate(names)}
    load_saved = {a: pltpu.make_async_copy(saved_h[a], saved[a], saved_sem.at[i]) for i, a in enumerate(SAVED)}
    load["ct"].start()
    for a in ("act_t", "slope"):
        load_saved[a].start()
    for a in ("w2", "w1", "wout", "wqkv"):
        load[a].start()
    for a in SAVED:
        if a not in ("act_t", "slope"):
            load_saved[a].start()
    part[...] = jnp.zeros_like(part)
    sums[...] = jnp.zeros_like(sums)
    load["ct"].wait()

    @pl.loop(0, ROWS // STEP)
    def _(i):
        rows = pl.ds(pl.multiple_of(i * STEP, STEP), STEP)
        g = jnp.concatenate([x[t, rows, :].astype(F32) * mask[...] for t in range(4)], axis=1)
        gmlp[rows, :] = g.astype(BF16)
        part[0] += fold(g)

    load["x"].start()
    load_saved["act_t"].wait()

    @pl.loop(0, 16)
    def _(i):
        t, c = i // 4, i % 4
        r = mm(saved["act_t"][cols(t, 1024), :], gmlp[:, cols(c, 256)]).astype(BF16)
        send_tile(stage, tile_sem, i, r, [
            (g_h["w2"].at[2 * c + e, cols(t, 1024), :], e * 128, 128) for e in range(2)])

    load_saved["slope"].wait()
    load["w2"].wait()
    slope = saved["slope"]

    @pl.loop(0, 16)
    def _(i):
        w = jnp.concatenate([w2[d, cols(i, 256), :] for d in range(8)], axis=1)
        gpre = mm_t(gmlp[...], w) * slope[:, cols(i, 256)].astype(F32)
        slope[:, cols(i, 256)] = gpre.astype(BF16)
        b1[i // 4, :, cols(i % 4, 256)] = jnp.sum(gpre, axis=0, keepdims=True)

    load_saved["nmid_t"].wait()

    @pl.loop(0, 16)
    def _(i):
        r = mm(saved["nmid_t"][...], slope[:, cols(i, 256)]).astype(BF16)
        send_tile(stage, tile_sem, i + 16, r, [(g_h["w1"].at[i // 4, :, cols(i % 4, 256)], 0, 256)])

    load["w1"].wait()

    @pl.loop(0, 4)
    def _(i):
        total = mm_t(slope[:, 0:1024], w1[0, cols(i, 256), :])
        for t in range(1, 4):
            total += mm_t(slope[:, t * 1024 : t * 1024 + 1024], w1[t, cols(i, 256), :])
        gn[:, cols(i, 256)] = total

    load_saved["resid"].wait()
    gain2 = vec(vectors, 5)

    @pl.loop(0, ROWS // STEP)
    def _(i):
        rows = pl.ds(pl.multiple_of(i * STEP, STEP), STEP)
        normed = gn[rows, :]
        g, scaled = grad_norm_rows(saved["resid"][rows, :], gain2, normed)
        g = g + gmlp[rows, :].astype(F32)
        part[1] += fold(normed)
        part[2] += fold(scaled)
        part[3] += fold(g)
        gn[rows, :] = g
        gattn[rows, :] = g.astype(BF16)

    load["wout"].wait()
    load_saved["ctx_t"].wait()

    @pl.loop(0, 4)
    def _(i):
        w = jnp.concatenate([wout[d, cols(i, 256), :] for d in range(8)], axis=1)
        gctx[:, cols(i, 256)] = mm_t(gattn[...], w).astype(BF16)
        r = mm(saved["ctx_t"][...], gattn[:, cols(i, 256)]).astype(BF16)
        send_tile(stage, tile_sem, i + 32, r, [(g_h["wout"].at[2 * i + e], e * 128, 128) for e in range(2)])

    for a in ("q", "k", "v", "ctx"):
        load_saved[a].wait()

    def get(pair, slot):
        return pltpu.make_async_copy(probs_h.at[pair], probs.at[slot], probs_sem.at[slot])

    get(0, 0).start()

    @pl.loop(0, 8)
    def _(pair):
        slot = pair % 2

        @pl.when(pair < 7)
        def _():
            get(pair + 1, 1 - slot).start()

        get(pair, slot).wait()
        attend_back_pair(pair, saved["q"], saved["k"], saved["v"], saved["ctx"], gctx, probs, slot, gmix, sums)

    load_saved["nin_t"].wait()

    @pl.loop(0, 12)
    def _(i):
        t, c = i // 3, i % 3
        r = mm(saved["nin_t"][...], gmix[t, :, cols(c, 256)]).astype(BF16)
        send_tile(stage, tile_sem, i + 36, r, [(g_h["wqkv"].at[t, :, cols(c, 256)], 0, 256)])

    load["wqkv"].wait()
    resid = saved["resid"]

    @pl.loop(0, 4)
    def _(i):
        total = mm_t(gmix[0], wqkv[0, cols(i, 256), :])
        for t in range(1, 4):
            total += mm_t(gmix[t], wqkv[t, cols(i, 256), :])
        resid[:, cols(i, 256)] = total

    load["x"].wait()
    gain1 = vec(vectors, 0)

    @pl.loop(0, ROWS // STEP)
    def _(i):
        rows = pl.ds(pl.multiple_of(i * STEP, STEP), STEP)
        normed = resid[rows, :]
        g, scaled = grad_norm_rows(wide(x, rows), gain1, normed)
        g = g + gn[rows, :]
        part[4] += fold(normed)
        part[5] += fold(scaled)
        for t in range(4):
            gtok[t, rows, :] = g[:, t * 256 : t * 256 + 256].astype(BF16)

    for row, i in ((7, 0), (6, 1), (5, 2), (4, 3), (1, 4), (0, 5)):
        sums[row : row + 1, :] = jnp.sum(part[i], axis=0, keepdims=True)
    sums_o[0:8, :] = sums[...]
    for t in range(4):
        sums_o[8 + t : 9 + t, :] = b1[t]
    done = pltpu.make_async_copy(gtok, gtok_h, in_sem.at[0])
    done.start()
    done.wait()
    drain(stage, tile_sem)


def backward(x, ct, wqkv, wout, w1, w2, vectors, mask, probs, saved):
    n = len(SAVED)
    outs = pl.pallas_call(
        backward_kernel,
        out_shape=[IMAGE, jax.ShapeDtypeStruct((12, D), F32), *GRADS.values()],
        in_specs=[ANY] * 6 + [VM, VM, ANY] + [ANY] * n,
        out_specs=[ANY, VM] + [ANY] * 4,
        scratch_shapes=[scratch(a) for a in SAVED.values()]
        + [scratch(a) for a in (x, wqkv, wout, w1, w2)]
        + [
            pltpu.VMEM((4, 1, 1024), F32),
            scratch(ACT),
            scratch(ACT),
            scratch(ACT),
            pltpu.VMEM((ROWS, D), F32),
            pltpu.VMEM((4, ROWS, 768), BF16),
            pltpu.VMEM((2, 2, ROWS, ROWS), BF16),
            pltpu.VMEM((8, D), F32),
            pltpu.VMEM((6, 8, D), F32),
            pltpu.VMEM((2, 1024, 256), BF16),
            pltpu.SemaphoreType.DMA((6,)),
            pltpu.SemaphoreType.DMA((2,)),
            pltpu.SemaphoreType.DMA((2,)),
            pltpu.SemaphoreType.DMA((n,)),
        ],
        compiler_params=pltpu.CompilerParams(vmem_limit_bytes=VMEM_BYTES),
        name="backward",
    )(x, ct, wqkv, wout, w1, w2, vectors, mask, probs, *[saved[a] for a in SAVED])
    return outs[0], outs[1], dict(zip(GRADS, outs[2:]))


def gather_plain(w_qkv, w_out, w_fc1, w_fc2):
    def all_of(shard, axis):
        return lax.all_gather(
            lax.all_gather(shard.astype(BF16), "dp", axis=axis, tiled=True), "tensor", axis=0
        )

    wqkv = all_of(w_qkv.reshape(-1, 768), 0)
    wout = all_of(w_out, 1).reshape(D, 8, 128).transpose(1, 0, 2)
    w1 = all_of(w_fc1, 0)
    w2 = all_of(w_fc2, 1).reshape(4 * D, 8, 128).transpose(1, 0, 2)
    return wqkv, wout, w1, w2


def scatter_plain(grads):
    def mine(grad, axis):
        part = lax.psum_scatter(grad, "tensor", scatter_dimension=0, tiled=True)
        return lax.psum_scatter(part, "dp", scatter_dimension=axis, tiled=True).astype(F32)

    g_qkv = mine(grads["wqkv"], 1)[0]
    g_out = mine(grads["wout"].transpose(1, 0, 2).reshape(D, D), 1)
    g_fc1 = mine(grads["w1"], 1)[0]
    g_fc2 = mine(grads["w2"].transpose(1, 0, 2).reshape(4 * D, D), 1)
    return g_qkv, g_out, g_fc1, g_fc2


def on_device(
    tokens_in,
    cotangent,
    slot_mask,
    norm1_gain,
    norm1_bias,
    w_qkv,
    b_qkv,
    w_out,
    b_out,
    norm2_gain,
    norm2_bias,
    w_fc1,
    b_fc1,
    w_fc2,
    b_fc2,
):
    def images(rows):
        return jnp.pad(rows.reshape(4, SEQ, 256), ((0, 0), (0, ROWS - SEQ), (0, 0)))

    def exchange(pieces):
        return lax.all_to_all(pieces, "tensor", split_axis=0, concat_axis=0, tiled=True)

    mask = jnp.broadcast_to(
        lax.dynamic_index_in_dim(slot_mask, lax.axis_index("tensor"), 0).astype(F32), (1, 256)
    )
    small = jnp.concatenate(
        (norm1_gain, norm1_bias, b_qkv[0], b_qkv[1], b_out, norm2_gain, norm2_bias, b_fc2)
    ).astype(BF16)
    vectors = lax.all_gather(
        lax.all_gather(small, "dp", axis=1, tiled=True), "tensor", axis=0
    ).astype(F32)
    hidden_bias = lax.all_gather(
        lax.all_gather(b_fc1.astype(BF16), "dp", axis=1, tiled=True), "tensor", axis=0
    ).astype(F32)
    x = exchange(images(tokens_in))
    ct = exchange(images(cotangent))
    weights = gather_plain(w_qkv, w_out, w_fc1, w_fc2)
    out, probs, saved = forward(x, *weights, vectors, hidden_bias, mask)
    gtok, sums, grads = backward(x, ct, *weights, vectors, mask, probs, saved)
    g_qkv, g_out, g_fc1, g_fc2 = scatter_plain(grads)

    def total(part, axis):
        part = lax.psum_scatter(part, "tensor", scatter_dimension=0, tiled=True)
        return lax.psum_scatter(part, "dp", scatter_dimension=axis, tiled=True)

    g_small = total(sums[0:8].reshape(8, 4, 256).transpose(1, 0, 2), 2)[0]
    g_hidden = total(sums[8:12], 1)

    def rows(pieces):
        return pieces[:, :SEQ].reshape(4 * SEQ, 256)

    return (
        rows(exchange(out)),
        rows(exchange(gtok)),
        g_small[0:1],
        g_small[1:2],
        g_qkv.reshape(w_qkv.shape),
        g_small[2:4][:, None],
        g_out,
        g_small[4:5],
        g_small[5:6],
        g_small[6:7],
        g_fc1,
        g_hidden,
        g_fc2,
        g_small[7:8],
    )


def solution(mesh):
    both, turned = P("dp", "tensor"), P("tensor", "dp")
    mixed, pair = P("dp", None, "tensor"), P(None, "tensor", "dp")
    params = (turned, turned, mixed, pair, turned, turned, turned, turned, both, turned, turned, turned)
    return jax.shard_map(
        on_device,
        mesh=mesh,
        in_specs=(both, both, P("dp"), *params),
        out_specs=(both, both, *params),
        check_vma=False,
    )
```

```python
import functools
import jax
import jax.numpy as jnp
from jax import lax
from jax.experimental import pallas as pl
from jax.experimental.pallas import tpu as pltpu
from jax.sharding import PartitionSpec as P

D = 1024
HD = 64
SEQ = 577
ROWS = 592
STEP = 16
F32 = jnp.float32
BF16 = jnp.bfloat16
LAST = (((1,), (1,)), ((), ()))
VMEM_BYTES = 66_000_000


def mm(a, b):
    return jnp.dot(a, b, preferred_element_type=F32)


def mm_t(a, b):
    return lax.dot_general(a, b, LAST, preferred_element_type=F32)


def cols(i, n):
    return pl.ds(pl.multiple_of(i * n, n), n)


def row_stats(values):
    mean = jnp.sum(values, axis=1, keepdims=True) * (1.0 / D)
    centered = values - mean
    var = jnp.sum(centered * centered, axis=1, keepdims=True) * (1.0 / D)
    inv = lax.rsqrt(var + 1e-05)
    return centered * inv, inv


def wide(ref, rows):
    return jnp.concatenate([ref[t, rows, :].astype(F32) for t in range(4)], axis=1)


def vec(vectors, row):
    return jnp.concatenate([vectors[t, row : row + 1, :] for t in range(4)], axis=1)


def norm_in(x, vectors, nin):
    gain, shift = vec(vectors, 0), vec(vectors, 1)

    @pl.loop(0, ROWS // STEP)
    def _(i):
        rows = pl.ds(pl.multiple_of(i * STEP, STEP), STEP)
        xhat, _ = row_stats(wide(x, rows))
        nin[rows, :] = (xhat * gain + shift).astype(BF16)


def flip(src, dst, n):
    @pl.loop(0, n // 256)
    def _(i):
        dst[cols(i, 256), :] = src[:, cols(i, 256)].T


def project(nin, wqkv, vectors, t, q, k, v):
    here = pl.ds(t * 256, 256)
    q[:, here] = (mm(nin[...], wqkv[t, :, 0:256]) + vectors[t, 2:3, :]).astype(BF16)
    k[:, here] = mm(nin[...], wqkv[t, :, 256:512]).astype(BF16)
    v[:, here] = (mm(nin[...], wqkv[t, :, 512:768]) + vectors[t, 3:4, :]).astype(BF16)


def attend_pair(pair, q, k, v, ctx, probs, slot):
    here = cols(pair, 128)
    lane = lax.broadcasted_iota(jnp.int32, (ROWS, 128), 1)
    row = lax.broadcasted_iota(jnp.int32, (ROWS, 128), 0)
    queries = q[:, here].astype(F32) * (HD**-0.5)
    keys = k[:, here].astype(F32)
    values = v[:, here]
    blocked = jnp.where(row >= SEQ, -1e30, 0.0)
    parts = []
    for h in range(2):
        own = (lane < 64) if h == 0 else (lane >= 64)
        spare = 64 if h == 0 else 0
        qa = jnp.where(own, queries, jnp.where(lane == spare, 1.0, 0.0)).astype(BF16)
        ka = jnp.where(lane == spare, blocked, keys).astype(BF16)
        scores = mm_t(ka, qa)
        top = jnp.max(scores, axis=0, keepdims=True)
        e = jnp.exp(scores - top)
        total = jnp.sum(e, axis=0, keepdims=True)
        p = (e * (1.0 / total)).astype(BF16)
        probs[slot, h] = p
        parts.append(
            lax.dot_general(p, values, (((0,), (0,)), ((), ())), preferred_element_type=F32)
        )
    ctx[:, here] = jnp.where(lane < 64, parts[0], parts[1]).astype(BF16)


def out_block(i, ctx, wout, x, vectors, resid):
    w = jnp.concatenate([wout[2 * i], wout[2 * i + 1]], axis=1)
    resid[:, cols(i, 256)] = x[i].astype(F32) + mm(ctx[...], w) + vectors[i, 4:5, :]


def norm_mid(resid, vectors, nmid):
    gain, shift = vec(vectors, 5), vec(vectors, 6)

    @pl.loop(0, ROWS // STEP)
    def _(i):
        rows = pl.ds(pl.multiple_of(i * STEP, STEP), STEP)
        xhat, _ = row_stats(resid[rows, :])
        nmid[rows, :] = (xhat * gain + shift).astype(BF16)


def hidden_tile(t, j, nmid, w1, b1, act, act_t, slope):
    here = pl.ds(pl.multiple_of(t * 1024 + j * 256, 256), 256)
    bias = b1[t, :, cols(j, 256)]
    pre = mm(nmid[...], w1[t, :, cols(j, 256)]) + bias
    sig = 1.0 / (1.0 + jnp.exp(-1.702 * pre))
    a = pre * sig
    slope[:, here] = (sig + 1.702 * a * (1.0 - sig)).astype(BF16)
    low = a.astype(BF16)
    act[:, here] = low
    act_t[here, :] = low.T


def down_block(i, act, w2, resid, vectors, mask, out):
    w = jnp.concatenate([w2[2 * i], w2[2 * i + 1]], axis=1)
    total = resid[:, cols(i, 256)] + mm(act[...], w) + vectors[i, 7:8, :]
    out[i] = (total * mask[...]).astype(BF16)


def grad_norm_rows(values, gain, n):
    xhat, inv = row_stats(values)
    e = n * gain
    first = jnp.sum(e, axis=1, keepdims=True) * (1.0 / D)
    second = jnp.sum(e * xhat, axis=1, keepdims=True) * (1.0 / D)
    return inv * (e - first - xhat * second), n * xhat


def fold(a):
    return a[0:8] + a[8:16]


def attend_back_pair(pair, q, k, v, ctx, gctx, probs, slot, gmix, sums):
    here = cols(pair, 128)
    lane = lax.broadcasted_iota(jnp.int32, (ROWS, 128), 1)
    queries, keys, values = q[:, here], k[:, here], v[:, here].astype(F32)
    go = gctx[:, here]
    go_f = go.astype(F32)
    dots = go_f * ctx[:, here].astype(F32)
    dq, dk, dv = [], [], []
    for h in range(2):
        own = (lane < 64) if h == 0 else (lane >= 64)
        spare = 64 if h == 0 else 0
        delta = -jnp.sum(jnp.where(own, dots, 0.0), axis=1, keepdims=True)
        high = delta.astype(BF16).astype(F32)
        rest = delta - high
        ga = jnp.where(
            own, go_f, jnp.where(lane == spare, high, jnp.where(lane == spare + 1, rest, 0.0))
        ).astype(BF16)
        marks = jnp.where((lane == spare) | (lane == spare + 1), 1.0, 0.0)
        va = jnp.where(own, values, marks).astype(BF16)
        p = probs[slot, h]
        gs = (p.astype(F32) * mm_t(va, ga)).astype(BF16)
        dv.append(mm(p, go))
        dk.append(mm(gs, queries))
        dq.append(
            lax.dot_general(gs, keys, (((0,), (0,)), ((), ())), preferred_element_type=F32)
        )
    scale = HD**-0.5
    low = lane < 64
    gq = jnp.where(low, dq[0], dq[1]) * scale
    gk = jnp.where(low, dk[0], dk[1]) * scale
    gv = jnp.where(low, dv[0], dv[1])
    t, half = pair // 2, pair % 2
    at = [pl.ds(pl.multiple_of(c * 256 + half * 128, 128), 128) for c in range(3)]
    gmix[t, :, at[0]] = gq.astype(BF16)
    gmix[t, :, at[1]] = gk.astype(BF16)
    gmix[t, :, at[2]] = gv.astype(BF16)
    sums[2:3, here] = jnp.sum(gq, axis=0, keepdims=True)
    sums[3:4, here] = jnp.sum(gv, axis=0, keepdims=True)


ACT = jax.ShapeDtypeStruct((ROWS, D), BF16)
TURNED = jax.ShapeDtypeStruct((D, ROWS), BF16)
SAVED = dict(
    nin_t=TURNED,
    q=ACT,
    k=ACT,
    v=ACT,
    ctx=ACT,
    ctx_t=TURNED,
    nmid_t=TURNED,
    resid=jax.ShapeDtypeStruct((ROWS, D), F32),
    act_t=jax.ShapeDtypeStruct((4 * D, ROWS), BF16),
    slope=jax.ShapeDtypeStruct((ROWS, 4 * D), BF16),
)
PROBS = jax.ShapeDtypeStruct((8, 2, ROWS, ROWS), BF16)
IMAGE = jax.ShapeDtypeStruct((4, ROWS, 256), BF16)
ANY = pl.BlockSpec(memory_space=pl.ANY)
VM = pl.BlockSpec(memory_space=pltpu.VMEM)


def scratch(like):
    return pltpu.VMEM(like.shape, like.dtype)


def forward_kernel(x_h, wqkv_h, wout_h, w1_h, w2_h, vectors, b1, mask, *rest):
    n = len(SAVED)
    out_h, probs_h = rest[0], rest[1]
    saved_h = dict(zip(SAVED, rest[2 : 2 + n]))
    rest = rest[2 + n :]
    saved = dict(zip(SAVED, rest[:n]))
    x, wqkv, wout, w1, w2, nin, nmid, act, probs, out, in_sem, probs_sem, out_sem = rest[n:]
    loads = [
        pltpu.make_async_copy(a, b, in_sem.at[i])
        for i, (a, b) in enumerate(((x_h, x), (wqkv_h, wqkv), (wout_h, wout), (w1_h, w1), (w2_h, w2)))
    ]
    for c in loads:
        c.start()
    loads[0].wait()
    norm_in(x, vectors, nin)
    loads[1].wait()
    for t in range(4):
        project(nin, wqkv, vectors, t, saved["q"], saved["k"], saved["v"])
    flip(nin, saved["nin_t"], D)

    def put(pair, slot):
        return pltpu.make_async_copy(probs.at[slot], probs_h.at[pair], probs_sem.at[slot])

    @pl.loop(0, 8)
    def _(pair):
        slot = pair % 2

        @pl.when(pair >= 2)
        def _():
            put(pair - 2, slot).wait()

        attend_pair(pair, saved["q"], saved["k"], saved["v"], saved["ctx"], probs, slot)
        put(pair, slot).start()

    put(6, 0).wait()
    put(7, 1).wait()
    loads[2].wait()

    @pl.loop(0, 4)
    def _(i):
        out_block(i, saved["ctx"], wout, x, vectors, saved["resid"])

    norm_mid(saved["resid"], vectors, nmid)
    loads[3].wait()

    @pl.loop(0, 16)
    def _(i):
        hidden_tile(i // 4, i % 4, nmid, w1, b1, act, saved["act_t"], saved["slope"])

    flip(saved["ctx"], saved["ctx_t"], D)
    flip(nmid, saved["nmid_t"], D)
    loads[4].wait()

    @pl.loop(0, 4)
    def _(i):
        down_block(i, act, w2, saved["resid"], vectors, mask, out)

    stores = [pltpu.make_async_copy(out, out_h, out_sem.at[n])]
    stores += [pltpu.make_async_copy(saved[a], saved_h[a], out_sem.at[i]) for i, a in enumerate(SAVED)]
    for c in stores:
        c.start()
    for c in stores:
        c.wait()


def forward(x, wqkv, wout, w1, w2, vectors, b1, mask):
    n = len(SAVED)
    outs = pl.pallas_call(
        forward_kernel,
        out_shape=[IMAGE, PROBS, *SAVED.values()],
        in_specs=[ANY] * 5 + [VM, VM, VM],
        out_specs=[ANY] * (2 + n),
        scratch_shapes=[scratch(a) for a in SAVED.values()]
        + [scratch(a) for a in (x, wqkv, wout, w1, w2)]
        + [
            scratch(ACT),
            scratch(ACT),
            pltpu.VMEM((ROWS, 4 * D), BF16),
            pltpu.VMEM((2, 2, ROWS, ROWS), BF16),
            scratch(IMAGE),
            pltpu.SemaphoreType.DMA((5,)),
            pltpu.SemaphoreType.DMA((2,)),
            pltpu.SemaphoreType.DMA((n + 1,)),
        ],
        compiler_params=pltpu.CompilerParams(vmem_limit_bytes=VMEM_BYTES),
        name="forward",
    )(x, wqkv, wout, w1, w2, vectors, b1, mask)
    return outs[0], outs[1], dict(zip(SAVED, outs[2:]))


GRADS = dict(
    wqkv=jax.ShapeDtypeStruct((4, 1024, 768), BF16),
    wout=jax.ShapeDtypeStruct((8, 1024, 128), BF16),
    w1=jax.ShapeDtypeStruct((4, 1024, 1024), BF16),
    w2=jax.ShapeDtypeStruct((8, 4096, 128), BF16),
)


def send_tile(stage, sem, i, value, targets):
    slot = lax.rem(i, 2)

    def copies(s):
        return [
            pltpu.make_async_copy(
                stage.at[s] if w == 256 else stage.at[s, :, pl.ds(c, w)], ref, sem.at[s]
            )
            for ref, c, w in targets
        ]

    @pl.when(i >= 2)
    def _():
        pltpu.make_async_copy(stage.at[slot], stage.at[slot], sem.at[slot]).wait()

    stage[slot] = value
    for c in copies(slot):
        c.start()


def drain(stage, sem):
    for slot in range(2):
        pltpu.make_async_copy(stage.at[slot], stage.at[slot], sem.at[slot]).wait()


def backward_kernel(x_h, ct_h, wqkv_h, wout_h, w1_h, w2_h, vectors, mask, probs_h, *rest):
    n = len(SAVED)
    saved_h = dict(zip(SAVED, rest[:n]))
    gtok_h, sums_o = rest[n], rest[n + 1]
    g_h = dict(zip(GRADS, rest[n + 2 : n + 6]))
    rest = rest[n + 6 :]
    saved = dict(zip(SAVED, rest[:n]))
    (x, wqkv, wout, w1, w2, b1, gmlp, gattn, gctx, gn, gmix, probs, sums, part, stage,
     in_sem, probs_sem, tile_sem, saved_sem) = rest[n:]
    gtok = x
    names = dict(ct=(ct_h, gtok), x=(x_h, x), w2=(w2_h, w2), w1=(w1_h, w1), wout=(wout_h, wout), wqkv=(wqkv_h, wqkv))
    load = {a: pltpu.make_async_copy(*names[a], in_sem.at[i]) for i, a in enumerate(names)}
    load_saved = {a: pltpu.make_async_copy(saved_h[a], saved[a], saved_sem.at[i]) for i, a in enumerate(SAVED)}
    load["ct"].start()
    for a in ("act_t", "slope"):
        load_saved[a].start()
    for a in ("w2", "w1", "wout", "wqkv"):
        load[a].start()
    for a in SAVED:
        if a not in ("act_t", "slope"):
            load_saved[a].start()
    part[...] = jnp.zeros_like(part)
    sums[...] = jnp.zeros_like(sums)
    load["ct"].wait()

    @pl.loop(0, ROWS // STEP)
    def _(i):
        rows = pl.ds(pl.multiple_of(i * STEP, STEP), STEP)
        g = jnp.concatenate([x[t, rows, :].astype(F32) * mask[...] for t in range(4)], axis=1)
        gmlp[rows, :] = g.astype(BF16)
        part[0] += fold(g)

    load["x"].start()
    load_saved["act_t"].wait()

    @pl.loop(0, 16)
    def _(i):
        t, c = i // 4, i % 4
        r = mm(saved["act_t"][cols(t, 1024), :], gmlp[:, cols(c, 256)]).astype(BF16)
        send_tile(stage, tile_sem, i, r, [
            (g_h["w2"].at[2 * c + e, cols(t, 1024), :], e * 128, 128) for e in range(2)])

    load_saved["slope"].wait()
    load["w2"].wait()
    slope = saved["slope"]

    @pl.loop(0, 16)
    def _(i):
        w = jnp.concatenate([w2[d, cols(i, 256), :] for d in range(8)], axis=1)
        gpre = mm_t(gmlp[...], w) * slope[:, cols(i, 256)].astype(F32)
        slope[:, cols(i, 256)] = gpre.astype(BF16)
        b1[i // 4, :, cols(i % 4, 256)] = jnp.sum(gpre, axis=0, keepdims=True)

    load_saved["nmid_t"].wait()

    @pl.loop(0, 16)
    def _(i):
        r = mm(saved["nmid_t"][...], slope[:, cols(i, 256)]).astype(BF16)
        send_tile(stage, tile_sem, i + 16, r, [(g_h["w1"].at[i // 4, :, cols(i % 4, 256)], 0, 256)])

    load["w1"].wait()

    @pl.loop(0, 4)
    def _(i):
        total = mm_t(slope[:, 0:1024], w1[0, cols(i, 256), :])
        for t in range(1, 4):
            total += mm_t(slope[:, t * 1024 : t * 1024 + 1024], w1[t, cols(i, 256), :])
        gn[:, cols(i, 256)] = total

    load_saved["resid"].wait()
    gain2 = vec(vectors, 5)

    @pl.loop(0, ROWS // STEP)
    def _(i):
        rows = pl.ds(pl.multiple_of(i * STEP, STEP), STEP)
        normed = gn[rows, :]
        g, scaled = grad_norm_rows(saved["resid"][rows, :], gain2, normed)
        g = g + gmlp[rows, :].astype(F32)
        part[1] += fold(normed)
        part[2] += fold(scaled)
        part[3] += fold(g)
        gn[rows, :] = g
        gattn[rows, :] = g.astype(BF16)

    load["wout"].wait()
    load_saved["ctx_t"].wait()

    @pl.loop(0, 4)
    def _(i):
        w = jnp.concatenate([wout[d, cols(i, 256), :] for d in range(8)], axis=1)
        gctx[:, cols(i, 256)] = mm_t(gattn[...], w).astype(BF16)
        r = mm(saved["ctx_t"][...], gattn[:, cols(i, 256)]).astype(BF16)
        send_tile(stage, tile_sem, i + 32, r, [(g_h["wout"].at[2 * i + e], e * 128, 128) for e in range(2)])

    for a in ("q", "k", "v", "ctx"):
        load_saved[a].wait()

    def get(pair, slot):
        return pltpu.make_async_copy(probs_h.at[pair], probs.at[slot], probs_sem.at[slot])

    get(0, 0).start()

    @pl.loop(0, 8)
    def _(pair):
        slot = pair % 2

        @pl.when(pair < 7)
        def _():
            get(pair + 1, 1 - slot).start()

        get(pair, slot).wait()
        attend_back_pair(pair, saved["q"], saved["k"], saved["v"], saved["ctx"], gctx, probs, slot, gmix, sums)

    load_saved["nin_t"].wait()

    @pl.loop(0, 12)
    def _(i):
        t, c = i // 3, i % 3
        r = mm(saved["nin_t"][...], gmix[t, :, cols(c, 256)]).astype(BF16)
        send_tile(stage, tile_sem, i + 36, r, [(g_h["wqkv"].at[t, :, cols(c, 256)], 0, 256)])

    load["wqkv"].wait()
    resid = saved["resid"]

    @pl.loop(0, 4)
    def _(i):
        total = mm_t(gmix[0], wqkv[0, cols(i, 256), :])
        for t in range(1, 4):
            total += mm_t(gmix[t], wqkv[t, cols(i, 256), :])
        resid[:, cols(i, 256)] = total

    load["x"].wait()
    gain1 = vec(vectors, 0)

    @pl.loop(0, ROWS // STEP)
    def _(i):
        rows = pl.ds(pl.multiple_of(i * STEP, STEP), STEP)
        normed = resid[rows, :]
        g, scaled = grad_norm_rows(wide(x, rows), gain1, normed)
        g = g + gn[rows, :]
        part[4] += fold(normed)
        part[5] += fold(scaled)
        for t in range(4):
            gtok[t, rows, :] = g[:, t * 256 : t * 256 + 256].astype(BF16)

    for row, i in ((7, 0), (6, 1), (5, 2), (4, 3), (1, 4), (0, 5)):
        sums[row : row + 1, :] = jnp.sum(part[i], axis=0, keepdims=True)
    sums_o[0:8, :] = sums[...]
    for t in range(4):
        sums_o[8 + t : 9 + t, :] = b1[t]
    done = pltpu.make_async_copy(gtok, gtok_h, in_sem.at[0])
    done.start()
    done.wait()
    drain(stage, tile_sem)


def backward(x, ct, wqkv, wout, w1, w2, vectors, mask, probs, saved):
    n = len(SAVED)
    outs = pl.pallas_call(
        backward_kernel,
        out_shape=[IMAGE, jax.ShapeDtypeStruct((12, D), F32), *GRADS.values()],
        in_specs=[ANY] * 6 + [VM, VM, ANY] + [ANY] * n,
        out_specs=[ANY, VM] + [ANY] * 4,
        scratch_shapes=[scratch(a) for a in SAVED.values()]
        + [scratch(a) for a in (x, wqkv, wout, w1, w2)]
        + [
            pltpu.VMEM((4, 1, 1024), F32),
            scratch(ACT),
            scratch(ACT),
            scratch(ACT),
            pltpu.VMEM((ROWS, D), F32),
            pltpu.VMEM((4, ROWS, 768), BF16),
            pltpu.VMEM((2, 2, ROWS, ROWS), BF16),
            pltpu.VMEM((8, D), F32),
            pltpu.VMEM((6, 8, D), F32),
            pltpu.VMEM((2, 1024, 256), BF16),
            pltpu.SemaphoreType.DMA((6,)),
            pltpu.SemaphoreType.DMA((2,)),
            pltpu.SemaphoreType.DMA((2,)),
            pltpu.SemaphoreType.DMA((n,)),
        ],
        compiler_params=pltpu.CompilerParams(vmem_limit_bytes=VMEM_BYTES),
        name="backward",
    )(x, ct, wqkv, wout, w1, w2, vectors, mask, probs, *[saved[a] for a in SAVED])
    return outs[0], outs[1], dict(zip(GRADS, outs[2:]))


MESH = pl.DeviceIdType.MESH
PARTS = dict(
    sv=((4, 4, 2, 16, 256), F32),
    wqkv=((4, 4, 2, 128, 768), BF16),
    wout=((4, 2, 4, 256, 128), BF16),
    w1=((4, 4, 2, 128, 1024), BF16),
    w2=((4, 2, 4, 1024, 128), BF16),
)
BY_COLUMN = ("wout", "w2")


def block_of(name, ref, t, yx, c):
    return ref.at[yx, c, t] if name in BY_COLUMN else ref.at[t, yx, c]


def half_of(ref, h):
    n = ref.shape[0] // 2
    return ref.at[pl.ds(h * n, n)]


class Place:
    def __init__(self):
        d, self.t = lax.axis_index("dp"), lax.axis_index("tensor")
        self.y, self.x, self.c = d // 4, d // 2 % 2, d % 2
        self.yx = d // 2
        self.x_yx = self.y * 2 + 1 - self.x
        self.y_yx = (1 - self.y) * 2 + self.x
        self.xy_yx = (1 - self.y) * 2 + 1 - self.x
        self.d = d
        self.x_id = (self.x_yx * 2 + self.c, self.t)
        self.y_id = (self.y_yx * 2 + self.c, self.t)
        self.c_id = (self.yx * 2 + 1 - self.c, self.t)

    def z_id(self, t):
        return (self.d, t)

    def greet(self):
        barrier = pltpu.get_barrier_semaphore()
        others = [self.x_id, self.y_id, self.c_id]
        others += [self.z_id(lax.rem(self.t + k, 4)) for k in (1, 2, 3)]
        for other in others:
            pl.semaphore_signal(barrier, inc=1, device_id=other, device_id_type=MESH)
        pl.semaphore_wait(barrier, 6)


def remote(src, dst, send, recv, where):
    return pltpu.make_async_remote_copy(
        src_ref=src, dst_ref=dst, send_sem=send, recv_sem=recv, device_id=where, device_id_type=MESH
    )


class Gather:
    SENDS = 2 * 3 + 4 * 6 + 4

    def __init__(self, place, name, own, whole, sems):
        self.p, self.name, self.own, self.whole = place, name, own, whole
        self.z_send, self.z_recv, self.xy_send, self.xy_recv, self.c_send, self.c_recv = sems

    def at(self, t, yx):
        return block_of(self.name, self.whole, t, yx, self.p.c)

    def z_copy(self, up, step):
        p = self.p
        s = p.t - (step - 1) if up else p.t + (step - 1)
        src = self.own if step == 1 else self.at(s, p.yx)
        dst = self.at(s, p.yx)
        to = p.t + 1 if up else p.t - 1
        return remote(src, dst, self.z_send.at[1 - up, step - 1], self.z_recv.at[s], p.z_id(to))

    def z_sends(self, step, act):
        p = self.p
        for up in (1, 0):
            going = (p.t < 3) & (p.t - (step - 1) >= 0) if up else (p.t > 0) & (p.t + (step - 1) <= 3)

            @pl.when(going)
            def _():
                c = self.z_copy(up, step)
                c.start() if act == "start" else c.wait_send()

    def xy_copy(self, k, s, mine=False):
        p = self.p
        yx = (p.yx, p.yx, p.yx, p.x_yx, p.yx, p.y_yx)[k]
        h = (0, 1, 0, 0, 1, 1)[k]
        to = (p.x_id, p.y_id, p.y_id, p.y_id, p.x_id, p.x_id)[k]
        dst = half_of(self.at(s, yx), h)
        src = half_of(self.own, h) if mine else dst
        return remote(src, dst, self.xy_send.at[s, k], self.xy_recv.at[s, k], to)

    def first(self, s, mine=False):
        for k in (0, 1):
            self.xy_copy(k, s, mine).start()

    def second(self, s, mine=False):
        for got, own, other in ((0, 2, 3), (1, 4, 5)):
            self.xy_copy(own, s, mine).start()
            self.xy_copy(got, s).wait_recv()
            self.xy_copy(other, s).start()

    def core_copy(self, s):
        c = self.p.c
        ref = self.whole.at[:, c, s] if self.name in BY_COLUMN else self.whole.at[s, :, c]
        return remote(ref, ref, self.c_send.at[s], self.c_recv.at[s], self.p.c_id)

    def last(self, s):
        for k in (2, 3, 4, 5):
            self.xy_copy(k, s).wait_recv()
        self.core_copy(s).start()

    def each(self, step, do):
        p = self.p
        if step == 0:
            do(p.t)
            return

        @pl.when(p.t - step >= 0)
        def _():
            do(p.t - step)

        @pl.when(p.t + step <= 3)
        def _():
            do(p.t + step)

    def stage(self, i):
        if i == 0:
            self.z_sends(1, "start")
            self.first(self.p.t, True)
        if 1 <= i <= 3:

            def arrived(s):
                remote(
                    self.at(s, self.p.yx), self.at(s, self.p.yx), self.z_send.at[0, 0], self.z_recv.at[s], self.p.c_id
                ).wait_recv()

            self.each(i, arrived)
            if i < 3:
                self.z_sends(i + 1, "start")
            self.each(i, self.first)
        if 1 <= i <= 4:
            self.each(i - 1, functools.partial(self.second, mine=i == 1))
        if 2 <= i <= 5:
            self.each(i - 2, self.last)

    def done(self):
        for s in range(4):
            self.core_copy(s).wait_recv()

    def finish(self):
        for step in (1, 2, 3):
            self.z_sends(step, "wait")
        for s in range(4):
            for k in range(6):
                self.xy_copy(k, s).wait_send()
            self.core_copy(s).wait_send()


GATHER_SEMS = [
    pltpu.SemaphoreType.DMA((2, 3)),
    pltpu.SemaphoreType.DMA((4,)),
    pltpu.SemaphoreType.DMA((4, 6)),
    pltpu.SemaphoreType.DMA((4, 6)),
    pltpu.SemaphoreType.DMA((4,)),
    pltpu.SemaphoreType.DMA((4,)),
]


class Swap:
    SEMS = [pltpu.SemaphoreType.DMA((4,)), pltpu.SemaphoreType.DMA((4,))]

    def __init__(self, place, pieces, whole, sems):
        self.p, self.pieces, self.whole = place, pieces, whole
        self.send, self.recv = sems

    def copy(self, k):
        p = self.p
        to = lax.rem(p.t + k, 4)
        return remote(self.pieces.at[to], self.whole.at[p.t], self.send.at[k], self.recv.at[k], p.z_id(to))

    def start(self):
        for k in (1, 3, 2):
            self.copy(k).start()

    def done(self):
        for k in (1, 2, 3):
            self.copy(k).wait_recv()

    def finish(self):
        for k in (1, 2, 3):
            self.copy(k).wait_send()


class Bounce:
    def __init__(self, src, buf, dst, sems):
        self.load = pltpu.make_async_copy(src, buf, sems.at[0])
        self.store = pltpu.make_async_copy(buf, dst, sems.at[1])


def gather_kernel(x_in, ct_in, *rest):
    names = list(PARTS)
    n = len(names)
    own = dict(zip(names, rest[:n]))
    x, ct = rest[n : n + 2]
    whole = dict(zip(names, rest[n + 2 : 2 * n + 2]))
    rest = rest[2 * n + 2 :]
    bufs, (x_buf, ct_buf) = dict(zip(names, rest[:n])), rest[n : n + 2]
    rest = rest[n + 2 :]
    local_sem, swap_sems, sems = rest[0], rest[1:5], rest[5:]
    place = Place()
    gathers = [
        Gather(place, a, own[a], whole[a], sems[6 * i : 6 * i + 6]) for i, a in enumerate(names)
    ]
    swaps = [Swap(place, x_in, x, swap_sems[0:2]), Swap(place, ct_in, ct, swap_sems[2:4])]
    local = [
        Bounce(own[a], bufs[a], block_of(a, whole[a], place.t, place.yx, place.c), local_sem.at[i])
        for i, a in enumerate(names)
    ]
    local += [
        Bounce(x_in.at[place.t], x_buf, x.at[place.t], local_sem.at[n]),
        Bounce(ct_in.at[place.t], ct_buf, ct.at[place.t], local_sem.at[n + 1]),
    ]
    for b in local:
        b.load.start()
    place.greet()
    for b in local:
        b.load.wait()
        b.store.start()
    swaps[0].start()
    stored = False
    for tick in range(n + 5):
        for i, g in enumerate(gathers):
            if tick - i == 2 and not stored:
                for b in local:
                    b.store.wait()
                stored = True
            if 0 <= tick - i <= 5:
                g.stage(tick - i)
        if tick == 3:
            swaps[1].start()
    for g in gathers:
        g.done()
    for s in swaps:
        s.done()
        s.finish()
    for g in gathers:
        g.finish()


def gather(x_in, ct_in, own):
    names = list(PARTS)
    n = len(names)
    outs = pl.pallas_call(
        gather_kernel,
        out_shape=[IMAGE, IMAGE] + [jax.ShapeDtypeStruct(*PARTS[a]) for a in names],
        in_specs=[ANY] * (n + 2),
        out_specs=[ANY] * (n + 2),
        scratch_shapes=[pltpu.VMEM(PARTS[a][0][3:], PARTS[a][1]) for a in names]
        + [pltpu.VMEM((ROWS, 256), BF16)] * 2
        + [pltpu.SemaphoreType.DMA((n + 2, 2))]
        + Swap.SEMS * 2
        + GATHER_SEMS * n,
        compiler_params=pltpu.CompilerParams(
            collective_id=0, has_side_effects=True, vmem_limit_bytes=VMEM_BYTES
        ),
        name="gather",
    )(x_in, ct_in, *[own[a] for a in names])
    return outs[0], outs[1], dict(zip(names, outs[2:]))


REDUCED = ("w2", "w1", "wout", "wqkv")


class Reduce:
    def __init__(self, place, name, grad, own, got, got1, got2, got3, result, sems):
        self.p, self.name, self.grad, self.own, self.got = place, name, grad, own, got
        self.got1, self.got2, self.got3, self.result = got1, got2, got3, result
        self.send, self.recv, self.local = sems

    def plane(self, c):
        return self.grad.at[:, c] if self.name in BY_COLUMN else self.grad.at[:, :, c]

    def block(self, ref, t, yx):
        return ref.at[yx, t] if self.name in BY_COLUMN else ref.at[t, yx]

    def core_copy(self):
        return remote(self.plane(1 - self.p.c), self.got, self.send.at[0], self.recv.at[0], self.p.c_id)

    def own_copy(self):
        return pltpu.make_async_copy(self.plane(self.p.c), self.own, self.local)

    def add(self, dst, *more):
        rows = dst.shape[0]
        n = min(64, rows)

        @pl.loop(0, rows // n)
        def _(i):
            r = pl.ds(pl.multiple_of(i * n, n), n)
            total = dst[r, :].astype(F32)
            for ref in more:
                total += ref[r, :].astype(F32)
            dst[r, :] = total.astype(BF16)

    def first_copy(self, by_y, j, t):
        p = self.p
        yx = (1 - p.y) * 2 + j if by_y else j * 2 + 1 - p.x
        src = half_of(self.block(self.own, t, yx), 0 if by_y else 1)
        k = (0 if by_y else 2) + j
        n = 1 + k * 4 + t
        return remote(src, self.got1.at[k, t], self.send.at[n], self.recv.at[n], p.y_id if by_y else p.x_id)

    def second_copy(self, j, t):
        p = self.p
        by_x = j == 0
        src = half_of(self.block(self.own, t, p.x_yx if by_x else p.y_yx), j)
        return remote(src, self.got2.at[j, t], self.send.at[17 + j * 4 + t], self.recv.at[17 + j * 4 + t],
                      p.x_id if by_x else p.y_id)

    def z_copy(self, k):
        p = self.p
        to = lax.rem(p.t + k, 4)
        src = self.block(self.own, to, p.yx)
        return remote(src, self.got3.at[k - 1], self.send.at[24 + k], self.recv.at[24 + k], p.z_id(to))

    def stage(self, i):
        p = self.p
        if i == 0:
            self.core_copy().start()
            self.own_copy().start()
        if i == 1:
            self.own_copy().wait()
            self.core_copy().wait_recv()
            self.sum_core()
        if i == 2:
            self.sum_first()
        if i == 3:
            self.sum_second()
        if i == 4:
            self.sum_last()

    def sum_core(self):
        p = self.p
        for yx, by_y, by_x in ((p.xy_yx, 1 - p.x, 1 - p.y), (p.y_yx, p.x, None), (p.x_yx, None, p.y), (p.yx, None, None)):
            for t in range(4):
                self.add(self.block(self.own, t, yx), self.block(self.got, t, yx))
                if by_y is not None:
                    self.first_copy(True, by_y, t).start()
                if by_x is not None:
                    self.first_copy(False, by_x, t).start()

    def sum_first(self):
        p = self.p
        for t in range(4):
            for j in range(2):
                self.first_copy(True, j, t).wait_recv()
                self.first_copy(False, j, t).wait_recv()
        for t in range(4):
            self.add(half_of(self.block(self.own, t, p.x_yx), 0), self.got1.at[1 - p.x, t])
            self.second_copy(0, t).start()
            self.add(half_of(self.block(self.own, t, p.y_yx), 1), self.got1.at[2 + 1 - p.y, t])
            self.second_copy(1, t).start()
        for t in range(4):
            self.add(half_of(self.block(self.own, t, p.yx), 0), self.got1.at[p.x, t])
            self.add(half_of(self.block(self.own, t, p.yx), 1), self.got1.at[2 + p.y, t])

    def sum_second(self):
        p = self.p
        for k in (1, 2, 3, 0):
            t = lax.rem(p.t + k, 4)
            for j in (0, 1):
                self.second_copy(j, t).wait_recv()
                self.add(half_of(self.block(self.own, t, p.yx), j), self.got2.at[j, t])
            if k:
                self.z_copy(k).start()

    def sum_last(self):
        p = self.p
        for k in (1, 2, 3):
            self.z_copy(k).wait_recv()
        mine = self.block(self.own, p.t, p.yx)
        rows = mine.shape[0]

        @pl.loop(0, rows // 64)
        def _(i):
            r = pl.ds(pl.multiple_of(i * 64, 64), 64)
            total = mine[r, :].astype(F32)
            for k in range(3):
                total += self.got3[k, r, :].astype(F32)
            self.result[r, :] = total

    def finish(self):
        self.core_copy().wait_send()
        for t in range(4):
            for j in range(2):
                self.first_copy(True, j, t).wait_send()
                self.first_copy(False, j, t).wait_send()
                self.second_copy(j, t).wait_send()
        for k in (1, 2, 3):
            self.z_copy(k).wait_send()


def reduce_shapes(name):
    shape = PARTS[name][0]
    rows, width = shape[3:]
    plane = (4, 4, rows, width)
    return plane, (4, 4, rows // 2, width), (2, 4, rows // 2, width), (3, rows, width), (rows, width)


class Total:
    def __init__(self, place, acc, sent, got, sems):
        self.p, self.acc, self.sent, self.got = place, acc, sent, got
        self.send, self.recv = sems

    def copies(self, i):
        p = self.p
        if i < 3:
            return [remote(self.sent.at[i], self.got.at[i], self.send.at[i], self.recv.at[i], (p.c_id, p.x_id, p.y_id)[i])]
        return [
            remote(self.sent.at[3], self.got.at[2 + k], self.send.at[2 + k], self.recv.at[2 + k], p.z_id(lax.rem(p.t + k, 4)))
            for k in (1, 2, 3)
        ]

    def start(self, i):
        self.sent[i] = self.acc[...]
        for c in self.copies(i):
            c.start()

    def end(self, i):
        for c in self.copies(i):
            c.wait()
        for k in (i,) if i < 3 else (3, 4, 5):
            self.acc[...] += self.got[k]


def reduce_kernel(out_in, gtok_in, sums_in, *rest):
    n = len(REDUCED)
    grads = dict(zip(REDUCED, rest[:n]))
    out, gtok, sums = rest[n : n + 3]
    results = dict(zip(REDUCED, rest[n + 3 : 2 * n + 3]))
    rest = rest[2 * n + 3 :]
    out_buf, gtok_buf, sent, got = rest[:4]
    local_sem, total_send, total_recv = rest[4:7]
    swap_sems = rest[7:11]
    rest = rest[11:]
    place = Place()
    parts = []
    for i, a in enumerate(REDUCED):
        own, got0, got1, got2, got3, send, recv, local = rest[8 * i : 8 * i + 8]
        parts.append(Reduce(place, a, grads[a], own, got0, got1, got2, got3, results[a], (send, recv, local)))
    swaps = [Swap(place, out_in, out, swap_sems[0:2]), Swap(place, gtok_in, gtok, swap_sems[2:4])]
    local = [
        Bounce(out_in.at[place.t], out_buf, out.at[place.t], local_sem.at[0]),
        Bounce(gtok_in.at[place.t], gtok_buf, gtok.at[place.t], local_sem.at[1]),
    ]
    for b in local:
        b.load.start()
    place.greet()
    for r in parts:
        r.stage(0)
    total = Total(place, sums, sent, got, (total_send, total_recv))
    sums[...] = sums_in[...]
    total.start(0)
    for b in local:
        b.load.wait()
        b.store.start()
    for s in swaps:
        s.start()
    small = 0
    for tick in range(1, n + 4):
        for i, r in enumerate(parts):
            if 1 <= tick - i <= 4:
                r.stage(tick - i)
        if small < 4:
            total.end(small)
            small += 1
            if small < 4:
                total.start(small)
    for b in local:
        b.store.wait()
    for s in swaps:
        s.done()
        s.finish()
    for r in parts:
        r.finish()


def reduce(out, gtok, sums, grads):
    n = len(REDUCED)
    shapes = [reduce_shapes(a) for a in REDUCED]
    outs = pl.pallas_call(
        reduce_kernel,
        out_shape=[IMAGE, IMAGE, jax.ShapeDtypeStruct((16, D), F32)]
        + [jax.ShapeDtypeStruct(s[4], F32) for s in shapes],
        in_specs=[ANY, ANY, VM] + [ANY] * n,
        out_specs=[ANY, ANY, VM] + [VM] * n,
        scratch_shapes=[pltpu.VMEM((ROWS, 256), BF16)] * 2
        + [pltpu.VMEM((4, 16, D), F32), pltpu.VMEM((6, 16, D), F32)]
        + [pltpu.SemaphoreType.DMA((2, 2)), pltpu.SemaphoreType.DMA((6,)), pltpu.SemaphoreType.DMA((6,))]
        + Swap.SEMS * 2
        + sum(
            (
                [pltpu.VMEM(s[0], BF16)] * 2
                + [pltpu.VMEM(s[k], BF16) for k in (1, 2, 3)]
                + [pltpu.SemaphoreType.DMA((28,)), pltpu.SemaphoreType.DMA((28,)), pltpu.SemaphoreType.DMA]
                for s in shapes
            ),
            [],
        ),
        compiler_params=pltpu.CompilerParams(
            collective_id=1, has_side_effects=True, vmem_limit_bytes=VMEM_BYTES
        ),
        name="reduce",
    )(out, gtok, sums, *[grads[a].reshape(PARTS[a][0]) for a in REDUCED])
    return outs[0], outs[1], outs[2], dict(zip(REDUCED, outs[3:]))
def gather_plain(w_qkv, w_out, w_fc1, w_fc2):
    def all_of(shard, axis):
        return lax.all_gather(
            lax.all_gather(shard.astype(BF16), "dp", axis=axis, tiled=True), "tensor", axis=0
        )

    wqkv = all_of(w_qkv.reshape(-1, 768), 0)
    wout = all_of(w_out, 1).reshape(D, 8, 128).transpose(1, 0, 2)
    w1 = all_of(w_fc1, 0)
    w2 = all_of(w_fc2, 1).reshape(4 * D, 8, 128).transpose(1, 0, 2)
    return wqkv, wout, w1, w2


def scatter_plain(grads):
    def mine(grad, axis):
        part = lax.psum_scatter(grad, "tensor", scatter_dimension=0, tiled=True)
        return lax.psum_scatter(part, "dp", scatter_dimension=axis, tiled=True).astype(F32)

    g_qkv = mine(grads["wqkv"], 1)[0]
    g_out = mine(grads["wout"].transpose(1, 0, 2).reshape(D, D), 1)
    g_fc1 = mine(grads["w1"], 1)[0]
    g_fc2 = mine(grads["w2"].transpose(1, 0, 2).reshape(4 * D, D), 1)
    return g_qkv, g_out, g_fc1, g_fc2


def on_device(
    dp,
    tokens_in,
    cotangent,
    slot_mask,
    norm1_gain,
    norm1_bias,
    w_qkv,
    b_qkv,
    w_out,
    b_out,
    norm2_gain,
    norm2_bias,
    w_fc1,
    b_fc1,
    w_fc2,
    b_fc2,
):
    def images(rows):
        return jnp.pad(rows.reshape(4, SEQ, 256), ((0, 0), (0, ROWS - SEQ), (0, 0)))

    def exchange(pieces):
        return lax.all_to_all(pieces, "tensor", split_axis=0, concat_axis=0, tiled=True)

    mask = jnp.broadcast_to(
        lax.dynamic_index_in_dim(slot_mask, lax.axis_index("tensor"), 0).astype(F32), (1, 256)
    )
    small = jnp.concatenate(
        (norm1_gain, norm1_bias, b_qkv[0], b_qkv[1], b_out, norm2_gain, norm2_bias, b_fc2)
    ).astype(BF16)
    d, t = lax.axis_index("dp"), lax.axis_index("tensor")
    if dp == 8:
        sv = lax.dynamic_update_slice(jnp.zeros((16, 256), F32), small.astype(F32), (0, d * 32))
        sv = sv.at[8, 0:128].set(b_fc1[0].astype(BF16).astype(F32))
        own = dict(
            sv=sv,
            wqkv=w_qkv.reshape(128, 768).astype(BF16),
            wout=w_out.astype(BF16),
            w1=w_fc1.astype(BF16),
            w2=w_fc2.astype(BF16),
        )
        x, ct, whole = gather(images(tokens_in), images(cotangent), own)
        vectors = jnp.sum(whole["sv"][:, :, :, 0:8], axis=(1, 2))
        hidden_bias = whole["sv"][:, :, :, 8, 0:128].reshape(4, 1, 1024)
        weights = [whole[a].reshape(GRADS[a].shape) for a in GRADS]
    else:
        vectors = lax.all_gather(
            lax.all_gather(small, "dp", axis=1, tiled=True), "tensor", axis=0
        ).astype(F32)
        hidden_bias = lax.all_gather(
            lax.all_gather(b_fc1.astype(BF16), "dp", axis=1, tiled=True), "tensor", axis=0
        ).astype(F32)
        x = exchange(images(tokens_in))
        ct = exchange(images(cotangent))
        weights = gather_plain(w_qkv, w_out, w_fc1, w_fc2)
    out, probs, saved = forward(x, *weights, vectors, hidden_bias, mask)
    gtok, sums, grads = backward(x, ct, *weights, vectors, mask, probs, saved)
    if dp == 8:
        out, gtok, sums, got = reduce(out, gtok, jnp.pad(sums, ((0, 4), (0, 0))), grads)
        g_qkv, g_out, g_fc1, g_fc2 = (got[a] for a in GRADS)
        g_small = lax.dynamic_slice(sums, (0, t * 256 + d * 32), (8, 32))
        g_hidden = lax.dynamic_slice(sums, (8 + t, d * 128), (1, 128))
    else:
        g_qkv, g_out, g_fc1, g_fc2 = scatter_plain(grads)
        out, gtok = exchange(out), exchange(gtok)

        def total(part, axis):
            part = lax.psum_scatter(part, "tensor", scatter_dimension=0, tiled=True)
            return lax.psum_scatter(part, "dp", scatter_dimension=axis, tiled=True)

        g_small = total(sums[0:8].reshape(8, 4, 256).transpose(1, 0, 2), 2)[0]
        g_hidden = total(sums[8:12], 1)

    def rows(pieces):
        return pieces[:, :SEQ].reshape(4 * SEQ, 256)

    return (
        rows(out),
        rows(gtok),
        g_small[0:1],
        g_small[1:2],
        g_qkv.reshape(w_qkv.shape),
        g_small[2:4][:, None],
        g_out,
        g_small[4:5],
        g_small[5:6],
        g_small[6:7],
        g_fc1,
        g_hidden,
        g_fc2,
        g_small[7:8],
    )


def solution(mesh):
    both, turned = P("dp", "tensor"), P("tensor", "dp")
    mixed, pair = P("dp", None, "tensor"), P(None, "tensor", "dp")
    params = (turned, turned, mixed, pair, turned, turned, turned, turned, both, turned, turned, turned)
    return jax.shard_map(
        functools.partial(on_device, mesh.shape["dp"]),
        mesh=mesh,
        in_specs=(both, both, P("dp"), *params),
        out_specs=(both, both, *params),
        check_vma=False,
    )
```

```python
import functools
import jax
import jax.numpy as jnp
from jax import lax
from jax.experimental import pallas as pl
from jax.experimental.pallas import tpu as pltpu
from jax.sharding import PartitionSpec as P

D = 1024
HD = 64
SEQ = 577
ROWS = 592
CHUNK = 32
F32 = jnp.float32
BF16 = jnp.bfloat16
LAST = (((1,), (1,)), ((), ()))
VMEM_BYTES = 66_000_000


def mm(a, b):
    return jnp.dot(a, b, preferred_element_type=F32)


def mm_t(a, b):
    return lax.dot_general(a, b, LAST, preferred_element_type=F32)


def cols(i, n):
    return pl.ds(pl.multiple_of(i * n, n), n)


def row_stats(values):
    mean = jnp.sum(values, axis=1, keepdims=True) * (1.0 / D)
    centered = values - mean
    var = jnp.sum(centered * centered, axis=1, keepdims=True) * (1.0 / D)
    inv = lax.rsqrt(var + 1e-05)
    return centered * inv, inv


def wide(ref, rows):
    return jnp.concatenate([ref[t, rows, :].astype(F32) for t in range(4)], axis=1)


def over_rows(do):
    @pl.loop(0, 576 // CHUNK)
    def _(i):
        do(pl.ds(pl.multiple_of(i * CHUNK, CHUNK), CHUNK))

    do(pl.ds(576, ROWS - 576))


def vec(vectors, row):
    return jnp.concatenate([vectors[t, row : row + 1, :] for t in range(4)], axis=1)


def norm_in(x, vectors, nin):
    gain, shift = vec(vectors, 0), vec(vectors, 1)

    @over_rows
    def _(rows):
        xhat, _ = row_stats(wide(x, rows))
        nin[rows, :] = (xhat * gain + shift).astype(BF16)


def flip(src, dst, n):
    @pl.loop(0, n // 256)
    def _(i):
        dst[cols(i, 256), :] = src[:, cols(i, 256)].T


def project(nin, wqkv, vectors, t, q, k, v):
    here = cols(t, 256)

    def part(c):
        return mm(nin[...], wqkv[t, :, :, :, c * 256 : c * 256 + 256].reshape(D, 256))

    q[:, here] = (part(0) + vectors[t, 2:3, :]).astype(BF16)
    k[:, here] = part(1).astype(BF16)
    v[:, here] = (part(2) + vectors[t, 3:4, :]).astype(BF16)


def attend_pair(pair, q, k, v, ctx, probs, slot):
    here = cols(pair, 128)
    lane = lax.broadcasted_iota(jnp.int32, (ROWS, 128), 1)
    row = lax.broadcasted_iota(jnp.int32, (ROWS, 128), 0)
    queries = q[:, here].astype(F32) * (HD**-0.5)
    keys = k[:, here].astype(F32)
    values = v[:, here]
    blocked = jnp.where(row >= SEQ, -1e30, 0.0)
    parts = []
    for h in range(2):
        own = (lane < 64) if h == 0 else (lane >= 64)
        spare = 64 if h == 0 else 0
        qa = jnp.where(own, queries, jnp.where(lane == spare, 1.0, 0.0)).astype(BF16)
        ka = jnp.where(lane == spare, blocked, keys).astype(BF16)
        scores = mm_t(ka, qa)
        top = jnp.max(scores, axis=0, keepdims=True)
        e = jnp.exp(scores - top)
        total = jnp.sum(e, axis=0, keepdims=True)
        p = (e * (1.0 / total)).astype(BF16)
        probs[slot, h] = p
        parts.append(
            lax.dot_general(p, values, (((0,), (0,)), ((), ())), preferred_element_type=F32)
        )
    ctx[:, here] = jnp.where(lane < 64, parts[0], parts[1]).astype(BF16)


def out_block(i, ctx, wout, x, vectors, resid):
    w = jnp.concatenate([wout[i, c].reshape(D, 128) for c in range(2)], axis=1)
    resid[:, cols(i, 256)] = x[i].astype(F32) + mm(ctx[...], w) + vectors[i, 4:5, :]


def norm_mid(resid, vectors, nmid):
    gain, shift = vec(vectors, 5), vec(vectors, 6)

    @over_rows
    def _(rows):
        xhat, _ = row_stats(resid[rows, :])
        nmid[rows, :] = (xhat * gain + shift).astype(BF16)


def hidden_tile(t, j, nmid, w1, b1, act, act_t, slope):
    here = pl.ds(pl.multiple_of(t * 1024 + j * 256, 256), 256)
    bias = b1[t, :, cols(j, 256)]
    pre = mm(nmid[...], w1[t, :, :, :, cols(j, 256)].reshape(D, 256)) + bias
    sig = 1.0 / (1.0 + jnp.exp(-1.702 * pre))
    a = pre * sig
    slope[:, here] = (sig + 1.702 * a * (1.0 - sig)).astype(BF16)
    low = a.astype(BF16)
    act[:, here] = low
    act_t[here, :] = low.T


def down_block(i, t, act, w2, total):
    w = jnp.concatenate([w2[i, c, t] for c in range(2)], axis=1)
    total[:, cols(i, 256)] += mm(act[:, cols(t, 1024)], w)


def finish_block(i, total, vectors, mask, out):
    out[i] = ((total[:, cols(i, 256)] + vectors[i, 7:8, :]) * mask[...]).astype(BF16)


def grad_norm_rows(values, gain, n):
    xhat, inv = row_stats(values)
    e = n * gain
    first = jnp.sum(e, axis=1, keepdims=True) * (1.0 / D)
    second = jnp.sum(e * xhat, axis=1, keepdims=True) * (1.0 / D)
    return inv * (e - first - xhat * second), n * xhat


def fold(a):
    return jnp.sum(a.reshape(-1, 8, D), axis=0)


def attend_back_pair(pair, q, k, v, ctx, gctx, probs, slot, gmix, sums):
    here = cols(pair, 128)
    lane = lax.broadcasted_iota(jnp.int32, (ROWS, 128), 1)
    queries, keys, values = q[:, here], k[:, here], v[:, here].astype(F32)
    go = gctx[:, here]
    go_f = go.astype(F32)
    dots = go_f * ctx[:, here].astype(F32)
    dq, dk, dv = [], [], []
    for h in range(2):
        own = (lane < 64) if h == 0 else (lane >= 64)
        spare = 64 if h == 0 else 0
        delta = -jnp.sum(jnp.where(own, dots, 0.0), axis=1, keepdims=True)
        high = delta.astype(BF16).astype(F32)
        rest = delta - high
        ga = jnp.where(
            own, go_f, jnp.where(lane == spare, high, jnp.where(lane == spare + 1, rest, 0.0))
        ).astype(BF16)
        marks = jnp.where((lane == spare) | (lane == spare + 1), 1.0, 0.0)
        va = jnp.where(own, values, marks).astype(BF16)
        p = probs[slot, h]
        gs = (p.astype(F32) * mm_t(va, ga)).astype(BF16)
        dv.append(mm(p, go))
        dk.append(mm(gs, queries))
        dq.append(
            lax.dot_general(gs, keys, (((0,), (0,)), ((), ())), preferred_element_type=F32)
        )
    scale = HD**-0.5
    low = lane < 64
    gq = jnp.where(low, dq[0], dq[1]) * scale
    gk = jnp.where(low, dk[0], dk[1]) * scale
    gv = jnp.where(low, dv[0], dv[1])
    t, half = pair // 2, pair % 2
    at = [pl.ds(pl.multiple_of(c * 256 + half * 128, 128), 128) for c in range(3)]
    gmix[t, :, at[0]] = gq.astype(BF16)
    gmix[t, :, at[1]] = gk.astype(BF16)
    gmix[t, :, at[2]] = gv.astype(BF16)
    sums[2:3, here] = jnp.sum(gq, axis=0, keepdims=True)
    sums[3:4, here] = jnp.sum(gv, axis=0, keepdims=True)


ACT = jax.ShapeDtypeStruct((ROWS, D), BF16)
TURNED = jax.ShapeDtypeStruct((D, ROWS), BF16)
SAVED = dict(
    nin_t=TURNED,
    q=ACT,
    k=ACT,
    v=ACT,
    ctx=ACT,
    ctx_t=TURNED,
    nmid_t=TURNED,
    resid=jax.ShapeDtypeStruct((ROWS, D), F32),
    act_t=jax.ShapeDtypeStruct((4 * D, ROWS), BF16),
    slope=jax.ShapeDtypeStruct((ROWS, 4 * D), BF16),
)
PROBS = jax.ShapeDtypeStruct((8, 2, ROWS, ROWS), BF16)
IMAGE = jax.ShapeDtypeStruct((4, ROWS, 256), BF16)
ANY = pl.BlockSpec(memory_space=pl.ANY)
VM = pl.BlockSpec(memory_space=pltpu.VMEM)


def scratch(like):
    return pltpu.VMEM(like.shape, like.dtype)


PARTS = dict(
    sv=((4, 4, 2, 16, 256), F32),
    wqkv=((4, 4, 2, 128, 768), BF16),
    wout=((4, 2, 4, 256, 128), BF16),
    w1=((4, 4, 2, 128, 1024), BF16),
    w2=((4, 2, 4, 1024, 128), BF16),
)
WEIGHTS = ("wqkv", "wout", "w1", "w2")


def part(name):
    return jax.ShapeDtypeStruct(*PARTS[name])


class Forward:
    SCRATCH = [scratch(a) for a in SAVED.values()] + [
        scratch(ACT),
        pltpu.VMEM((ROWS, 4 * D), BF16),
        pltpu.VMEM((ROWS, D), F32),
        pltpu.VMEM((2, 2, ROWS, ROWS), BF16),
        scratch(IMAGE),
        pltpu.SemaphoreType.DMA((2,)),
        pltpu.SemaphoreType.DMA((len(SAVED) + 1,)),
    ]

    def __init__(self, x, weights, vectors, b1, mask, out_h, probs_h, saved_h, refs):
        n = len(SAVED)
        self.x, self.w, self.vectors, self.b1, self.mask = x, weights, vectors, b1, mask
        self.out_h, self.probs_h, self.saved_h = out_h, probs_h, saved_h
        self.saved = dict(zip(SAVED, refs[:n]))
        self.normed, self.act, self.total, self.probs, self.out, self.probs_sem, self.out_sem = refs[n:]

    def start_norm(self):
        norm_in(self.x, self.vectors, self.normed)
        flip(self.normed, self.saved["nin_t"], D)

    def put(self, pair, slot):
        return pltpu.make_async_copy(self.probs.at[slot], self.probs_h.at[pair], self.probs_sem.at[slot])

    def heads(self, s, i):
        a = self.saved
        project(self.normed, self.w["wqkv"], self.vectors, s, a["q"], a["k"], a["v"])

        @pl.loop(0, 2)
        def _(slot):
            pair = s * 2 + slot
            if i:
                self.put(pair, slot).wait()
            attend_pair(pair, a["q"], a["k"], a["v"], a["ctx"], self.probs, slot)
            self.put(pair, slot).start()

    def middle(self):
        a = self.saved

        @pl.loop(0, 4)
        def _(i):
            out_block(i, a["ctx"], self.w["wout"], self.x, self.vectors, a["resid"])
            self.total[:, cols(i, 256)] = a["resid"][:, cols(i, 256)]

        norm_mid(a["resid"], self.vectors, self.normed)

    def hidden(self, s):
        @pl.loop(0, 4)
        def _(j):
            hidden_tile(s, j, self.normed, self.w["w1"], self.b1, self.act, self.saved["act_t"], self.saved["slope"])

    def down(self, s):
        @pl.loop(0, 4)
        def _(i):
            down_block(i, s, self.act, self.w["w2"], self.total)

    def turn(self):
        flip(self.saved["ctx"], self.saved["ctx_t"], D)
        flip(self.normed, self.saved["nmid_t"], D)

    def finish(self):
        @pl.loop(0, 4)
        def _(i):
            finish_block(i, self.total, self.vectors, self.mask, self.out)

    def stores(self, names):
        at = list(SAVED)
        return [
            pltpu.make_async_copy(self.saved[a], self.saved_h[a], self.out_sem.at[at.index(a)]) for a in names
        ]

    def store_out(self):
        return pltpu.make_async_copy(self.out, self.out_h, self.out_sem.at[len(SAVED)])

    def drain_last(self, s):
        for slot in range(2):
            self.put(s * 2 + slot, slot).wait()

    def drain(self):
        for slot in range(2):
            self.put(6 + slot, slot).wait()


def forward_kernel(x_h, wqkv_h, wout_h, w1_h, w2_h, vectors, b1, mask, *rest):
    n = len(SAVED)
    saved_h = dict(zip(SAVED, rest[2 : 2 + n]))
    x, *weights, in_sem = rest[2 + n : 8 + n]
    loads = [
        pltpu.make_async_copy(a, b, in_sem.at[i])
        for i, (a, b) in enumerate(zip((x_h, wqkv_h, wout_h, w1_h, w2_h), (x, *weights)))
    ]
    for c in loads:
        c.start()
    for c in loads:
        c.wait()
    f = Forward(x, dict(zip(WEIGHTS, weights)), vectors, b1, mask, rest[0], rest[1], saved_h, rest[8 + n :])
    f.start_norm()
    for s in range(4):
        f.heads(s, s)
    f.middle()
    for s in range(4):
        f.hidden(s)
        f.down(s)
    f.turn()
    f.finish()
    f.drain()
    stores = [*f.stores(SAVED), f.store_out()]
    for c in stores:
        c.start()
    for c in stores:
        c.wait()


def forward(x, weights, vectors, b1, mask):
    n = len(SAVED)
    outs = pl.pallas_call(
        forward_kernel,
        out_shape=[IMAGE, PROBS, *SAVED.values()],
        in_specs=[ANY] * 5 + [VM, VM, VM],
        out_specs=[ANY] * (2 + n),
        scratch_shapes=[scratch(IMAGE)]
        + [scratch(part(a)) for a in WEIGHTS]
        + [pltpu.SemaphoreType.DMA((5,))]
        + Forward.SCRATCH,
        compiler_params=pltpu.CompilerParams(vmem_limit_bytes=VMEM_BYTES),
        name="forward",
    )(x, *[weights[a] for a in WEIGHTS], vectors, b1, mask)
    return outs[0], outs[1], dict(zip(SAVED, outs[2:]))


GRADS = dict(
    wqkv=jax.ShapeDtypeStruct((4, 1024, 768), BF16),
    wout=jax.ShapeDtypeStruct((8, 1024, 128), BF16),
    w1=jax.ShapeDtypeStruct((4, 1024, 1024), BF16),
    w2=jax.ShapeDtypeStruct((8, 4096, 128), BF16),
)


def send_tile(stage, sem, i, value, targets):
    slot = lax.rem(i, 2)

    def copies(s):
        return [
            pltpu.make_async_copy(
                stage.at[s] if w == 256 else stage.at[s, :, pl.ds(c, w)], ref, sem.at[s]
            )
            for ref, c, w in targets
        ]

    @pl.when(i >= 2)
    def _():
        pltpu.make_async_copy(stage.at[slot], stage.at[slot], sem.at[slot]).wait()

    stage[slot] = value
    for c in copies(slot):
        c.start()


def drain(stage, sem):
    for slot in range(2):
        pltpu.make_async_copy(stage.at[slot], stage.at[slot], sem.at[slot]).wait()


def backward_kernel(x_h, ct_h, wqkv_h, wout_h, w1_h, w2_h, vectors, mask, probs_h, *rest):
    n = len(SAVED)
    saved_h = dict(zip(SAVED, rest[:n]))
    gtok_h, sums_o = rest[n], rest[n + 1]
    g_h = dict(zip(GRADS, rest[n + 2 : n + 6]))
    rest = rest[n + 6 :]
    saved = dict(zip(SAVED, rest[:n]))
    (x, wqkv, wout, w1, w2, b1, gmlp, gattn, gctx, gn, gmix, probs, sums, part, stage,
     in_sem, probs_sem, tile_sem, saved_sem) = rest[n:]
    gtok = x
    names = dict(ct=(ct_h, gtok), x=(x_h, x), w2=(w2_h, w2), w1=(w1_h, w1), wout=(wout_h, wout), wqkv=(wqkv_h, wqkv))
    load = {a: pltpu.make_async_copy(*names[a], in_sem.at[i]) for i, a in enumerate(names)}
    load_saved = {a: pltpu.make_async_copy(saved_h[a], saved[a], saved_sem.at[i]) for i, a in enumerate(SAVED)}
    load["ct"].start()
    for a in ("act_t", "slope"):
        load_saved[a].start()
    for a in ("w2", "w1", "wout", "wqkv"):
        load[a].start()
    for a in SAVED:
        if a not in ("act_t", "slope"):
            load_saved[a].start()
    part[...] = jnp.zeros_like(part)
    sums[...] = jnp.zeros_like(sums)
    load["ct"].wait()

    @over_rows
    def _(rows):
        g = jnp.concatenate([x[t, rows, :].astype(F32) * mask[...] for t in range(4)], axis=1)
        gmlp[rows, :] = g.astype(BF16)
        part[0] += fold(g)

    load["x"].start()
    load_saved["act_t"].wait()

    @pl.loop(0, 16)
    def _(i):
        t, c = i // 4, i % 4
        r = mm(saved["act_t"][cols(t, 1024), :], gmlp[:, cols(c, 256)]).astype(BF16)
        send_tile(stage, tile_sem, i, r, [
            (g_h["w2"].at[2 * c + e, cols(t, 1024), :], e * 128, 128) for e in range(2)])

    load_saved["slope"].wait()
    load["w2"].wait()
    slope = saved["slope"]

    @pl.loop(0, 16)
    def _(i):
        w = jnp.concatenate([w2[d, cols(i, 256), :] for d in range(8)], axis=1)
        gpre = mm_t(gmlp[...], w) * slope[:, cols(i, 256)].astype(F32)
        slope[:, cols(i, 256)] = gpre.astype(BF16)
        b1[i // 4, :, cols(i % 4, 256)] = jnp.sum(gpre, axis=0, keepdims=True)

    load_saved["nmid_t"].wait()

    @pl.loop(0, 16)
    def _(i):
        r = mm(saved["nmid_t"][...], slope[:, cols(i, 256)]).astype(BF16)
        send_tile(stage, tile_sem, i + 16, r, [(g_h["w1"].at[i // 4, :, cols(i % 4, 256)], 0, 256)])

    load["w1"].wait()

    @pl.loop(0, 4)
    def _(i):
        total = mm_t(slope[:, 0:1024], w1[0, cols(i, 256), :])
        for t in range(1, 4):
            total += mm_t(slope[:, t * 1024 : t * 1024 + 1024], w1[t, cols(i, 256), :])
        gn[:, cols(i, 256)] = total

    load_saved["resid"].wait()
    gain2 = vec(vectors, 5)

    @over_rows
    def _(rows):
        normed = gn[rows, :]
        g, scaled = grad_norm_rows(saved["resid"][rows, :], gain2, normed)
        g = g + gmlp[rows, :].astype(F32)
        part[1] += fold(normed)
        part[2] += fold(scaled)
        part[3] += fold(g)
        gn[rows, :] = g
        gattn[rows, :] = g.astype(BF16)

    load["wout"].wait()
    load_saved["ctx_t"].wait()

    @pl.loop(0, 4)
    def _(i):
        w = jnp.concatenate([wout[d, cols(i, 256), :] for d in range(8)], axis=1)
        gctx[:, cols(i, 256)] = mm_t(gattn[...], w).astype(BF16)
        r = mm(saved["ctx_t"][...], gattn[:, cols(i, 256)]).astype(BF16)
        send_tile(stage, tile_sem, i + 32, r, [(g_h["wout"].at[2 * i + e], e * 128, 128) for e in range(2)])

    for a in ("q", "k", "v", "ctx"):
        load_saved[a].wait()

    def get(pair, slot):
        return pltpu.make_async_copy(probs_h.at[pair], probs.at[slot], probs_sem.at[slot])

    get(0, 0).start()

    @pl.loop(0, 8)
    def _(pair):
        slot = pair % 2

        @pl.when(pair < 7)
        def _():
            get(pair + 1, 1 - slot).start()

        get(pair, slot).wait()
        attend_back_pair(pair, saved["q"], saved["k"], saved["v"], saved["ctx"], gctx, probs, slot, gmix, sums)

    load_saved["nin_t"].wait()

    @pl.loop(0, 12)
    def _(i):
        t, c = i // 3, i % 3
        r = mm(saved["nin_t"][...], gmix[t, :, cols(c, 256)]).astype(BF16)
        send_tile(stage, tile_sem, i + 36, r, [(g_h["wqkv"].at[t, :, cols(c, 256)], 0, 256)])

    load["wqkv"].wait()
    resid = saved["resid"]

    @pl.loop(0, 4)
    def _(i):
        total = mm_t(gmix[0], wqkv[0, cols(i, 256), :])
        for t in range(1, 4):
            total += mm_t(gmix[t], wqkv[t, cols(i, 256), :])
        resid[:, cols(i, 256)] = total

    load["x"].wait()
    gain1 = vec(vectors, 0)

    @over_rows
    def _(rows):
        normed = resid[rows, :]
        g, scaled = grad_norm_rows(wide(x, rows), gain1, normed)
        g = g + gn[rows, :]
        part[4] += fold(normed)
        part[5] += fold(scaled)
        for t in range(4):
            gtok[t, rows, :] = g[:, t * 256 : t * 256 + 256].astype(BF16)

    for row, i in ((7, 0), (6, 1), (5, 2), (4, 3), (1, 4), (0, 5)):
        sums[row : row + 1, :] = jnp.sum(part[i], axis=0, keepdims=True)
    sums_o[0:8, :] = sums[...]
    for t in range(4):
        sums_o[8 + t : 9 + t, :] = b1[t]
    done = pltpu.make_async_copy(gtok, gtok_h, in_sem.at[0])
    done.start()
    done.wait()
    drain(stage, tile_sem)


def backward(x, ct, wqkv, wout, w1, w2, vectors, mask, probs, saved):
    n = len(SAVED)
    outs = pl.pallas_call(
        backward_kernel,
        out_shape=[IMAGE, jax.ShapeDtypeStruct((12, D), F32), *GRADS.values()],
        in_specs=[ANY] * 6 + [VM, VM, ANY] + [ANY] * n,
        out_specs=[ANY, VM] + [ANY] * 4,
        scratch_shapes=[scratch(a) for a in SAVED.values()]
        + [scratch(a) for a in (x, wqkv, wout, w1, w2)]
        + [
            pltpu.VMEM((4, 1, 1024), F32),
            scratch(ACT),
            scratch(ACT),
            scratch(ACT),
            pltpu.VMEM((ROWS, D), F32),
            pltpu.VMEM((4, ROWS, 768), BF16),
            pltpu.VMEM((2, 2, ROWS, ROWS), BF16),
            pltpu.VMEM((8, D), F32),
            pltpu.VMEM((6, 8, D), F32),
            pltpu.VMEM((2, 1024, 256), BF16),
            pltpu.SemaphoreType.DMA((6,)),
            pltpu.SemaphoreType.DMA((2,)),
            pltpu.SemaphoreType.DMA((2,)),
            pltpu.SemaphoreType.DMA((n,)),
        ],
        compiler_params=pltpu.CompilerParams(vmem_limit_bytes=VMEM_BYTES),
        name="backward",
    )(x, ct, wqkv, wout, w1, w2, vectors, mask, probs, *[saved[a] for a in SAVED])
    return outs[0], outs[1], dict(zip(GRADS, outs[2:]))


MESH = pl.DeviceIdType.MESH
BY_COLUMN = ("wout", "w2")


def block_of(name, ref, t, yx, c):
    return ref.at[yx, c, t] if name in BY_COLUMN else ref.at[t, yx, c]


def half_of(ref, h):
    n = ref.shape[0] // 2
    return ref.at[pl.ds(h * n, n)]


class Place:
    def __init__(self):
        d, self.t = lax.axis_index("dp"), lax.axis_index("tensor")
        self.y, self.x, self.c = d // 4, d // 2 % 2, d % 2
        self.yx = d // 2
        self.x_yx = self.y * 2 + 1 - self.x
        self.y_yx = (1 - self.y) * 2 + self.x
        self.xy_yx = (1 - self.y) * 2 + 1 - self.x
        self.d = d
        self.x_id = (self.x_yx * 2 + self.c, self.t)
        self.y_id = (self.y_yx * 2 + self.c, self.t)
        self.c_id = (self.yx * 2 + 1 - self.c, self.t)

    def z_id(self, t):
        return (self.d, t)

    def order(self, i):
        t = self.t
        return (t, t + 1 - 2 * (t % 2), 2 - t // 2, 3 - 3 * (t // 2))[i]

    def greet(self):
        barrier = pltpu.get_barrier_semaphore()
        others = [self.x_id, self.y_id, self.c_id]
        others += [self.z_id(lax.rem(self.t + k, 4)) for k in (1, 2, 3)]
        for other in others:
            pl.semaphore_signal(barrier, inc=1, device_id=other, device_id_type=MESH)
        pl.semaphore_wait(barrier, 6)


def remote(src, dst, send, recv, where):
    return pltpu.make_async_remote_copy(
        src_ref=src, dst_ref=dst, send_sem=send, recv_sem=recv, device_id=where, device_id_type=MESH
    )


class Gather:
    SEMS = [
        pltpu.SemaphoreType.DMA((2, 4)),
        pltpu.SemaphoreType.DMA((4,)),
        pltpu.SemaphoreType.DMA((4, 6)),
        pltpu.SemaphoreType.DMA((4, 6)),
        pltpu.SemaphoreType.DMA((4,)),
        pltpu.SemaphoreType.DMA((4,)),
    ]

    def __init__(self, place, name, own, whole, sems):
        self.p, self.name, self.own, self.whole = place, name, own, whole
        self.z_send, self.z_recv, self.xy_send, self.xy_recv, self.c_send, self.c_recv = sems

    def at(self, s, yx):
        return block_of(self.name, self.whole, s, yx, self.p.c)

    def z_copies(self, s, act, src=None):
        p = self.p
        dst = self.at(s, p.yx)
        for way, going, to in ((0, (s <= p.t) & (p.t < 3), p.t + 1), (1, (s >= p.t) & (p.t > 0), p.t - 1)):

            @pl.when(going)
            def _():
                c = remote(dst if src is None else src, dst, self.z_send.at[way, s], self.z_recv.at[s], p.z_id(to))
                c.start() if act == "start" else c.wait_send()

    def xy_copy(self, k, s, mine=False):
        p = self.p
        yx = (p.yx, p.yx, p.yx, p.x_yx, p.yx, p.y_yx)[k]
        h = (0, 1, 0, 0, 1, 1)[k]
        to = (p.x_id, p.y_id, p.y_id, p.y_id, p.x_id, p.x_id)[k]
        dst = half_of(self.at(s, yx), h)
        src = half_of(self.own, h) if mine else dst
        return remote(src, dst, self.xy_send.at[s, k], self.xy_recv.at[s, k], to)

    def open(self):
        s = self.p.t
        self.z_copies(s, "start", self.own)
        for k in (0, 1):
            self.xy_copy(k, s, True).start()

    def arrive(self, i):
        s = self.p.order(i)
        here = self.at(s, self.p.yx)
        remote(here, here, self.z_send.at[0, s], self.z_recv.at[s], self.p.c_id).wait_recv()
        self.z_copies(s, "start")
        for k in (0, 1):
            self.xy_copy(k, s).start()

    def second(self, i):
        s = self.p.order(i)
        for got, own, other in ((0, 2, 3), (1, 4, 5)):
            self.xy_copy(own, s, i == 0).start()
            self.xy_copy(got, s).wait_recv()
            self.xy_copy(other, s).start()

    def core_copy(self, s):
        c = self.p.c
        ref = self.whole.at[:, c, s] if self.name in BY_COLUMN else self.whole.at[s, :, c]
        return remote(ref, ref, self.c_send.at[s], self.c_recv.at[s], self.p.c_id)

    def last(self, i):
        s = self.p.order(i)
        for k in (2, 3, 4, 5):
            self.xy_copy(k, s).wait_recv()
        self.core_copy(s).start()

    def have(self, i):
        self.core_copy(self.p.order(i)).wait_recv()

    def finish(self):
        for s in range(4):
            self.z_copies(s, "wait")
            for k in range(6):
                self.xy_copy(k, s).wait_send()
            self.core_copy(s).wait_send()


class Swap:
    SEMS = [pltpu.SemaphoreType.DMA((4,)), pltpu.SemaphoreType.DMA((4,))]

    def __init__(self, place, pieces, whole, sems):
        self.p, self.pieces, self.whole = place, pieces, whole
        self.send, self.recv = sems

    def copy(self, k):
        p = self.p
        to = lax.rem(p.t + k, 4)
        return remote(self.pieces.at[to], self.whole.at[p.t], self.send.at[k], self.recv.at[k], p.z_id(to))

    def start(self):
        for k in (1, 3, 2):
            self.copy(k).start()

    def done(self):
        for k in (1, 2, 3):
            self.copy(k).wait_recv()

    def finish(self):
        for k in (1, 2, 3):
            self.copy(k).wait_send()


class Bounce:
    def __init__(self, src, buf, dst, sems):
        self.load = pltpu.make_async_copy(src, buf, sems.at[0])
        self.store = pltpu.make_async_copy(buf, dst, sems.at[1])


SEQUENCE = (
    ("sv", "O"), ("wout", "O"), ("wqkv", "O"), ("sv", "S", 0), ("wout", "A", 1), ("sv", "A", 1), ("w1", "O"),
    ("wout", "S", 0), ("wqkv", "A", 1), ("sv", "S", 1), ("wqkv", "S", 0), ("wout", "A", 2), ("w1", "S", 0),
    ("wout", "A", 3), ("sv", "L", 0), ("sv", "A", 2), ("sv", "A", 3), ("wqkv", "S", 1), ("w1", "A", 1),
    ("wqkv", "A", 2), ("wqkv", "A", 3), ("XS",), ("sv", "L", 1), ("sv", "S", 2), ("w1", "S", 1),
    ("wout", "S", 1), ("sv", "S", 3), ("wout", "S", 2), ("sv", "L", 2), ("w2", "O"), ("wout", "S", 3),
    ("sv", "L", 3), ("wqkv", "S", 2), ("wqkv", "S", 3), ("w1", "A", 2), ("wqkv", "L", 0), ("w2", "S", 0),
    ("LN1",), ("w1", "A", 3), ("wqkv", "L", 1), ("wqkv", "L", 2), ("wout", "L", 0), ("w1", "L", 0), ("Q", 0),
    ("w2", "A", 1), ("wout", "L", 1), ("wout", "L", 2), ("w1", "S", 2), ("wqkv", "L", 3), ("w2", "A", 2),
    ("Q", 1), ("Q", 2), ("w2", "A", 3), ("w1", "S", 3), ("wout", "L", 3), ("w2", "S", 1), ("w1", "L", 1),
    ("Q", 3), ("CS",), ("OUT",), ("w1", "L", 2), ("F", 0), ("w2", "S", 2), ("w2", "S", 3), ("w2", "L", 0),
    ("F", 1), ("w1", "L", 3), ("w2", "L", 1), ("F", 2), ("F", 3), ("D", 0), ("w2", "L", 2), ("D", 1),
    ("w2", "L", 3), ("D", 2), ("D", 3), ("END",),
)


def spread_kernel(x_in, ct_in, mask, *rest):
    names, n, m = list(PARTS), len(PARTS), len(SAVED)
    own = dict(zip(names, rest[:n]))
    x_h, ct_h, out_h, probs_h, vectors = rest[n : n + 5]
    rest = rest[n + 5 :]
    whole_h, saved_h = dict(zip(WEIGHTS, rest[:4])), dict(zip(SAVED, rest[4 : 4 + m]))
    rest = rest[4 + m :]
    x, ct, b1 = rest[:3]
    whole = dict(zip(names, rest[3 : 3 + n]))
    rest = rest[3 + n :]
    local_sem, keep_sem = rest[0], rest[1]
    swap_sems, rest = rest[2:6], rest[6:]
    sems, refs = rest[: 6 * n], rest[6 * n :]
    p = Place()
    f = Forward(x, whole, vectors, b1, mask, out_h, probs_h, saved_h, refs)
    gathers = {a: Gather(p, a, own[a], whole[a], sems[6 * i : 6 * i + 6]) for i, a in enumerate(names)}
    swaps = dict(XS=Swap(p, x_in, x, swap_sems[0:2]), CS=Swap(p, ct_in, ct, swap_sems[2:4]))
    local = [
        pltpu.make_async_copy(own[a], block_of(a, whole[a], p.t, p.yx, p.c), local_sem.at[i])
        for i, a in enumerate(names)
    ]
    local += [
        pltpu.make_async_copy(x_in.at[p.t], x.at[p.t], local_sem.at[n]),
        pltpu.make_async_copy(ct_in.at[p.t], ct.at[p.t], local_sem.at[n + 1]),
    ]
    for c in local:
        c.start()
    p.greet()
    pending = []
    settled = False

    def keep(src, dst):
        c = pltpu.make_async_copy(src, dst, keep_sem.at[len(pending)])
        c.start()
        pending.append(c)

    for name, *step in SEQUENCE:
        if name in gathers:
            g, kind = gathers[name], step[0]
            if kind == "O":
                g.open()
            elif kind == "A":
                g.arrive(step[1])
            elif kind == "S":
                g.second(step[1])
            else:
                if not settled:
                    for c in local:
                        c.wait()
                    settled = True
                g.last(step[1])
        elif name in swaps:
            swaps[name].start()
        elif name == "LN1":
            for i in range(4):
                gathers["sv"].have(i)
            sv = whole["sv"]
            for t in range(4):
                vectors[t] = jnp.sum(sv[t, :, :, 0:8].reshape(8, 8, 256), axis=0)
                for d in range(8):
                    b1[t, :, d * 128 : d * 128 + 128] = sv[t, d // 2, d % 2, 8:9, 0:128]
            swaps["XS"].done()
            keep(x, x_h)
            f.start_norm()
        elif name == "Q":
            gathers["wqkv"].have(step[0])
            f.heads(p.order(step[0]), step[0])
        elif name == "OUT":
            for i in range(4):
                gathers["wout"].have(i)
            keep(whole["wqkv"], whole_h["wqkv"])
            keep(whole["wout"], whole_h["wout"])
            f.middle()
            for c in f.stores(("q", "k", "v", "ctx", "nin_t", "resid")):
                c.start()
        elif name == "F":
            gathers["w1"].have(step[0])
            f.hidden(p.order(step[0]))
        elif name == "D":
            if step[0] == 0:
                keep(whole["w1"], whole_h["w1"])
                for c in f.stores(("act_t", "slope")):
                    c.start()
            gathers["w2"].have(step[0])
            f.down(p.order(step[0]))
        elif name == "END":
            keep(whole["w2"], whole_h["w2"])
            f.finish()
            f.store_out().start()
            swaps["CS"].done()
            keep(ct, ct_h)
            f.turn()
            for c in f.stores(("ctx_t", "nmid_t")):
                c.start()
    f.drain_last(p.order(3))
    for c in [*pending, *f.stores(SAVED), f.store_out()]:
        c.wait()
    for s in swaps.values():
        s.finish()
    for g in gathers.values():
        g.finish()


def spread(x_in, ct_in, mask, own):
    names, n, m = list(PARTS), len(PARTS), len(SAVED)
    outs = pl.pallas_call(
        spread_kernel,
        out_shape=[IMAGE, IMAGE, IMAGE, PROBS, jax.ShapeDtypeStruct((4, 8, 256), F32)]
        + [part(a) for a in WEIGHTS]
        + list(SAVED.values()),
        in_specs=[ANY, ANY, VM] + [ANY] * n,
        out_specs=[ANY] * 4 + [VM] + [ANY] * (4 + m),
        scratch_shapes=[scratch(IMAGE), scratch(IMAGE), pltpu.VMEM((4, 1, 1024), F32)]
        + [scratch(part(a)) for a in names]
        + [pltpu.SemaphoreType.DMA((n + 2,)), pltpu.SemaphoreType.DMA((6,))]
        + Swap.SEMS * 2
        + Gather.SEMS * n
        + Forward.SCRATCH,
        compiler_params=pltpu.CompilerParams(
            collective_id=0, has_side_effects=True, vmem_limit_bytes=VMEM_BYTES
        ),
        name="spread",
    )(x_in, ct_in, mask, *[own[a] for a in names])
    x, ct, out, probs, vectors = outs[:5]
    return x, ct, out, probs, vectors, dict(zip(WEIGHTS, outs[5:9])), dict(zip(SAVED, outs[9:]))


REDUCED = ("w2", "w1", "wout", "wqkv")


class Reduce:
    def __init__(self, place, name, grad, own, got, got1, got2, got3, result, sems):
        self.p, self.name, self.grad, self.own, self.got = place, name, grad, own, got
        self.got1, self.got2, self.got3, self.result = got1, got2, got3, result
        self.send, self.recv, self.local = sems

    def plane(self, c):
        return self.grad.at[:, c] if self.name in BY_COLUMN else self.grad.at[:, :, c]

    def block(self, ref, t, yx):
        return ref.at[yx, t] if self.name in BY_COLUMN else ref.at[t, yx]

    def core_copy(self):
        return remote(self.plane(1 - self.p.c), self.got, self.send.at[0], self.recv.at[0], self.p.c_id)

    def own_copy(self):
        return pltpu.make_async_copy(self.plane(self.p.c), self.own, self.local)

    def add(self, dst, *more):
        rows = dst.shape[0]
        n = min(64, rows)

        @pl.loop(0, rows // n)
        def _(i):
            r = pl.ds(pl.multiple_of(i * n, n), n)
            total = dst[r, :].astype(F32)
            for ref in more:
                total += ref[r, :].astype(F32)
            dst[r, :] = total.astype(BF16)

    def first_copy(self, by_y, j, t):
        p = self.p
        yx = (1 - p.y) * 2 + j if by_y else j * 2 + 1 - p.x
        src = half_of(self.block(self.own, t, yx), 0 if by_y else 1)
        k = (0 if by_y else 2) + j
        n = 1 + k * 4 + t
        return remote(src, self.got1.at[k, t], self.send.at[n], self.recv.at[n], p.y_id if by_y else p.x_id)

    def second_copy(self, j, t):
        p = self.p
        by_x = j == 0
        src = half_of(self.block(self.own, t, p.x_yx if by_x else p.y_yx), j)
        return remote(src, self.got2.at[j, t], self.send.at[17 + j * 4 + t], self.recv.at[17 + j * 4 + t],
                      p.x_id if by_x else p.y_id)

    def z_copy(self, k):
        p = self.p
        to = lax.rem(p.t + k, 4)
        src = self.block(self.own, to, p.yx)
        return remote(src, self.got3.at[k - 1], self.send.at[24 + k], self.recv.at[24 + k], p.z_id(to))

    def stage(self, i):
        p = self.p
        if i == 0:
            self.core_copy().start()
            self.own_copy().start()
        if i == 1:
            self.own_copy().wait()
            self.core_copy().wait_recv()
            self.sum_core()
        if i == 2:
            self.sum_first()
        if i == 3:
            self.sum_second()
        if i == 4:
            self.sum_last()

    def sum_core(self):
        p = self.p
        for yx, by_y, by_x in ((p.xy_yx, 1 - p.x, 1 - p.y), (p.y_yx, p.x, None), (p.x_yx, None, p.y), (p.yx, None, None)):
            for t in range(4):
                self.add(self.block(self.own, t, yx), self.block(self.got, t, yx))
                if by_y is not None:
                    self.first_copy(True, by_y, t).start()
                if by_x is not None:
                    self.first_copy(False, by_x, t).start()

    def sum_first(self):
        p = self.p
        for t in range(4):
            for j in range(2):
                self.first_copy(True, j, t).wait_recv()
                self.first_copy(False, j, t).wait_recv()
        for t in range(4):
            self.add(half_of(self.block(self.own, t, p.x_yx), 0), self.got1.at[1 - p.x, t])
            self.second_copy(0, t).start()
            self.add(half_of(self.block(self.own, t, p.y_yx), 1), self.got1.at[2 + 1 - p.y, t])
            self.second_copy(1, t).start()
        for t in range(4):
            self.add(half_of(self.block(self.own, t, p.yx), 0), self.got1.at[p.x, t])
            self.add(half_of(self.block(self.own, t, p.yx), 1), self.got1.at[2 + p.y, t])

    def sum_second(self):
        p = self.p
        for k in (1, 2, 3, 0):
            t = lax.rem(p.t + k, 4)
            for j in (0, 1):
                self.second_copy(j, t).wait_recv()
                self.add(half_of(self.block(self.own, t, p.yx), j), self.got2.at[j, t])
            if k:
                self.z_copy(k).start()

    def sum_last(self):
        p = self.p
        for k in (1, 2, 3):
            self.z_copy(k).wait_recv()
        mine = self.block(self.own, p.t, p.yx)
        rows = mine.shape[0]

        @pl.loop(0, rows // 64)
        def _(i):
            r = pl.ds(pl.multiple_of(i * 64, 64), 64)
            total = mine[r, :].astype(F32)
            for k in range(3):
                total += self.got3[k, r, :].astype(F32)
            self.result[r, :] = total

    def finish(self):
        self.core_copy().wait_send()
        for t in range(4):
            for j in range(2):
                self.first_copy(True, j, t).wait_send()
                self.first_copy(False, j, t).wait_send()
                self.second_copy(j, t).wait_send()
        for k in (1, 2, 3):
            self.z_copy(k).wait_send()


def reduce_shapes(name):
    shape = PARTS[name][0]
    rows, width = shape[3:]
    plane = (4, 4, rows, width)
    return plane, (4, 4, rows // 2, width), (2, 4, rows // 2, width), (3, rows, width), (rows, width)


class Total:
    def __init__(self, place, acc, sent, got, sems):
        self.p, self.acc, self.sent, self.got = place, acc, sent, got
        self.send, self.recv = sems

    def copies(self, i):
        p = self.p
        if i < 3:
            return [remote(self.sent.at[i], self.got.at[i], self.send.at[i], self.recv.at[i], (p.c_id, p.x_id, p.y_id)[i])]
        return [
            remote(self.sent.at[3], self.got.at[2 + k], self.send.at[2 + k], self.recv.at[2 + k], p.z_id(lax.rem(p.t + k, 4)))
            for k in (1, 2, 3)
        ]

    def start(self, i):
        self.sent[i] = self.acc[...]
        for c in self.copies(i):
            c.start()

    def end(self, i):
        for c in self.copies(i):
            c.wait()
        for k in (i,) if i < 3 else (3, 4, 5):
            self.acc[...] += self.got[k]


def reduce_kernel(out_in, gtok_in, sums_in, *rest):
    n = len(REDUCED)
    grads = dict(zip(REDUCED, rest[:n]))
    out, gtok, sums = rest[n : n + 3]
    results = dict(zip(REDUCED, rest[n + 3 : 2 * n + 3]))
    rest = rest[2 * n + 3 :]
    out_buf, gtok_buf, sent, got = rest[:4]
    local_sem, total_send, total_recv = rest[4:7]
    swap_sems = rest[7:11]
    rest = rest[11:]
    place = Place()
    parts = []
    for i, a in enumerate(REDUCED):
        own, got0, got1, got2, got3, send, recv, local = rest[8 * i : 8 * i + 8]
        parts.append(Reduce(place, a, grads[a], own, got0, got1, got2, got3, results[a], (send, recv, local)))
    swaps = [Swap(place, out_in, out, swap_sems[0:2]), Swap(place, gtok_in, gtok, swap_sems[2:4])]
    local = [
        Bounce(out_in.at[place.t], out_buf, out.at[place.t], local_sem.at[0]),
        Bounce(gtok_in.at[place.t], gtok_buf, gtok.at[place.t], local_sem.at[1]),
    ]
    for b in local:
        b.load.start()
    place.greet()
    for r in parts:
        r.stage(0)
    total = Total(place, sums, sent, got, (total_send, total_recv))
    sums[...] = sums_in[...]
    total.start(0)
    for b in local:
        b.load.wait()
        b.store.start()
    for s in swaps:
        s.start()
    small = 0
    for tick in range(1, n + 4):
        for i, r in enumerate(parts):
            if 1 <= tick - i <= 4:
                r.stage(tick - i)
        if small < 4:
            total.end(small)
            small += 1
            if small < 4:
                total.start(small)
    for b in local:
        b.store.wait()
    for s in swaps:
        s.done()
        s.finish()
    for r in parts:
        r.finish()


def reduce(out, gtok, sums, grads):
    n = len(REDUCED)
    shapes = [reduce_shapes(a) for a in REDUCED]
    outs = pl.pallas_call(
        reduce_kernel,
        out_shape=[IMAGE, IMAGE, jax.ShapeDtypeStruct((16, D), F32)]
        + [jax.ShapeDtypeStruct(s[4], F32) for s in shapes],
        in_specs=[ANY, ANY, VM] + [ANY] * n,
        out_specs=[ANY, ANY, VM] + [VM] * n,
        scratch_shapes=[pltpu.VMEM((ROWS, 256), BF16)] * 2
        + [pltpu.VMEM((4, 16, D), F32), pltpu.VMEM((6, 16, D), F32)]
        + [pltpu.SemaphoreType.DMA((2, 2)), pltpu.SemaphoreType.DMA((6,)), pltpu.SemaphoreType.DMA((6,))]
        + Swap.SEMS * 2
        + sum(
            (
                [pltpu.VMEM(s[0], BF16)] * 2
                + [pltpu.VMEM(s[k], BF16) for k in (1, 2, 3)]
                + [pltpu.SemaphoreType.DMA((28,)), pltpu.SemaphoreType.DMA((28,)), pltpu.SemaphoreType.DMA]
                for s in shapes
            ),
            [],
        ),
        compiler_params=pltpu.CompilerParams(
            collective_id=1, has_side_effects=True, vmem_limit_bytes=VMEM_BYTES
        ),
        name="reduce",
    )(out, gtok, sums, *[grads[a].reshape(PARTS[a][0]) for a in REDUCED])
    return outs[0], outs[1], outs[2], dict(zip(REDUCED, outs[3:]))
def gather_plain(w_qkv, w_out, w_fc1, w_fc2):
    def all_of(shard, axis):
        return lax.all_gather(
            lax.all_gather(shard.astype(BF16), "dp", axis=axis, tiled=True), "tensor", axis=0
        )

    wqkv = all_of(w_qkv.reshape(-1, 768), 0)
    wout = all_of(w_out, 1).reshape(D, 8, 128).transpose(1, 0, 2)
    w1 = all_of(w_fc1, 0)
    w2 = all_of(w_fc2, 1).reshape(4 * D, 8, 128).transpose(1, 0, 2)
    return wqkv, wout, w1, w2


def scatter_plain(grads):
    def mine(grad, axis):
        part = lax.psum_scatter(grad, "tensor", scatter_dimension=0, tiled=True)
        return lax.psum_scatter(part, "dp", scatter_dimension=axis, tiled=True).astype(F32)

    g_qkv = mine(grads["wqkv"], 1)[0]
    g_out = mine(grads["wout"].transpose(1, 0, 2).reshape(D, D), 1)
    g_fc1 = mine(grads["w1"], 1)[0]
    g_fc2 = mine(grads["w2"].transpose(1, 0, 2).reshape(4 * D, D), 1)
    return g_qkv, g_out, g_fc1, g_fc2


def on_device(
    dp,
    tokens_in,
    cotangent,
    slot_mask,
    norm1_gain,
    norm1_bias,
    w_qkv,
    b_qkv,
    w_out,
    b_out,
    norm2_gain,
    norm2_bias,
    w_fc1,
    b_fc1,
    w_fc2,
    b_fc2,
):
    def images(rows):
        return jnp.pad(rows.reshape(4, SEQ, 256), ((0, 0), (0, ROWS - SEQ), (0, 0)))

    def exchange(pieces):
        return lax.all_to_all(pieces, "tensor", split_axis=0, concat_axis=0, tiled=True)

    mask = jnp.broadcast_to(
        lax.dynamic_index_in_dim(slot_mask, lax.axis_index("tensor"), 0).astype(F32), (1, 256)
    )
    small = jnp.concatenate(
        (norm1_gain, norm1_bias, b_qkv[0], b_qkv[1], b_out, norm2_gain, norm2_bias, b_fc2)
    ).astype(BF16)
    d, t = lax.axis_index("dp"), lax.axis_index("tensor")
    if dp == 8:
        sv = lax.dynamic_update_slice(jnp.zeros((16, 256), F32), small.astype(F32), (0, d * 32))
        sv = sv.at[8, 0:128].set(b_fc1[0].astype(BF16).astype(F32))
        own = dict(
            sv=sv,
            wqkv=w_qkv.reshape(128, 768).astype(BF16),
            wout=w_out.astype(BF16),
            w1=w_fc1.astype(BF16),
            w2=w_fc2.astype(BF16),
        )
        x, ct, out, probs, vectors, weights, saved = spread(images(tokens_in), images(cotangent), mask, own)
    else:
        vectors = lax.all_gather(
            lax.all_gather(small, "dp", axis=1, tiled=True), "tensor", axis=0
        ).astype(F32)
        hidden_bias = lax.all_gather(
            lax.all_gather(b_fc1.astype(BF16), "dp", axis=1, tiled=True), "tensor", axis=0
        ).astype(F32)
        x = exchange(images(tokens_in))
        ct = exchange(images(cotangent))
        plain = gather_plain(w_qkv, w_out, w_fc1, w_fc2)
        weights = {a: b.reshape(PARTS[a][0]) for a, b in zip(WEIGHTS, plain)}
        out, probs, saved = forward(x, weights, vectors, hidden_bias, mask)
    flat = [weights[a].reshape(GRADS[a].shape) for a in GRADS]
    gtok, sums, grads = backward(x, ct, *flat, vectors, mask, probs, saved)
    if dp == 8:
        out, gtok, sums, got = reduce(out, gtok, jnp.pad(sums, ((0, 4), (0, 0))), grads)
        g_qkv, g_out, g_fc1, g_fc2 = (got[a] for a in GRADS)
        g_small = lax.dynamic_slice(sums, (0, t * 256 + d * 32), (8, 32))
        g_hidden = lax.dynamic_slice(sums, (8 + t, d * 128), (1, 128))
    else:
        g_qkv, g_out, g_fc1, g_fc2 = scatter_plain(grads)
        out, gtok = exchange(out), exchange(gtok)

        def total(part, axis):
            part = lax.psum_scatter(part, "tensor", scatter_dimension=0, tiled=True)
            return lax.psum_scatter(part, "dp", scatter_dimension=axis, tiled=True)

        g_small = total(sums[0:8].reshape(8, 4, 256).transpose(1, 0, 2), 2)[0]
        g_hidden = total(sums[8:12], 1)

    def rows(pieces):
        return pieces[:, :SEQ].reshape(4 * SEQ, 256)

    return (
        rows(out),
        rows(gtok),
        g_small[0:1],
        g_small[1:2],
        g_qkv.reshape(w_qkv.shape),
        g_small[2:4][:, None],
        g_out,
        g_small[4:5],
        g_small[5:6],
        g_small[6:7],
        g_fc1,
        g_hidden,
        g_fc2,
        g_small[7:8],
    )


def solution(mesh):
    both, turned = P("dp", "tensor"), P("tensor", "dp")
    mixed, pair = P("dp", None, "tensor"), P(None, "tensor", "dp")
    params = (turned, turned, mixed, pair, turned, turned, turned, turned, both, turned, turned, turned)
    return jax.shard_map(
        functools.partial(on_device, mesh.shape["dp"]),
        mesh=mesh,
        in_specs=(both, both, P("dp"), *params),
        out_specs=(both, both, *params),
        check_vma=False,
    )
```

```python
import functools
import jax
import jax.numpy as jnp
from jax import lax
from jax.experimental import pallas as pl
from jax.experimental.pallas import tpu as pltpu
from jax.sharding import PartitionSpec as P

D = 1024
HD = 64
SEQ = 577
ROWS = 592
CHUNK = 32
F32 = jnp.float32
BF16 = jnp.bfloat16
LAST = (((1,), (1,)), ((), ()))
VMEM_BYTES = 67_043_328


def mm(a, b):
    return jnp.dot(a, b, preferred_element_type=F32)


def t_mm(a, b):
    return lax.dot_general(a, b, (((0,), (0,)), ((), ())), preferred_element_type=F32)


def mm_t(a, b):
    return lax.dot_general(a, b, LAST, preferred_element_type=F32)


def cols(i, n):
    return pl.ds(pl.multiple_of(i * n, n), n)


def row_stats(values):
    mean = jnp.sum(values, axis=1, keepdims=True) * (1.0 / D)
    centered = values - mean
    var = jnp.sum(centered * centered, axis=1, keepdims=True) * (1.0 / D)
    inv = lax.rsqrt(var + 1e-05)
    return centered * inv, inv


def wide(ref, rows):
    return jnp.concatenate([ref[t, rows, :].astype(F32) for t in range(4)], axis=1)


def over_rows(do):
    @pl.loop(0, 576 // CHUNK)
    def _(i):
        do(pl.ds(pl.multiple_of(i * CHUNK, CHUNK), CHUNK))

    do(pl.ds(576, ROWS - 576))


def vec(vectors, row):
    return jnp.concatenate([vectors[t, row : row + 1, :] for t in range(4)], axis=1)


def norm_in(x, vectors, nin):
    gain, shift = vec(vectors, 0), vec(vectors, 1)

    @over_rows
    def _(rows):
        xhat, _ = row_stats(wide(x, rows))
        nin[rows, :] = (xhat * gain + shift).astype(BF16)


def flip(src, dst, n):
    @pl.loop(0, n // 256)
    def _(i):
        dst[i] = src[:, cols(i, 256)].T.reshape(2, 128, ROWS)


def project(nin, wqkv, vectors, t, q, k, v):
    here = cols(t, 256)

    g = mm(nin[...], wqkv[t].reshape(D, 768))
    q[:, here] = (g[:, 0:256] + vectors[t, 2:3, :]).astype(BF16)
    k[:, here] = g[:, 256:512].astype(BF16)
    v[:, here] = (g[:, 512:768] + vectors[t, 3:4, :]).astype(BF16)


def head_lanes(h):
    lane = lax.broadcasted_iota(jnp.int32, (ROWS, 128), 1)
    own = (lane >= h * 64) & (lane < h * 64 + 64)
    return lane, own, 64 - h * 64


def attend_pair(pair, q, k, v, ctx, probs, slot):
    here = cols(pair, 128)
    lane = lax.broadcasted_iota(jnp.int32, (ROWS, 128), 1)
    row = lax.broadcasted_iota(jnp.int32, (ROWS, 128), 0)
    queries = q[:, here].astype(F32) * (HD**-0.5)
    keys = k[:, here].astype(F32)
    values = v[:, here]
    blocked = jnp.where(row >= SEQ, -1e30, 0.0)
    parts = []
    for h in range(2):
        own = (lane < 64) if h == 0 else (lane >= 64)
        spare = 64 if h == 0 else 0
        qa = jnp.where(own, queries, jnp.where(lane == spare, 1.0, 0.0)).astype(BF16)
        ka = jnp.where(lane == spare, blocked, keys).astype(BF16)
        scores = mm_t(ka, qa)
        top = jnp.max(scores, axis=0, keepdims=True)
        e = jnp.exp(scores - top)
        total = jnp.sum(e, axis=0, keepdims=True)
        p = (e * (1.0 / total)).astype(BF16)
        probs[slot, h] = p
        parts.append(
            lax.dot_general(p, values, (((0,), (0,)), ((), ())), preferred_element_type=F32)
        )
    ctx[:, here] = jnp.where(lane < 64, parts[0], parts[1]).astype(BF16)


def out_block(i, ctx, wout, x, vectors, resid):
    w = jnp.concatenate([wout[i, c].reshape(D, 128) for c in range(2)], axis=1)
    resid[:, cols(i, 256)] = x[i].astype(F32) + mm(ctx[...], w) + vectors[i, 4:5, :]


def norm_mid(resid, vectors, nmid):
    gain, shift = vec(vectors, 5), vec(vectors, 6)

    @over_rows
    def _(rows):
        xhat, _ = row_stats(resid[rows, :])
        nmid[rows, :] = (xhat * gain + shift).astype(BF16)


def hidden_tile(t, j, nmid, w1, b1, act, slope):
    here = pl.ds(pl.multiple_of(t * 1024 + j * 256, 256), 256)
    bias = b1[t, :, cols(j, 256)]
    pre = mm(nmid[...], w1[t, :, :, :, cols(j, 256)].reshape(D, 256)) + bias
    sig = 1.0 / (1.0 + jnp.exp(-1.702 * pre))
    a = pre * sig
    slope[:, here] = (sig + 1.702 * a * (1.0 - sig)).astype(BF16)
    act[:, here] = a.astype(BF16)


def down_block(i, t, act, w2, total):
    w = jnp.concatenate([w2[i, c, t] for c in range(2)], axis=1)
    total[:, cols(i, 256)] += mm(act[:, cols(t, 1024)], w)


def finish_block(i, total, vectors, mask, out):
    out[i] = ((total[:, cols(i, 256)] + vectors[i, 7:8, :]) * mask[...]).astype(BF16)


def grad_norm_rows(values, gain, n):
    xhat, inv = row_stats(values)
    e = n * gain
    first = jnp.sum(e, axis=1, keepdims=True) * (1.0 / D)
    second = jnp.sum(e * xhat, axis=1, keepdims=True) * (1.0 / D)
    return inv * (e - first - xhat * second), n * xhat


def fold(a):
    return jnp.sum(a.reshape(-1, 8, D), axis=0)


def attend_back_pair(queries, keys, values, out, go, probs):
    values_f, go_f = values.astype(F32), go.astype(F32)
    dots = go_f * out.astype(F32)
    dq, dk, dv = [], [], []
    for h in range(2):
        lane, own, spare = head_lanes(h)
        delta = -jnp.sum(jnp.where(own, dots, 0.0), axis=1, keepdims=True)
        high = delta.astype(BF16).astype(F32)
        ga = jnp.where(
            own, go_f, jnp.where(lane == spare, high, jnp.where(lane == spare + 1, delta - high, 0.0))
        ).astype(BF16)
        marks = jnp.where((lane == spare) | (lane == spare + 1), 1.0, 0.0)
        va = jnp.where(own, values_f, marks).astype(BF16)
        p = probs[h]
        gs = (p.astype(F32) * mm_t(va, ga)).astype(BF16)
        dv.append(mm(p, go))
        dk.append(mm(gs, queries))
        dq.append(
            lax.dot_general(gs, keys, (((0,), (0,)), ((), ())), preferred_element_type=F32)
        )
    low = head_lanes(0)[1]
    scale = HD**-0.5
    return (
        jnp.where(low, dq[0], dq[1]) * scale,
        jnp.where(low, dk[0], dk[1]) * scale,
        jnp.where(low, dv[0], dv[1]),
    )


ACT = jax.ShapeDtypeStruct((ROWS, D), BF16)
TURNED = jax.ShapeDtypeStruct((4, 2, 128, ROWS), BF16)
SAVED = dict(
    nin_t=TURNED,
    q=ACT,
    k=ACT,
    v=ACT,
    ctx=ACT,
    ctx_t=TURNED,
    nmid_t=TURNED,
    resid=jax.ShapeDtypeStruct((ROWS, D), F32),
    act=jax.ShapeDtypeStruct((ROWS, 4 * D), BF16),
    slope=jax.ShapeDtypeStruct((ROWS, 4 * D), BF16),
)
PROBS = jax.ShapeDtypeStruct((8, 2, ROWS, ROWS), BF16)
IMAGE = jax.ShapeDtypeStruct((4, ROWS, 256), BF16)
ANY = pl.BlockSpec(memory_space=pl.ANY)
VM = pl.BlockSpec(memory_space=pltpu.VMEM)


def scratch(like):
    return pltpu.VMEM(like.shape, like.dtype)


PARTS = dict(
    sv=((4, 4, 2, 16, 256), F32),
    wqkv=((4, 4, 2, 128, 768), BF16),
    wout=((4, 2, 4, 256, 128), BF16),
    w1=((4, 4, 2, 128, 1024), BF16),
    w2=((4, 2, 4, 1024, 128), BF16),
)
WEIGHTS = ("wqkv", "wout", "w1", "w2")


def part(name):
    return jax.ShapeDtypeStruct(*PARTS[name])


class Forward:
    SCRATCH = [scratch(a) for a in SAVED.values()] + [
        scratch(ACT),
        pltpu.VMEM((2, 2, ROWS, ROWS), BF16),
        pltpu.SemaphoreType.DMA((2,)),
        pltpu.SemaphoreType.DMA((len(SAVED) + 1,)),
    ]

    def __init__(self, x, weights, vectors, b1, mask, out, out_h, probs_h, saved_h, refs):
        n = len(SAVED)
        self.x, self.w, self.vectors, self.b1, self.mask = x, weights, vectors, b1, mask
        self.out, self.out_h, self.probs_h, self.saved_h = out, out_h, probs_h, saved_h
        self.saved = dict(zip(SAVED, refs[:n]))
        self.total = self.saved["resid"]
        self.normed, self.probs, self.probs_sem, self.out_sem = refs[n:]
        self.act = self.saved["act"]

    def start_norm(self):
        norm_in(self.x, self.vectors, self.normed)
        flip(self.normed, self.saved["nin_t"], D)

    def put(self, pair, slot):
        return pltpu.make_async_copy(self.probs.at[slot], self.probs_h.at[pair], self.probs_sem.at[slot])

    def heads(self, s, i):
        a = self.saved
        project(self.normed, self.w["wqkv"], self.vectors, s, a["q"], a["k"], a["v"])

        @pl.loop(0, 2)
        def _(slot):
            pair = s * 2 + slot
            if i:
                self.put(pair, slot).wait()
            attend_pair(pair, a["q"], a["k"], a["v"], a["ctx"], self.probs, slot)
            self.put(pair, slot).start()

    def middle(self):
        a = self.saved

        @pl.loop(0, 4)
        def _(i):
            out_block(i, a["ctx"], self.w["wout"], self.x, self.vectors, a["resid"])

        norm_mid(a["resid"], self.vectors, self.normed)

    def hidden(self, s):
        @pl.loop(0, 4)
        def _(j):
            hidden_tile(s, j, self.normed, self.w["w1"], self.b1, self.act, self.saved["slope"])

    def down(self, s):
        @pl.loop(0, 4)
        def _(i):
            down_block(i, s, self.act, self.w["w2"], self.total)

    def turn(self):
        flip(self.saved["ctx"], self.saved["ctx_t"], D)
        flip(self.normed, self.saved["nmid_t"], D)

    def finish(self):
        @pl.loop(0, 4)
        def _(i):
            finish_block(i, self.total, self.vectors, self.mask, self.out)

    def stores(self, names):
        at = list(SAVED)
        return [
            pltpu.make_async_copy(self.saved[a], self.saved_h[a], self.out_sem.at[at.index(a)]) for a in names
        ]

    def store_out(self):
        return pltpu.make_async_copy(self.out, self.out_h, self.out_sem.at[len(SAVED)])

    def drain_last(self, s):
        for slot in range(2):
            self.put(s * 2 + slot, slot).wait()

    def drain(self):
        for slot in range(2):
            self.put(6 + slot, slot).wait()


def forward_kernel(x_h, wqkv_h, wout_h, w1_h, w2_h, vectors, b1, mask, *rest):
    n = len(SAVED)
    saved_h = dict(zip(SAVED, rest[2 : 2 + n]))
    x, out, *weights, in_sem = rest[2 + n : 9 + n]
    loads = [
        pltpu.make_async_copy(a, b, in_sem.at[i])
        for i, (a, b) in enumerate(zip((x_h, wqkv_h, wout_h, w1_h, w2_h), (x, *weights)))
    ]
    for c in loads:
        c.start()
    for c in loads:
        c.wait()
    f = Forward(x, dict(zip(WEIGHTS, weights)), vectors, b1, mask, out, rest[0], rest[1], saved_h, rest[9 + n :])
    f.start_norm()
    for s in range(4):
        f.heads(s, s)
    f.middle()
    for c in f.stores(("resid",)):
        c.start()
        c.wait()
    for s in range(4):
        f.hidden(s)
        f.down(s)
    f.turn()
    f.finish()
    f.drain()
    stores = [*f.stores([a for a in SAVED if a != "resid"]), f.store_out()]
    for c in stores:
        c.start()
    for c in stores:
        c.wait()


def forward(x, weights, vectors, b1, mask):
    n = len(SAVED)
    outs = pl.pallas_call(
        forward_kernel,
        out_shape=[IMAGE, PROBS, *SAVED.values()],
        in_specs=[ANY] * 5 + [VM, VM, VM],
        out_specs=[ANY] * (2 + n),
        scratch_shapes=[scratch(IMAGE), scratch(IMAGE)]
        + [scratch(part(a)) for a in WEIGHTS]
        + [pltpu.SemaphoreType.DMA((5,))]
        + Forward.SCRATCH,
        compiler_params=pltpu.CompilerParams(vmem_limit_bytes=VMEM_BYTES),
        name="forward",
    )(x, *[weights[a] for a in WEIGHTS], vectors, b1, mask)
    return outs[0], outs[1], dict(zip(SAVED, outs[2:]))


GRADS = dict(
    wqkv=jax.ShapeDtypeStruct((4, 1024, 768), BF16),
    wout=jax.ShapeDtypeStruct((8, 1024, 128), BF16),
    w1=jax.ShapeDtypeStruct((4, 1024, 1024), BF16),
    w2=jax.ShapeDtypeStruct((8, 4096, 128), BF16),
)


def send_tile(stage, sem, i, value, targets):
    slot = lax.rem(i, 2)

    def copies(s):
        return [
            pltpu.make_async_copy(
                stage.at[s] if w == 256 else stage.at[s, :, pl.ds(c, w)], ref, sem.at[s]
            )
            for ref, c, w in targets
        ]

    @pl.when(i >= 2)
    def _():
        pltpu.make_async_copy(stage.at[slot], stage.at[slot], sem.at[slot]).wait()

    stage[slot] = value
    for c in copies(slot):
        c.start()


def drain(stage, sem):
    for slot in range(2):
        pltpu.make_async_copy(stage.at[slot], stage.at[slot], sem.at[slot]).wait()


def backward_kernel(x_h, ct_h, wqkv_h, wout_h, w1_h, w2_h, vectors, mask, probs_h, *rest):
    n = len(SAVED)
    saved_h = dict(zip(SAVED, rest[:n]))
    gtok_h, sums_o = rest[n], rest[n + 1]
    g_h = dict(zip(GRADS, rest[n + 2 : n + 6]))
    rest = rest[n + 6 :]
    saved = dict(zip(SAVED, rest[:n]))
    (x, wqkv, wout, w1, w2, b1, gmlp, gattn, gctx, gn, gmix, probs, sums, part, stage,
     in_sem, probs_sem, tile_sem, saved_sem) = rest[n:]
    gtok = x
    names = dict(ct=(ct_h, gtok), x=(x_h, x), w2=(w2_h, w2), w1=(w1_h, w1), wout=(wout_h, wout), wqkv=(wqkv_h, wqkv))
    load = {a: pltpu.make_async_copy(*names[a], in_sem.at[i]) for i, a in enumerate(names)}
    load_saved = {a: pltpu.make_async_copy(saved_h[a], saved[a], saved_sem.at[i]) for i, a in enumerate(SAVED)}
    load["ct"].start()
    load_saved["act"].start()
    load_saved["slope"].start()
    for a in ("w2", "w1", "wout", "wqkv"):
        load[a].start()
    for a in SAVED:
        if a not in ("act", "slope"):
            load_saved[a].start()
    part[...] = jnp.zeros_like(part)
    sums[...] = jnp.zeros_like(sums)
    load["ct"].wait()

    @over_rows
    def _(rows):
        g = jnp.concatenate([x[t, rows, :].astype(F32) * mask[...] for t in range(4)], axis=1)
        gmlp[rows, :] = g.astype(BF16)
        part[0] += fold(g)

    load["x"].start()
    load_saved["act"].wait()

    @pl.loop(0, 16)
    def _(i):
        t, c = i // 4, i % 4
        r = t_mm(saved["act"][:, cols(t, 1024)], gmlp[:, cols(c, 256)]).astype(BF16)
        send_tile(stage, tile_sem, i, r, [
            (g_h["w2"].at[2 * c + e, cols(t, 1024), :], e * 128, 128) for e in range(2)])

    load_saved["slope"].wait()
    load["w2"].wait()
    slope = saved["slope"]

    @pl.loop(0, 16)
    def _(i):
        w = jnp.concatenate([w2[d, cols(i, 256), :] for d in range(8)], axis=1)
        gpre = mm_t(gmlp[...], w) * slope[:, cols(i, 256)].astype(F32)
        slope[:, cols(i, 256)] = gpre.astype(BF16)
        b1[i // 4, :, cols(i % 4, 256)] = jnp.sum(gpre, axis=0, keepdims=True)

    load_saved["nmid_t"].wait()

    @pl.loop(0, 16)
    def _(i):
        r = mm(saved["nmid_t"][...].reshape(D, ROWS), slope[:, cols(i, 256)]).astype(BF16)
        send_tile(stage, tile_sem, i + 16, r, [(g_h["w1"].at[i // 4, :, cols(i % 4, 256)], 0, 256)])

    load["w1"].wait()

    @pl.loop(0, 4)
    def _(i):
        total = mm_t(slope[:, 0:1024], w1[0, cols(i, 256), :])
        for t in range(1, 4):
            total += mm_t(slope[:, t * 1024 : t * 1024 + 1024], w1[t, cols(i, 256), :])
        gn[:, cols(i, 256)] = total

    load_saved["resid"].wait()
    gain2 = vec(vectors, 5)

    @over_rows
    def _(rows):
        normed = gn[rows, :]
        g, scaled = grad_norm_rows(saved["resid"][rows, :], gain2, normed)
        g = g + gmlp[rows, :].astype(F32)
        part[1] += fold(normed)
        part[2] += fold(scaled)
        part[3] += fold(g)
        gn[rows, :] = g
        gattn[rows, :] = g.astype(BF16)

    load["wout"].wait()
    load_saved["ctx_t"].wait()

    @pl.loop(0, 4)
    def _(i):
        w = jnp.concatenate([wout[d, cols(i, 256), :] for d in range(8)], axis=1)
        gctx[:, cols(i, 256)] = mm_t(gattn[...], w).astype(BF16)
        r = mm(saved["ctx_t"][...].reshape(D, ROWS), gattn[:, cols(i, 256)]).astype(BF16)
        send_tile(stage, tile_sem, i + 32, r, [(g_h["wout"].at[2 * i + e], e * 128, 128) for e in range(2)])

    for a in ("q", "k", "v", "ctx"):
        load_saved[a].wait()

    def get(pair, slot):
        return pltpu.make_async_copy(probs_h.at[pair], probs.at[slot], probs_sem.at[slot])

    get(0, 0).start()

    @pl.loop(0, 8)
    def _(pair):
        slot = pair % 2

        @pl.when(pair < 7)
        def _():
            get(pair + 1, 1 - slot).start()

        get(pair, slot).wait()
        here = cols(pair, 128)

        got = attend_back_pair(
            *(saved[a][:, here] for a in ("q", "k", "v", "ctx")), gctx[:, here], probs.at[slot]
        )
        for c in range(3):
            at = pl.ds(pl.multiple_of(c * 256 + (pair % 2) * 128, 128), 128)
            gmix[pair // 2, :, at] = got[c].astype(BF16)
        sums[2:3, here] = jnp.sum(got[0], axis=0, keepdims=True)
        sums[3:4, here] = jnp.sum(got[2], axis=0, keepdims=True)

    load_saved["nin_t"].wait()

    @pl.loop(0, 12)
    def _(i):
        t, c = i // 3, i % 3
        r = mm(saved["nin_t"][...].reshape(D, ROWS), gmix[t, :, cols(c, 256)]).astype(BF16)
        send_tile(stage, tile_sem, i + 36, r, [(g_h["wqkv"].at[t, :, cols(c, 256)], 0, 256)])

    load["wqkv"].wait()
    resid = saved["resid"]

    @pl.loop(0, 4)
    def _(i):
        total = mm_t(gmix[0], wqkv[0, cols(i, 256), :])
        for t in range(1, 4):
            total += mm_t(gmix[t], wqkv[t, cols(i, 256), :])
        resid[:, cols(i, 256)] = total

    load["x"].wait()
    gain1 = vec(vectors, 0)

    @over_rows
    def _(rows):
        normed = resid[rows, :]
        g, scaled = grad_norm_rows(wide(x, rows), gain1, normed)
        g = g + gn[rows, :]
        part[4] += fold(normed)
        part[5] += fold(scaled)
        for t in range(4):
            gtok[t, rows, :] = g[:, t * 256 : t * 256 + 256].astype(BF16)

    for row, i in ((7, 0), (6, 1), (5, 2), (4, 3), (1, 4), (0, 5)):
        sums[row : row + 1, :] = jnp.sum(part[i], axis=0, keepdims=True)
    sums_o[0:8, :] = sums[...]
    for t in range(4):
        sums_o[8 + t : 9 + t, :] = b1[t]
    done = pltpu.make_async_copy(gtok, gtok_h, in_sem.at[0])
    done.start()
    done.wait()
    drain(stage, tile_sem)


def backward(x, ct, wqkv, wout, w1, w2, vectors, mask, probs, saved):
    n = len(SAVED)
    outs = pl.pallas_call(
        backward_kernel,
        out_shape=[IMAGE, jax.ShapeDtypeStruct((12, D), F32), *GRADS.values()],
        in_specs=[ANY] * 6 + [VM, VM, ANY] + [ANY] * n,
        out_specs=[ANY, VM] + [ANY] * 4,
        scratch_shapes=[scratch(a) for a in SAVED.values()]
        + [scratch(a) for a in (x, wqkv, wout, w1, w2)]
        + [
            pltpu.VMEM((4, 1, 1024), F32),
            scratch(ACT),
            scratch(ACT),
            scratch(ACT),
            pltpu.VMEM((ROWS, D), F32),
            pltpu.VMEM((4, ROWS, 768), BF16),
            pltpu.VMEM((2, 2, ROWS, ROWS), BF16),
            pltpu.VMEM((8, D), F32),
            pltpu.VMEM((6, 8, D), F32),
            pltpu.VMEM((2, 1024, 256), BF16),
            pltpu.SemaphoreType.DMA((6,)),
            pltpu.SemaphoreType.DMA((2,)),
            pltpu.SemaphoreType.DMA((2,)),
            pltpu.SemaphoreType.DMA((n,)),
        ],
        compiler_params=pltpu.CompilerParams(vmem_limit_bytes=VMEM_BYTES),
        name="backward",
    )(x, ct, wqkv, wout, w1, w2, vectors, mask, probs, *[saved[a] for a in SAVED])
    return outs[0], outs[1], dict(zip(GRADS, outs[2:]))


MESH = pl.DeviceIdType.MESH
BY_COLUMN = ("wout", "w2")


def block_of(name, ref, t, yx, c):
    return ref.at[yx, c, t] if name in BY_COLUMN else ref.at[t, yx, c]


def half_of(ref, h):
    n = ref.shape[0] // 2
    return ref.at[pl.ds(h * n, n)]


class Place:
    def __init__(self):
        d, self.t = lax.axis_index("dp"), lax.axis_index("tensor")
        self.y, self.x, self.c = d // 4, d // 2 % 2, d % 2
        self.yx = d // 2
        self.x_yx = self.y * 2 + 1 - self.x
        self.y_yx = (1 - self.y) * 2 + self.x
        self.xy_yx = (1 - self.y) * 2 + 1 - self.x
        self.d = d
        self.x_id = (self.x_yx * 2 + self.c, self.t)
        self.y_id = (self.y_yx * 2 + self.c, self.t)
        self.c_id = (self.yx * 2 + 1 - self.c, self.t)

    def z_id(self, t):
        return (self.d, t)

    def order(self, i):
        t = self.t
        near, far = (t, t + 1 - 2 * (t % 2)), (2 - t // 2, 3 - 3 * (t // 2))
        if isinstance(i, int):
            return (near + far)[i]
        half, odd = i // 2, i % 2
        return (1 - half) * (near[0] + odd * (near[1] - near[0])) + half * (far[0] + odd * (far[1] - far[0]))

    def greet(self):
        barrier = pltpu.get_barrier_semaphore()
        others = [self.x_id, self.y_id, self.c_id]
        others += [self.z_id(lax.rem(self.t + k, 4)) for k in (1, 2, 3)]
        for other in others:
            pl.semaphore_signal(barrier, inc=1, device_id=other, device_id_type=MESH)
        pl.semaphore_wait(barrier, 6)


def remote(src, dst, send, recv, where):
    return pltpu.make_async_remote_copy(
        src_ref=src, dst_ref=dst, send_sem=send, recv_sem=recv, device_id=where, device_id_type=MESH
    )


class Gather:
    SEMS = [
        pltpu.SemaphoreType.DMA((2, 4)),
        pltpu.SemaphoreType.DMA((4,)),
        pltpu.SemaphoreType.DMA((4, 6)),
        pltpu.SemaphoreType.DMA((4, 6)),
        pltpu.SemaphoreType.DMA((4,)),
        pltpu.SemaphoreType.DMA((4,)),
    ]

    def __init__(self, place, name, own, whole, sems):
        self.p, self.name, self.own, self.whole = place, name, own, whole
        self.z_send, self.z_recv, self.xy_send, self.xy_recv, self.c_send, self.c_recv = sems

    def at(self, s, yx):
        return block_of(self.name, self.whole, s, yx, self.p.c)

    def z_copies(self, s, act, src=None):
        p = self.p
        dst = self.at(s, p.yx)
        for way, going, to in ((0, (s <= p.t) & (p.t < 3), p.t + 1), (1, (s >= p.t) & (p.t > 0), p.t - 1)):

            @pl.when(going)
            def _():
                c = remote(dst if src is None else src, dst, self.z_send.at[way, s], self.z_recv.at[s], p.z_id(to))
                c.start() if act == "start" else c.wait_send()

    def xy_copy(self, k, s, mine=False):
        p = self.p
        yx = (p.yx, p.yx, p.yx, p.x_yx, p.yx, p.y_yx)[k]
        h = (0, 1, 0, 0, 1, 1)[k]
        to = (p.x_id, p.y_id, p.y_id, p.y_id, p.x_id, p.x_id)[k]
        dst = half_of(self.at(s, yx), h)
        src = half_of(self.own, h) if mine else dst
        return remote(src, dst, self.xy_send.at[s, k], self.xy_recv.at[s, k], to)

    def straight(self, k):
        p = self.p
        return remote(
            self.own, self.at(p.t, p.yx), self.z_send.at[0, k], self.z_recv.at[p.t], p.z_id(lax.rem(p.t + k, 4))
        )

    def open(self):
        s = self.p.t
        if self.name == "sv":
            for k in (1, 2, 3):
                self.straight(k).start()
        else:
            self.z_copies(s, "start", self.own)
        for k in (0, 1):
            self.xy_copy(k, s, True).start()

    def arrive(self, i):
        s = self.p.order(i)
        here = self.at(s, self.p.yx)
        remote(here, here, self.z_send.at[0, s], self.z_recv.at[s], self.p.c_id).wait_recv()
        if self.name != "sv":
            self.z_copies(s, "start")
        for k in (0, 1):
            self.xy_copy(k, s).start()

    def second(self, i):
        s = self.p.order(i)
        for got, own, other in ((0, 2, 3), (1, 4, 5)):
            self.xy_copy(own, s, isinstance(i, int) and i == 0).start()
            self.xy_copy(got, s).wait_recv()
            self.xy_copy(other, s).start()

    def core_copy(self, s):
        c = self.p.c
        ref = self.whole.at[:, c, s] if self.name in BY_COLUMN else self.whole.at[s, :, c]
        return remote(ref, ref, self.c_send.at[s], self.c_recv.at[s], self.p.c_id)

    def last(self, i):
        s = self.p.order(i)
        for k in (2, 3, 4, 5):
            self.xy_copy(k, s).wait_recv()
        self.core_copy(s).start()

    def have(self, i):
        self.core_copy(self.p.order(i)).wait_recv()

    def finish(self):
        for s in range(4):
            if self.name != "sv":
                self.z_copies(s, "wait")
            elif s:
                self.straight(s).wait_send()
            for k in range(6):
                self.xy_copy(k, s).wait_send()
            self.core_copy(s).wait_send()


class Swap:
    SEMS = [pltpu.SemaphoreType.DMA((4,)), pltpu.SemaphoreType.DMA((4,))]

    def __init__(self, place, pieces, whole, sems):
        self.p, self.pieces, self.whole = place, pieces, whole
        self.send, self.recv = sems

    def copy(self, k):
        p = self.p
        to = lax.rem(p.t + k, 4)
        return remote(self.pieces.at[to], self.whole.at[p.t], self.send.at[k], self.recv.at[k], p.z_id(to))

    def start(self):
        for k in (1, 3, 2):
            self.copy(k).start()

    def done(self):
        for k in (1, 2, 3):
            self.copy(k).wait_recv()

    def finish(self):
        for k in (1, 2, 3):
            self.copy(k).wait_send()


class Mail:
    def __init__(self, place, buf, sem):
        self.p, self.buf, self.sem, self.depth = place, buf, sem, buf.shape[0]

    def copy(self, slot, dst, recv):
        return remote(self.buf.at[slot], dst, self.sem.at[slot], recv, self.p.c_id)

    def post(self, i, parts, dst, recv):
        slot = lax.rem(i, self.depth)

        @pl.when(i >= self.depth)
        def _():
            self.copy(slot, dst, recv).wait_send()

        for k, part in enumerate(parts):
            self.buf[slot, k] = part
        self.copy(slot, dst, recv).start()

    def finish(self):
        for slot in range(self.depth):
            self.copy(slot, self.buf.at[slot], self.sem.at[slot]).wait_send()


def column_pair(ref, q, c):
    return jnp.concatenate([ref[:, cols(q * 4 + c, 128)], ref[:, cols(q * 4 + 2 + c, 128)]], axis=1)


ACTS = ("sv", "wqkv", "wout", "w1", "w2", "XS", "CS", "LN1", "Q", "OUT", "F", "D", "END", "K1")
KINDS = ("", "O", "A", "S", "L")
SEQUENCE = (
    210, 110, 130, 10, 221, 410, 121, 310, 430, 222, 230, 21, 223, 30, 131, 330, 122, 22, 23, 231, 123, 500,
    132, 31, 32, 33, 140, 321, 232, 421, 240, 331, 133, 40, 41, 141, 322, 42, 43, 241, 233, 700, 323, 242,
    142, 800, 440, 431, 801, 143, 422, 332, 340, 341, 802, 243, 333, 803, 423, 432, 600, 900, 1000, 342, 433,
    343, 1001, 1002, 441, 442, 1003, 1300, 1100, 443, 1101, 1102, 1103, 1200,
)


def spread_kernel(x_in, ct_in, mask, *rest):
    names, n, m = list(PARTS), len(PARTS), len(SAVED)
    own = dict(zip(names, rest[:n]))
    x_h, ct_h, out_h, probs_h, vectors = rest[n : n + 5]
    rest = rest[n + 5 :]
    whole_h, saved_h = dict(zip(WEIGHTS, rest[:4])), dict(zip(SAVED, rest[4 : 4 + m]))
    rest = rest[4 + m :]
    x, ct, out, b1 = rest[:4]
    whole = dict(zip(names, rest[4 : 4 + n]))
    rest = rest[4 + n :]
    local_sem, keep_sem = rest[0], rest[1]
    swap_sems, rest = rest[2:6], rest[6:]
    sems, refs = rest[: 6 * n], rest[6 * n :]
    p = Place()
    f = Forward(x, whole, vectors, b1, mask, out, out_h, probs_h, saved_h, refs)
    gathers = {a: Gather(p, a, own[a], whole[a], sems[6 * i : 6 * i + 6]) for i, a in enumerate(names)}
    swaps = dict(XS=Swap(p, x_in, x, swap_sems[0:2]), CS=Swap(p, ct_in, ct, swap_sems[2:4]))
    local = [
        pltpu.make_async_copy(own[a], block_of(a, whole[a], p.t, p.yx, p.c), local_sem.at[i])
        for i, a in enumerate(names)
    ]
    local += [
        pltpu.make_async_copy(x_in.at[p.t], x.at[p.t], local_sem.at[n]),
        pltpu.make_async_copy(ct_in.at[p.t], ct.at[p.t], local_sem.at[n + 1]),
    ]
    for c in local:
        c.start()
    p.greet()
    pending = []
    settled = []
    resid_stored = f.stores(("resid",))

    def keep(src, dst):
        c = pltpu.make_async_copy(src, dst, keep_sem.at[len(pending)])
        c.start()
        pending.append(c)

    def do(code, step):
        name, kind = ACTS[code // 100], KINDS[code // 10 % 10]
        if name in gathers:
            g = gathers[name]
            if kind == "O":
                g.open()
            elif kind == "A":
                g.arrive(step)
            elif kind == "S":
                g.second(step)
            else:
                if not settled:
                    for c in local:
                        c.wait()
                    settled.append(True)
                g.last(step)
        elif name in swaps:
            swaps[name].start()
        elif name == "LN1":
            for i in range(4):
                gathers["sv"].have(i)
            sv = whole["sv"]
            for t in range(4):
                vectors[t] = jnp.sum(sv[t, :, :, 0:8].reshape(8, 8, 256), axis=0)
                for d in range(8):
                    b1[t, :, d * 128 : d * 128 + 128] = sv[t, d // 2, d % 2, 8:9, 0:128]
            swaps["XS"].done()
            keep(x, x_h)
            f.start_norm()
        elif name == "Q":
            gathers["wqkv"].have(step)
            f.heads(p.order(step), step)
        elif name == "OUT":
            for i in range(4):
                gathers["wout"].have(i)
            keep(whole["wqkv"], whole_h["wqkv"])
            keep(whole["wout"], whole_h["wout"])
            f.middle()
            f.turn()
            for c in (*f.stores(("q", "k", "v", "ctx", "nin_t", "ctx_t", "nmid_t")), *resid_stored):
                c.start()
        elif name == "F":
            gathers["w1"].have(step)
            f.hidden(p.order(step))
        elif name == "K1":
            keep(whole["w1"], whole_h["w1"])
            for c in f.stores(("slope", "act")):
                c.start()
            for c in resid_stored:
                c.wait()
        elif name == "D":
            gathers["w2"].have(step)
            f.down(p.order(step))
        elif name == "END":
            keep(whole["w2"], whole_h["w2"])
            f.finish()
            f.store_out().start()
            swaps["CS"].done()
            keep(ct, ct_h)
    for item in SEQUENCE:
        if isinstance(item, int):
            do(item, item % 10)
            continue

        @pl.loop(0, 4 + max(code % 10 for code in item))
        def _(m, item=item):
            for code in item:
                lag = code % 10

                @pl.when((m >= lag) & (m < lag + 4))
                def _():
                    do(code, m - lag)

    f.drain_last(p.order(3))
    for c in [*pending, *f.stores([a for a in SAVED if a != "resid"]), f.store_out()]:
        c.wait()
    for s in swaps.values():
        s.finish()
    for g in gathers.values():
        g.finish()


def spread(x_in, ct_in, mask, own):
    names, n, m = list(PARTS), len(PARTS), len(SAVED)
    outs = pl.pallas_call(
        spread_kernel,
        out_shape=[IMAGE, IMAGE, IMAGE, PROBS, jax.ShapeDtypeStruct((4, 8, 256), F32)]
        + [part(a) for a in WEIGHTS]
        + list(SAVED.values()),
        in_specs=[ANY, ANY, VM] + [ANY] * n,
        out_specs=[ANY] * 4 + [VM] + [ANY] * (4 + m),
        scratch_shapes=[scratch(IMAGE), scratch(IMAGE), scratch(IMAGE), pltpu.VMEM((4, 1, 1024), F32)]
        + [scratch(part(a)) for a in names]
        + [pltpu.SemaphoreType.DMA((n + 2,)), pltpu.SemaphoreType.DMA((7,))]
        + Swap.SEMS * 2
        + Gather.SEMS * n
        + Forward.SCRATCH,
        compiler_params=pltpu.CompilerParams(
            collective_id=0, has_side_effects=True, vmem_limit_bytes=VMEM_BYTES
        ),
        name="spread",
    )(x_in, ct_in, mask, *[own[a] for a in names])
    return outs[:5], dict(zip(WEIGHTS, outs[5:9])), dict(zip(SAVED, outs[9:]))


REDUCED = ("w2", "w1", "wout", "wqkv")


def turn_of(i):
    return (1 - i // 2) * (1 - i % 2) * 3 + i // 2 * (2 - i % 2)


class Reduce:
    def __init__(self, place, name, refs):
        self.p, self.name = place, name
        self.own, self.got1, self.got2, self.got3 = refs[:4]
        self.c_recv, self.send, self.recv, self.z_send, self.z_recv = refs[4:]

    @staticmethod
    def scratch(name):
        rows, width = PARTS[name][0][3:]
        return [
            pltpu.VMEM((4, 4, rows, width), BF16),
            pltpu.VMEM((4, 4, rows // 2, width), BF16),
            pltpu.VMEM((2, 4, rows // 2, width), BF16),
            pltpu.VMEM((5, rows, width), BF16),
            pltpu.SemaphoreType.DMA((4,)),
            pltpu.SemaphoreType.DMA((4, 6)),
            pltpu.SemaphoreType.DMA((4, 6)),
            pltpu.SemaphoreType.DMA((4,)),
            pltpu.SemaphoreType.DMA((5,)),
        ]

    def block(self, ref, t, yx):
        return ref.at[yx, t] if self.name in BY_COLUMN else ref.at[t, yx]

    def wait_bytes(self, ref, sem):
        remote(ref, ref, self.z_send.at[0], sem, self.p.c_id).wait_recv()

    def add(self, dst, *more):
        rows, width = dst.shape
        n = min(rows, 64 if width > 128 else 512)

        @pl.loop(0, rows // n)
        def _(i):
            r = pl.ds(pl.multiple_of(i * n, n), n)
            total = dst[r, :]
            for ref in more:
                total += ref[r, :]
            dst[r, :] = total

    def first_copy(self, by_y, j, t):
        p = self.p
        yx = (1 - p.y) * 2 + j if by_y else j * 2 + 1 - p.x
        src = half_of(self.block(self.own, t, yx), 0 if by_y else 1)
        k = (0 if by_y else 2) + j
        return remote(src, self.got1.at[k, t], self.send.at[t, k], self.recv.at[t, k], p.y_id if by_y else p.x_id)

    def second_copy(self, j, t):
        p = self.p
        by_x = j == 0
        src = half_of(self.block(self.own, t, p.x_yx if by_x else p.y_yx), j)
        return remote(src, self.got2.at[j, t], self.send.at[t, 4 + j], self.recv.at[t, 4 + j],
                      p.x_id if by_x else p.y_id)

    def other_core(self, t=None):
        ref = self.own if t is None else self.own.at[:, t] if self.name in BY_COLUMN else self.own.at[t]
        self.wait_bytes(ref, self.c_recv.at[0 if t is None else t])

    def begin(self, t):
        p = self.p
        self.first_copy(True, 1 - p.x, t).start()
        self.first_copy(False, 1 - p.y, t).start()
        self.first_copy(True, p.x, t).start()
        self.first_copy(False, p.y, t).start()

    def cross(self, i):
        p, t = self.p, turn_of(i)
        for j in range(2):
            self.first_copy(True, j, t).wait_recv()
            self.first_copy(False, j, t).wait_recv()
        self.add(half_of(self.block(self.own, t, p.x_yx), 0), self.got1.at[1 - p.x, t])
        self.second_copy(0, t).start()
        self.add(half_of(self.block(self.own, t, p.y_yx), 1), self.got1.at[2 + 1 - p.y, t])
        self.second_copy(1, t).start()
        self.add(half_of(self.block(self.own, t, p.yx), 0), self.got1.at[p.x, t])
        self.add(half_of(self.block(self.own, t, p.yx), 1), self.got1.at[2 + p.y, t])

    def along(self, i):
        p, t = self.p, turn_of(i)
        mine = self.block(self.own, t, p.yx)
        for j in (0, 1):
            self.second_copy(j, t).wait_recv()
            self.add(half_of(mine, j), self.got2.at[j, t])
        for up, ends in ((True, (p.t == 0) & (t > 0)), (False, (p.t == 3) & (t < 3))):

            @pl.when(ends)
            def _():
                self.send_z(t, up).start()

    def pass_on(self, i, hop):
        p, t = self.p, turn_of(i)
        mine = self.block(self.own, t, p.yx)
        for up, here in ((True, (p.t == hop) & (t > hop)), (False, (p.t == 3 - hop) & (t < 3 - hop))):

            @pl.when(here)
            def _():
                self.wait_bytes(self.got3.at[t], self.z_recv.at[t])
                self.add(mine, self.got3.at[t])
                self.send_z(t, up).start()

    def send_z(self, t, up):
        p = self.p
        slot = t if up else t + (4 - t) * ((3 + t - p.t) // 2)
        return remote(self.block(self.own, t, p.yx), self.got3.at[slot], self.z_send.at[t], self.z_recv.at[slot],
                      p.z_id(p.t + 1 if up else p.t - 1))

    def end(self, result):
        p = self.p
        mine = self.block(self.own, p.t, p.yx)
        rows, width = mine.shape
        n = min(rows, 32 if width > 128 else 256)

        def through(ref):
            @pl.loop(0, rows // n)
            def _(i):
                r = pl.ds(pl.multiple_of(i * n, n), n)
                result[r, :] = (mine if ref is mine else result)[r, :].astype(F32) + (
                    0.0 if ref is mine else ref[r, :].astype(F32)
                )

        through(mine)
        for slot, there in ((p.t, p.t > 0), (4, p.t < 3)):

            @pl.when(there)
            def _():
                self.wait_bytes(self.got3.at[slot], self.z_recv.at[slot])
                through(self.got3.at[slot])

    def finish(self):
        p = self.p
        for t in range(4):
            for j in range(2):
                self.first_copy(True, j, t).wait_send()
                self.first_copy(False, j, t).wait_send()
                self.second_copy(j, t).wait_send()

            @pl.when(p.t != t)
            def _():
                block = self.block(self.own, t, p.yx)
                remote(block, block, self.z_send.at[t], self.z_recv.at[t], p.c_id).wait_send()


class Total:
    SCRATCH = [
        pltpu.VMEM((4, 16, D), F32),
        pltpu.VMEM((6, 16, D), F32),
        pltpu.SemaphoreType.DMA((6,)),
        pltpu.SemaphoreType.DMA((6,)),
    ]

    def __init__(self, place, acc, refs):
        self.p, self.acc = place, acc
        self.sent, self.got, self.send, self.recv = refs

    def copies(self, i):
        p = self.p
        if i < 3:
            return [remote(self.sent.at[i], self.got.at[i], self.send.at[i], self.recv.at[i], (p.c_id, p.x_id, p.y_id)[i])]
        return [
            remote(self.sent.at[3], self.got.at[2 + k], self.send.at[2 + k], self.recv.at[2 + k], p.z_id(lax.rem(p.t + k, 4)))
            for k in (1, 2, 3)
        ]

    def start(self, i):
        self.sent[i] = self.acc[...]
        for c in self.copies(i):
            c.start()

    def end(self, i):
        for c in self.copies(i):
            c.wait()
        for k in (i,) if i < 3 else (3, 4, 5):
            self.acc[...] += self.got[k]


class Stream:
    def __init__(self, n, src, buf, sem):
        self.n, self.src, self.buf, self.sem = n, src, buf, sem
        self.depth = buf.shape[0]

    def copies(self, i):
        slot = lax.rem(i, self.depth)
        return [
            pltpu.make_async_copy(a, b, self.sem.at[slot, k])
            for k, (a, b) in enumerate(self.src(i, self.buf.at[slot]))
        ]

    def start(self):
        for i in range(min(self.depth - 1, self.n)):
            for c in self.copies(jnp.int32(i)):
                c.start()

    def next(self, i):
        for c in self.copies(i):
            c.wait()

        @pl.when(i + self.depth - 1 < self.n)
        def _():
            for c in self.copies(i + self.depth - 1):
                c.start()

        return self.buf.at[lax.rem(i, self.depth)]


def accumulate(ref, here, value, step):
    @pl.when(step == 0)
    def _():
        ref[:, here] = value

    @pl.when(step > 0)
    def _():
        ref[:, here] += value


BACK = ("w2", "w1", "wout", "wqkv", "T", "G0", "GS", "GM", "SHARE", "HG", "HS", "HM", "GN", "GR", "OA", "OM", "AT", "AM", "GI", "GT")
STEPS = ("", "X", "Z", "E", "Y", "W")
COLLECT = (
    500, (600, 701,), (900,), 1200, 800, 1300, 1400, 10, 13, 11, 12, 1500, (1600, 1701, 20,), 311, 1800, 211,
    312, 40, 43, 53, 42, 41, 210, 1900, 213, 313, 310, (1000, 1101,), 212, 220, 51, 110, 223, 323, 50, 111,
    322, 321, 343, 112, 342, 52, 320, 352, 113, 400, 221, 241, 341, 120, 222, 243, 240, 353, 250, 340, 350,
    121, 253, 122, 140, 351, 251, 242, 123, 30, 141, 142, 401, 151, 252, 152, 330, 402, 150, 143, 230, 153,
    403, 130,
)


class Backward:
    NAMES = (
        ("image", "gmlp", "slope", "gmix", "gn", "resid", "split", "ctx_t", "b1", "part_sums", "load_sem")
        + ("col_buf", "col_sem", "row_buf", "row_sem", "head_buf", "head_sem", "probs", "probs_sem")
        + ("up_mail", "up_mail_sem", "mix_mail", "mix_mail_sem", "out_mail", "out_mail_sem", "down_mail", "down_mail_sem")
    )
    SCRATCH = [
        scratch(IMAGE),
        scratch(ACT),
        pltpu.VMEM((ROWS, 4 * D), BF16),
        pltpu.VMEM((ROWS, 3 * D), BF16),
        pltpu.VMEM((ROWS, D), F32),
        pltpu.VMEM((ROWS, D), F32),
        pltpu.VMEM((2, 4, 128, ROWS), BF16),
        pltpu.VMEM((4, 2, 128, ROWS), BF16),
        pltpu.VMEM((4, 1, 1024), F32),
        pltpu.VMEM((6, 8, D), F32),
        pltpu.SemaphoreType.DMA((12,)),
        pltpu.VMEM((3, 4, 2, 2, 256, 128), BF16),
        pltpu.SemaphoreType.DMA((3, 2)),
        pltpu.VMEM((3, 2, 2, 128, 1024), BF16),
        pltpu.SemaphoreType.DMA((3, 1)),
        pltpu.VMEM((3, 4, ROWS, 128), BF16),
        pltpu.SemaphoreType.DMA((3, 4)),
        pltpu.VMEM((2, 2, ROWS, ROWS), BF16),
        pltpu.SemaphoreType.DMA((2, 1)),
        pltpu.VMEM((2, 4, 128, 512), BF16),
        pltpu.SemaphoreType.DMA((2,)),
        pltpu.VMEM((2, 4, 128, 768), BF16),
        pltpu.SemaphoreType.DMA((2,)),
        pltpu.VMEM((2, 2, 4, 256, 128), BF16),
        pltpu.SemaphoreType.DMA((2,)),
        pltpu.VMEM((1, 4, 1024, 128), BF16),
        pltpu.SemaphoreType.DMA((1,)),
    ]

    def __init__(self, p, reduces, swaps_of, total, hbm, vectors, sums, refs):
        for a, b in zip(self.NAMES, refs):
            setattr(self, a, b)
        self.p, self.reduces, self.total, self.vectors, self.sums = p, reduces, total, vectors, sums
        self.hbm = hbm
        self.out_swap, self.tok_swap = swaps_of(self.image)
        self.ups_mail = Mail(p, self.up_mail, self.up_mail_sem)
        self.mixes_mail = Mail(p, self.mix_mail, self.mix_mail_sem)
        self.downs_mail = Mail(p, self.down_mail, self.down_mail_sem)
        self.outs_mail = Mail(p, self.out_mail, self.out_mail_sem)
        h = hbm
        self.out_buf = self.probs.at[0, 0, :, pl.ds(0, 256)]
        self.loads = {
            a: self.load(i, *b)
            for i, (a, b) in enumerate(
                dict(
                    ct=(h["ct"], self.image),
                    slope=(h["slope"], self.slope),
                    nin0=(h["nin_t"].at[:, p.c], self.split.at[0]),
                    nin1=(h["nin_t"].at[:, 1 - p.c], self.split.at[1]),
                    out=(h["out"].at[p.t], self.out_buf),
                    resid=(h["resid"], self.resid),
                    ctx_t=(h["ctx_t"], self.ctx_t),
                    x=(h["x"], self.image),
                ).items()
            )
        }
        self.nmid = [
            self.load(2, h["nmid_t"].at[:, p.c], self.split.at[0]),
            self.load(3, h["nmid_t"].at[:, 1 - p.c], self.split.at[1]),
        ]
        self.out_done = self.load(4, self.out_buf, h["out_o"].at[p.t])
        self.tok_done = self.load(0, self.image.at[p.t], h["gtok_o"].at[p.t])

        def down_src(i, b):
            return [
                (h["w2"].at[:, :, turn_of(i // 2), pl.ds(i % 2 * 512 + k * 256, 256)], b.at[:, :, k]) for k in range(2)
            ]

        def out_src(i, b):
            return [(h["wout"].at[:, :, i * 2 + k], b.at[:, :, k]) for k in range(2)]

        def head_src(i, b):
            at = cols(turn_of(i // 2) * 2 + i % 2, 128)
            return [(h[a].at[:, at], b.at[k]) for k, a in enumerate(("q", "k", "v", "ctx"))]

        self.downs = Stream(8, down_src, self.col_buf, self.col_sem)
        self.outs = Stream(2, out_src, self.col_buf, self.col_sem)
        self.ups = Stream(
            8, lambda i, b: [(h["w1"].at[i % 4, pl.ds(i // 4 * 2, 2)], b)], self.row_buf, self.row_sem
        )
        self.mixes = Stream(
            8,
            lambda i, b: [(h["wqkv"].at[i % 4, pl.ds(i // 4 * 2, 2)], b.at[:, :, :, pl.ds(0, 768)])],
            self.row_buf,
            self.row_sem,
        )
        self.heads = Stream(8, head_src, self.head_buf, self.head_sem)
        self.heads_p = Stream(
            8, lambda i, b: [(h["probs"].at[turn_of(i // 2) * 2 + i % 2], b)], self.probs, self.probs_sem
        )

    def load(self, i, src, dst):
        return pltpu.make_async_copy(src, dst, self.load_sem.at[i])

    def act_load(self, i):
        return self.load(8 + i, self.hbm["act"].at[:, cols(turn_of(i), 1024)], self.gmix.at[:, cols(i % 3, 1024)])

    def begin(self):
        self.loads["ct"].start()
        for i in range(3):
            self.act_load(i).start()
        self.loads["slope"].start()
        self.downs.start()
        self.ups.start()
        for a in ("out", "resid", "ctx_t", "nin0", "nin1"):
            self.loads[a].start()
        self.heads.start()
        self.part_sums[...] = jnp.zeros_like(self.part_sums)
        self.sums[...] = jnp.zeros_like(self.sums)

    def mask_cotangent(self):
        self.loads["ct"].wait()
        mask = self.hbm["mask"]

        @over_rows
        def _(rows):
            g = wide(self.image, rows) * jnp.concatenate([mask[...]] * 4, axis=1)
            self.gmlp[rows, :] = g.astype(BF16)
            self.part_sums[0] += fold(g)

        self.loads["out"].wait()
        self.out_done.start()

    def four_columns(self, c):
        return jnp.concatenate([self.gmlp[:, cols(yx * 2 + c, 128)] for yx in range(4)], axis=1)

    def down_share(self, i):
        r, t = self.reduces["w2"], turn_of(i)
        self.act_load(i).wait()
        g = t_mm(self.gmix[:, cols(i % 3, 1024)], self.four_columns(1 - self.p.c)).astype(BF16)
        self.downs_mail.post(
            i, [g[:, k * 128 : k * 128 + 128] for k in range(4)], r.own.at[:, t], r.c_recv.at[t]
        )

    def down_own(self, i):
        r, t = self.reduces["w2"], turn_of(i)
        r.other_core(t)
        g = t_mm(self.gmix[:, cols(i % 3, 1024)], self.four_columns(self.p.c))
        for k in range(4):
            r.own[k, t] = (g[:, k * 128 : k * 128 + 128] + r.own[k, t].astype(F32)).astype(BF16)
        r.begin(t)

        @pl.when(i == 0)
        def _():
            self.act_load(3).start()

    def share(self):
        self.out_swap.start()

    def whole_rows(self, tile):
        return jnp.concatenate([tile[d // 2, d % 2].reshape(512, 128) for d in range(8)], axis=1)

    def post_rows(self, mail, n, g, r, t, here):
        g = g.astype(BF16).reshape(4, 128, -1)
        mail.post(n, [g[k] for k in range(4)], r.own.at[t, :, :, here], r.c_recv.at[t])

    def hidden(self, i):
        t = turn_of(i)

        @pl.when(i == 0)
        def _():
            self.loads["slope"].wait()

        @pl.loop(0, 2)
        def _(j):
            w = self.whole_rows(self.downs.next(2 * i + j))
            here = cols(t * 2 + j, 512)
            gpre = mm_t(self.gmlp[...], w) * self.slope[:, here].astype(F32)
            self.slope[:, here] = gpre.astype(BF16)
            self.b1[t, :, cols(j, 512)] = jnp.sum(gpre, axis=0, keepdims=True)

    def hidden_share(self, i):
        r, t = self.reduces["w1"], turn_of(i)

        @pl.loop(0, 2)
        def _(j):
            g = mm(self.split[1].reshape(512, ROWS), self.slope[:, cols(t * 2 + j, 512)])
            self.post_rows(self.ups_mail, 2 * i + j, g, r, t, cols(j, 512))

    def add_own(self, r, t, here, value):
        width = value.shape[1]
        had = r.own[t, :, :, here].astype(F32)
        r.own[t, :, :, here] = (value.reshape(4, 128, width) + had).astype(BF16)

    def hidden_own(self, i):
        r, t = self.reduces["w1"], turn_of(i)
        r.other_core(t)

        @pl.loop(0, 2)
        def _(j):
            g = mm(self.split[0].reshape(512, ROWS), self.slope[:, cols(t * 2 + j, 512)])
            self.add_own(r, t, cols(j, 512), g)

        r.begin(t)

    def through_up(self):
        self.outs.start()

        @pl.loop(0, 8)
        def _(i):
            w = self.ups.next(i)
            g = mm_t(self.slope[:, cols(i % 4, 1024)], w[...].reshape(512, D))
            accumulate(self.gn, cols(i // 4, 512), g, i % 4)

        self.mixes.start()

    def norm_mid(self):
        self.loads["resid"].wait()
        gain = vec(self.vectors, 5)

        @over_rows
        def _(rows):
            normed = self.gn[rows, :]
            g, scaled = grad_norm_rows(self.resid[rows, :], gain, normed)
            g = g + self.gmlp[rows, :].astype(F32)
            self.part_sums[1] += fold(normed)
            self.part_sums[2] += fold(scaled)
            self.part_sums[3] += fold(g)
            self.gn[rows, :] = g
            self.gmlp[rows, :] = g.astype(BF16)

    def attn_out(self):
        r, p = self.reduces["wout"], self.p
        self.loads["ctx_t"].wait()
        self.out_done.wait()
        self.heads_p.start()

        @pl.loop(0, 2)
        def _(q):
            g = mm(self.ctx_t[...].reshape(D, ROWS), column_pair(self.gmlp, q, 1 - p.c)).astype(BF16)
            self.outs_mail.post(
                q,
                [g[:, k * 128 : k * 128 + 128].reshape(4, 256, 128) for k in range(2)],
                r.own.at[pl.ds(q * 2, 2)],
                r.c_recv.at[0],
            )

        @pl.loop(0, 2)
        def _(i):
            g = mm_t(self.gmlp[...], self.whole_rows(self.outs.next(i))).astype(BF16)
            for k in range(2):
                self.image[i * 2 + k] = g[:, k * 256 : k * 256 + 256]

    def attn_out_own(self):
        r, p = self.reduces["wout"], self.p
        r.other_core()

        @pl.loop(0, 2)
        def _(q):
            g = mm(self.ctx_t[...].reshape(D, ROWS), column_pair(self.gmlp, q, p.c))
            for k in range(2):
                had = r.own[q * 2 + k].astype(F32)
                r.own[q * 2 + k] = (g[:, k * 128 : k * 128 + 128].reshape(4, 256, 128) + had).astype(BF16)

        for i in range(4):
            r.begin(turn_of(i))
        for a in ("nin0", "nin1"):
            self.loads[a].wait()

    def attend(self, i):
        r, t = self.reduces["wqkv"], turn_of(i)

        @pl.loop(0, 2)
        def _(h):
            ins = self.heads.next(2 * i + h)
            probs = self.heads_p.next(2 * i + h)
            got = attend_back_pair(*(ins[k] for k in range(4)), self.image[t, :, cols(h, 128)], probs)
            for c in range(3):
                self.gmix[:, pl.ds(pl.multiple_of(t * 768 + c * 256 + h * 128, 128), 128)] = got[c].astype(BF16)
            here = cols(t * 2 + h, 128)
            self.sums[2:3, here] = jnp.sum(got[0], axis=0, keepdims=True)
            self.sums[3:4, here] = jnp.sum(got[2], axis=0, keepdims=True)

        g = mm(self.split[1].reshape(512, ROWS), self.gmix[:, cols(t, 768)])
        self.post_rows(self.mixes_mail, i, g, r, t, pl.ds(0, 768))

    def attend_own(self, i):
        r, t = self.reduces["wqkv"], turn_of(i)
        r.other_core(t)
        self.add_own(r, t, slice(None), mm(self.split[0].reshape(512, ROWS), self.gmix[:, cols(t, 768)]))
        r.begin(t)

    def through_mix(self):
        self.loads["x"].start()
        for c in self.nmid:
            c.start()

        @pl.loop(0, 8)
        def _(i):
            w = self.mixes.next(i)
            g = mm_t(self.gmix[:, cols(i % 4, 768)], w[:, :, :, 0:768].reshape(512, 768))
            accumulate(self.resid, cols(i // 4, 512), g, i % 4)

    def norm_in(self):
        self.loads["x"].wait()
        gain = vec(self.vectors, 0)

        @over_rows
        def _(rows):
            normed = self.resid[rows, :]
            g, scaled = grad_norm_rows(wide(self.image, rows), gain, normed)
            g = g + self.gn[rows, :]
            self.part_sums[4] += fold(normed)
            self.part_sums[5] += fold(scaled)
            for t in range(4):
                self.image[t, rows, :] = g[:, t * 256 : t * 256 + 256].astype(BF16)

        self.tok_swap.start()
        self.tok_done.start()
        sums = self.sums
        for row, i in ((7, 0), (6, 1), (5, 2), (4, 3), (1, 4), (0, 5)):
            sums[row : row + 1, :] = jnp.sum(self.part_sums[i], axis=0, keepdims=True)
        for t in range(4):
            sums[8 + t : 9 + t, :] = self.b1[t]
        self.total.start(0)
        for c in self.nmid:
            c.wait()

    def finish(self):
        self.tok_done.wait()
        for m in (self.ups_mail, self.mixes_mail, self.outs_mail, self.downs_mail):
            m.finish()
        for s in (self.out_swap, self.tok_swap):
            s.done()
            s.finish()
        for r in self.reduces.values():
            r.finish()


HBM = ("x", "out", "ct", "probs") + WEIGHTS


def collect_kernel(vectors, mask, *rest):
    names = HBM + tuple(SAVED)
    n = len(names)
    hbm = dict(zip(names, rest[:n]), mask=mask)
    out_o, gtok_o, sums = rest[n : n + 3]
    hbm |= dict(out_o=out_o, gtok_o=gtok_o)
    results = dict(zip(REDUCED, rest[n + 3 : n + 7]))
    rest = rest[n + 7 :]
    m = len(Backward.SCRATCH)
    refs, rest = rest[:m], rest[m:]
    out_sems, tok_sems, total_refs, rest = rest[0:2], rest[2:4], rest[4:8], rest[8:]
    p = Place()
    reduces = {a: Reduce(p, a, rest[9 * i : 9 * i + 9]) for i, a in enumerate(REDUCED)}
    total = Total(p, sums, total_refs)

    def swaps_of(image):
        return Swap(p, hbm["out"], out_o, out_sems), Swap(p, image, gtok_o, tok_sems)

    b = Backward(p, reduces, swaps_of, total, hbm, vectors, sums, refs)
    acts = dict(
        G0=b.mask_cotangent, GS=b.down_share, GM=b.down_own, SHARE=b.share, HG=b.hidden, HS=b.hidden_share, HM=b.hidden_own, GN=b.through_up, GR=b.norm_mid, OA=b.attn_out,
        OM=b.attn_out_own, AT=b.attend, AM=b.attend_own, GI=b.through_mix, GT=b.norm_in,
    )
    counted = ("GS", "GM", "HG", "HS", "HM", "AT", "AM")

    def act(code, i):
        name, kind = BACK[code // 100], STEPS[code // 10 % 10]
        if name in reduces:
            r = reduces[name]
            if kind == "E":
                r.end(results[name])
            elif kind in ("Y", "W"):
                r.pass_on(i, 1 if kind == "Y" else 2)
            else:
                (r.cross if kind == "X" else r.along)(i)
        elif name == "T":
            total.end(i)
            if i < 3:
                total.start(i + 1)
        elif name in counted:
            acts[name](i)
        else:
            acts[name]()

    b.begin()
    p.greet()
    for step in COLLECT:
        if isinstance(step, int):
            act(step, step % 10)
            continue

        @pl.loop(0, 4 + max(code % 10 for code in step))
        def _(m, step=step):
            for code in step:
                lag = code % 10

                @pl.when((m >= lag) & (m < lag + 4))
                def _():
                    act(code, m - lag)

    b.finish()


def collect(vectors, mask, hbm):
    names = HBM + tuple(SAVED)
    outs = pl.pallas_call(
        collect_kernel,
        out_shape=[IMAGE, IMAGE, jax.ShapeDtypeStruct((16, D), F32)]
        + [jax.ShapeDtypeStruct(PARTS[a][0][3:], F32) for a in REDUCED],
        in_specs=[VM, VM] + [ANY] * len(names),
        out_specs=[ANY, ANY, VM] + [VM] * 4,
        scratch_shapes=Backward.SCRATCH
        + Swap.SEMS * 2
        + Total.SCRATCH
        + sum((Reduce.scratch(a) for a in REDUCED), []),
        compiler_params=pltpu.CompilerParams(
            collective_id=1, has_side_effects=True, vmem_limit_bytes=VMEM_BYTES
        ),
        name="collect",
    )(vectors, mask, *[hbm[a] for a in names])
    return outs[0], outs[1], outs[2], dict(zip(REDUCED, outs[3:]))


def gather_plain(w_qkv, w_out, w_fc1, w_fc2):
    def all_of(shard, axis):
        return lax.all_gather(
            lax.all_gather(shard.astype(BF16), "dp", axis=axis, tiled=True), "tensor", axis=0
        )

    wqkv = all_of(w_qkv.reshape(-1, 768), 0)
    wout = all_of(w_out, 1).reshape(D, 8, 128).transpose(1, 0, 2)
    w1 = all_of(w_fc1, 0)
    w2 = all_of(w_fc2, 1).reshape(4 * D, 8, 128).transpose(1, 0, 2)
    return wqkv, wout, w1, w2


def scatter_plain(grads):
    def mine(grad, axis):
        part = lax.psum_scatter(grad, "tensor", scatter_dimension=0, tiled=True)
        return lax.psum_scatter(part, "dp", scatter_dimension=axis, tiled=True).astype(F32)

    g_qkv = mine(grads["wqkv"], 1)[0]
    g_out = mine(grads["wout"].transpose(1, 0, 2).reshape(D, D), 1)
    g_fc1 = mine(grads["w1"], 1)[0]
    g_fc2 = mine(grads["w2"].transpose(1, 0, 2).reshape(4 * D, D), 1)
    return g_qkv, g_out, g_fc1, g_fc2


def on_device(
    dp,
    tokens_in,
    cotangent,
    slot_mask,
    norm1_gain,
    norm1_bias,
    w_qkv,
    b_qkv,
    w_out,
    b_out,
    norm2_gain,
    norm2_bias,
    w_fc1,
    b_fc1,
    w_fc2,
    b_fc2,
):
    def images(rows):
        return jnp.pad(rows.reshape(4, SEQ, 256), ((0, 0), (0, ROWS - SEQ), (0, 0)))

    def exchange(pieces):
        return lax.all_to_all(pieces, "tensor", split_axis=0, concat_axis=0, tiled=True)

    mask = jnp.broadcast_to(
        lax.dynamic_index_in_dim(slot_mask, lax.axis_index("tensor"), 0).astype(F32), (1, 256)
    )
    small = jnp.concatenate(
        (norm1_gain, norm1_bias, b_qkv[0], b_qkv[1], b_out, norm2_gain, norm2_bias, b_fc2)
    ).astype(BF16)
    d, t = lax.axis_index("dp"), lax.axis_index("tensor")
    if dp == 8:
        sv = lax.dynamic_update_slice(jnp.zeros((16, 256), F32), small.astype(F32), (0, d * 32))
        sv = sv.at[8, 0:128].set(b_fc1[0].astype(BF16).astype(F32))
        own = dict(
            sv=sv,
            wqkv=w_qkv.reshape(128, 768).astype(BF16),
            wout=w_out.astype(BF16),
            w1=w_fc1.astype(BF16),
            w2=w_fc2.astype(BF16),
        )
        first, weights, saved = spread(images(tokens_in), images(cotangent), mask, own)
        x, ct, out, probs, vectors = first
        hbm = dict(x=x, out=out, ct=ct, probs=probs, **weights, **saved)
        out, gtok, sums, got = collect(vectors, mask, hbm)
    else:
        vectors = lax.all_gather(
            lax.all_gather(small, "dp", axis=1, tiled=True), "tensor", axis=0
        ).astype(F32)
        hidden_bias = lax.all_gather(
            lax.all_gather(b_fc1.astype(BF16), "dp", axis=1, tiled=True), "tensor", axis=0
        ).astype(F32)
        x = exchange(images(tokens_in))
        ct = exchange(images(cotangent))
        plain = gather_plain(w_qkv, w_out, w_fc1, w_fc2)
        weights = {a: b.reshape(PARTS[a][0]) for a, b in zip(WEIGHTS, plain)}
        out, probs, saved = forward(x, weights, vectors, hidden_bias, mask)
    if dp == 8:
        g_qkv, g_out, g_fc1, g_fc2 = (got[a] for a in GRADS)
        g_small = lax.dynamic_slice(sums, (0, t * 256 + d * 32), (8, 32))
        g_hidden = lax.dynamic_slice(sums, (8 + t, d * 128), (1, 128))
    else:
        flat = [weights[a].reshape(GRADS[a].shape) for a in GRADS]
        gtok, sums, grads = backward(x, ct, *flat, vectors, mask, probs, saved)
        g_qkv, g_out, g_fc1, g_fc2 = scatter_plain(grads)
        out, gtok = exchange(out), exchange(gtok)

        def total(part, axis):
            part = lax.psum_scatter(part, "tensor", scatter_dimension=0, tiled=True)
            return lax.psum_scatter(part, "dp", scatter_dimension=axis, tiled=True)

        g_small = total(sums[0:8].reshape(8, 4, 256).transpose(1, 0, 2), 2)[0]
        g_hidden = total(sums[8:12], 1)

    def rows(pieces):
        return pieces[:, :SEQ].reshape(4 * SEQ, 256)

    return (
        rows(out),
        rows(gtok),
        g_small[0:1],
        g_small[1:2],
        g_qkv.reshape(w_qkv.shape),
        g_small[2:4][:, None],
        g_out,
        g_small[4:5],
        g_small[5:6],
        g_small[6:7],
        g_fc1,
        g_hidden,
        g_fc2,
        g_small[7:8],
    )


def solution(mesh):
    both, turned = P("dp", "tensor"), P("tensor", "dp")
    mixed, pair = P("dp", None, "tensor"), P(None, "tensor", "dp")
    params = (turned, turned, mixed, pair, turned, turned, turned, turned, both, turned, turned, turned)
    return jax.shard_map(
        functools.partial(on_device, mesh.shape["dp"]),
        mesh=mesh,
        in_specs=(both, both, P("dp"), *params),
        out_specs=(both, both, *params),
        check_vma=False,
    )
```

```python
import functools
import jax
import jax.numpy as jnp
from jax import lax
from jax.experimental import pallas as pl
from jax.experimental.pallas import tpu as pltpu
from jax.sharding import PartitionSpec as P

D = 1024
HD = 64
SEQ = 577
ROWS = 592
CHUNK = 96
F32 = jnp.float32
BF16 = jnp.bfloat16
LAST = (((1,), (1,)), ((), ()))
VMEM_BYTES = 67_043_328


def mm(a, b):
    return jnp.dot(a, b, preferred_element_type=F32)


def t_mm(a, b):
    return lax.dot_general(a, b, (((0,), (0,)), ((), ())), preferred_element_type=F32)


def mm_t(a, b):
    return lax.dot_general(a, b, LAST, preferred_element_type=F32)


def cols(i, n):
    return pl.ds(pl.multiple_of(i * n, n), n)


def row_stats(values):
    mean = jnp.sum(values, axis=1, keepdims=True) * (1.0 / D)
    centered = values - mean
    var = jnp.sum(centered * centered, axis=1, keepdims=True) * (1.0 / D)
    inv = lax.rsqrt(var + 1e-05)
    return centered * inv, inv


def wide(ref, rows):
    return jnp.concatenate([ref[t, rows, :].astype(F32) for t in range(4)], axis=1)


def over_rows(do):
    @pl.loop(0, 576 // CHUNK)
    def _(i):
        do(pl.ds(pl.multiple_of(i * CHUNK, CHUNK), CHUNK))

    do(pl.ds(576, ROWS - 576))


def vec(vectors, row):
    return jnp.concatenate([vectors[t, row : row + 1, :] for t in range(4)], axis=1)


def norm_in(x, vectors, nin):
    gain, shift = vec(vectors, 0), vec(vectors, 1)

    @over_rows
    def _(rows):
        xhat, _ = row_stats(wide(x, rows))
        nin[rows, :] = (xhat * gain + shift).astype(BF16)


def flip(src, dst, n):
    @pl.loop(0, n // 256)
    def _(i):
        dst[i] = src[:, cols(i, 256)].T.reshape(2, 128, ROWS)


def project(nin, wqkv, vectors, t, q, k, v):
    here = cols(t, 256)

    g = mm(nin[...], wqkv[t].reshape(D, 768))
    q[:, here] = (g[:, 0:256] + vectors[t, 2:3, :]).astype(BF16)
    k[:, here] = g[:, 256:512].astype(BF16)
    v[:, here] = (g[:, 512:768] + vectors[t, 3:4, :]).astype(BF16)


def head_lanes(h):
    lane = lax.broadcasted_iota(jnp.int32, (ROWS, 128), 1)
    own = (lane >= h * 64) & (lane < h * 64 + 64)
    return lane, own, 64 - h * 64


def attend_pair(pair, q, k, v, ctx, probs, slot):
    here = cols(pair, 128)
    lane = lax.broadcasted_iota(jnp.int32, (ROWS, 128), 1)
    row = lax.broadcasted_iota(jnp.int32, (ROWS, 128), 0)
    queries = q[:, here].astype(F32) * (HD**-0.5)
    keys = k[:, here].astype(F32)
    values = v[:, here]
    blocked = jnp.where(row >= SEQ, -1e30, 0.0)
    parts = []
    for h in range(2):
        own = (lane < 64) if h == 0 else (lane >= 64)
        spare = 64 if h == 0 else 0
        qa = jnp.where(own, queries, jnp.where(lane == spare, 1.0, 0.0)).astype(BF16)
        ka = jnp.where(lane == spare, blocked, keys).astype(BF16)
        scores = mm_t(ka, qa)
        top = jnp.max(scores, axis=0, keepdims=True)
        e = jnp.exp(scores - top)
        total = jnp.sum(e, axis=0, keepdims=True)
        p = (e * (1.0 / total)).astype(BF16)
        probs[slot, h] = p
        parts.append(
            lax.dot_general(p, values, (((0,), (0,)), ((), ())), preferred_element_type=F32)
        )
    ctx[:, here] = jnp.where(lane < 64, parts[0], parts[1]).astype(BF16)


def out_block(i, ctx, wout, x, vectors, resid):
    w = jnp.concatenate([wout[i, c].reshape(D, 128) for c in range(2)], axis=1)
    resid[:, cols(i, 256)] = x[i].astype(F32) + mm(ctx[...], w) + vectors[i, 4:5, :]


def norm_mid(resid, vectors, nmid):
    gain, shift = vec(vectors, 5), vec(vectors, 6)

    @over_rows
    def _(rows):
        xhat, _ = row_stats(resid[rows, :])
        nmid[rows, :] = (xhat * gain + shift).astype(BF16)


def hidden_tile(t, j, nmid, w1, b1, act, slope):
    here = pl.ds(pl.multiple_of(t * 1024 + j * 256, 256), 256)
    bias = b1[t, :, cols(j, 256)]
    pre = mm(nmid[...], w1[t, :, :, :, cols(j, 256)].reshape(D, 256)) + bias
    sig = 1.0 / (1.0 + jnp.exp(-1.702 * pre))
    a = pre * sig
    slope[:, here] = (sig + 1.702 * a * (1.0 - sig)).astype(BF16)
    act[:, here] = a.astype(BF16)


def down_block(i, t, act, w2, total):
    w = jnp.concatenate([w2[i, c, t] for c in range(2)], axis=1)
    total[:, cols(i, 256)] += mm(act[:, cols(t, 1024)], w)


def finish_block(i, total, vectors, mask, out):
    out[i] = ((total[:, cols(i, 256)] + vectors[i, 7:8, :]) * mask[...]).astype(BF16)


def grad_norm_rows(values, gain, n):
    xhat, inv = row_stats(values)
    e = n * gain
    first = jnp.sum(e, axis=1, keepdims=True) * (1.0 / D)
    second = jnp.sum(e * xhat, axis=1, keepdims=True) * (1.0 / D)
    return inv * (e - first - xhat * second), n * xhat


def fold(a):
    return jnp.sum(a.reshape(-1, 8, D), axis=0)


def attend_back_pair(queries, keys, values, out, go, probs):
    values_f, go_f = values.astype(F32), go.astype(F32)
    dots = go_f * out.astype(F32)
    dq, dk, dv = [], [], []
    for h in range(2):
        lane, own, spare = head_lanes(h)
        delta = -jnp.sum(jnp.where(own, dots, 0.0), axis=1, keepdims=True)
        high = delta.astype(BF16).astype(F32)
        ga = jnp.where(
            own, go_f, jnp.where(lane == spare, high, jnp.where(lane == spare + 1, delta - high, 0.0))
        ).astype(BF16)
        marks = jnp.where((lane == spare) | (lane == spare + 1), 1.0, 0.0)
        va = jnp.where(own, values_f, marks).astype(BF16)
        p = probs[h]
        gs = (p.astype(F32) * mm_t(va, ga)).astype(BF16)
        dv.append(mm(p, go))
        dk.append(mm(gs, queries))
        dq.append(
            lax.dot_general(gs, keys, (((0,), (0,)), ((), ())), preferred_element_type=F32)
        )
    low = head_lanes(0)[1]
    scale = HD**-0.5
    return (
        jnp.where(low, dq[0], dq[1]) * scale,
        jnp.where(low, dk[0], dk[1]) * scale,
        jnp.where(low, dv[0], dv[1]),
    )


ACT = jax.ShapeDtypeStruct((ROWS, D), BF16)
TURNED = jax.ShapeDtypeStruct((4, 2, 128, ROWS), BF16)
SAVED = dict(
    nin_t=TURNED,
    q=ACT,
    k=ACT,
    v=ACT,
    ctx=ACT,
    ctx_t=TURNED,
    nmid_t=TURNED,
    resid=jax.ShapeDtypeStruct((ROWS, D), F32),
    act=jax.ShapeDtypeStruct((ROWS, 4 * D), BF16),
    slope=jax.ShapeDtypeStruct((ROWS, 4 * D), BF16),
)
PROBS = jax.ShapeDtypeStruct((8, 2, ROWS, ROWS), BF16)
IMAGE = jax.ShapeDtypeStruct((4, ROWS, 256), BF16)
ANY = pl.BlockSpec(memory_space=pl.ANY)
VM = pl.BlockSpec(memory_space=pltpu.VMEM)


def scratch(like):
    return pltpu.VMEM(like.shape, like.dtype)


PARTS = dict(
    sv=((4, 4, 2, 16, 256), F32),
    wqkv=((4, 4, 2, 128, 768), BF16),
    wout=((4, 2, 4, 256, 128), BF16),
    w1=((4, 4, 2, 128, 1024), BF16),
    w2=((4, 2, 4, 1024, 128), BF16),
)
WEIGHTS = ("wqkv", "wout", "w1", "w2")


def part(name):
    return jax.ShapeDtypeStruct(*PARTS[name])


class Forward:
    SCRATCH = [scratch(a) for a in SAVED.values()] + [
        scratch(ACT),
        pltpu.VMEM((2, 2, ROWS, ROWS), BF16),
        pltpu.SemaphoreType.DMA((2,)),
        pltpu.SemaphoreType.DMA((len(SAVED) + 1,)),
    ]

    def __init__(self, x, weights, vectors, b1, mask, out, out_h, probs_h, saved_h, refs):
        n = len(SAVED)
        self.x, self.w, self.vectors, self.b1, self.mask = x, weights, vectors, b1, mask
        self.out, self.out_h, self.probs_h, self.saved_h = out, out_h, probs_h, saved_h
        self.saved = dict(zip(SAVED, refs[:n]))
        self.total = self.saved["resid"]
        self.normed, self.probs, self.probs_sem, self.out_sem = refs[n:]
        self.act = self.saved["act"]

    def start_norm(self):
        norm_in(self.x, self.vectors, self.normed)
        flip(self.normed, self.saved["nin_t"], D)

    def put(self, pair, slot):
        return pltpu.make_async_copy(self.probs.at[slot], self.probs_h.at[pair], self.probs_sem.at[slot])

    def heads(self, s, i):
        a = self.saved
        project(self.normed, self.w["wqkv"], self.vectors, s, a["q"], a["k"], a["v"])

        @pl.loop(0, 2)
        def _(slot):
            pair = s * 2 + slot
            if i:
                self.put(pair, slot).wait()
            attend_pair(pair, a["q"], a["k"], a["v"], a["ctx"], self.probs, slot)
            self.put(pair, slot).start()

    def middle(self):
        a = self.saved

        @pl.loop(0, 4)
        def _(i):
            out_block(i, a["ctx"], self.w["wout"], self.x, self.vectors, a["resid"])

        norm_mid(a["resid"], self.vectors, self.normed)

    def hidden(self, s):
        @pl.loop(0, 4)
        def _(j):
            hidden_tile(s, j, self.normed, self.w["w1"], self.b1, self.act, self.saved["slope"])

    def down(self, s):
        @pl.loop(0, 4)
        def _(i):
            down_block(i, s, self.act, self.w["w2"], self.total)

    def turn(self):
        flip(self.saved["ctx"], self.saved["ctx_t"], D)
        flip(self.normed, self.saved["nmid_t"], D)

    def finish(self):
        @pl.loop(0, 4)
        def _(i):
            finish_block(i, self.total, self.vectors, self.mask, self.out)

    def stores(self, names):
        at = list(SAVED)
        return [
            pltpu.make_async_copy(self.saved[a], self.saved_h[a], self.out_sem.at[at.index(a)]) for a in names
        ]

    def store_out(self):
        return pltpu.make_async_copy(self.out, self.out_h, self.out_sem.at[len(SAVED)])

    def drain_last(self, s):
        for slot in range(2):
            self.put(s * 2 + slot, slot).wait()

    def drain(self):
        for slot in range(2):
            self.put(6 + slot, slot).wait()


def forward_kernel(x_h, wqkv_h, wout_h, w1_h, w2_h, vectors, b1, mask, *rest):
    n = len(SAVED)
    saved_h = dict(zip(SAVED, rest[2 : 2 + n]))
    x, out, *weights, in_sem = rest[2 + n : 9 + n]
    loads = [
        pltpu.make_async_copy(a, b, in_sem.at[i])
        for i, (a, b) in enumerate(zip((x_h, wqkv_h, wout_h, w1_h, w2_h), (x, *weights)))
    ]
    for c in loads:
        c.start()
    for c in loads:
        c.wait()
    f = Forward(x, dict(zip(WEIGHTS, weights)), vectors, b1, mask, out, rest[0], rest[1], saved_h, rest[9 + n :])
    f.start_norm()
    for s in range(4):
        f.heads(s, s)
    f.middle()
    for c in f.stores(("resid",)):
        c.start()
        c.wait()
    for s in range(4):
        f.hidden(s)
        f.down(s)
    f.turn()
    f.finish()
    f.drain()
    stores = [*f.stores([a for a in SAVED if a != "resid"]), f.store_out()]
    for c in stores:
        c.start()
    for c in stores:
        c.wait()


def forward(x, weights, vectors, b1, mask):
    n = len(SAVED)
    outs = pl.pallas_call(
        forward_kernel,
        out_shape=[IMAGE, PROBS, *SAVED.values()],
        in_specs=[ANY] * 5 + [VM, VM, VM],
        out_specs=[ANY] * (2 + n),
        scratch_shapes=[scratch(IMAGE), scratch(IMAGE)]
        + [scratch(part(a)) for a in WEIGHTS]
        + [pltpu.SemaphoreType.DMA((5,))]
        + Forward.SCRATCH,
        compiler_params=pltpu.CompilerParams(vmem_limit_bytes=VMEM_BYTES),
        name="forward",
    )(x, *[weights[a] for a in WEIGHTS], vectors, b1, mask)
    return outs[0], outs[1], dict(zip(SAVED, outs[2:]))


GRADS = dict(
    wqkv=jax.ShapeDtypeStruct((4, 1024, 768), BF16),
    wout=jax.ShapeDtypeStruct((8, 1024, 128), BF16),
    w1=jax.ShapeDtypeStruct((4, 1024, 1024), BF16),
    w2=jax.ShapeDtypeStruct((8, 4096, 128), BF16),
)


def send_tile(stage, sem, i, value, targets):
    slot = lax.rem(i, 2)

    def copies(s):
        return [
            pltpu.make_async_copy(
                stage.at[s] if w == 256 else stage.at[s, :, pl.ds(c, w)], ref, sem.at[s]
            )
            for ref, c, w in targets
        ]

    @pl.when(i >= 2)
    def _():
        pltpu.make_async_copy(stage.at[slot], stage.at[slot], sem.at[slot]).wait()

    stage[slot] = value
    for c in copies(slot):
        c.start()


def drain(stage, sem):
    for slot in range(2):
        pltpu.make_async_copy(stage.at[slot], stage.at[slot], sem.at[slot]).wait()


def backward_kernel(x_h, ct_h, wqkv_h, wout_h, w1_h, w2_h, vectors, mask, probs_h, *rest):
    n = len(SAVED)
    saved_h = dict(zip(SAVED, rest[:n]))
    gtok_h, sums_o = rest[n], rest[n + 1]
    g_h = dict(zip(GRADS, rest[n + 2 : n + 6]))
    rest = rest[n + 6 :]
    saved = dict(zip(SAVED, rest[:n]))
    (x, wqkv, wout, w1, w2, b1, gmlp, gattn, gctx, gn, gmix, probs, sums, part, stage,
     in_sem, probs_sem, tile_sem, saved_sem) = rest[n:]
    gtok = x
    names = dict(ct=(ct_h, gtok), x=(x_h, x), w2=(w2_h, w2), w1=(w1_h, w1), wout=(wout_h, wout), wqkv=(wqkv_h, wqkv))
    load = {a: pltpu.make_async_copy(*names[a], in_sem.at[i]) for i, a in enumerate(names)}
    load_saved = {a: pltpu.make_async_copy(saved_h[a], saved[a], saved_sem.at[i]) for i, a in enumerate(SAVED)}
    load["ct"].start()
    load_saved["act"].start()
    load_saved["slope"].start()
    for a in ("w2", "w1", "wout", "wqkv"):
        load[a].start()
    for a in SAVED:
        if a not in ("act", "slope"):
            load_saved[a].start()
    part[...] = jnp.zeros_like(part)
    sums[...] = jnp.zeros_like(sums)
    load["ct"].wait()

    @over_rows
    def _(rows):
        g = jnp.concatenate([x[t, rows, :].astype(F32) * mask[...] for t in range(4)], axis=1)
        gmlp[rows, :] = g.astype(BF16)
        part[0] += fold(g)

    load["x"].start()
    load_saved["act"].wait()

    @pl.loop(0, 16)
    def _(i):
        t, c = i // 4, i % 4
        r = t_mm(saved["act"][:, cols(t, 1024)], gmlp[:, cols(c, 256)]).astype(BF16)
        send_tile(stage, tile_sem, i, r, [
            (g_h["w2"].at[2 * c + e, cols(t, 1024), :], e * 128, 128) for e in range(2)])

    load_saved["slope"].wait()
    load["w2"].wait()
    slope = saved["slope"]

    @pl.loop(0, 16)
    def _(i):
        w = jnp.concatenate([w2[d, cols(i, 256), :] for d in range(8)], axis=1)
        gpre = mm_t(gmlp[...], w) * slope[:, cols(i, 256)].astype(F32)
        slope[:, cols(i, 256)] = gpre.astype(BF16)
        b1[i // 4, :, cols(i % 4, 256)] = jnp.sum(gpre, axis=0, keepdims=True)

    load_saved["nmid_t"].wait()

    @pl.loop(0, 16)
    def _(i):
        r = mm(saved["nmid_t"][...].reshape(D, ROWS), slope[:, cols(i, 256)]).astype(BF16)
        send_tile(stage, tile_sem, i + 16, r, [(g_h["w1"].at[i // 4, :, cols(i % 4, 256)], 0, 256)])

    load["w1"].wait()

    @pl.loop(0, 4)
    def _(i):
        total = mm_t(slope[:, 0:1024], w1[0, cols(i, 256), :])
        for t in range(1, 4):
            total += mm_t(slope[:, t * 1024 : t * 1024 + 1024], w1[t, cols(i, 256), :])
        gn[:, cols(i, 256)] = total

    load_saved["resid"].wait()
    gain2 = vec(vectors, 5)

    @over_rows
    def _(rows):
        normed = gn[rows, :]
        g, scaled = grad_norm_rows(saved["resid"][rows, :], gain2, normed)
        g = g + gmlp[rows, :].astype(F32)
        part[1] += fold(normed)
        part[2] += fold(scaled)
        part[3] += fold(g)
        gn[rows, :] = g
        gattn[rows, :] = g.astype(BF16)

    load["wout"].wait()
    load_saved["ctx_t"].wait()

    @pl.loop(0, 4)
    def _(i):
        w = jnp.concatenate([wout[d, cols(i, 256), :] for d in range(8)], axis=1)
        gctx[:, cols(i, 256)] = mm_t(gattn[...], w).astype(BF16)
        r = mm(saved["ctx_t"][...].reshape(D, ROWS), gattn[:, cols(i, 256)]).astype(BF16)
        send_tile(stage, tile_sem, i + 32, r, [(g_h["wout"].at[2 * i + e], e * 128, 128) for e in range(2)])

    for a in ("q", "k", "v", "ctx"):
        load_saved[a].wait()

    def get(pair, slot):
        return pltpu.make_async_copy(probs_h.at[pair], probs.at[slot], probs_sem.at[slot])

    get(0, 0).start()

    @pl.loop(0, 8)
    def _(pair):
        slot = pair % 2

        @pl.when(pair < 7)
        def _():
            get(pair + 1, 1 - slot).start()

        get(pair, slot).wait()
        here = cols(pair, 128)

        got = attend_back_pair(
            *(saved[a][:, here] for a in ("q", "k", "v", "ctx")), gctx[:, here], probs.at[slot]
        )
        for c in range(3):
            at = pl.ds(pl.multiple_of(c * 256 + (pair % 2) * 128, 128), 128)
            gmix[pair // 2, :, at] = got[c].astype(BF16)
        sums[2:3, here] = jnp.sum(got[0], axis=0, keepdims=True)
        sums[3:4, here] = jnp.sum(got[2], axis=0, keepdims=True)

    load_saved["nin_t"].wait()

    @pl.loop(0, 12)
    def _(i):
        t, c = i // 3, i % 3
        r = mm(saved["nin_t"][...].reshape(D, ROWS), gmix[t, :, cols(c, 256)]).astype(BF16)
        send_tile(stage, tile_sem, i + 36, r, [(g_h["wqkv"].at[t, :, cols(c, 256)], 0, 256)])

    load["wqkv"].wait()
    resid = saved["resid"]

    @pl.loop(0, 4)
    def _(i):
        total = mm_t(gmix[0], wqkv[0, cols(i, 256), :])
        for t in range(1, 4):
            total += mm_t(gmix[t], wqkv[t, cols(i, 256), :])
        resid[:, cols(i, 256)] = total

    load["x"].wait()
    gain1 = vec(vectors, 0)

    @over_rows
    def _(rows):
        normed = resid[rows, :]
        g, scaled = grad_norm_rows(wide(x, rows), gain1, normed)
        g = g + gn[rows, :]
        part[4] += fold(normed)
        part[5] += fold(scaled)
        for t in range(4):
            gtok[t, rows, :] = g[:, t * 256 : t * 256 + 256].astype(BF16)

    for row, i in ((7, 0), (6, 1), (5, 2), (4, 3), (1, 4), (0, 5)):
        sums[row : row + 1, :] = jnp.sum(part[i], axis=0, keepdims=True)
    sums_o[0:8, :] = sums[...]
    for t in range(4):
        sums_o[8 + t : 9 + t, :] = b1[t]
    done = pltpu.make_async_copy(gtok, gtok_h, in_sem.at[0])
    done.start()
    done.wait()
    drain(stage, tile_sem)


def backward(x, ct, wqkv, wout, w1, w2, vectors, mask, probs, saved):
    n = len(SAVED)
    outs = pl.pallas_call(
        backward_kernel,
        out_shape=[IMAGE, jax.ShapeDtypeStruct((12, D), F32), *GRADS.values()],
        in_specs=[ANY] * 6 + [VM, VM, ANY] + [ANY] * n,
        out_specs=[ANY, VM] + [ANY] * 4,
        scratch_shapes=[scratch(a) for a in SAVED.values()]
        + [scratch(a) for a in (x, wqkv, wout, w1, w2)]
        + [
            pltpu.VMEM((4, 1, 1024), F32),
            scratch(ACT),
            scratch(ACT),
            scratch(ACT),
            pltpu.VMEM((ROWS, D), F32),
            pltpu.VMEM((4, ROWS, 768), BF16),
            pltpu.VMEM((2, 2, ROWS, ROWS), BF16),
            pltpu.VMEM((8, D), F32),
            pltpu.VMEM((6, 8, D), F32),
            pltpu.VMEM((2, 1024, 256), BF16),
            pltpu.SemaphoreType.DMA((6,)),
            pltpu.SemaphoreType.DMA((2,)),
            pltpu.SemaphoreType.DMA((2,)),
            pltpu.SemaphoreType.DMA((n,)),
        ],
        compiler_params=pltpu.CompilerParams(vmem_limit_bytes=VMEM_BYTES),
        name="backward",
    )(x, ct, wqkv, wout, w1, w2, vectors, mask, probs, *[saved[a] for a in SAVED])
    return outs[0], outs[1], dict(zip(GRADS, outs[2:]))


MESH = pl.DeviceIdType.MESH
BY_COLUMN = ("wout", "w2")


def block_of(name, ref, t, yx, c):
    return ref.at[yx, c, t] if name in BY_COLUMN else ref.at[t, yx, c]


def half_of(ref, h):
    n = ref.shape[0] // 2
    return ref.at[pl.ds(h * n, n)]


class Place:
    def __init__(self):
        d, self.t = lax.axis_index("dp"), lax.axis_index("tensor")
        self.y, self.x, self.c = d // 4, d // 2 % 2, d % 2
        self.yx = d // 2
        self.x_yx = self.y * 2 + 1 - self.x
        self.y_yx = (1 - self.y) * 2 + self.x
        self.xy_yx = (1 - self.y) * 2 + 1 - self.x
        self.d = d
        self.x_id = (self.x_yx * 2 + self.c, self.t)
        self.y_id = (self.y_yx * 2 + self.c, self.t)
        self.c_id = (self.yx * 2 + 1 - self.c, self.t)

    def z_id(self, t):
        return (self.d, t)

    def order(self, i):
        t = self.t
        near, far = (t, t + 1 - 2 * (t % 2)), (2 - t // 2, 3 - 3 * (t // 2))
        if isinstance(i, int):
            return (near + far)[i]
        half, odd = i // 2, i % 2
        return (1 - half) * (near[0] + odd * (near[1] - near[0])) + half * (far[0] + odd * (far[1] - far[0]))

    def greet(self):
        barrier = pltpu.get_barrier_semaphore()
        others = [self.x_id, self.y_id, self.c_id]
        others += [self.z_id(lax.rem(self.t + k, 4)) for k in (1, 2, 3)]
        for other in others:
            pl.semaphore_signal(barrier, inc=1, device_id=other, device_id_type=MESH)
        pl.semaphore_wait(barrier, 6)


def remote(src, dst, send, recv, where):
    return pltpu.make_async_remote_copy(
        src_ref=src, dst_ref=dst, send_sem=send, recv_sem=recv, device_id=where, device_id_type=MESH
    )


class Gather:
    SEMS = [
        pltpu.SemaphoreType.DMA((2, 4)),
        pltpu.SemaphoreType.DMA((4,)),
        pltpu.SemaphoreType.DMA((4, 6)),
        pltpu.SemaphoreType.DMA((4, 6)),
        pltpu.SemaphoreType.DMA((4,)),
        pltpu.SemaphoreType.DMA((4,)),
    ]

    def __init__(self, place, name, own, whole, sems):
        self.p, self.name, self.own, self.whole = place, name, own, whole
        self.z_send, self.z_recv, self.xy_send, self.xy_recv, self.c_send, self.c_recv = sems

    def at(self, s, yx):
        return block_of(self.name, self.whole, s, yx, self.p.c)

    def z_copies(self, s, act, src=None):
        p = self.p
        dst = self.at(s, p.yx)
        for way, going, to in ((0, (s <= p.t) & (p.t < 3), p.t + 1), (1, (s >= p.t) & (p.t > 0), p.t - 1)):

            @pl.when(going)
            def _():
                c = remote(dst if src is None else src, dst, self.z_send.at[way, s], self.z_recv.at[s], p.z_id(to))
                c.start() if act == "start" else c.wait_send()

    def xy_copy(self, k, s, mine=False):
        p = self.p
        yx = (p.yx, p.yx, p.yx, p.x_yx, p.yx, p.y_yx)[k]
        h = (0, 1, 0, 0, 1, 1)[k]
        to = (p.x_id, p.y_id, p.y_id, p.y_id, p.x_id, p.x_id)[k]
        dst = half_of(self.at(s, yx), h)
        src = half_of(self.own, h) if mine else dst
        return remote(src, dst, self.xy_send.at[s, k], self.xy_recv.at[s, k], to)

    def straight(self, k):
        p = self.p
        return remote(
            self.own, self.at(p.t, p.yx), self.z_send.at[0, k], self.z_recv.at[p.t], p.z_id(lax.rem(p.t + k, 4))
        )

    def open(self):
        s = self.p.t
        if self.name == "sv":
            for k in (1, 2, 3):
                self.straight(k).start()
        else:
            self.z_copies(s, "start", self.own)
        for k in (0, 1):
            self.xy_copy(k, s, True).start()

    def arrive(self, i):
        s = self.p.order(i)
        here = self.at(s, self.p.yx)
        remote(here, here, self.z_send.at[0, s], self.z_recv.at[s], self.p.c_id).wait_recv()
        if self.name != "sv":
            self.z_copies(s, "start")
        for k in (0, 1):
            self.xy_copy(k, s).start()

    def second(self, i):
        s = self.p.order(i)
        for got, own, other in ((0, 2, 3), (1, 4, 5)):
            self.xy_copy(own, s, isinstance(i, int) and i == 0).start()
            self.xy_copy(got, s).wait_recv()
            self.xy_copy(other, s).start()

    def core_copy(self, s):
        c = self.p.c
        ref = self.whole.at[:, c, s] if self.name in BY_COLUMN else self.whole.at[s, :, c]
        return remote(ref, ref, self.c_send.at[s], self.c_recv.at[s], self.p.c_id)

    def last(self, i):
        s = self.p.order(i)
        for k in (2, 3, 4, 5):
            self.xy_copy(k, s).wait_recv()
        self.core_copy(s).start()

    def have(self, i):
        self.core_copy(self.p.order(i)).wait_recv()

    def finish(self):
        for s in range(4):
            if self.name != "sv":
                self.z_copies(s, "wait")
            elif s:
                self.straight(s).wait_send()
            for k in range(6):
                self.xy_copy(k, s).wait_send()
            self.core_copy(s).wait_send()


class Swap:
    SEMS = [pltpu.SemaphoreType.DMA((4,)), pltpu.SemaphoreType.DMA((4,))]

    def __init__(self, place, pieces, whole, sems):
        self.p, self.pieces, self.whole = place, pieces, whole
        self.send, self.recv = sems

    def copy(self, k):
        p = self.p
        to = lax.rem(p.t + k, 4)
        return remote(self.pieces.at[to], self.whole.at[p.t], self.send.at[k], self.recv.at[k], p.z_id(to))

    def start(self):
        for k in (1, 3, 2):
            self.copy(k).start()

    def done(self):
        for k in (1, 2, 3):
            self.copy(k).wait_recv()

    def finish(self):
        for k in (1, 2, 3):
            self.copy(k).wait_send()


class Mail:
    def __init__(self, place, buf, sem):
        self.p, self.buf, self.sem, self.depth = place, buf, sem, buf.shape[0]

    def copy(self, slot, dst, recv):
        return remote(self.buf.at[slot], dst, self.sem.at[slot], recv, self.p.c_id)

    def post(self, i, parts, dst, recv):
        slot = lax.rem(i, self.depth)

        @pl.when(i >= self.depth)
        def _():
            self.copy(slot, dst, recv).wait_send()

        for k, part in enumerate(parts):
            self.buf[slot, k] = part
        self.copy(slot, dst, recv).start()

    def finish(self):
        for slot in range(self.depth):
            self.copy(slot, self.buf.at[slot], self.sem.at[slot]).wait_send()


def column_pair(ref, q, c):
    return jnp.concatenate([ref[:, cols(q * 4 + c, 128)], ref[:, cols(q * 4 + 2 + c, 128)]], axis=1)


ACTS = ("sv", "wqkv", "wout", "w1", "w2", "XS", "CS", "LN1", "Q", "OUT", "F", "D", "END", "K1")
KINDS = ("", "O", "A", "S", "L")
SEQUENCE = (
    210, 110, 130, 10, 221, 410, 121, 310, 430, 222, 230, 21, 223, 30, 131, 330, 122, 22, 23, 231, 123, 500,
    132, 31, 32, 33, 140, 321, 232, 421, 240, 331, 133, 40, 41, 141, 322, 42, 43, 241, 233, 700, 323, 242,
    142, 800, 440, 431, 801, 143, 422, 332, 340, 341, 802, 243, 333, 803, 423, 432, 600, 900, 1000, 342, 433,
    343, 1001, 1002, 441, 442, 1003, 1300, 1100, 443, 1101, 1102, 1103, 1200,
)


def spread_kernel(slot_mask, x_in, ct_in, *rest):
    names, n, m = list(PARTS), len(PARTS), len(SAVED)
    small, (w_qkv, w_out, w_fc1, w_fc2), rest = rest[:8], rest[8:12], rest[12 - n :]
    x_h, ct_h, out_h, probs_h, vectors = rest[n : n + 5]
    rest = rest[n + 5 :]
    whole_h, saved_h = dict(zip(WEIGHTS, rest[:4])), dict(zip(SAVED, rest[4 : 4 + m]))
    rest = rest[4 + m :]
    x, ct, out, b1, mask, stack = rest[:6]
    whole = dict(zip(names, rest[6 : 6 + n]))
    rest = rest[6 + n :]
    local_sem, keep_sem = rest[0], rest[1]
    swap_sems, rest = rest[2:6], rest[6:]
    sems, refs = rest[: 6 * n], rest[6 * n :]
    p = Place()
    own = {a: block_of(a, whole[a], p.t, p.yx, p.c) for a in names}
    f = Forward(x, whole, vectors, b1, mask, out, out_h, probs_h, saved_h, refs)
    gathers = {a: Gather(p, a, own[a], whole[a], sems[6 * i : 6 * i + 6]) for i, a in enumerate(names)}
    swaps = dict(XS=Swap(p, x_in, x, swap_sems[0:2]), CS=Swap(p, ct_in, ct, swap_sems[2:4]))
    local = [
        pltpu.make_async_copy(x_in.at[p.t], x.at[p.t], local_sem.at[0]),
        pltpu.make_async_copy(ct_in.at[p.t], ct.at[p.t], local_sem.at[1]),
    ]
    for c in local:
        c.start()
    mask[...] = jnp.full((1, 256), slot_mask[p.t].astype(F32))
    for i in range(3):
        own["wqkv"][:, i * 256 : i * 256 + 256] = w_qkv[i].astype(BF16)
    own["wout"][...] = w_out[...].astype(BF16)
    own["w1"][...] = w_fc1[...].astype(BF16)
    own["w2"][...] = w_fc2[...].astype(BF16)
    for row, ref in enumerate((small[0], small[1], small[2].at[0], small[2].at[1], *small[3:7])):
        stack[row : row + 1, :] = ref[...]
    lane = lax.broadcasted_iota(jnp.int32, (32, 256), 1)
    row = lax.broadcasted_iota(jnp.int32, (32, 256), 0)
    place = jnp.where(lane == row + p.d * 32, 1.0, 0.0).astype(BF16)
    own["sv"][8:16, :] = jnp.zeros((8, 256), F32)
    own["sv"][0:8, :] = mm(stack[...].astype(BF16), place)
    own["sv"][8:9, 0:128] = small[7][...].astype(BF16).astype(F32)
    p.greet()
    pending = []
    settled = []
    resid_stored = f.stores(("resid",))

    def keep(src, dst):
        c = pltpu.make_async_copy(src, dst, keep_sem.at[len(pending)])
        c.start()
        pending.append(c)

    def do(code, step):
        name, kind = ACTS[code // 100], KINDS[code // 10 % 10]
        if name in gathers:
            g = gathers[name]
            if kind == "O":
                g.open()
            elif kind == "A":
                g.arrive(step)
            elif kind == "S":
                g.second(step)
            else:
                if not settled:
                    for c in local:
                        c.wait()
                    settled.append(True)
                g.last(step)
        elif name in swaps:
            swaps[name].start()
        elif name == "LN1":
            for i in range(4):
                gathers["sv"].have(i)
            sv = whole["sv"]
            for t in range(4):
                vectors[t] = jnp.sum(sv[t, :, :, 0:8].reshape(8, 8, 256), axis=0)
                for d in range(8):
                    b1[t, :, d * 128 : d * 128 + 128] = sv[t, d // 2, d % 2, 8:9, 0:128]
            swaps["XS"].done()
            keep(x, x_h)
            f.start_norm()
        elif name == "Q":
            gathers["wqkv"].have(step)
            f.heads(p.order(step), step)
        elif name == "OUT":
            for i in range(4):
                gathers["wout"].have(i)
            keep(whole["wqkv"], whole_h["wqkv"])
            keep(whole["wout"], whole_h["wout"])
            f.middle()
            f.turn()
            for c in (*f.stores(("q", "k", "v", "ctx", "nin_t", "ctx_t", "nmid_t")), *resid_stored):
                c.start()
        elif name == "F":
            gathers["w1"].have(step)
            f.hidden(p.order(step))
        elif name == "K1":
            keep(whole["w1"], whole_h["w1"])
            for c in f.stores(("slope", "act")):
                c.start()
            for c in resid_stored:
                c.wait()
        elif name == "D":
            gathers["w2"].have(step)
            f.down(p.order(step))
        elif name == "END":
            keep(whole["w2"], whole_h["w2"])
            f.finish()
            f.store_out().start()
            swaps["CS"].done()
            keep(ct, ct_h)
    for item in SEQUENCE:
        if isinstance(item, int):
            do(item, item % 10)
            continue

        @pl.loop(0, 4 + max(code % 10 for code in item))
        def _(m, item=item):
            for code in item:
                lag = code % 10

                @pl.when((m >= lag) & (m < lag + 4))
                def _():
                    do(code, m - lag)

    f.drain_last(p.order(3))
    for c in [*pending, *f.stores([a for a in SAVED if a != "resid"]), f.store_out()]:
        c.wait()
    for s in swaps.values():
        s.finish()
    for g in gathers.values():
        g.finish()


def spread(slot_mask, x_in, ct_in, small, big):
    names, n, m = list(PARTS), len(PARTS), len(SAVED)
    outs = pl.pallas_call(
        spread_kernel,
        out_shape=[IMAGE, IMAGE, IMAGE, PROBS, jax.ShapeDtypeStruct((4, 8, 256), F32)]
        + [part(a) for a in WEIGHTS]
        + list(SAVED.values()),
        in_specs=[pl.BlockSpec(memory_space=pltpu.SMEM), ANY, ANY] + [VM] * (len(small) + len(big)),
        out_specs=[ANY] * 4 + [VM] + [ANY] * (4 + m),
        scratch_shapes=[scratch(IMAGE), scratch(IMAGE), scratch(IMAGE), pltpu.VMEM((4, 1, 1024), F32)]
        + [pltpu.VMEM((1, 256), F32), pltpu.VMEM((8, 32), F32)]
        + [scratch(part(a)) for a in names]
        + [pltpu.SemaphoreType.DMA((2,)), pltpu.SemaphoreType.DMA((7,))]
        + Swap.SEMS * 2
        + Gather.SEMS * n
        + Forward.SCRATCH,
        compiler_params=pltpu.CompilerParams(
            collective_id=0, has_side_effects=True, vmem_limit_bytes=VMEM_BYTES
        ),
        name="spread",
    )(slot_mask, x_in, ct_in, *small, *big)
    return outs[:5], dict(zip(WEIGHTS, outs[5:9])), dict(zip(SAVED, outs[9:]))


REDUCED = ("w2", "w1", "wout", "wqkv")


def turn_of(i):
    return (1 - i // 2) * (1 - i % 2) * 3 + i // 2 * (2 - i % 2)


class Reduce:
    def __init__(self, place, name, refs):
        self.p, self.name = place, name
        self.own, self.got1, self.got2, self.got3 = refs[:4]
        self.c_recv, self.send, self.recv, self.z_send, self.z_recv = refs[4:]

    @staticmethod
    def scratch(name):
        rows, width = PARTS[name][0][3:]
        return [
            pltpu.VMEM((4, 4, rows, width), BF16),
            pltpu.VMEM((4, 4, rows // 2, width), BF16),
            pltpu.VMEM((2, 4, rows // 2, width), BF16),
            pltpu.VMEM((5, rows, width), BF16),
            pltpu.SemaphoreType.DMA((4,)),
            pltpu.SemaphoreType.DMA((4, 6)),
            pltpu.SemaphoreType.DMA((4, 6)),
            pltpu.SemaphoreType.DMA((4,)),
            pltpu.SemaphoreType.DMA((5,)),
        ]

    def block(self, ref, t, yx):
        return ref.at[yx, t] if self.name in BY_COLUMN else ref.at[t, yx]

    def wait_bytes(self, ref, sem):
        remote(ref, ref, self.z_send.at[0], sem, self.p.c_id).wait_recv()

    def add(self, dst, *more):
        rows, width = dst.shape
        n = min(rows, 64 if width > 128 else 512)

        @pl.loop(0, rows // n)
        def _(i):
            r = pl.ds(pl.multiple_of(i * n, n), n)
            total = dst[r, :]
            for ref in more:
                total += ref[r, :]
            dst[r, :] = total

    def first_copy(self, by_y, j, t):
        p = self.p
        yx = (1 - p.y) * 2 + j if by_y else j * 2 + 1 - p.x
        src = half_of(self.block(self.own, t, yx), 0 if by_y else 1)
        k = (0 if by_y else 2) + j
        return remote(src, self.got1.at[k, t], self.send.at[t, k], self.recv.at[t, k], p.y_id if by_y else p.x_id)

    def second_copy(self, j, t):
        p = self.p
        by_x = j == 0
        src = half_of(self.block(self.own, t, p.x_yx if by_x else p.y_yx), j)
        return remote(src, self.got2.at[j, t], self.send.at[t, 4 + j], self.recv.at[t, 4 + j],
                      p.x_id if by_x else p.y_id)

    def other_core(self, t=None):
        ref = self.own if t is None else self.own.at[:, t] if self.name in BY_COLUMN else self.own.at[t]
        self.wait_bytes(ref, self.c_recv.at[0 if t is None else t])

    def begin(self, t):
        p = self.p
        self.first_copy(True, 1 - p.x, t).start()
        self.first_copy(False, 1 - p.y, t).start()
        self.first_copy(True, p.x, t).start()
        self.first_copy(False, p.y, t).start()

    def cross(self, i):
        p, t = self.p, turn_of(i)
        for j in range(2):
            self.first_copy(True, j, t).wait_recv()
            self.first_copy(False, j, t).wait_recv()
        self.add(half_of(self.block(self.own, t, p.x_yx), 0), self.got1.at[1 - p.x, t])
        self.second_copy(0, t).start()
        self.add(half_of(self.block(self.own, t, p.y_yx), 1), self.got1.at[2 + 1 - p.y, t])
        self.second_copy(1, t).start()
        self.add(half_of(self.block(self.own, t, p.yx), 0), self.got1.at[p.x, t])
        self.add(half_of(self.block(self.own, t, p.yx), 1), self.got1.at[2 + p.y, t])

    def along(self, i):
        p, t = self.p, turn_of(i)
        mine = self.block(self.own, t, p.yx)
        for j in (0, 1):
            self.second_copy(j, t).wait_recv()
            self.add(half_of(mine, j), self.got2.at[j, t])
        for up, ends in ((True, (p.t == 0) & (t > 0)), (False, (p.t == 3) & (t < 3))):

            @pl.when(ends)
            def _():
                self.send_z(t, up).start()

    def pass_on(self, i, hop):
        p, t = self.p, turn_of(i)
        mine = self.block(self.own, t, p.yx)
        for up, here in ((True, (p.t == hop) & (t > hop)), (False, (p.t == 3 - hop) & (t < 3 - hop))):

            @pl.when(here)
            def _():
                self.wait_bytes(self.got3.at[t], self.z_recv.at[t])
                self.add(mine, self.got3.at[t])
                self.send_z(t, up).start()

    def send_z(self, t, up):
        p = self.p
        slot = t if up else t + (4 - t) * ((3 + t - p.t) // 2)
        return remote(self.block(self.own, t, p.yx), self.got3.at[slot], self.z_send.at[t], self.z_recv.at[slot],
                      p.z_id(p.t + 1 if up else p.t - 1))

    def end(self, result):
        p = self.p
        mine = self.block(self.own, p.t, p.yx)
        rows, width = mine.shape
        n = min(rows, 32 if width > 128 else 256)

        pieces = [(result, slice(None))]
        if self.name == "wqkv":
            pieces = [(result.at[i], slice(i * 256, i * 256 + 256)) for i in range(3)]

        def through(ref):
            @pl.loop(0, rows // n)
            def _(i):
                r = pl.ds(pl.multiple_of(i * n, n), n)
                for to, lanes in pieces:
                    more = ref[r, lanes].astype(F32)
                    to[r, :] = more if ref is mine else to[r, :] + more

        through(mine)
        for slot, there in ((p.t, p.t > 0), (4, p.t < 3)):

            @pl.when(there)
            def _():
                self.wait_bytes(self.got3.at[slot], self.z_recv.at[slot])
                through(self.got3.at[slot])

    def finish(self):
        p = self.p
        for t in range(4):
            for j in range(2):
                self.first_copy(True, j, t).wait_send()
                self.first_copy(False, j, t).wait_send()
                self.second_copy(j, t).wait_send()

            @pl.when(p.t != t)
            def _():
                block = self.block(self.own, t, p.yx)
                remote(block, block, self.z_send.at[t], self.z_recv.at[t], p.c_id).wait_send()


class Total:
    SCRATCH = [
        pltpu.VMEM((4, 16, D), F32),
        pltpu.VMEM((6, 16, D), F32),
        pltpu.SemaphoreType.DMA((6,)),
        pltpu.SemaphoreType.DMA((6,)),
    ]

    def __init__(self, place, acc, refs):
        self.p, self.acc = place, acc
        self.sent, self.got, self.send, self.recv = refs

    def copies(self, i):
        p = self.p
        if i < 3:
            return [remote(self.sent.at[i], self.got.at[i], self.send.at[i], self.recv.at[i], (p.c_id, p.x_id, p.y_id)[i])]
        return [
            remote(self.sent.at[3], self.got.at[2 + k], self.send.at[2 + k], self.recv.at[2 + k], p.z_id(lax.rem(p.t + k, 4)))
            for k in (1, 2, 3)
        ]

    def start(self, i):
        self.sent[i] = self.acc[...]
        for c in self.copies(i):
            c.start()

    def end(self, i):
        for c in self.copies(i):
            c.wait()
        for k in (i,) if i < 3 else (3, 4, 5):
            self.acc[...] += self.got[k]


class Stream:
    def __init__(self, n, src, buf, sem):
        self.n, self.src, self.buf, self.sem = n, src, buf, sem
        self.depth = buf.shape[0]

    def copies(self, i):
        slot = lax.rem(i, self.depth)
        return [
            pltpu.make_async_copy(a, b, self.sem.at[slot, k])
            for k, (a, b) in enumerate(self.src(i, self.buf.at[slot]))
        ]

    def start(self):
        for i in range(min(self.depth - 1, self.n)):
            for c in self.copies(jnp.int32(i)):
                c.start()

    def next(self, i):
        for c in self.copies(i):
            c.wait()

        @pl.when(i + self.depth - 1 < self.n)
        def _():
            for c in self.copies(i + self.depth - 1):
                c.start()

        return self.buf.at[lax.rem(i, self.depth)]


def accumulate(ref, here, value, step):
    @pl.when(step == 0)
    def _():
        ref[:, here] = value

    @pl.when(step > 0)
    def _():
        ref[:, here] += value


BACK = ("w2", "w1", "wout", "wqkv", "T", "G0", "GS", "GM", "SHARE", "HG", "HS", "HM", "GN", "GR", "OA", "OM", "AT", "AM", "GI", "GT")
STEPS = ("", "X", "Z", "E", "Y", "W")
COLLECT = (
    500, (600, 701,), (900,), 1200, 800, 1300, 1400, 10, 13, 11, 12, 1500, (1600, 1701, 20,), 311, 1800, 211,
    312, 40, 43, 53, 42, 41, 210, 1900, 213, 313, 310, (1000, 1101,), 212, 220, 51, 110, 223, 323, 50, 111,
    322, 321, 343, 112, 342, 52, 320, 352, 113, 400, 221, 241, 341, 120, 222, 243, 240, 353, 250, 340, 350,
    121, 253, 122, 140, 351, 251, 242, 123, 30, 141, 142, 401, 151, 252, 152, 330, 402, 150, 143, 230, 153,
    403, 130,
)


class Backward:
    NAMES = (
        ("image", "gmlp", "slope", "gmix", "gn", "resid", "split", "ctx_t", "b1", "part_sums", "load_sem")
        + ("col_buf", "col_sem", "row_buf", "row_sem", "head_buf", "head_sem", "probs", "probs_sem")
        + ("up_mail", "up_mail_sem", "mix_mail", "mix_mail_sem", "out_mail", "out_mail_sem", "down_mail", "down_mail_sem")
    )
    SCRATCH = [
        scratch(IMAGE),
        scratch(ACT),
        pltpu.VMEM((ROWS, 4 * D), BF16),
        pltpu.VMEM((ROWS, 3 * D), BF16),
        pltpu.VMEM((ROWS, D), F32),
        pltpu.VMEM((ROWS, D), F32),
        pltpu.VMEM((2, 4, 128, ROWS), BF16),
        pltpu.VMEM((4, 2, 128, ROWS), BF16),
        pltpu.VMEM((4, 1, 1024), F32),
        pltpu.VMEM((6, 8, D), F32),
        pltpu.SemaphoreType.DMA((12,)),
        pltpu.VMEM((3, 4, 2, 2, 256, 128), BF16),
        pltpu.SemaphoreType.DMA((3, 2)),
        pltpu.VMEM((3, 2, 2, 128, 1024), BF16),
        pltpu.SemaphoreType.DMA((3, 1)),
        pltpu.VMEM((3, 4, ROWS, 128), BF16),
        pltpu.SemaphoreType.DMA((3, 4)),
        pltpu.VMEM((2, 2, ROWS, ROWS), BF16),
        pltpu.SemaphoreType.DMA((2, 1)),
        pltpu.VMEM((2, 4, 128, 512), BF16),
        pltpu.SemaphoreType.DMA((2,)),
        pltpu.VMEM((2, 4, 128, 768), BF16),
        pltpu.SemaphoreType.DMA((2,)),
        pltpu.VMEM((2, 2, 4, 256, 128), BF16),
        pltpu.SemaphoreType.DMA((2,)),
        pltpu.VMEM((1, 4, 1024, 128), BF16),
        pltpu.SemaphoreType.DMA((1,)),
    ]

    def __init__(self, p, reduces, swaps_of, total, hbm, vectors, sums, refs):
        for a, b in zip(self.NAMES, refs):
            setattr(self, a, b)
        self.p, self.reduces, self.total, self.vectors, self.sums = p, reduces, total, vectors, sums
        self.hbm = hbm
        self.out_swap, self.tok_swap = swaps_of(self.image)
        self.ups_mail = Mail(p, self.up_mail, self.up_mail_sem)
        self.mixes_mail = Mail(p, self.mix_mail, self.mix_mail_sem)
        self.downs_mail = Mail(p, self.down_mail, self.down_mail_sem)
        self.outs_mail = Mail(p, self.out_mail, self.out_mail_sem)
        h = hbm
        self.out_buf = self.probs.at[0, 0, :, pl.ds(0, 256)]
        self.loads = {
            a: self.load(i, *b)
            for i, (a, b) in enumerate(
                dict(
                    ct=(h["ct"], self.image),
                    slope=(h["slope"], self.slope),
                    nin0=(h["nin_t"].at[:, p.c], self.split.at[0]),
                    nin1=(h["nin_t"].at[:, 1 - p.c], self.split.at[1]),
                    out=(h["out"].at[p.t], self.out_buf),
                    resid=(h["resid"], self.resid),
                    ctx_t=(h["ctx_t"], self.ctx_t),
                    x=(h["x"], self.image),
                ).items()
            )
        }
        self.nmid = [
            self.load(2, h["nmid_t"].at[:, p.c], self.split.at[0]),
            self.load(3, h["nmid_t"].at[:, 1 - p.c], self.split.at[1]),
        ]
        self.out_done = self.load(4, self.out_buf, h["out_o"].at[p.t])
        self.tok_done = self.load(0, self.image.at[p.t], h["gtok_o"].at[p.t])

        def down_src(i, b):
            return [
                (h["w2"].at[:, :, turn_of(i // 2), pl.ds(i % 2 * 512 + k * 256, 256)], b.at[:, :, k]) for k in range(2)
            ]

        def out_src(i, b):
            return [(h["wout"].at[:, :, i * 2 + k], b.at[:, :, k]) for k in range(2)]

        def head_src(i, b):
            at = cols(turn_of(i // 2) * 2 + i % 2, 128)
            return [(h[a].at[:, at], b.at[k]) for k, a in enumerate(("q", "k", "v", "ctx"))]

        self.downs = Stream(8, down_src, self.col_buf, self.col_sem)
        self.outs = Stream(2, out_src, self.col_buf, self.col_sem)
        self.ups = Stream(
            8, lambda i, b: [(h["w1"].at[i % 4, pl.ds(i // 4 * 2, 2)], b)], self.row_buf, self.row_sem
        )
        self.mixes = Stream(
            8,
            lambda i, b: [(h["wqkv"].at[i % 4, pl.ds(i // 4 * 2, 2)], b.at[:, :, :, pl.ds(0, 768)])],
            self.row_buf,
            self.row_sem,
        )
        self.heads = Stream(8, head_src, self.head_buf, self.head_sem)
        self.heads_p = Stream(
            8, lambda i, b: [(h["probs"].at[turn_of(i // 2) * 2 + i % 2], b)], self.probs, self.probs_sem
        )

    def load(self, i, src, dst):
        return pltpu.make_async_copy(src, dst, self.load_sem.at[i])

    def act_load(self, i):
        return self.load(8 + i, self.hbm["act"].at[:, cols(turn_of(i), 1024)], self.gmix.at[:, cols(i % 3, 1024)])

    def begin(self):
        self.loads["ct"].start()
        for i in range(3):
            self.act_load(i).start()
        self.loads["slope"].start()
        self.downs.start()
        self.ups.start()
        for a in ("out", "resid", "ctx_t", "nin0", "nin1"):
            self.loads[a].start()
        self.heads.start()
        self.part_sums[...] = jnp.zeros_like(self.part_sums)
        self.sums[...] = jnp.zeros_like(self.sums)

    def mask_cotangent(self):
        self.loads["ct"].wait()
        mask = self.hbm["mask"]

        @over_rows
        def _(rows):
            g = wide(self.image, rows) * jnp.concatenate([mask[...]] * 4, axis=1)
            self.gmlp[rows, :] = g.astype(BF16)
            self.part_sums[0] += fold(g)

        self.loads["out"].wait()
        self.out_done.start()

    def four_columns(self, c):
        return jnp.concatenate([self.gmlp[:, cols(yx * 2 + c, 128)] for yx in range(4)], axis=1)

    def down_share(self, i):
        r, t = self.reduces["w2"], turn_of(i)
        self.act_load(i).wait()
        g = t_mm(self.gmix[:, cols(i % 3, 1024)], self.four_columns(1 - self.p.c)).astype(BF16)
        self.downs_mail.post(
            i, [g[:, k * 128 : k * 128 + 128] for k in range(4)], r.own.at[:, t], r.c_recv.at[t]
        )

    def down_own(self, i):
        r, t = self.reduces["w2"], turn_of(i)
        r.other_core(t)
        g = t_mm(self.gmix[:, cols(i % 3, 1024)], self.four_columns(self.p.c))
        for k in range(4):
            r.own[k, t] = (g[:, k * 128 : k * 128 + 128] + r.own[k, t].astype(F32)).astype(BF16)
        r.begin(t)

        @pl.when(i == 0)
        def _():
            self.act_load(3).start()

    def share(self):
        self.out_swap.start()

    def whole_rows(self, tile):
        return jnp.concatenate([tile[d // 2, d % 2].reshape(512, 128) for d in range(8)], axis=1)

    def post_rows(self, mail, n, g, r, t, here):
        g = g.astype(BF16).reshape(4, 128, -1)
        mail.post(n, [g[k] for k in range(4)], r.own.at[t, :, :, here], r.c_recv.at[t])

    def hidden(self, i):
        t = turn_of(i)

        @pl.when(i == 0)
        def _():
            self.loads["slope"].wait()

        @pl.loop(0, 2)
        def _(j):
            w = self.whole_rows(self.downs.next(2 * i + j))
            here = cols(t * 2 + j, 512)
            gpre = mm_t(self.gmlp[...], w) * self.slope[:, here].astype(F32)
            self.slope[:, here] = gpre.astype(BF16)
            self.b1[t, :, cols(j, 512)] = jnp.sum(gpre, axis=0, keepdims=True)

    def hidden_share(self, i):
        r, t = self.reduces["w1"], turn_of(i)

        @pl.loop(0, 2)
        def _(j):
            g = mm(self.split[1].reshape(512, ROWS), self.slope[:, cols(t * 2 + j, 512)])
            self.post_rows(self.ups_mail, 2 * i + j, g, r, t, cols(j, 512))

    def add_own(self, r, t, here, value):
        width = value.shape[1]
        had = r.own[t, :, :, here].astype(F32)
        r.own[t, :, :, here] = (value.reshape(4, 128, width) + had).astype(BF16)

    def hidden_own(self, i):
        r, t = self.reduces["w1"], turn_of(i)
        r.other_core(t)

        @pl.loop(0, 2)
        def _(j):
            g = mm(self.split[0].reshape(512, ROWS), self.slope[:, cols(t * 2 + j, 512)])
            self.add_own(r, t, cols(j, 512), g)

        r.begin(t)

    def through_up(self):
        self.outs.start()

        @pl.loop(0, 8)
        def _(i):
            w = self.ups.next(i)
            g = mm_t(self.slope[:, cols(i % 4, 1024)], w[...].reshape(512, D))
            accumulate(self.gn, cols(i // 4, 512), g, i % 4)

        self.mixes.start()

    def norm_mid(self):
        self.loads["resid"].wait()
        gain = vec(self.vectors, 5)

        @over_rows
        def _(rows):
            normed = self.gn[rows, :]
            g, scaled = grad_norm_rows(self.resid[rows, :], gain, normed)
            g = g + self.gmlp[rows, :].astype(F32)
            self.part_sums[1] += fold(normed)
            self.part_sums[2] += fold(scaled)
            self.part_sums[3] += fold(g)
            self.gn[rows, :] = g
            self.gmlp[rows, :] = g.astype(BF16)

    def attn_out(self):
        r, p = self.reduces["wout"], self.p
        self.loads["ctx_t"].wait()
        self.out_done.wait()
        self.heads_p.start()

        @pl.loop(0, 2)
        def _(q):
            g = mm(self.ctx_t[...].reshape(D, ROWS), column_pair(self.gmlp, q, 1 - p.c)).astype(BF16)
            self.outs_mail.post(
                q,
                [g[:, k * 128 : k * 128 + 128].reshape(4, 256, 128) for k in range(2)],
                r.own.at[pl.ds(q * 2, 2)],
                r.c_recv.at[0],
            )

        @pl.loop(0, 2)
        def _(i):
            g = mm_t(self.gmlp[...], self.whole_rows(self.outs.next(i))).astype(BF16)
            for k in range(2):
                self.image[i * 2 + k] = g[:, k * 256 : k * 256 + 256]

    def attn_out_own(self):
        r, p = self.reduces["wout"], self.p
        r.other_core()

        @pl.loop(0, 2)
        def _(q):
            g = mm(self.ctx_t[...].reshape(D, ROWS), column_pair(self.gmlp, q, p.c))
            for k in range(2):
                had = r.own[q * 2 + k].astype(F32)
                r.own[q * 2 + k] = (g[:, k * 128 : k * 128 + 128].reshape(4, 256, 128) + had).astype(BF16)

        for i in range(4):
            r.begin(turn_of(i))
        for a in ("nin0", "nin1"):
            self.loads[a].wait()

    def attend(self, i):
        r, t = self.reduces["wqkv"], turn_of(i)

        @pl.loop(0, 2)
        def _(h):
            ins = self.heads.next(2 * i + h)
            probs = self.heads_p.next(2 * i + h)
            got = attend_back_pair(*(ins[k] for k in range(4)), self.image[t, :, cols(h, 128)], probs)
            for c in range(3):
                self.gmix[:, pl.ds(pl.multiple_of(t * 768 + c * 256 + h * 128, 128), 128)] = got[c].astype(BF16)
            here = cols(t * 2 + h, 128)
            self.sums[2:3, here] = jnp.sum(got[0], axis=0, keepdims=True)
            self.sums[3:4, here] = jnp.sum(got[2], axis=0, keepdims=True)

        g = mm(self.split[1].reshape(512, ROWS), self.gmix[:, cols(t, 768)])
        self.post_rows(self.mixes_mail, i, g, r, t, pl.ds(0, 768))

    def attend_own(self, i):
        r, t = self.reduces["wqkv"], turn_of(i)
        r.other_core(t)
        self.add_own(r, t, slice(None), mm(self.split[0].reshape(512, ROWS), self.gmix[:, cols(t, 768)]))
        r.begin(t)

    def through_mix(self):
        self.loads["x"].start()
        for c in self.nmid:
            c.start()

        @pl.loop(0, 8)
        def _(i):
            w = self.mixes.next(i)
            g = mm_t(self.gmix[:, cols(i % 4, 768)], w[:, :, :, 0:768].reshape(512, 768))
            accumulate(self.resid, cols(i // 4, 512), g, i % 4)

    def norm_in(self):
        self.loads["x"].wait()
        gain = vec(self.vectors, 0)

        @over_rows
        def _(rows):
            normed = self.resid[rows, :]
            g, scaled = grad_norm_rows(wide(self.image, rows), gain, normed)
            g = g + self.gn[rows, :]
            self.part_sums[4] += fold(normed)
            self.part_sums[5] += fold(scaled)
            for t in range(4):
                self.image[t, rows, :] = g[:, t * 256 : t * 256 + 256].astype(BF16)

        self.tok_swap.start()
        self.tok_done.start()
        sums = self.sums
        for row, i in ((7, 0), (6, 1), (5, 2), (4, 3), (1, 4), (0, 5)):
            sums[row : row + 1, :] = jnp.sum(self.part_sums[i], axis=0, keepdims=True)
        for t in range(4):
            sums[8 + t : 9 + t, :] = self.b1[t]
        self.total.start(0)
        for c in self.nmid:
            c.wait()

    def finish(self):
        self.tok_done.wait()
        for m in (self.ups_mail, self.mixes_mail, self.outs_mail, self.downs_mail):
            m.finish()
        for s in (self.out_swap, self.tok_swap):
            s.done()
            s.finish()
        for r in self.reduces.values():
            r.finish()


HBM = ("x", "out", "ct", "probs") + WEIGHTS


def collect_kernel(slot_mask, vectors, *rest):
    names = HBM + tuple(SAVED)
    n = len(names)
    hbm = dict(zip(names, rest[:n]))
    out_o, gtok_o = rest[n : n + 2]
    hbm |= dict(out_o=out_o, gtok_o=gtok_o)
    results = dict(zip(REDUCED, rest[n + 2 : n + 6]))
    small, rest = rest[n + 6 : n + 14], rest[n + 14 :]
    mask, sums, rest = rest[0], rest[1], rest[2:]
    mask[...] = jnp.full((1, 256), slot_mask[lax.axis_index("tensor")].astype(F32))
    hbm["mask"] = mask
    m = len(Backward.SCRATCH)
    refs, rest = rest[:m], rest[m:]
    out_sems, tok_sems, total_refs, rest = rest[0:2], rest[2:4], rest[4:8], rest[8:]
    p = Place()
    reduces = {a: Reduce(p, a, rest[9 * i : 9 * i + 9]) for i, a in enumerate(REDUCED)}
    total = Total(p, sums, total_refs)

    def swaps_of(image):
        return Swap(p, hbm["out"], out_o, out_sems), Swap(p, image, gtok_o, tok_sems)

    b = Backward(p, reduces, swaps_of, total, hbm, vectors, sums, refs)
    acts = dict(
        G0=b.mask_cotangent, GS=b.down_share, GM=b.down_own, SHARE=b.share, HG=b.hidden, HS=b.hidden_share, HM=b.hidden_own, GN=b.through_up, GR=b.norm_mid, OA=b.attn_out,
        OM=b.attn_out_own, AT=b.attend, AM=b.attend_own, GI=b.through_mix, GT=b.norm_in,
    )
    counted = ("GS", "GM", "HG", "HS", "HM", "AT", "AM")

    def act(code, i):
        name, kind = BACK[code // 100], STEPS[code // 10 % 10]
        if name in reduces:
            r = reduces[name]
            if kind == "E":
                r.end(results[name])
            elif kind in ("Y", "W"):
                r.pass_on(i, 1 if kind == "Y" else 2)
            else:
                (r.cross if kind == "X" else r.along)(i)
        elif name == "T":
            total.end(i)
            if i < 3:
                total.start(i + 1)
        elif name in counted:
            acts[name](i)
        else:
            acts[name]()

    b.begin()
    p.greet()
    for step in COLLECT:
        if isinstance(step, int):
            act(step, step % 10)
            continue

        @pl.loop(0, 4 + max(code % 10 for code in step))
        def _(m, step=step):
            for code in step:
                lag = code % 10

                @pl.when((m >= lag) & (m < lag + 4))
                def _():
                    act(code, m - lag)

    here = pl.ds(pl.multiple_of(p.t * 256 + p.d // 4 * 128, 128), 128)
    four = sums[0:8, here]
    mine = sum(jnp.where(p.d % 4 == k, four[:, k * 32 : k * 32 + 32], 0.0) for k in range(4))
    for i, row in enumerate((0, 1, None, 4, 5, 6, 7)):
        if row is None:
            small[i][...] = mine[2:4]
        else:
            small[i][...] = mine[row : row + 1]
    hidden = sums[8:12, pl.ds(pl.multiple_of(p.d * 128, 128), 128)]
    small[7][...] = sum(jnp.where(p.t == k, hidden[k : k + 1], 0.0) for k in range(4))
    b.finish()


def collect(slot_mask, vectors, hbm):
    names = HBM + tuple(SAVED)
    outs = pl.pallas_call(
        collect_kernel,
        out_shape=[IMAGE, IMAGE]
        + [jax.ShapeDtypeStruct((3, 128, 256) if a == "wqkv" else PARTS[a][0][3:], F32) for a in REDUCED]
        + [jax.ShapeDtypeStruct((2 if i == 2 else 1, 128 if i == 7 else 32), F32) for i in range(8)],
        in_specs=[pl.BlockSpec(memory_space=pltpu.SMEM), VM] + [ANY] * len(names),
        out_specs=[ANY, ANY] + [VM] * 12,
        scratch_shapes=[pltpu.VMEM((1, 256), F32), pltpu.VMEM((16, D), F32)]
        + Backward.SCRATCH
        + Swap.SEMS * 2
        + Total.SCRATCH
        + sum((Reduce.scratch(a) for a in REDUCED), []),
        compiler_params=pltpu.CompilerParams(
            collective_id=1, has_side_effects=True, vmem_limit_bytes=VMEM_BYTES
        ),
        name="collect",
    )(slot_mask, vectors, *[hbm[a] for a in names])
    return outs[0], outs[1], dict(zip(REDUCED, outs[2:6])), outs[6:]


def gather_plain(w_qkv, w_out, w_fc1, w_fc2):
    def all_of(shard, axis):
        return lax.all_gather(
            lax.all_gather(shard.astype(BF16), "dp", axis=axis, tiled=True), "tensor", axis=0
        )

    wqkv = all_of(w_qkv.reshape(-1, 768), 0)
    wout = all_of(w_out, 1).reshape(D, 8, 128).transpose(1, 0, 2)
    w1 = all_of(w_fc1, 0)
    w2 = all_of(w_fc2, 1).reshape(4 * D, 8, 128).transpose(1, 0, 2)
    return wqkv, wout, w1, w2


def scatter_plain(grads):
    def mine(grad, axis):
        part = lax.psum_scatter(grad, "tensor", scatter_dimension=0, tiled=True)
        return lax.psum_scatter(part, "dp", scatter_dimension=axis, tiled=True).astype(F32)

    g_qkv = mine(grads["wqkv"], 1)[0]
    g_out = mine(grads["wout"].transpose(1, 0, 2).reshape(D, D), 1)
    g_fc1 = mine(grads["w1"], 1)[0]
    g_fc2 = mine(grads["w2"].transpose(1, 0, 2).reshape(4 * D, D), 1)
    return g_qkv, g_out, g_fc1, g_fc2


def on_device(
    dp,
    tokens_in,
    cotangent,
    slot_mask,
    norm1_gain,
    norm1_bias,
    w_qkv,
    b_qkv,
    w_out,
    b_out,
    norm2_gain,
    norm2_bias,
    w_fc1,
    b_fc1,
    w_fc2,
    b_fc2,
):
    def images(rows):
        return jnp.pad(rows.reshape(4, SEQ, 256), ((0, 0), (0, ROWS - SEQ), (0, 0)))

    def exchange(pieces):
        return lax.all_to_all(pieces, "tensor", split_axis=0, concat_axis=0, tiled=True)

    if dp == 8:
        small = (norm1_gain, norm1_bias, b_qkv, b_out, norm2_gain, norm2_bias, b_fc2, b_fc1)
        big = (w_qkv.transpose(1, 0, 2), w_out, w_fc1, w_fc2)
        first, weights, saved = spread(slot_mask, images(tokens_in), images(cotangent), small, big)
        x, ct, out, probs, vectors = first
        hbm = dict(x=x, out=out, ct=ct, probs=probs, **weights, **saved)
        out, gtok, got, g_small = collect(slot_mask, vectors, hbm)
    else:
        mask = jnp.broadcast_to(
            lax.dynamic_index_in_dim(slot_mask, lax.axis_index("tensor"), 0).astype(F32), (1, 256)
        )
        small = jnp.concatenate(
            (norm1_gain, norm1_bias, b_qkv[0], b_qkv[1], b_out, norm2_gain, norm2_bias, b_fc2)
        ).astype(BF16)
        vectors = lax.all_gather(
            lax.all_gather(small, "dp", axis=1, tiled=True), "tensor", axis=0
        ).astype(F32)
        hidden_bias = lax.all_gather(
            lax.all_gather(b_fc1.astype(BF16), "dp", axis=1, tiled=True), "tensor", axis=0
        ).astype(F32)
        x = exchange(images(tokens_in))
        ct = exchange(images(cotangent))
        plain = gather_plain(w_qkv, w_out, w_fc1, w_fc2)
        weights = {a: b.reshape(PARTS[a][0]) for a, b in zip(WEIGHTS, plain)}
        out, probs, saved = forward(x, weights, vectors, hidden_bias, mask)
    if dp == 8:
        g_qkv, g_out, g_fc1, g_fc2 = (got[a] for a in GRADS)
        g_qkv = g_qkv.transpose(1, 0, 2)
    else:
        flat = [weights[a].reshape(GRADS[a].shape) for a in GRADS]
        gtok, sums, grads = backward(x, ct, *flat, vectors, mask, probs, saved)
        g_qkv, g_out, g_fc1, g_fc2 = scatter_plain(grads)
        out, gtok = exchange(out), exchange(gtok)

        def total(part, axis):
            part = lax.psum_scatter(part, "tensor", scatter_dimension=0, tiled=True)
            return lax.psum_scatter(part, "dp", scatter_dimension=axis, tiled=True)

        s = total(sums[0:8].reshape(8, 4, 256).transpose(1, 0, 2), 2)[0]
        g_small = (s[0:1], s[1:2], s[2:4], s[4:5], s[5:6], s[6:7], s[7:8], total(sums[8:12], 1))

    def rows(pieces):
        return pieces[:, :SEQ].reshape(4 * SEQ, 256)

    return (
        rows(out),
        rows(gtok),
        g_small[0],
        g_small[1],
        g_qkv.reshape(w_qkv.shape),
        g_small[2][:, None],
        g_out,
        g_small[3],
        g_small[4],
        g_small[5],
        g_fc1,
        g_small[7],
        g_fc2,
        g_small[6],
    )


def solution(mesh):
    both, turned = P("dp", "tensor"), P("tensor", "dp")
    mixed, pair = P("dp", None, "tensor"), P(None, "tensor", "dp")
    params = (turned, turned, mixed, pair, turned, turned, turned, turned, both, turned, turned, turned)
    return jax.shard_map(
        functools.partial(on_device, mesh.shape["dp"]),
        mesh=mesh,
        in_specs=(both, both, P("dp"), *params),
        out_specs=(both, both, *params),
        check_vma=False,
    )
```

```python
import functools
import jax
import jax.numpy as jnp
from jax import lax
from jax.experimental import pallas as pl
from jax.experimental.pallas import tpu as pltpu
from jax.sharding import PartitionSpec as P

D = 1024
HD = 64
SEQ = 577
ROWS = 592
CHUNK = 96
F32 = jnp.float32
BF16 = jnp.bfloat16
LAST = (((1,), (1,)), ((), ()))
VMEM_BYTES = 67_043_328


def mm(a, b):
    return jnp.dot(a, b, preferred_element_type=F32)


def t_mm(a, b):
    return lax.dot_general(a, b, (((0,), (0,)), ((), ())), preferred_element_type=F32)


def mm_t(a, b):
    return lax.dot_general(a, b, LAST, preferred_element_type=F32)


def cols(i, n):
    return pl.ds(pl.multiple_of(i * n, n), n)


def row_stats(values):
    mean = jnp.sum(values, axis=1, keepdims=True) * (1.0 / D)
    centered = values - mean
    var = jnp.sum(centered * centered, axis=1, keepdims=True) * (1.0 / D)
    inv = lax.rsqrt(var + 1e-05)
    return centered * inv, inv


def wide(ref, rows):
    return jnp.concatenate([ref[t, rows, :].astype(F32) for t in range(4)], axis=1)


def over_rows(do):
    @pl.loop(0, 576 // CHUNK)
    def _(i):
        do(pl.ds(pl.multiple_of(i * CHUNK, CHUNK), CHUNK))

    do(pl.ds(576, ROWS - 576))


def vec(vectors, row):
    return jnp.concatenate([vectors[t, row : row + 1, :] for t in range(4)], axis=1)


def norm_in(x, vectors, nin):
    gain, shift = vec(vectors, 0), vec(vectors, 1)

    @over_rows
    def _(rows):
        xhat, _ = row_stats(wide(x, rows))
        nin[rows, :] = (xhat * gain + shift).astype(BF16)


def flip(src, dst, n):
    @pl.loop(0, n // 256)
    def _(i):
        dst[i] = src[:, cols(i, 256)].T.reshape(2, 128, ROWS)


def project(nin, wqkv, vectors, t, q, k, v):
    here = cols(t, 256)

    g = mm(nin[...], wqkv[t].reshape(D, 768))
    q[:, here] = (g[:, 0:256] + vectors[t, 2:3, :]).astype(BF16)
    k[:, here] = g[:, 256:512].astype(BF16)
    v[:, here] = (g[:, 512:768] + vectors[t, 3:4, :]).astype(BF16)


def head_lanes(h):
    lane = lax.broadcasted_iota(jnp.int32, (ROWS, 128), 1)
    own = (lane >= h * 64) & (lane < h * 64 + 64)
    return lane, own, 64 - h * 64


def attend_pair(pair, q, k, v, ctx, probs, slot):
    here = cols(pair, 128)
    lane = lax.broadcasted_iota(jnp.int32, (ROWS, 128), 1)
    row = lax.broadcasted_iota(jnp.int32, (ROWS, 128), 0)
    queries = q[:, here].astype(F32) * (HD**-0.5)
    keys = k[:, here].astype(F32)
    values = v[:, here]
    blocked = jnp.where(row >= SEQ, -1e30, 0.0)
    parts = []
    for h in range(2):
        own = (lane < 64) if h == 0 else (lane >= 64)
        spare = 64 if h == 0 else 0
        qa = jnp.where(own, queries, jnp.where(lane == spare, 1.0, 0.0)).astype(BF16)
        ka = jnp.where(lane == spare, blocked, keys).astype(BF16)
        scores = mm_t(ka, qa)
        top = jnp.max(scores, axis=0, keepdims=True)
        e = jnp.exp(scores - top)
        total = jnp.sum(e, axis=0, keepdims=True)
        p = (e * (1.0 / total)).astype(BF16)
        probs[slot, h] = p
        parts.append(
            lax.dot_general(p, values, (((0,), (0,)), ((), ())), preferred_element_type=F32)
        )
    ctx[:, here] = jnp.where(lane < 64, parts[0], parts[1]).astype(BF16)


def out_block(i, ctx, wout, x, vectors, resid):
    w = jnp.concatenate([wout[i, c].reshape(D, 128) for c in range(2)], axis=1)
    resid[:, cols(i, 256)] = x[i].astype(F32) + mm(ctx[...], w) + vectors[i, 4:5, :]


def norm_mid(resid, vectors, nmid):
    gain, shift = vec(vectors, 5), vec(vectors, 6)

    @over_rows
    def _(rows):
        xhat, _ = row_stats(resid[rows, :])
        nmid[rows, :] = (xhat * gain + shift).astype(BF16)


def hidden_tile(t, j, nmid, w1, b1, act, slope):
    here = pl.ds(pl.multiple_of(t * 1024 + j * 256, 256), 256)
    bias = b1[t, :, cols(j, 256)]
    pre = mm(nmid[...], w1[t, :, :, :, cols(j, 256)].reshape(D, 256)) + bias
    sig = 1.0 / (1.0 + jnp.exp(-1.702 * pre))
    a = pre * sig
    slope[:, here] = (sig + 1.702 * a * (1.0 - sig)).astype(BF16)
    act[:, here] = a.astype(BF16)


def down_block(i, t, act, w2, total):
    w = jnp.concatenate([w2[i, c, t] for c in range(2)], axis=1)
    total[:, cols(i, 256)] += mm(act[:, cols(t, 1024)], w)


def finish_block(i, total, vectors, mask, out):
    out[i] = ((total[:, cols(i, 256)] + vectors[i, 7:8, :]) * mask[...]).astype(BF16)


def grad_norm_rows(values, gain, n):
    xhat, inv = row_stats(values)
    e = n * gain
    first = jnp.sum(e, axis=1, keepdims=True) * (1.0 / D)
    second = jnp.sum(e * xhat, axis=1, keepdims=True) * (1.0 / D)
    return inv * (e - first - xhat * second), n * xhat


def fold(a):
    return jnp.sum(a.reshape(-1, 8, D), axis=0)


def attend_back_pair(queries, keys, values, out, go, probs):
    values_f, go_f = values.astype(F32), go.astype(F32)
    dots = go_f * out.astype(F32)
    dq, dk, dv = [], [], []
    for h in range(2):
        lane, own, spare = head_lanes(h)
        delta = -jnp.sum(jnp.where(own, dots, 0.0), axis=1, keepdims=True)
        high = delta.astype(BF16).astype(F32)
        ga = jnp.where(
            own, go_f, jnp.where(lane == spare, high, jnp.where(lane == spare + 1, delta - high, 0.0))
        ).astype(BF16)
        marks = jnp.where((lane == spare) | (lane == spare + 1), 1.0, 0.0)
        va = jnp.where(own, values_f, marks).astype(BF16)
        p = probs[h]
        gs = (p.astype(F32) * mm_t(va, ga)).astype(BF16)
        dv.append(mm(p, go))
        dk.append(mm(gs, queries))
        dq.append(
            lax.dot_general(gs, keys, (((0,), (0,)), ((), ())), preferred_element_type=F32)
        )
    low = head_lanes(0)[1]
    scale = HD**-0.5
    return (
        jnp.where(low, dq[0], dq[1]) * scale,
        jnp.where(low, dk[0], dk[1]) * scale,
        jnp.where(low, dv[0], dv[1]),
    )


ACT = jax.ShapeDtypeStruct((ROWS, D), BF16)
TURNED = jax.ShapeDtypeStruct((4, 2, 128, ROWS), BF16)
SAVED = dict(
    nin_t=TURNED,
    q=ACT,
    k=ACT,
    v=ACT,
    ctx=ACT,
    ctx_t=TURNED,
    nmid_t=TURNED,
    resid=jax.ShapeDtypeStruct((ROWS, D), F32),
    act=jax.ShapeDtypeStruct((ROWS, 4 * D), BF16),
    slope=jax.ShapeDtypeStruct((ROWS, 4 * D), BF16),
)
PROBS = jax.ShapeDtypeStruct((8, 2, ROWS, ROWS), BF16)
IMAGE = jax.ShapeDtypeStruct((4, ROWS, 256), BF16)
ANY = pl.BlockSpec(memory_space=pl.ANY)
VM = pl.BlockSpec(memory_space=pltpu.VMEM)


def scratch(like):
    return pltpu.VMEM(like.shape, like.dtype)


PARTS = dict(
    sv=((4, 4, 2, 16, 256), F32),
    wqkv=((4, 4, 2, 128, 768), BF16),
    wout=((4, 2, 4, 256, 128), BF16),
    w1=((4, 4, 2, 128, 1024), BF16),
    w2=((4, 2, 4, 1024, 128), BF16),
)
WEIGHTS = ("wqkv", "wout", "w1", "w2")


def part(name):
    return jax.ShapeDtypeStruct(*PARTS[name])


class Forward:
    SCRATCH = [scratch(a) for a in SAVED.values()] + [
        scratch(ACT),
        pltpu.VMEM((2, 2, ROWS, ROWS), BF16),
        pltpu.SemaphoreType.DMA((2,)),
        pltpu.SemaphoreType.DMA((len(SAVED) + 1,)),
    ]

    def __init__(self, x, weights, vectors, b1, mask, out, out_h, probs_h, saved_h, refs):
        n = len(SAVED)
        self.x, self.w, self.vectors, self.b1, self.mask = x, weights, vectors, b1, mask
        self.out, self.out_h, self.probs_h, self.saved_h = out, out_h, probs_h, saved_h
        self.saved = dict(zip(SAVED, refs[:n]))
        self.total = self.saved["resid"]
        self.normed, self.probs, self.probs_sem, self.out_sem = refs[n:]
        self.act = self.saved["act"]

    def start_norm(self):
        norm_in(self.x, self.vectors, self.normed)
        flip(self.normed, self.saved["nin_t"], D)

    def put(self, pair, slot):
        return pltpu.make_async_copy(self.probs.at[slot], self.probs_h.at[pair], self.probs_sem.at[slot])

    def heads(self, s, i):
        a = self.saved
        project(self.normed, self.w["wqkv"], self.vectors, s, a["q"], a["k"], a["v"])

        @pl.loop(0, 2)
        def _(slot):
            pair = s * 2 + slot
            if i:
                self.put(pair, slot).wait()
            attend_pair(pair, a["q"], a["k"], a["v"], a["ctx"], self.probs, slot)
            self.put(pair, slot).start()

    def middle(self):
        a = self.saved

        @pl.loop(0, 4)
        def _(i):
            out_block(i, a["ctx"], self.w["wout"], self.x, self.vectors, a["resid"])

        norm_mid(a["resid"], self.vectors, self.normed)

    def hidden(self, s):
        @pl.loop(0, 4)
        def _(j):
            hidden_tile(s, j, self.normed, self.w["w1"], self.b1, self.act, self.saved["slope"])

    def down(self, s):
        @pl.loop(0, 4)
        def _(i):
            down_block(i, s, self.act, self.w["w2"], self.total)

    def turn(self):
        flip(self.saved["ctx"], self.saved["ctx_t"], D)
        flip(self.normed, self.saved["nmid_t"], D)

    def finish(self):
        @pl.loop(0, 4)
        def _(i):
            finish_block(i, self.total, self.vectors, self.mask, self.out)

    def stores(self, names):
        at = list(SAVED)
        return [
            pltpu.make_async_copy(self.saved[a], self.saved_h[a], self.out_sem.at[at.index(a)]) for a in names
        ]

    def store_out(self):
        return pltpu.make_async_copy(self.out, self.out_h, self.out_sem.at[len(SAVED)])

    def drain_last(self, s):
        for slot in range(2):
            self.put(s * 2 + slot, slot).wait()

    def drain(self):
        for slot in range(2):
            self.put(6 + slot, slot).wait()


def forward_kernel(x_h, wqkv_h, wout_h, w1_h, w2_h, vectors, b1, mask, *rest):
    n = len(SAVED)
    saved_h = dict(zip(SAVED, rest[2 : 2 + n]))
    x, out, *weights, in_sem = rest[2 + n : 9 + n]
    loads = [
        pltpu.make_async_copy(a, b, in_sem.at[i])
        for i, (a, b) in enumerate(zip((x_h, wqkv_h, wout_h, w1_h, w2_h), (x, *weights)))
    ]
    for c in loads:
        c.start()
    for c in loads:
        c.wait()
    f = Forward(x, dict(zip(WEIGHTS, weights)), vectors, b1, mask, out, rest[0], rest[1], saved_h, rest[9 + n :])
    f.start_norm()
    for s in range(4):
        f.heads(s, s)
    f.middle()
    for c in f.stores(("resid",)):
        c.start()
        c.wait()
    for s in range(4):
        f.hidden(s)
        f.down(s)
    f.turn()
    f.finish()
    f.drain()
    stores = [*f.stores([a for a in SAVED if a != "resid"]), f.store_out()]
    for c in stores:
        c.start()
    for c in stores:
        c.wait()


def forward(x, weights, vectors, b1, mask):
    n = len(SAVED)
    outs = pl.pallas_call(
        forward_kernel,
        out_shape=[IMAGE, PROBS, *SAVED.values()],
        in_specs=[ANY] * 5 + [VM, VM, VM],
        out_specs=[ANY] * (2 + n),
        scratch_shapes=[scratch(IMAGE), scratch(IMAGE)]
        + [scratch(part(a)) for a in WEIGHTS]
        + [pltpu.SemaphoreType.DMA((5,))]
        + Forward.SCRATCH,
        compiler_params=pltpu.CompilerParams(vmem_limit_bytes=VMEM_BYTES),
        name="forward",
    )(x, *[weights[a] for a in WEIGHTS], vectors, b1, mask)
    return outs[0], outs[1], dict(zip(SAVED, outs[2:]))


GRADS = dict(
    wqkv=jax.ShapeDtypeStruct((4, 1024, 768), BF16),
    wout=jax.ShapeDtypeStruct((8, 1024, 128), BF16),
    w1=jax.ShapeDtypeStruct((4, 1024, 1024), BF16),
    w2=jax.ShapeDtypeStruct((8, 4096, 128), BF16),
)


def send_tile(stage, sem, i, value, targets):
    slot = lax.rem(i, 2)

    def copies(s):
        return [
            pltpu.make_async_copy(
                stage.at[s] if w == 256 else stage.at[s, :, pl.ds(c, w)], ref, sem.at[s]
            )
            for ref, c, w in targets
        ]

    @pl.when(i >= 2)
    def _():
        pltpu.make_async_copy(stage.at[slot], stage.at[slot], sem.at[slot]).wait()

    stage[slot] = value
    for c in copies(slot):
        c.start()


def drain(stage, sem):
    for slot in range(2):
        pltpu.make_async_copy(stage.at[slot], stage.at[slot], sem.at[slot]).wait()


def backward_kernel(x_h, ct_h, wqkv_h, wout_h, w1_h, w2_h, vectors, mask, probs_h, *rest):
    n = len(SAVED)
    saved_h = dict(zip(SAVED, rest[:n]))
    gtok_h, sums_o = rest[n], rest[n + 1]
    g_h = dict(zip(GRADS, rest[n + 2 : n + 6]))
    rest = rest[n + 6 :]
    saved = dict(zip(SAVED, rest[:n]))
    (x, wqkv, wout, w1, w2, b1, gmlp, gattn, gctx, gn, gmix, probs, sums, part, stage,
     in_sem, probs_sem, tile_sem, saved_sem) = rest[n:]
    gtok = x
    names = dict(ct=(ct_h, gtok), x=(x_h, x), w2=(w2_h, w2), w1=(w1_h, w1), wout=(wout_h, wout), wqkv=(wqkv_h, wqkv))
    load = {a: pltpu.make_async_copy(*names[a], in_sem.at[i]) for i, a in enumerate(names)}
    load_saved = {a: pltpu.make_async_copy(saved_h[a], saved[a], saved_sem.at[i]) for i, a in enumerate(SAVED)}
    load["ct"].start()
    load_saved["act"].start()
    load_saved["slope"].start()
    for a in ("w2", "w1", "wout", "wqkv"):
        load[a].start()
    for a in SAVED:
        if a not in ("act", "slope"):
            load_saved[a].start()
    part[...] = jnp.zeros_like(part)
    sums[...] = jnp.zeros_like(sums)
    load["ct"].wait()

    @over_rows
    def _(rows):
        g = jnp.concatenate([x[t, rows, :].astype(F32) * mask[...] for t in range(4)], axis=1)
        gmlp[rows, :] = g.astype(BF16)
        part[0] += fold(g)

    load["x"].start()
    load_saved["act"].wait()

    @pl.loop(0, 16)
    def _(i):
        t, c = i // 4, i % 4
        r = t_mm(saved["act"][:, cols(t, 1024)], gmlp[:, cols(c, 256)]).astype(BF16)
        send_tile(stage, tile_sem, i, r, [
            (g_h["w2"].at[2 * c + e, cols(t, 1024), :], e * 128, 128) for e in range(2)])

    load_saved["slope"].wait()
    load["w2"].wait()
    slope = saved["slope"]

    @pl.loop(0, 16)
    def _(i):
        w = jnp.concatenate([w2[d, cols(i, 256), :] for d in range(8)], axis=1)
        gpre = mm_t(gmlp[...], w) * slope[:, cols(i, 256)].astype(F32)
        slope[:, cols(i, 256)] = gpre.astype(BF16)
        b1[i // 4, :, cols(i % 4, 256)] = jnp.sum(gpre, axis=0, keepdims=True)

    load_saved["nmid_t"].wait()

    @pl.loop(0, 16)
    def _(i):
        r = mm(saved["nmid_t"][...].reshape(D, ROWS), slope[:, cols(i, 256)]).astype(BF16)
        send_tile(stage, tile_sem, i + 16, r, [(g_h["w1"].at[i // 4, :, cols(i % 4, 256)], 0, 256)])

    load["w1"].wait()

    @pl.loop(0, 4)
    def _(i):
        total = mm_t(slope[:, 0:1024], w1[0, cols(i, 256), :])
        for t in range(1, 4):
            total += mm_t(slope[:, t * 1024 : t * 1024 + 1024], w1[t, cols(i, 256), :])
        gn[:, cols(i, 256)] = total

    load_saved["resid"].wait()
    gain2 = vec(vectors, 5)

    @over_rows
    def _(rows):
        normed = gn[rows, :]
        g, scaled = grad_norm_rows(saved["resid"][rows, :], gain2, normed)
        g = g + gmlp[rows, :].astype(F32)
        part[1] += fold(normed)
        part[2] += fold(scaled)
        part[3] += fold(g)
        gn[rows, :] = g
        gattn[rows, :] = g.astype(BF16)

    load["wout"].wait()
    load_saved["ctx_t"].wait()

    @pl.loop(0, 4)
    def _(i):
        w = jnp.concatenate([wout[d, cols(i, 256), :] for d in range(8)], axis=1)
        gctx[:, cols(i, 256)] = mm_t(gattn[...], w).astype(BF16)
        r = mm(saved["ctx_t"][...].reshape(D, ROWS), gattn[:, cols(i, 256)]).astype(BF16)
        send_tile(stage, tile_sem, i + 32, r, [(g_h["wout"].at[2 * i + e], e * 128, 128) for e in range(2)])

    for a in ("q", "k", "v", "ctx"):
        load_saved[a].wait()

    def get(pair, slot):
        return pltpu.make_async_copy(probs_h.at[pair], probs.at[slot], probs_sem.at[slot])

    get(0, 0).start()

    @pl.loop(0, 8)
    def _(pair):
        slot = pair % 2

        @pl.when(pair < 7)
        def _():
            get(pair + 1, 1 - slot).start()

        get(pair, slot).wait()
        here = cols(pair, 128)

        got = attend_back_pair(
            *(saved[a][:, here] for a in ("q", "k", "v", "ctx")), gctx[:, here], probs.at[slot]
        )
        for c in range(3):
            at = pl.ds(pl.multiple_of(c * 256 + (pair % 2) * 128, 128), 128)
            gmix[pair // 2, :, at] = got[c].astype(BF16)
        sums[2:3, here] = jnp.sum(got[0], axis=0, keepdims=True)
        sums[3:4, here] = jnp.sum(got[2], axis=0, keepdims=True)

    load_saved["nin_t"].wait()

    @pl.loop(0, 12)
    def _(i):
        t, c = i // 3, i % 3
        r = mm(saved["nin_t"][...].reshape(D, ROWS), gmix[t, :, cols(c, 256)]).astype(BF16)
        send_tile(stage, tile_sem, i + 36, r, [(g_h["wqkv"].at[t, :, cols(c, 256)], 0, 256)])

    load["wqkv"].wait()
    resid = saved["resid"]

    @pl.loop(0, 4)
    def _(i):
        total = mm_t(gmix[0], wqkv[0, cols(i, 256), :])
        for t in range(1, 4):
            total += mm_t(gmix[t], wqkv[t, cols(i, 256), :])
        resid[:, cols(i, 256)] = total

    load["x"].wait()
    gain1 = vec(vectors, 0)

    @over_rows
    def _(rows):
        normed = resid[rows, :]
        g, scaled = grad_norm_rows(wide(x, rows), gain1, normed)
        g = g + gn[rows, :]
        part[4] += fold(normed)
        part[5] += fold(scaled)
        for t in range(4):
            gtok[t, rows, :] = g[:, t * 256 : t * 256 + 256].astype(BF16)

    for row, i in ((7, 0), (6, 1), (5, 2), (4, 3), (1, 4), (0, 5)):
        sums[row : row + 1, :] = jnp.sum(part[i], axis=0, keepdims=True)
    sums_o[0:8, :] = sums[...]
    for t in range(4):
        sums_o[8 + t : 9 + t, :] = b1[t]
    done = pltpu.make_async_copy(gtok, gtok_h, in_sem.at[0])
    done.start()
    done.wait()
    drain(stage, tile_sem)


def backward(x, ct, wqkv, wout, w1, w2, vectors, mask, probs, saved):
    n = len(SAVED)
    outs = pl.pallas_call(
        backward_kernel,
        out_shape=[IMAGE, jax.ShapeDtypeStruct((12, D), F32), *GRADS.values()],
        in_specs=[ANY] * 6 + [VM, VM, ANY] + [ANY] * n,
        out_specs=[ANY, VM] + [ANY] * 4,
        scratch_shapes=[scratch(a) for a in SAVED.values()]
        + [scratch(a) for a in (x, wqkv, wout, w1, w2)]
        + [
            pltpu.VMEM((4, 1, 1024), F32),
            scratch(ACT),
            scratch(ACT),
            scratch(ACT),
            pltpu.VMEM((ROWS, D), F32),
            pltpu.VMEM((4, ROWS, 768), BF16),
            pltpu.VMEM((2, 2, ROWS, ROWS), BF16),
            pltpu.VMEM((8, D), F32),
            pltpu.VMEM((6, 8, D), F32),
            pltpu.VMEM((2, 1024, 256), BF16),
            pltpu.SemaphoreType.DMA((6,)),
            pltpu.SemaphoreType.DMA((2,)),
            pltpu.SemaphoreType.DMA((2,)),
            pltpu.SemaphoreType.DMA((n,)),
        ],
        compiler_params=pltpu.CompilerParams(vmem_limit_bytes=VMEM_BYTES),
        name="backward",
    )(x, ct, wqkv, wout, w1, w2, vectors, mask, probs, *[saved[a] for a in SAVED])
    return outs[0], outs[1], dict(zip(GRADS, outs[2:]))


MESH = pl.DeviceIdType.MESH
BY_COLUMN = ("wout", "w2")


def block_of(name, ref, t, yx, c):
    return ref.at[yx, c, t] if name in BY_COLUMN else ref.at[t, yx, c]


def half_of(ref, h):
    n = ref.shape[0] // 2
    return ref.at[pl.ds(h * n, n)]


class Place:
    def __init__(self):
        d, self.t = lax.axis_index("dp"), lax.axis_index("tensor")
        self.y, self.x, self.c = d // 4, d // 2 % 2, d % 2
        self.yx = d // 2
        self.x_yx = self.y * 2 + 1 - self.x
        self.y_yx = (1 - self.y) * 2 + self.x
        self.xy_yx = (1 - self.y) * 2 + 1 - self.x
        self.d = d
        self.x_id = (self.x_yx * 2 + self.c, self.t)
        self.y_id = (self.y_yx * 2 + self.c, self.t)
        self.c_id = (self.yx * 2 + 1 - self.c, self.t)

    def z_id(self, t):
        return (self.d, t)

    def order(self, i):
        t = self.t
        near, far = (t, t + 1 - 2 * (t % 2)), (2 - t // 2, 3 - 3 * (t // 2))
        if isinstance(i, int):
            return (near + far)[i]
        half, odd = i // 2, i % 2
        return (1 - half) * (near[0] + odd * (near[1] - near[0])) + half * (far[0] + odd * (far[1] - far[0]))

    def greet(self):
        barrier = pltpu.get_barrier_semaphore()
        others = [self.x_id, self.y_id, self.c_id]
        others += [self.z_id(lax.rem(self.t + k, 4)) for k in (1, 2, 3)]
        for other in others:
            pl.semaphore_signal(barrier, inc=1, device_id=other, device_id_type=MESH)
        pl.semaphore_wait(barrier, 6)


def remote(src, dst, send, recv, where):
    return pltpu.make_async_remote_copy(
        src_ref=src, dst_ref=dst, send_sem=send, recv_sem=recv, device_id=where, device_id_type=MESH
    )


class Gather:
    SEMS = [
        pltpu.SemaphoreType.DMA((2, 4)),
        pltpu.SemaphoreType.DMA((4,)),
        pltpu.SemaphoreType.DMA((4, 6)),
        pltpu.SemaphoreType.DMA((4, 6)),
        pltpu.SemaphoreType.DMA((4,)),
        pltpu.SemaphoreType.DMA((4,)),
    ]

    def __init__(self, place, name, own, whole, sems):
        self.p, self.name, self.own, self.whole = place, name, own, whole
        self.z_send, self.z_recv, self.xy_send, self.xy_recv, self.c_send, self.c_recv = sems

    def at(self, s, yx):
        return block_of(self.name, self.whole, s, yx, self.p.c)

    def z_copies(self, s, act, src=None):
        p = self.p
        dst = self.at(s, p.yx)
        for way, going, to in ((0, (s <= p.t) & (p.t < 3), p.t + 1), (1, (s >= p.t) & (p.t > 0), p.t - 1)):

            @pl.when(going)
            def _():
                c = remote(dst if src is None else src, dst, self.z_send.at[way, s], self.z_recv.at[s], p.z_id(to))
                c.start() if act == "start" else c.wait_send()

    def xy_copy(self, k, s, mine=False):
        p = self.p
        yx = (p.yx, p.yx, p.yx, p.x_yx, p.yx, p.y_yx)[k]
        h = (0, 1, 0, 0, 1, 1)[k]
        to = (p.x_id, p.y_id, p.y_id, p.y_id, p.x_id, p.x_id)[k]
        dst = half_of(self.at(s, yx), h)
        src = half_of(self.own, h) if mine else dst
        return remote(src, dst, self.xy_send.at[s, k], self.xy_recv.at[s, k], to)

    def straight(self, k):
        p = self.p
        return remote(
            self.own, self.at(p.t, p.yx), self.z_send.at[0, k], self.z_recv.at[p.t], p.z_id(lax.rem(p.t + k, 4))
        )

    def open(self):
        s = self.p.t
        if self.name == "sv":
            for k in (1, 2, 3):
                self.straight(k).start()
        else:
            self.z_copies(s, "start", self.own)
        for k in (0, 1):
            self.xy_copy(k, s, True).start()

    def arrive(self, i):
        s = self.p.order(i)
        here = self.at(s, self.p.yx)
        remote(here, here, self.z_send.at[0, s], self.z_recv.at[s], self.p.c_id).wait_recv()
        if self.name != "sv":
            self.z_copies(s, "start")
        for k in (0, 1):
            self.xy_copy(k, s).start()

    def second(self, i):
        s = self.p.order(i)
        for got, own, other in ((0, 2, 3), (1, 4, 5)):
            self.xy_copy(own, s, isinstance(i, int) and i == 0).start()
            self.xy_copy(got, s).wait_recv()
            self.xy_copy(other, s).start()

    def core_copy(self, s):
        c = self.p.c
        ref = self.whole.at[:, c, s] if self.name in BY_COLUMN else self.whole.at[s, :, c]
        return remote(ref, ref, self.c_send.at[s], self.c_recv.at[s], self.p.c_id)

    def last(self, i):
        s = self.p.order(i)
        for k in (2, 3, 4, 5):
            self.xy_copy(k, s).wait_recv()
        self.core_copy(s).start()

    def have(self, i):
        self.core_copy(self.p.order(i)).wait_recv()

    def finish(self):
        for s in range(4):
            if self.name != "sv":
                self.z_copies(s, "wait")
            elif s:
                self.straight(s).wait_send()
            for k in range(6):
                self.xy_copy(k, s).wait_send()
            self.core_copy(s).wait_send()


class Swap:
    SEMS = [pltpu.SemaphoreType.DMA((4,)), pltpu.SemaphoreType.DMA((4,))]

    def __init__(self, place, pieces, whole, sems):
        self.p, self.pieces, self.whole = place, pieces, whole
        self.send, self.recv = sems

    def copy(self, k):
        p = self.p
        to = lax.rem(p.t + k, 4)
        return remote(self.pieces.at[to], self.whole.at[p.t], self.send.at[k], self.recv.at[k], p.z_id(to))

    def start(self):
        for k in (1, 3, 2):
            self.copy(k).start()

    def done(self):
        for k in (1, 2, 3):
            self.copy(k).wait_recv()

    def finish(self):
        for k in (1, 2, 3):
            self.copy(k).wait_send()


class Mail:
    def __init__(self, place, buf, sem):
        self.p, self.buf, self.sem, self.depth = place, buf, sem, buf.shape[0]

    def copy(self, slot, dst, recv):
        return remote(self.buf.at[slot], dst, self.sem.at[slot], recv, self.p.c_id)

    def post(self, i, parts, dst, recv):
        slot = lax.rem(i, self.depth)

        @pl.when(i >= self.depth)
        def _():
            self.copy(slot, dst, recv).wait_send()

        for k, part in enumerate(parts):
            self.buf[slot, k] = part
        self.copy(slot, dst, recv).start()

    def finish(self):
        for slot in range(self.depth):
            self.copy(slot, self.buf.at[slot], self.sem.at[slot]).wait_send()


def column_pair(ref, q, c):
    return jnp.concatenate([ref[:, cols(q * 4 + c, 128)], ref[:, cols(q * 4 + 2 + c, 128)]], axis=1)


ACTS = ("sv", "wqkv", "wout", "w1", "w2", "XS", "CS", "LN1", "Q", "OUT", "F", "D", "END", "K1")
KINDS = ("", "O", "A", "S", "L")
SEQUENCE = (
    210, 110, 130, 10, 221, 410, 121, 310, 430, 222, 230, 21, 223, 30, 131, 330, 122, 22, 23, 231, 123, 500,
    132, 31, 32, 33, 140, 321, 232, 421, 240, 331, 133, 40, 41, 141, 322, 42, 43, 241, 233, 700, 323, 242,
    142, 800, 440, 431, 801, 143, 422, 332, 340, 341, 802, 243, 333, 803, 423, 432, 600, 900, 1000, 342, 433,
    343, 1001, 1002, 441, 442, 1003, 1300, 1100, 443, 1101, 1102, 1103, 1200,
)


def cut(raw, pieces):
    for i in range(4):
        pieces[i, 576:ROWS, :] = jnp.zeros((ROWS - 576, 256), BF16)
        for r in (*range(0, 576, CHUNK), 576):
            n = min(CHUNK, SEQ - r)
            pieces[i, r : r + n, :] = raw[SEQ * i + r : SEQ * i + r + n, :]


def spread_kernel(slot_mask, x_raw, ct_raw, *rest):
    names, n, m = list(PARTS), len(PARTS), len(SAVED)
    small, (w_qkv, w_out, w_fc1, w_fc2), rest = rest[:8], rest[8:12], rest[12 - n :]
    x_h, ct_h, out_h, probs_h, vectors = rest[n : n + 5]
    rest = rest[n + 5 :]
    whole_h, saved_h = dict(zip(WEIGHTS, rest[:4])), dict(zip(SAVED, rest[4 : 4 + m]))
    rest = rest[4 + m :]
    x, ct, out, b1, mask, stack, raw, x_in, ct_in = rest[:9]
    whole = dict(zip(names, rest[9 : 9 + n]))
    rest = rest[9 + n :]
    local_sem, keep_sem = rest[0], rest[1]
    swap_sems, rest = rest[2:6], rest[6:]
    sems, refs = rest[: 6 * n], rest[6 * n :]
    p = Place()
    own = {a: block_of(a, whole[a], p.t, p.yx, p.c) for a in names}
    f = Forward(x, whole, vectors, b1, mask, out, out_h, probs_h, saved_h, refs)
    gathers = {a: Gather(p, a, own[a], whole[a], sems[6 * i : 6 * i + 6]) for i, a in enumerate(names)}
    swaps = dict(XS=Swap(p, x_in, x, swap_sems[0:2]), CS=Swap(p, ct_in, ct, swap_sems[2:4]))
    local = [
        pltpu.make_async_copy(x_in.at[p.t], x.at[p.t], local_sem.at[0]),
        pltpu.make_async_copy(ct_in.at[p.t], ct.at[p.t], local_sem.at[1]),
    ]
    raw_loads = [pltpu.make_async_copy(a, raw, local_sem.at[2 + i]) for i, a in enumerate((x_raw, ct_raw))]
    raw_loads[0].start()
    mask[...] = jnp.full((1, 256), slot_mask[p.t].astype(F32))
    for row, ref in enumerate((small[0], small[1], small[2].at[0], small[2].at[1], *small[3:7])):
        stack[row : row + 1, :] = ref[...]
    lane = lax.broadcasted_iota(jnp.int32, (32, 256), 1)
    row = lax.broadcasted_iota(jnp.int32, (32, 256), 0)
    place = jnp.where(lane == row + p.d * 32, 1.0, 0.0).astype(BF16)
    own["sv"][8:16, :] = jnp.zeros((8, 256), F32)
    own["sv"][0:8, :] = mm(stack[...].astype(BF16), place)
    own["sv"][8:9, 0:128] = small[7][...].astype(BF16).astype(F32)
    raw_loads[0].wait()
    cut(raw, x_in)
    raw_loads[1].start()
    local[0].start()
    p.greet()
    pending = []
    settled = []
    resid_stored = f.stores(("resid",))

    def keep(src, dst):
        c = pltpu.make_async_copy(src, dst, keep_sem.at[len(pending)])
        c.start()
        pending.append(c)

    def ready(name):
        if name == "wqkv":
            for i in range(3):
                own[name][:, i * 256 : i * 256 + 256] = w_qkv[i].astype(BF16)
        elif name != "sv":
            own[name][...] = dict(wout=w_out, w1=w_fc1, w2=w_fc2)[name][...].astype(BF16)

    def do(code, step):
        name, kind = ACTS[code // 100], KINDS[code // 10 % 10]
        if name in gathers:
            g = gathers[name]
            if kind == "O":
                ready(name)
                g.open()
            elif kind == "A":
                g.arrive(step)
            elif kind == "S":
                g.second(step)
            else:
                if not settled:
                    local[0].wait()
                    settled.append(True)
                g.last(step)
        elif name in swaps:
            if name == "CS":
                raw_loads[1].wait()
                cut(raw, ct_in)
                local[1].start()
            swaps[name].start()
        elif name == "LN1":
            for i in range(4):
                gathers["sv"].have(i)
            sv = whole["sv"]
            for t in range(4):
                vectors[t] = jnp.sum(sv[t, :, :, 0:8].reshape(8, 8, 256), axis=0)
                for d in range(8):
                    b1[t, :, d * 128 : d * 128 + 128] = sv[t, d // 2, d % 2, 8:9, 0:128]
            swaps["XS"].done()
            keep(x, x_h)
            f.start_norm()
        elif name == "Q":
            gathers["wqkv"].have(step)
            f.heads(p.order(step), step)
        elif name == "OUT":
            for i in range(4):
                gathers["wout"].have(i)
            keep(whole["wqkv"], whole_h["wqkv"])
            keep(whole["wout"], whole_h["wout"])
            f.middle()
            f.turn()
            for c in (*f.stores(("q", "k", "v", "ctx", "nin_t", "ctx_t", "nmid_t")), *resid_stored):
                c.start()
        elif name == "F":
            gathers["w1"].have(step)
            f.hidden(p.order(step))
        elif name == "K1":
            keep(whole["w1"], whole_h["w1"])
            for c in f.stores(("slope", "act")):
                c.start()
            for c in resid_stored:
                c.wait()
        elif name == "D":
            gathers["w2"].have(step)
            f.down(p.order(step))
        elif name == "END":
            keep(whole["w2"], whole_h["w2"])
            f.finish()
            f.store_out().start()
            swaps["CS"].done()
            local[1].wait()
            keep(ct, ct_h)
    for item in SEQUENCE:
        if isinstance(item, int):
            do(item, item % 10)
            continue

        @pl.loop(0, 4 + max(code % 10 for code in item))
        def _(m, item=item):
            for code in item:
                lag = code % 10

                @pl.when((m >= lag) & (m < lag + 4))
                def _():
                    do(code, m - lag)

    f.drain_last(p.order(3))
    for c in [*pending, *f.stores([a for a in SAVED if a != "resid"]), f.store_out()]:
        c.wait()
    for s in swaps.values():
        s.finish()
    for g in gathers.values():
        g.finish()


def spread(slot_mask, x_raw, ct_raw, small, big):
    names, n, m = list(PARTS), len(PARTS), len(SAVED)
    outs = pl.pallas_call(
        spread_kernel,
        out_shape=[IMAGE, IMAGE, IMAGE, PROBS, jax.ShapeDtypeStruct((4, 8, 256), F32)]
        + [part(a) for a in WEIGHTS]
        + list(SAVED.values()),
        in_specs=[pl.BlockSpec(memory_space=pltpu.SMEM), ANY, ANY] + [VM] * (len(small) + len(big)),
        out_specs=[ANY] * 4 + [VM] + [ANY] * (4 + m),
        scratch_shapes=[scratch(IMAGE), scratch(IMAGE), scratch(IMAGE), pltpu.VMEM((4, 1, 1024), F32)]
        + [pltpu.VMEM((1, 256), F32), pltpu.VMEM((8, 32), F32), scratch(x_raw), scratch(IMAGE), scratch(IMAGE)]
        + [scratch(part(a)) for a in names]
        + [pltpu.SemaphoreType.DMA((4,)), pltpu.SemaphoreType.DMA((7,))]
        + Swap.SEMS * 2
        + Gather.SEMS * n
        + Forward.SCRATCH,
        compiler_params=pltpu.CompilerParams(
            collective_id=0, has_side_effects=True, vmem_limit_bytes=VMEM_BYTES
        ),
        name="spread",
    )(slot_mask, x_raw, ct_raw, *small, *big)
    return outs[:5], dict(zip(WEIGHTS, outs[5:9])), dict(zip(SAVED, outs[9:]))


REDUCED = ("w2", "w1", "wout", "wqkv")


def turn_of(i):
    return (1 - i // 2) * (1 - i % 2) * 3 + i // 2 * (2 - i % 2)


class Reduce:
    def __init__(self, place, name, refs):
        self.p, self.name = place, name
        self.own, self.got1, self.got2, self.got3 = refs[:4]
        self.c_recv, self.send, self.recv, self.z_send, self.z_recv = refs[4:]

    @staticmethod
    def scratch(name):
        rows, width = PARTS[name][0][3:]
        return [
            pltpu.VMEM((4, 4, rows, width), BF16),
            pltpu.VMEM((4, 4, rows // 2, width), BF16),
            pltpu.VMEM((2, 4, rows // 2, width), BF16),
            pltpu.VMEM((5, rows, width), BF16),
            pltpu.SemaphoreType.DMA((4,)),
            pltpu.SemaphoreType.DMA((4, 6)),
            pltpu.SemaphoreType.DMA((4, 6)),
            pltpu.SemaphoreType.DMA((4,)),
            pltpu.SemaphoreType.DMA((5,)),
        ]

    def block(self, ref, t, yx):
        return ref.at[yx, t] if self.name in BY_COLUMN else ref.at[t, yx]

    def wait_bytes(self, ref, sem):
        remote(ref, ref, self.z_send.at[0], sem, self.p.c_id).wait_recv()

    def add(self, dst, *more):
        rows, width = dst.shape
        n = min(rows, 64 if width > 128 else 512)

        @pl.loop(0, rows // n)
        def _(i):
            r = pl.ds(pl.multiple_of(i * n, n), n)
            total = dst[r, :]
            for ref in more:
                total += ref[r, :]
            dst[r, :] = total

    def first_copy(self, by_y, j, t):
        p = self.p
        yx = (1 - p.y) * 2 + j if by_y else j * 2 + 1 - p.x
        src = half_of(self.block(self.own, t, yx), 0 if by_y else 1)
        k = (0 if by_y else 2) + j
        return remote(src, self.got1.at[k, t], self.send.at[t, k], self.recv.at[t, k], p.y_id if by_y else p.x_id)

    def second_copy(self, j, t):
        p = self.p
        by_x = j == 0
        src = half_of(self.block(self.own, t, p.x_yx if by_x else p.y_yx), j)
        return remote(src, self.got2.at[j, t], self.send.at[t, 4 + j], self.recv.at[t, 4 + j],
                      p.x_id if by_x else p.y_id)

    def other_core(self, t=None):
        ref = self.own if t is None else self.own.at[:, t] if self.name in BY_COLUMN else self.own.at[t]
        self.wait_bytes(ref, self.c_recv.at[0 if t is None else t])

    def begin(self, t):
        p = self.p
        self.first_copy(True, 1 - p.x, t).start()
        self.first_copy(False, 1 - p.y, t).start()
        self.first_copy(True, p.x, t).start()
        self.first_copy(False, p.y, t).start()

    def cross(self, i):
        p, t = self.p, turn_of(i)
        for j in range(2):
            self.first_copy(True, j, t).wait_recv()
            self.first_copy(False, j, t).wait_recv()
        self.add(half_of(self.block(self.own, t, p.x_yx), 0), self.got1.at[1 - p.x, t])
        self.second_copy(0, t).start()
        self.add(half_of(self.block(self.own, t, p.y_yx), 1), self.got1.at[2 + 1 - p.y, t])
        self.second_copy(1, t).start()
        self.add(half_of(self.block(self.own, t, p.yx), 0), self.got1.at[p.x, t])
        self.add(half_of(self.block(self.own, t, p.yx), 1), self.got1.at[2 + p.y, t])

    def along(self, i):
        p, t = self.p, turn_of(i)
        mine = self.block(self.own, t, p.yx)
        for j in (0, 1):
            self.second_copy(j, t).wait_recv()
            self.add(half_of(mine, j), self.got2.at[j, t])
        for up, ends in ((True, (p.t == 0) & (t > 0)), (False, (p.t == 3) & (t < 3))):

            @pl.when(ends)
            def _():
                self.send_z(t, up).start()

    def pass_on(self, i, hop):
        p, t = self.p, turn_of(i)
        mine = self.block(self.own, t, p.yx)
        for up, here in ((True, (p.t == hop) & (t > hop)), (False, (p.t == 3 - hop) & (t < 3 - hop))):

            @pl.when(here)
            def _():
                self.wait_bytes(self.got3.at[t], self.z_recv.at[t])
                self.add(mine, self.got3.at[t])
                self.send_z(t, up).start()

    def send_z(self, t, up):
        p = self.p
        slot = t if up else t + (4 - t) * ((3 + t - p.t) // 2)
        return remote(self.block(self.own, t, p.yx), self.got3.at[slot], self.z_send.at[t], self.z_recv.at[slot],
                      p.z_id(p.t + 1 if up else p.t - 1))

    def end(self, result):
        p = self.p
        mine = self.block(self.own, p.t, p.yx)
        rows, width = mine.shape
        n = min(rows, 32 if width > 128 else 256)

        pieces = [(result, slice(None))]
        if self.name == "wqkv":
            pieces = [(result.at[i], slice(i * 256, i * 256 + 256)) for i in range(3)]

        def through(ref):
            @pl.loop(0, rows // n)
            def _(i):
                r = pl.ds(pl.multiple_of(i * n, n), n)
                for to, lanes in pieces:
                    more = ref[r, lanes].astype(F32)
                    to[r, :] = more if ref is mine else to[r, :] + more

        through(mine)
        for slot, there in ((p.t, p.t > 0), (4, p.t < 3)):

            @pl.when(there)
            def _():
                self.wait_bytes(self.got3.at[slot], self.z_recv.at[slot])
                through(self.got3.at[slot])

    def finish(self):
        p = self.p
        for t in range(4):
            for j in range(2):
                self.first_copy(True, j, t).wait_send()
                self.first_copy(False, j, t).wait_send()
                self.second_copy(j, t).wait_send()

            @pl.when(p.t != t)
            def _():
                block = self.block(self.own, t, p.yx)
                remote(block, block, self.z_send.at[t], self.z_recv.at[t], p.c_id).wait_send()


class Total:
    SCRATCH = [
        pltpu.VMEM((4, 16, D), F32),
        pltpu.VMEM((6, 16, D), F32),
        pltpu.SemaphoreType.DMA((6,)),
        pltpu.SemaphoreType.DMA((6,)),
    ]

    def __init__(self, place, acc, refs):
        self.p, self.acc = place, acc
        self.sent, self.got, self.send, self.recv = refs

    def copies(self, i):
        p = self.p
        if i < 3:
            return [remote(self.sent.at[i], self.got.at[i], self.send.at[i], self.recv.at[i], (p.c_id, p.x_id, p.y_id)[i])]
        return [
            remote(self.sent.at[3], self.got.at[2 + k], self.send.at[2 + k], self.recv.at[2 + k], p.z_id(lax.rem(p.t + k, 4)))
            for k in (1, 2, 3)
        ]

    def start(self, i):
        self.sent[i] = self.acc[...]
        for c in self.copies(i):
            c.start()

    def end(self, i):
        for c in self.copies(i):
            c.wait()
        for k in (i,) if i < 3 else (3, 4, 5):
            self.acc[...] += self.got[k]


class Stream:
    def __init__(self, n, src, buf, sem):
        self.n, self.src, self.buf, self.sem = n, src, buf, sem
        self.depth = buf.shape[0]

    def copies(self, i):
        slot = lax.rem(i, self.depth)
        return [
            pltpu.make_async_copy(a, b, self.sem.at[slot, k])
            for k, (a, b) in enumerate(self.src(i, self.buf.at[slot]))
        ]

    def start(self):
        for i in range(min(self.depth - 1, self.n)):
            for c in self.copies(jnp.int32(i)):
                c.start()

    def next(self, i):
        for c in self.copies(i):
            c.wait()

        @pl.when(i + self.depth - 1 < self.n)
        def _():
            for c in self.copies(i + self.depth - 1):
                c.start()

        return self.buf.at[lax.rem(i, self.depth)]


def accumulate(ref, here, value, step):
    @pl.when(step == 0)
    def _():
        ref[:, here] = value

    @pl.when(step > 0)
    def _():
        ref[:, here] += value


BACK = ("w2", "w1", "wout", "wqkv", "T", "G0", "GS", "GM", "SHARE", "HG", "HS", "HM", "GN", "GR", "OA", "OM", "AT", "AM", "GI", "GT")
STEPS = ("", "X", "Z", "E", "Y", "W")
COLLECT = (
    500, (600, 701,), (900,), 1200, 800, 1300, 1400, 10, 13, 11, 12, 1500, (1600, 1701, 20,), 311, 1800, 211,
    312, 40, 43, 53, 42, 41, 210, 1900, 213, 313, 310, (1000, 1101,), 212, 220, 51, 110, 223, 323, 50, 111,
    322, 321, 343, 112, 342, 52, 320, 352, 113, 400, 221, 241, 341, 120, 222, 243, 240, 353, 250, 340, 350,
    121, 253, 122, 140, 351, 251, 242, 123, 30, 141, 142, 401, 151, 252, 152, 330, 402, 150, 143, 230, 153,
    403, 130,
)


class Backward:
    NAMES = (
        ("image", "gmlp", "slope", "gmix", "gn", "resid", "split", "ctx_t", "b1", "part_sums", "load_sem")
        + ("col_buf", "col_sem", "row_buf", "row_sem", "head_buf", "head_sem", "probs", "probs_sem")
        + ("up_mail", "up_mail_sem", "mix_mail", "mix_mail_sem", "out_mail", "out_mail_sem", "down_mail", "down_mail_sem")
    )
    SCRATCH = [
        scratch(IMAGE),
        scratch(ACT),
        pltpu.VMEM((ROWS, 4 * D), BF16),
        pltpu.VMEM((ROWS, 3 * D), BF16),
        pltpu.VMEM((ROWS, D), F32),
        pltpu.VMEM((ROWS, D), F32),
        pltpu.VMEM((2, 4, 128, ROWS), BF16),
        pltpu.VMEM((4, 2, 128, ROWS), BF16),
        pltpu.VMEM((4, 1, 1024), F32),
        pltpu.VMEM((6, 8, D), F32),
        pltpu.SemaphoreType.DMA((12,)),
        pltpu.VMEM((3, 4, 2, 2, 256, 128), BF16),
        pltpu.SemaphoreType.DMA((3, 2)),
        pltpu.VMEM((3, 2, 2, 128, 1024), BF16),
        pltpu.SemaphoreType.DMA((3, 1)),
        pltpu.VMEM((3, 4, ROWS, 128), BF16),
        pltpu.SemaphoreType.DMA((3, 4)),
        pltpu.VMEM((2, 2, ROWS, ROWS), BF16),
        pltpu.SemaphoreType.DMA((2, 1)),
        pltpu.VMEM((2, 4, 128, 512), BF16),
        pltpu.SemaphoreType.DMA((2,)),
        pltpu.VMEM((2, 4, 128, 768), BF16),
        pltpu.SemaphoreType.DMA((2,)),
        pltpu.VMEM((2, 2, 4, 256, 128), BF16),
        pltpu.SemaphoreType.DMA((2,)),
        pltpu.VMEM((1, 4, 1024, 128), BF16),
        pltpu.SemaphoreType.DMA((1,)),
    ]

    def __init__(self, p, reduces, swaps_of, total, hbm, vectors, sums, refs):
        for a, b in zip(self.NAMES, refs):
            setattr(self, a, b)
        self.p, self.reduces, self.total, self.vectors, self.sums = p, reduces, total, vectors, sums
        self.hbm = hbm
        self.out_swap, self.tok_swap = swaps_of(self.image)
        self.ups_mail = Mail(p, self.up_mail, self.up_mail_sem)
        self.mixes_mail = Mail(p, self.mix_mail, self.mix_mail_sem)
        self.downs_mail = Mail(p, self.down_mail, self.down_mail_sem)
        self.outs_mail = Mail(p, self.out_mail, self.out_mail_sem)
        h = hbm
        self.out_buf = self.probs.at[0, 0, :, pl.ds(0, 256)]
        self.loads = {
            a: self.load(i, *b)
            for i, (a, b) in enumerate(
                dict(
                    ct=(h["ct"], self.image),
                    slope=(h["slope"], self.slope),
                    nin0=(h["nin_t"].at[:, p.c], self.split.at[0]),
                    nin1=(h["nin_t"].at[:, 1 - p.c], self.split.at[1]),
                    out=(h["out"].at[p.t], self.out_buf),
                    resid=(h["resid"], self.resid),
                    ctx_t=(h["ctx_t"], self.ctx_t),
                    x=(h["x"], self.image),
                ).items()
            )
        }
        self.nmid = [
            self.load(2, h["nmid_t"].at[:, p.c], self.split.at[0]),
            self.load(3, h["nmid_t"].at[:, 1 - p.c], self.split.at[1]),
        ]
        self.out_done = self.load(4, self.out_buf, h["out_o"].at[p.t])
        self.tok_done = self.load(0, self.image.at[p.t], h["gtok_o"].at[p.t])

        def down_src(i, b):
            return [
                (h["w2"].at[:, :, turn_of(i // 2), pl.ds(i % 2 * 512 + k * 256, 256)], b.at[:, :, k]) for k in range(2)
            ]

        def out_src(i, b):
            return [(h["wout"].at[:, :, i * 2 + k], b.at[:, :, k]) for k in range(2)]

        def head_src(i, b):
            at = cols(turn_of(i // 2) * 2 + i % 2, 128)
            return [(h[a].at[:, at], b.at[k]) for k, a in enumerate(("q", "k", "v", "ctx"))]

        self.downs = Stream(8, down_src, self.col_buf, self.col_sem)
        self.outs = Stream(2, out_src, self.col_buf, self.col_sem)
        self.ups = Stream(
            8, lambda i, b: [(h["w1"].at[i % 4, pl.ds(i // 4 * 2, 2)], b)], self.row_buf, self.row_sem
        )
        self.mixes = Stream(
            8,
            lambda i, b: [(h["wqkv"].at[i % 4, pl.ds(i // 4 * 2, 2)], b.at[:, :, :, pl.ds(0, 768)])],
            self.row_buf,
            self.row_sem,
        )
        self.heads = Stream(8, head_src, self.head_buf, self.head_sem)
        self.heads_p = Stream(
            8, lambda i, b: [(h["probs"].at[turn_of(i // 2) * 2 + i % 2], b)], self.probs, self.probs_sem
        )

    def load(self, i, src, dst):
        return pltpu.make_async_copy(src, dst, self.load_sem.at[i])

    def act_load(self, i):
        return self.load(8 + i, self.hbm["act"].at[:, cols(turn_of(i), 1024)], self.gmix.at[:, cols(i % 3, 1024)])

    def begin(self):
        self.loads["ct"].start()
        for i in range(3):
            self.act_load(i).start()
        self.loads["slope"].start()
        self.downs.start()
        self.ups.start()
        for a in ("out", "resid", "ctx_t", "nin0", "nin1"):
            self.loads[a].start()
        self.heads.start()
        self.part_sums[...] = jnp.zeros_like(self.part_sums)
        self.sums[...] = jnp.zeros_like(self.sums)

    def mask_cotangent(self):
        self.loads["ct"].wait()
        mask = self.hbm["mask"]

        @over_rows
        def _(rows):
            g = wide(self.image, rows) * jnp.concatenate([mask[...]] * 4, axis=1)
            self.gmlp[rows, :] = g.astype(BF16)
            self.part_sums[0] += fold(g)

        self.loads["out"].wait()
        self.out_done.start()

    def four_columns(self, c):
        return jnp.concatenate([self.gmlp[:, cols(yx * 2 + c, 128)] for yx in range(4)], axis=1)

    def down_share(self, i):
        r, t = self.reduces["w2"], turn_of(i)
        self.act_load(i).wait()
        g = t_mm(self.gmix[:, cols(i % 3, 1024)], self.four_columns(1 - self.p.c)).astype(BF16)
        self.downs_mail.post(
            i, [g[:, k * 128 : k * 128 + 128] for k in range(4)], r.own.at[:, t], r.c_recv.at[t]
        )

    def down_own(self, i):
        r, t = self.reduces["w2"], turn_of(i)
        r.other_core(t)
        g = t_mm(self.gmix[:, cols(i % 3, 1024)], self.four_columns(self.p.c))
        for k in range(4):
            r.own[k, t] = (g[:, k * 128 : k * 128 + 128] + r.own[k, t].astype(F32)).astype(BF16)
        r.begin(t)

        @pl.when(i == 0)
        def _():
            self.act_load(3).start()

    def share(self):
        self.out_swap.start()

    def whole_rows(self, tile):
        return jnp.concatenate([tile[d // 2, d % 2].reshape(512, 128) for d in range(8)], axis=1)

    def post_rows(self, mail, n, g, r, t, here):
        g = g.astype(BF16).reshape(4, 128, -1)
        mail.post(n, [g[k] for k in range(4)], r.own.at[t, :, :, here], r.c_recv.at[t])

    def hidden(self, i):
        t = turn_of(i)

        @pl.when(i == 0)
        def _():
            self.loads["slope"].wait()

        @pl.loop(0, 2)
        def _(j):
            w = self.whole_rows(self.downs.next(2 * i + j))
            here = cols(t * 2 + j, 512)
            gpre = mm_t(self.gmlp[...], w) * self.slope[:, here].astype(F32)
            self.slope[:, here] = gpre.astype(BF16)
            self.b1[t, :, cols(j, 512)] = jnp.sum(gpre, axis=0, keepdims=True)

    def hidden_share(self, i):
        r, t = self.reduces["w1"], turn_of(i)

        @pl.loop(0, 2)
        def _(j):
            g = mm(self.split[1].reshape(512, ROWS), self.slope[:, cols(t * 2 + j, 512)])
            self.post_rows(self.ups_mail, 2 * i + j, g, r, t, cols(j, 512))

    def add_own(self, r, t, here, value):
        width = value.shape[1]
        had = r.own[t, :, :, here].astype(F32)
        r.own[t, :, :, here] = (value.reshape(4, 128, width) + had).astype(BF16)

    def hidden_own(self, i):
        r, t = self.reduces["w1"], turn_of(i)
        r.other_core(t)

        @pl.loop(0, 2)
        def _(j):
            g = mm(self.split[0].reshape(512, ROWS), self.slope[:, cols(t * 2 + j, 512)])
            self.add_own(r, t, cols(j, 512), g)

        r.begin(t)

    def through_up(self):
        self.outs.start()

        @pl.loop(0, 8)
        def _(i):
            w = self.ups.next(i)
            g = mm_t(self.slope[:, cols(i % 4, 1024)], w[...].reshape(512, D))
            accumulate(self.gn, cols(i // 4, 512), g, i % 4)

        self.mixes.start()

    def norm_mid(self):
        self.loads["resid"].wait()
        gain = vec(self.vectors, 5)

        @over_rows
        def _(rows):
            normed = self.gn[rows, :]
            g, scaled = grad_norm_rows(self.resid[rows, :], gain, normed)
            g = g + self.gmlp[rows, :].astype(F32)
            self.part_sums[1] += fold(normed)
            self.part_sums[2] += fold(scaled)
            self.part_sums[3] += fold(g)
            self.gn[rows, :] = g
            self.gmlp[rows, :] = g.astype(BF16)

    def attn_out(self):
        r, p = self.reduces["wout"], self.p
        self.loads["ctx_t"].wait()
        self.out_done.wait()
        self.heads_p.start()

        @pl.loop(0, 2)
        def _(q):
            g = mm(self.ctx_t[...].reshape(D, ROWS), column_pair(self.gmlp, q, 1 - p.c)).astype(BF16)
            self.outs_mail.post(
                q,
                [g[:, k * 128 : k * 128 + 128].reshape(4, 256, 128) for k in range(2)],
                r.own.at[pl.ds(q * 2, 2)],
                r.c_recv.at[0],
            )

        @pl.loop(0, 2)
        def _(i):
            g = mm_t(self.gmlp[...], self.whole_rows(self.outs.next(i))).astype(BF16)
            for k in range(2):
                self.image[i * 2 + k] = g[:, k * 256 : k * 256 + 256]

    def attn_out_own(self):
        r, p = self.reduces["wout"], self.p
        r.other_core()

        @pl.loop(0, 2)
        def _(q):
            g = mm(self.ctx_t[...].reshape(D, ROWS), column_pair(self.gmlp, q, p.c))
            for k in range(2):
                had = r.own[q * 2 + k].astype(F32)
                r.own[q * 2 + k] = (g[:, k * 128 : k * 128 + 128].reshape(4, 256, 128) + had).astype(BF16)

        for i in range(4):
            r.begin(turn_of(i))
        for a in ("nin0", "nin1"):
            self.loads[a].wait()

    def attend(self, i):
        r, t = self.reduces["wqkv"], turn_of(i)

        @pl.loop(0, 2)
        def _(h):
            ins = self.heads.next(2 * i + h)
            probs = self.heads_p.next(2 * i + h)
            got = attend_back_pair(*(ins[k] for k in range(4)), self.image[t, :, cols(h, 128)], probs)
            for c in range(3):
                self.gmix[:, pl.ds(pl.multiple_of(t * 768 + c * 256 + h * 128, 128), 128)] = got[c].astype(BF16)
            here = cols(t * 2 + h, 128)
            self.sums[2:3, here] = jnp.sum(got[0], axis=0, keepdims=True)
            self.sums[3:4, here] = jnp.sum(got[2], axis=0, keepdims=True)

        g = mm(self.split[1].reshape(512, ROWS), self.gmix[:, cols(t, 768)])
        self.post_rows(self.mixes_mail, i, g, r, t, pl.ds(0, 768))

    def attend_own(self, i):
        r, t = self.reduces["wqkv"], turn_of(i)
        r.other_core(t)
        self.add_own(r, t, slice(None), mm(self.split[0].reshape(512, ROWS), self.gmix[:, cols(t, 768)]))
        r.begin(t)

    def through_mix(self):
        self.loads["x"].start()
        for c in self.nmid:
            c.start()

        @pl.loop(0, 8)
        def _(i):
            w = self.mixes.next(i)
            g = mm_t(self.gmix[:, cols(i % 4, 768)], w[:, :, :, 0:768].reshape(512, 768))
            accumulate(self.resid, cols(i // 4, 512), g, i % 4)

    def norm_in(self):
        self.loads["x"].wait()
        gain = vec(self.vectors, 0)

        @over_rows
        def _(rows):
            normed = self.resid[rows, :]
            g, scaled = grad_norm_rows(wide(self.image, rows), gain, normed)
            g = g + self.gn[rows, :]
            self.part_sums[4] += fold(normed)
            self.part_sums[5] += fold(scaled)
            for t in range(4):
                self.image[t, rows, :] = g[:, t * 256 : t * 256 + 256].astype(BF16)

        self.tok_swap.start()
        self.tok_done.start()
        sums = self.sums
        for row, i in ((7, 0), (6, 1), (5, 2), (4, 3), (1, 4), (0, 5)):
            sums[row : row + 1, :] = jnp.sum(self.part_sums[i], axis=0, keepdims=True)
        for t in range(4):
            sums[8 + t : 9 + t, :] = self.b1[t]
        self.total.start(0)
        for c in self.nmid:
            c.wait()

    def finish(self):
        self.tok_done.wait()
        for m in (self.ups_mail, self.mixes_mail, self.outs_mail, self.downs_mail):
            m.finish()
        for s in (self.out_swap, self.tok_swap):
            s.done()
            s.finish()
        for r in self.reduces.values():
            r.finish()


HBM = ("x", "out", "ct", "probs") + WEIGHTS


def collect_kernel(slot_mask, vectors, *rest):
    names = HBM + tuple(SAVED)
    n = len(names)
    hbm = dict(zip(names, rest[:n]))
    out_o, gtok_o = rest[n : n + 2]
    hbm |= dict(out_o=out_o, gtok_o=gtok_o)
    results = dict(zip(REDUCED, rest[n + 2 : n + 6]))
    small, rest = rest[n + 6 : n + 14], rest[n + 14 :]
    mask, sums, rest = rest[0], rest[1], rest[2:]
    mask[...] = jnp.full((1, 256), slot_mask[lax.axis_index("tensor")].astype(F32))
    hbm["mask"] = mask
    m = len(Backward.SCRATCH)
    refs, rest = rest[:m], rest[m:]
    out_sems, tok_sems, total_refs, rest = rest[0:2], rest[2:4], rest[4:8], rest[8:]
    p = Place()
    reduces = {a: Reduce(p, a, rest[9 * i : 9 * i + 9]) for i, a in enumerate(REDUCED)}
    total = Total(p, sums, total_refs)

    def swaps_of(image):
        return Swap(p, hbm["out"], out_o, out_sems), Swap(p, image, gtok_o, tok_sems)

    b = Backward(p, reduces, swaps_of, total, hbm, vectors, sums, refs)
    acts = dict(
        G0=b.mask_cotangent, GS=b.down_share, GM=b.down_own, SHARE=b.share, HG=b.hidden, HS=b.hidden_share, HM=b.hidden_own, GN=b.through_up, GR=b.norm_mid, OA=b.attn_out,
        OM=b.attn_out_own, AT=b.attend, AM=b.attend_own, GI=b.through_mix, GT=b.norm_in,
    )
    counted = ("GS", "GM", "HG", "HS", "HM", "AT", "AM")

    def act(code, i):
        name, kind = BACK[code // 100], STEPS[code // 10 % 10]
        if name in reduces:
            r = reduces[name]
            if kind == "E":
                r.end(results[name])
            elif kind in ("Y", "W"):
                r.pass_on(i, 1 if kind == "Y" else 2)
            else:
                (r.cross if kind == "X" else r.along)(i)
        elif name == "T":
            total.end(i)
            if i < 3:
                total.start(i + 1)
        elif name in counted:
            acts[name](i)
        else:
            acts[name]()

    b.begin()
    p.greet()
    for step in COLLECT:
        if isinstance(step, int):
            act(step, step % 10)
            continue

        @pl.loop(0, 4 + max(code % 10 for code in step))
        def _(m, step=step):
            for code in step:
                lag = code % 10

                @pl.when((m >= lag) & (m < lag + 4))
                def _():
                    act(code, m - lag)

    here = pl.ds(pl.multiple_of(p.t * 256 + p.d // 4 * 128, 128), 128)
    four = sums[0:8, here]
    mine = sum(jnp.where(p.d % 4 == k, four[:, k * 32 : k * 32 + 32], 0.0) for k in range(4))
    for i, row in enumerate((0, 1, None, 4, 5, 6, 7)):
        if row is None:
            small[i][...] = mine[2:4]
        else:
            small[i][...] = mine[row : row + 1]
    hidden = sums[8:12, pl.ds(pl.multiple_of(p.d * 128, 128), 128)]
    small[7][...] = sum(jnp.where(p.t == k, hidden[k : k + 1], 0.0) for k in range(4))
    b.finish()


def collect(slot_mask, vectors, hbm):
    names = HBM + tuple(SAVED)
    outs = pl.pallas_call(
        collect_kernel,
        out_shape=[IMAGE, IMAGE]
        + [jax.ShapeDtypeStruct((3, 128, 256) if a == "wqkv" else PARTS[a][0][3:], F32) for a in REDUCED]
        + [jax.ShapeDtypeStruct((2 if i == 2 else 1, 128 if i == 7 else 32), F32) for i in range(8)],
        in_specs=[pl.BlockSpec(memory_space=pltpu.SMEM), VM] + [ANY] * len(names),
        out_specs=[ANY, ANY] + [VM] * 12,
        scratch_shapes=[pltpu.VMEM((1, 256), F32), pltpu.VMEM((16, D), F32)]
        + Backward.SCRATCH
        + Swap.SEMS * 2
        + Total.SCRATCH
        + sum((Reduce.scratch(a) for a in REDUCED), []),
        compiler_params=pltpu.CompilerParams(
            collective_id=1, has_side_effects=True, vmem_limit_bytes=VMEM_BYTES
        ),
        name="collect",
    )(slot_mask, vectors, *[hbm[a] for a in names])
    return outs[0], outs[1], dict(zip(REDUCED, outs[2:6])), outs[6:]


def gather_plain(w_qkv, w_out, w_fc1, w_fc2):
    def all_of(shard, axis):
        return lax.all_gather(
            lax.all_gather(shard.astype(BF16), "dp", axis=axis, tiled=True), "tensor", axis=0
        )

    wqkv = all_of(w_qkv.reshape(-1, 768), 0)
    wout = all_of(w_out, 1).reshape(D, 8, 128).transpose(1, 0, 2)
    w1 = all_of(w_fc1, 0)
    w2 = all_of(w_fc2, 1).reshape(4 * D, 8, 128).transpose(1, 0, 2)
    return wqkv, wout, w1, w2


def scatter_plain(grads):
    def mine(grad, axis):
        part = lax.psum_scatter(grad, "tensor", scatter_dimension=0, tiled=True)
        return lax.psum_scatter(part, "dp", scatter_dimension=axis, tiled=True).astype(F32)

    g_qkv = mine(grads["wqkv"], 1)[0]
    g_out = mine(grads["wout"].transpose(1, 0, 2).reshape(D, D), 1)
    g_fc1 = mine(grads["w1"], 1)[0]
    g_fc2 = mine(grads["w2"].transpose(1, 0, 2).reshape(4 * D, D), 1)
    return g_qkv, g_out, g_fc1, g_fc2


def on_device(
    dp,
    tokens_in,
    cotangent,
    slot_mask,
    norm1_gain,
    norm1_bias,
    w_qkv,
    b_qkv,
    w_out,
    b_out,
    norm2_gain,
    norm2_bias,
    w_fc1,
    b_fc1,
    w_fc2,
    b_fc2,
):
    def images(rows):
        return jnp.pad(rows.reshape(4, SEQ, 256), ((0, 0), (0, ROWS - SEQ), (0, 0)))

    def exchange(pieces):
        return lax.all_to_all(pieces, "tensor", split_axis=0, concat_axis=0, tiled=True)

    if dp == 8:
        small = (norm1_gain, norm1_bias, b_qkv, b_out, norm2_gain, norm2_bias, b_fc2, b_fc1)
        big = (w_qkv.transpose(1, 0, 2), w_out, w_fc1, w_fc2)
        first, weights, saved = spread(slot_mask, tokens_in, cotangent, small, big)
        x, ct, out, probs, vectors = first
        hbm = dict(x=x, out=out, ct=ct, probs=probs, **weights, **saved)
        out, gtok, got, g_small = collect(slot_mask, vectors, hbm)
    else:
        mask = jnp.broadcast_to(
            lax.dynamic_index_in_dim(slot_mask, lax.axis_index("tensor"), 0).astype(F32), (1, 256)
        )
        small = jnp.concatenate(
            (norm1_gain, norm1_bias, b_qkv[0], b_qkv[1], b_out, norm2_gain, norm2_bias, b_fc2)
        ).astype(BF16)
        vectors = lax.all_gather(
            lax.all_gather(small, "dp", axis=1, tiled=True), "tensor", axis=0
        ).astype(F32)
        hidden_bias = lax.all_gather(
            lax.all_gather(b_fc1.astype(BF16), "dp", axis=1, tiled=True), "tensor", axis=0
        ).astype(F32)
        x = exchange(images(tokens_in))
        ct = exchange(images(cotangent))
        plain = gather_plain(w_qkv, w_out, w_fc1, w_fc2)
        weights = {a: b.reshape(PARTS[a][0]) for a, b in zip(WEIGHTS, plain)}
        out, probs, saved = forward(x, weights, vectors, hidden_bias, mask)
    if dp == 8:
        g_qkv, g_out, g_fc1, g_fc2 = (got[a] for a in GRADS)
        g_qkv = g_qkv.transpose(1, 0, 2)
    else:
        flat = [weights[a].reshape(GRADS[a].shape) for a in GRADS]
        gtok, sums, grads = backward(x, ct, *flat, vectors, mask, probs, saved)
        g_qkv, g_out, g_fc1, g_fc2 = scatter_plain(grads)
        out, gtok = exchange(out), exchange(gtok)

        def total(part, axis):
            part = lax.psum_scatter(part, "tensor", scatter_dimension=0, tiled=True)
            return lax.psum_scatter(part, "dp", scatter_dimension=axis, tiled=True)

        s = total(sums[0:8].reshape(8, 4, 256).transpose(1, 0, 2), 2)[0]
        g_small = (s[0:1], s[1:2], s[2:4], s[4:5], s[5:6], s[6:7], s[7:8], total(sums[8:12], 1))

    def rows(pieces):
        return pieces[:, :SEQ].reshape(4 * SEQ, 256)

    return (
        rows(out),
        rows(gtok),
        g_small[0],
        g_small[1],
        g_qkv.reshape(w_qkv.shape),
        g_small[2][:, None],
        g_out,
        g_small[3],
        g_small[4],
        g_small[5],
        g_fc1,
        g_small[7],
        g_fc2,
        g_small[6],
    )


def solution(mesh):
    both, turned = P("dp", "tensor"), P("tensor", "dp")
    mixed, pair = P("dp", None, "tensor"), P(None, "tensor", "dp")
    params = (turned, turned, mixed, pair, turned, turned, turned, turned, both, turned, turned, turned)
    return jax.shard_map(
        functools.partial(on_device, mesh.shape["dp"]),
        mesh=mesh,
        in_specs=(both, both, P("dp"), *params),
        out_specs=(both, both, *params),
        check_vma=False,
    )
```

```python
import functools
import jax
import jax.numpy as jnp
from jax import lax
from jax.experimental import pallas as pl
from jax.experimental.pallas import tpu as pltpu
from jax.sharding import PartitionSpec as P

D = 1024
HD = 64
SEQ = 577
ROWS = 592
CHUNK = 96
F32 = jnp.float32
BF16 = jnp.bfloat16
LAST = (((1,), (1,)), ((), ()))
VMEM_BYTES = 67_043_328


def mm(a, b):
    return jnp.dot(a, b, preferred_element_type=F32)


def t_mm(a, b):
    return lax.dot_general(a, b, (((0,), (0,)), ((), ())), preferred_element_type=F32)


def mm_t(a, b):
    return lax.dot_general(a, b, LAST, preferred_element_type=F32)


def cols(i, n):
    return pl.ds(pl.multiple_of(i * n, n), n)


def row_stats(values):
    mean = jnp.sum(values, axis=1, keepdims=True) * (1.0 / D)
    centered = values - mean
    var = jnp.sum(centered * centered, axis=1, keepdims=True) * (1.0 / D)
    inv = lax.rsqrt(var + 1e-05)
    return centered * inv, inv


def wide(ref, rows):
    return jnp.concatenate([ref[t, rows, :].astype(F32) for t in range(4)], axis=1)


def over_rows(do):
    @pl.loop(0, 576 // CHUNK)
    def _(i):
        do(pl.ds(pl.multiple_of(i * CHUNK, CHUNK), CHUNK))

    do(pl.ds(576, ROWS - 576))


def vec(vectors, row):
    return jnp.concatenate([vectors[t, row : row + 1, :] for t in range(4)], axis=1)


def norm_in(x, vectors, nin):
    gain, shift = vec(vectors, 0), vec(vectors, 1)

    @over_rows
    def _(rows):
        xhat, _ = row_stats(wide(x, rows))
        nin[rows, :] = (xhat * gain + shift).astype(BF16)


def flip(src, dst, n):
    @pl.loop(0, n // 256)
    def _(i):
        dst[i] = src[:, cols(i, 256)].T.reshape(2, 128, ROWS)


def project(nin, wqkv, vectors, t, q, k, v):
    here = cols(t, 256)

    g = mm(nin[...], wqkv[t].reshape(D, 768))
    q[:, here] = (g[:, 0:256] + vectors[t, 2:3, :]).astype(BF16)
    k[:, here] = g[:, 256:512].astype(BF16)
    v[:, here] = (g[:, 512:768] + vectors[t, 3:4, :]).astype(BF16)


def head_lanes(h):
    lane = lax.broadcasted_iota(jnp.int32, (ROWS, 128), 1)
    own = (lane >= h * 64) & (lane < h * 64 + 64)
    return lane, own, 64 - h * 64


def attend_pair(pair, q, k, v, ctx, probs, slot):
    here = cols(pair, 128)
    lane = lax.broadcasted_iota(jnp.int32, (ROWS, 128), 1)
    row = lax.broadcasted_iota(jnp.int32, (ROWS, 128), 0)
    queries = q[:, here].astype(F32) * (HD**-0.5)
    keys = k[:, here].astype(F32)
    values = v[:, here]
    blocked = jnp.where(row >= SEQ, -1e30, 0.0)
    parts = []
    for h in range(2):
        own = (lane < 64) if h == 0 else (lane >= 64)
        spare = 64 if h == 0 else 0
        qa = jnp.where(own, queries, jnp.where(lane == spare, 1.0, 0.0)).astype(BF16)
        ka = jnp.where(lane == spare, blocked, keys).astype(BF16)
        scores = mm_t(ka, qa)
        top = jnp.max(scores, axis=0, keepdims=True)
        e = jnp.exp(scores - top)
        total = jnp.sum(e, axis=0, keepdims=True)
        p = (e * (1.0 / total)).astype(BF16)
        probs[slot, h] = p
        parts.append(
            lax.dot_general(p, values, (((0,), (0,)), ((), ())), preferred_element_type=F32)
        )
    ctx[:, here] = jnp.where(lane < 64, parts[0], parts[1]).astype(BF16)


def out_block(i, ctx, wout, x, vectors, resid):
    w = jnp.concatenate([wout[i, c].reshape(D, 128) for c in range(2)], axis=1)
    resid[:, cols(i, 256)] = x[i].astype(F32) + mm(ctx[...], w) + vectors[i, 4:5, :]


def norm_mid(resid, vectors, nmid):
    gain, shift = vec(vectors, 5), vec(vectors, 6)

    @over_rows
    def _(rows):
        xhat, _ = row_stats(resid[rows, :])
        nmid[rows, :] = (xhat * gain + shift).astype(BF16)


def hidden_tile(t, j, nmid, w1, b1, act, slope):
    here = pl.ds(pl.multiple_of(t * 1024 + j * 256, 256), 256)
    bias = b1[t, :, cols(j, 256)]
    pre = mm(nmid[...], w1[t, :, :, :, cols(j, 256)].reshape(D, 256)) + bias
    sig = 1.0 / (1.0 + jnp.exp(-1.702 * pre))
    a = pre * sig
    slope[:, here] = (sig + 1.702 * a * (1.0 - sig)).astype(BF16)
    act[:, here] = a.astype(BF16)


def down_block(i, t, act, w2, total):
    w = jnp.concatenate([w2[i, c, t] for c in range(2)], axis=1)
    total[:, cols(i, 256)] += mm(act[:, cols(t, 1024)], w)


def finish_block(i, total, vectors, mask, out):
    out[i] = ((total[:, cols(i, 256)] + vectors[i, 7:8, :]) * mask[...]).astype(BF16)


def grad_norm_rows(values, gain, n):
    xhat, inv = row_stats(values)
    e = n * gain
    first = jnp.sum(e, axis=1, keepdims=True) * (1.0 / D)
    second = jnp.sum(e * xhat, axis=1, keepdims=True) * (1.0 / D)
    return inv * (e - first - xhat * second), n * xhat


def fold(a):
    return jnp.sum(a.reshape(-1, 8, D), axis=0)


def attend_back_pair(queries, keys, values, out, go, probs):
    values_f, go_f = values.astype(F32), go.astype(F32)
    dots = go_f * out.astype(F32)
    dq, dk, dv = [], [], []
    for h in range(2):
        lane, own, spare = head_lanes(h)
        delta = -jnp.sum(jnp.where(own, dots, 0.0), axis=1, keepdims=True)
        high = delta.astype(BF16).astype(F32)
        ga = jnp.where(
            own, go_f, jnp.where(lane == spare, high, jnp.where(lane == spare + 1, delta - high, 0.0))
        ).astype(BF16)
        marks = jnp.where((lane == spare) | (lane == spare + 1), 1.0, 0.0)
        va = jnp.where(own, values_f, marks).astype(BF16)
        p = probs[h]
        gs = (p.astype(F32) * mm_t(va, ga)).astype(BF16)
        dv.append(mm(p, go))
        dk.append(mm(gs, queries))
        dq.append(
            lax.dot_general(gs, keys, (((0,), (0,)), ((), ())), preferred_element_type=F32)
        )
    low = head_lanes(0)[1]
    scale = HD**-0.5
    return (
        jnp.where(low, dq[0], dq[1]) * scale,
        jnp.where(low, dk[0], dk[1]) * scale,
        jnp.where(low, dv[0], dv[1]),
    )


ACT = jax.ShapeDtypeStruct((ROWS, D), BF16)
TURNED = jax.ShapeDtypeStruct((4, 2, 128, ROWS), BF16)
SAVED = dict(
    nin_t=TURNED,
    q=ACT,
    k=ACT,
    v=ACT,
    ctx=ACT,
    ctx_t=TURNED,
    nmid_t=TURNED,
    resid=jax.ShapeDtypeStruct((ROWS, D), F32),
    act=jax.ShapeDtypeStruct((ROWS, 4 * D), BF16),
    slope=jax.ShapeDtypeStruct((ROWS, 4 * D), BF16),
)
PROBS = jax.ShapeDtypeStruct((8, 2, ROWS, ROWS), BF16)
IMAGE = jax.ShapeDtypeStruct((4, ROWS, 256), BF16)
ANY = pl.BlockSpec(memory_space=pl.ANY)
VM = pl.BlockSpec(memory_space=pltpu.VMEM)


def scratch(like):
    return pltpu.VMEM(like.shape, like.dtype)


PARTS = dict(
    sv=((4, 4, 2, 16, 256), F32),
    wqkv=((4, 4, 2, 128, 768), BF16),
    wout=((4, 2, 4, 256, 128), BF16),
    w1=((4, 4, 2, 128, 1024), BF16),
    w2=((4, 2, 4, 1024, 128), BF16),
)
WEIGHTS = ("wqkv", "wout", "w1", "w2")


def part(name):
    return jax.ShapeDtypeStruct(*PARTS[name])


class Forward:
    SCRATCH = [scratch(a) for a in SAVED.values()] + [
        scratch(ACT),
        pltpu.VMEM((2, 2, ROWS, ROWS), BF16),
        pltpu.SemaphoreType.DMA((2,)),
        pltpu.SemaphoreType.DMA((len(SAVED) + 1,)),
    ]

    def __init__(self, x, weights, vectors, b1, mask, out, out_h, probs_h, saved_h, refs):
        n = len(SAVED)
        self.x, self.w, self.vectors, self.b1, self.mask = x, weights, vectors, b1, mask
        self.out, self.out_h, self.probs_h, self.saved_h = out, out_h, probs_h, saved_h
        self.saved = dict(zip(SAVED, refs[:n]))
        self.total = self.saved["resid"]
        self.normed, self.probs, self.probs_sem, self.out_sem = refs[n:]
        self.act = self.saved["act"]

    def start_norm(self):
        norm_in(self.x, self.vectors, self.normed)
        flip(self.normed, self.saved["nin_t"], D)

    def put(self, pair, slot):
        return pltpu.make_async_copy(self.probs.at[slot], self.probs_h.at[pair], self.probs_sem.at[slot])

    def heads(self, s, i):
        a = self.saved
        project(self.normed, self.w["wqkv"], self.vectors, s, a["q"], a["k"], a["v"])

        @pl.loop(0, 2)
        def _(slot):
            pair = s * 2 + slot
            if i:
                self.put(pair, slot).wait()
            attend_pair(pair, a["q"], a["k"], a["v"], a["ctx"], self.probs, slot)
            self.put(pair, slot).start()

    def middle(self):
        a = self.saved

        @pl.loop(0, 4)
        def _(i):
            out_block(i, a["ctx"], self.w["wout"], self.x, self.vectors, a["resid"])

        norm_mid(a["resid"], self.vectors, self.normed)

    def hidden(self, s):
        @pl.loop(0, 4)
        def _(j):
            hidden_tile(s, j, self.normed, self.w["w1"], self.b1, self.act, self.saved["slope"])

    def down(self, s):
        @pl.loop(0, 4)
        def _(i):
            down_block(i, s, self.act, self.w["w2"], self.total)

    def turn(self):
        flip(self.saved["ctx"], self.saved["ctx_t"], D)
        flip(self.normed, self.saved["nmid_t"], D)

    def finish(self):
        @pl.loop(0, 4)
        def _(i):
            finish_block(i, self.total, self.vectors, self.mask, self.out)

    def stores(self, names):
        at = list(SAVED)
        return [
            pltpu.make_async_copy(self.saved[a], self.saved_h[a], self.out_sem.at[at.index(a)]) for a in names
        ]

    def store_out(self):
        return pltpu.make_async_copy(self.out, self.out_h, self.out_sem.at[len(SAVED)])

    def drain_last(self, s):
        for slot in range(2):
            self.put(s * 2 + slot, slot).wait()

    def drain(self):
        for slot in range(2):
            self.put(6 + slot, slot).wait()


def forward_kernel(x_h, wqkv_h, wout_h, w1_h, w2_h, vectors, b1, mask, *rest):
    n = len(SAVED)
    saved_h = dict(zip(SAVED, rest[2 : 2 + n]))
    x, out, *weights, in_sem = rest[2 + n : 9 + n]
    loads = [
        pltpu.make_async_copy(a, b, in_sem.at[i])
        for i, (a, b) in enumerate(zip((x_h, wqkv_h, wout_h, w1_h, w2_h), (x, *weights)))
    ]
    for c in loads:
        c.start()
    for c in loads:
        c.wait()
    f = Forward(x, dict(zip(WEIGHTS, weights)), vectors, b1, mask, out, rest[0], rest[1], saved_h, rest[9 + n :])
    f.start_norm()
    for s in range(4):
        f.heads(s, s)
    f.middle()
    for c in f.stores(("resid",)):
        c.start()
        c.wait()
    for s in range(4):
        f.hidden(s)
        f.down(s)
    f.turn()
    f.finish()
    f.drain()
    stores = [*f.stores([a for a in SAVED if a != "resid"]), f.store_out()]
    for c in stores:
        c.start()
    for c in stores:
        c.wait()


def forward(x, weights, vectors, b1, mask):
    n = len(SAVED)
    outs = pl.pallas_call(
        forward_kernel,
        out_shape=[IMAGE, PROBS, *SAVED.values()],
        in_specs=[ANY] * 5 + [VM, VM, VM],
        out_specs=[ANY] * (2 + n),
        scratch_shapes=[scratch(IMAGE), scratch(IMAGE)]
        + [scratch(part(a)) for a in WEIGHTS]
        + [pltpu.SemaphoreType.DMA((5,))]
        + Forward.SCRATCH,
        compiler_params=pltpu.CompilerParams(vmem_limit_bytes=VMEM_BYTES),
        name="forward",
    )(x, *[weights[a] for a in WEIGHTS], vectors, b1, mask)
    return outs[0], outs[1], dict(zip(SAVED, outs[2:]))


GRADS = dict(
    wqkv=jax.ShapeDtypeStruct((4, 1024, 768), BF16),
    wout=jax.ShapeDtypeStruct((8, 1024, 128), BF16),
    w1=jax.ShapeDtypeStruct((4, 1024, 1024), BF16),
    w2=jax.ShapeDtypeStruct((8, 4096, 128), BF16),
)


def send_tile(stage, sem, i, value, targets):
    slot = lax.rem(i, 2)

    def copies(s):
        return [
            pltpu.make_async_copy(
                stage.at[s] if w == 256 else stage.at[s, :, pl.ds(c, w)], ref, sem.at[s]
            )
            for ref, c, w in targets
        ]

    @pl.when(i >= 2)
    def _():
        pltpu.make_async_copy(stage.at[slot], stage.at[slot], sem.at[slot]).wait()

    stage[slot] = value
    for c in copies(slot):
        c.start()


def drain(stage, sem):
    for slot in range(2):
        pltpu.make_async_copy(stage.at[slot], stage.at[slot], sem.at[slot]).wait()


def backward_kernel(x_h, ct_h, wqkv_h, wout_h, w1_h, w2_h, vectors, mask, probs_h, *rest):
    n = len(SAVED)
    saved_h = dict(zip(SAVED, rest[:n]))
    gtok_h, sums_o = rest[n], rest[n + 1]
    g_h = dict(zip(GRADS, rest[n + 2 : n + 6]))
    rest = rest[n + 6 :]
    saved = dict(zip(SAVED, rest[:n]))
    (x, wqkv, wout, w1, w2, b1, gmlp, gattn, gctx, gn, gmix, probs, sums, part, stage,
     in_sem, probs_sem, tile_sem, saved_sem) = rest[n:]
    gtok = x
    names = dict(ct=(ct_h, gtok), x=(x_h, x), w2=(w2_h, w2), w1=(w1_h, w1), wout=(wout_h, wout), wqkv=(wqkv_h, wqkv))
    load = {a: pltpu.make_async_copy(*names[a], in_sem.at[i]) for i, a in enumerate(names)}
    load_saved = {a: pltpu.make_async_copy(saved_h[a], saved[a], saved_sem.at[i]) for i, a in enumerate(SAVED)}
    load["ct"].start()
    load_saved["act"].start()
    load_saved["slope"].start()
    for a in ("w2", "w1", "wout", "wqkv"):
        load[a].start()
    for a in SAVED:
        if a not in ("act", "slope"):
            load_saved[a].start()
    part[...] = jnp.zeros_like(part)
    sums[...] = jnp.zeros_like(sums)
    load["ct"].wait()

    @over_rows
    def _(rows):
        g = jnp.concatenate([x[t, rows, :].astype(F32) * mask[...] for t in range(4)], axis=1)
        gmlp[rows, :] = g.astype(BF16)
        part[0] += fold(g)

    load["x"].start()
    load_saved["act"].wait()

    @pl.loop(0, 16)
    def _(i):
        t, c = i // 4, i % 4
        r = t_mm(saved["act"][:, cols(t, 1024)], gmlp[:, cols(c, 256)]).astype(BF16)
        send_tile(stage, tile_sem, i, r, [
            (g_h["w2"].at[2 * c + e, cols(t, 1024), :], e * 128, 128) for e in range(2)])

    load_saved["slope"].wait()
    load["w2"].wait()
    slope = saved["slope"]

    @pl.loop(0, 16)
    def _(i):
        w = jnp.concatenate([w2[d, cols(i, 256), :] for d in range(8)], axis=1)
        gpre = mm_t(gmlp[...], w) * slope[:, cols(i, 256)].astype(F32)
        slope[:, cols(i, 256)] = gpre.astype(BF16)
        b1[i // 4, :, cols(i % 4, 256)] = jnp.sum(gpre, axis=0, keepdims=True)

    load_saved["nmid_t"].wait()

    @pl.loop(0, 16)
    def _(i):
        r = mm(saved["nmid_t"][...].reshape(D, ROWS), slope[:, cols(i, 256)]).astype(BF16)
        send_tile(stage, tile_sem, i + 16, r, [(g_h["w1"].at[i // 4, :, cols(i % 4, 256)], 0, 256)])

    load["w1"].wait()

    @pl.loop(0, 4)
    def _(i):
        total = mm_t(slope[:, 0:1024], w1[0, cols(i, 256), :])
        for t in range(1, 4):
            total += mm_t(slope[:, t * 1024 : t * 1024 + 1024], w1[t, cols(i, 256), :])
        gn[:, cols(i, 256)] = total

    load_saved["resid"].wait()
    gain2 = vec(vectors, 5)

    @over_rows
    def _(rows):
        normed = gn[rows, :]
        g, scaled = grad_norm_rows(saved["resid"][rows, :], gain2, normed)
        g = g + gmlp[rows, :].astype(F32)
        part[1] += fold(normed)
        part[2] += fold(scaled)
        part[3] += fold(g)
        gn[rows, :] = g
        gattn[rows, :] = g.astype(BF16)

    load["wout"].wait()
    load_saved["ctx_t"].wait()

    @pl.loop(0, 4)
    def _(i):
        w = jnp.concatenate([wout[d, cols(i, 256), :] for d in range(8)], axis=1)
        gctx[:, cols(i, 256)] = mm_t(gattn[...], w).astype(BF16)
        r = mm(saved["ctx_t"][...].reshape(D, ROWS), gattn[:, cols(i, 256)]).astype(BF16)
        send_tile(stage, tile_sem, i + 32, r, [(g_h["wout"].at[2 * i + e], e * 128, 128) for e in range(2)])

    for a in ("q", "k", "v", "ctx"):
        load_saved[a].wait()

    def get(pair, slot):
        return pltpu.make_async_copy(probs_h.at[pair], probs.at[slot], probs_sem.at[slot])

    get(0, 0).start()

    @pl.loop(0, 8)
    def _(pair):
        slot = pair % 2

        @pl.when(pair < 7)
        def _():
            get(pair + 1, 1 - slot).start()

        get(pair, slot).wait()
        here = cols(pair, 128)

        got = attend_back_pair(
            *(saved[a][:, here] for a in ("q", "k", "v", "ctx")), gctx[:, here], probs.at[slot]
        )
        for c in range(3):
            at = pl.ds(pl.multiple_of(c * 256 + (pair % 2) * 128, 128), 128)
            gmix[pair // 2, :, at] = got[c].astype(BF16)
        sums[2:3, here] = jnp.sum(got[0], axis=0, keepdims=True)
        sums[3:4, here] = jnp.sum(got[2], axis=0, keepdims=True)

    load_saved["nin_t"].wait()

    @pl.loop(0, 12)
    def _(i):
        t, c = i // 3, i % 3
        r = mm(saved["nin_t"][...].reshape(D, ROWS), gmix[t, :, cols(c, 256)]).astype(BF16)
        send_tile(stage, tile_sem, i + 36, r, [(g_h["wqkv"].at[t, :, cols(c, 256)], 0, 256)])

    load["wqkv"].wait()
    resid = saved["resid"]

    @pl.loop(0, 4)
    def _(i):
        total = mm_t(gmix[0], wqkv[0, cols(i, 256), :])
        for t in range(1, 4):
            total += mm_t(gmix[t], wqkv[t, cols(i, 256), :])
        resid[:, cols(i, 256)] = total

    load["x"].wait()
    gain1 = vec(vectors, 0)

    @over_rows
    def _(rows):
        normed = resid[rows, :]
        g, scaled = grad_norm_rows(wide(x, rows), gain1, normed)
        g = g + gn[rows, :]
        part[4] += fold(normed)
        part[5] += fold(scaled)
        for t in range(4):
            gtok[t, rows, :] = g[:, t * 256 : t * 256 + 256].astype(BF16)

    for row, i in ((7, 0), (6, 1), (5, 2), (4, 3), (1, 4), (0, 5)):
        sums[row : row + 1, :] = jnp.sum(part[i], axis=0, keepdims=True)
    sums_o[0:8, :] = sums[...]
    for t in range(4):
        sums_o[8 + t : 9 + t, :] = b1[t]
    done = pltpu.make_async_copy(gtok, gtok_h, in_sem.at[0])
    done.start()
    done.wait()
    drain(stage, tile_sem)


def backward(x, ct, wqkv, wout, w1, w2, vectors, mask, probs, saved):
    n = len(SAVED)
    outs = pl.pallas_call(
        backward_kernel,
        out_shape=[IMAGE, jax.ShapeDtypeStruct((12, D), F32), *GRADS.values()],
        in_specs=[ANY] * 6 + [VM, VM, ANY] + [ANY] * n,
        out_specs=[ANY, VM] + [ANY] * 4,
        scratch_shapes=[scratch(a) for a in SAVED.values()]
        + [scratch(a) for a in (x, wqkv, wout, w1, w2)]
        + [
            pltpu.VMEM((4, 1, 1024), F32),
            scratch(ACT),
            scratch(ACT),
            scratch(ACT),
            pltpu.VMEM((ROWS, D), F32),
            pltpu.VMEM((4, ROWS, 768), BF16),
            pltpu.VMEM((2, 2, ROWS, ROWS), BF16),
            pltpu.VMEM((8, D), F32),
            pltpu.VMEM((6, 8, D), F32),
            pltpu.VMEM((2, 1024, 256), BF16),
            pltpu.SemaphoreType.DMA((6,)),
            pltpu.SemaphoreType.DMA((2,)),
            pltpu.SemaphoreType.DMA((2,)),
            pltpu.SemaphoreType.DMA((n,)),
        ],
        compiler_params=pltpu.CompilerParams(vmem_limit_bytes=VMEM_BYTES),
        name="backward",
    )(x, ct, wqkv, wout, w1, w2, vectors, mask, probs, *[saved[a] for a in SAVED])
    return outs[0], outs[1], dict(zip(GRADS, outs[2:]))


MESH = pl.DeviceIdType.MESH
BY_COLUMN = ("wout", "w2")


def block_of(name, ref, t, yx, c):
    return ref.at[yx, c, t] if name in BY_COLUMN else ref.at[t, yx, c]


def half_of(ref, h):
    n = ref.shape[0] // 2
    return ref.at[pl.ds(h * n, n)]


class Place:
    def __init__(self):
        d, self.t = lax.axis_index("dp"), lax.axis_index("tensor")
        self.y, self.x, self.c = d // 4, d // 2 % 2, d % 2
        self.yx = d // 2
        self.x_yx = self.y * 2 + 1 - self.x
        self.y_yx = (1 - self.y) * 2 + self.x
        self.xy_yx = (1 - self.y) * 2 + 1 - self.x
        self.d = d
        self.x_id = (self.x_yx * 2 + self.c, self.t)
        self.y_id = (self.y_yx * 2 + self.c, self.t)
        self.c_id = (self.yx * 2 + 1 - self.c, self.t)

    def z_id(self, t):
        return (self.d, t)

    def order(self, i):
        t = self.t
        near, far = (t, t + 1 - 2 * (t % 2)), (2 - t // 2, 3 - 3 * (t // 2))
        if isinstance(i, int):
            return (near + far)[i]
        half, odd = i // 2, i % 2
        return (1 - half) * (near[0] + odd * (near[1] - near[0])) + half * (far[0] + odd * (far[1] - far[0]))

    def greet(self):
        barrier = pltpu.get_barrier_semaphore()
        others = [self.x_id, self.y_id, self.c_id]
        others += [self.z_id(lax.rem(self.t + k, 4)) for k in (1, 2, 3)]
        for other in others:
            pl.semaphore_signal(barrier, inc=1, device_id=other, device_id_type=MESH)
        pl.semaphore_wait(barrier, 6)


def remote(src, dst, send, recv, where):
    return pltpu.make_async_remote_copy(
        src_ref=src, dst_ref=dst, send_sem=send, recv_sem=recv, device_id=where, device_id_type=MESH
    )


class Gather:
    SEMS = [
        pltpu.SemaphoreType.DMA((2, 4)),
        pltpu.SemaphoreType.DMA((4,)),
        pltpu.SemaphoreType.DMA((4, 6)),
        pltpu.SemaphoreType.DMA((4, 6)),
        pltpu.SemaphoreType.DMA((4,)),
        pltpu.SemaphoreType.DMA((4,)),
    ]

    def __init__(self, place, name, own, whole, sems):
        self.p, self.name, self.own, self.whole = place, name, own, whole
        self.z_send, self.z_recv, self.xy_send, self.xy_recv, self.c_send, self.c_recv = sems

    def at(self, s, yx):
        return block_of(self.name, self.whole, s, yx, self.p.c)

    def z_copies(self, s, act, src=None):
        p = self.p
        dst = self.at(s, p.yx)
        for way, going, to in ((0, (s <= p.t) & (p.t < 3), p.t + 1), (1, (s >= p.t) & (p.t > 0), p.t - 1)):

            @pl.when(going)
            def _():
                c = remote(dst if src is None else src, dst, self.z_send.at[way, s], self.z_recv.at[s], p.z_id(to))
                c.start() if act == "start" else c.wait_send()

    def xy_copy(self, k, s, mine=False):
        p = self.p
        yx = (p.yx, p.yx, p.yx, p.x_yx, p.yx, p.y_yx)[k]
        h = (0, 1, 0, 0, 1, 1)[k]
        to = (p.x_id, p.y_id, p.y_id, p.y_id, p.x_id, p.x_id)[k]
        dst = half_of(self.at(s, yx), h)
        src = half_of(self.own, h) if mine else dst
        return remote(src, dst, self.xy_send.at[s, k], self.xy_recv.at[s, k], to)

    def straight(self, k):
        p = self.p
        return remote(
            self.own, self.at(p.t, p.yx), self.z_send.at[0, k], self.z_recv.at[p.t], p.z_id(lax.rem(p.t + k, 4))
        )

    def open(self):
        s = self.p.t
        if self.name == "sv":
            for k in (1, 2, 3):
                self.straight(k).start()
        else:
            self.z_copies(s, "start", self.own)
        for k in (0, 1):
            self.xy_copy(k, s, True).start()

    def arrive(self, i):
        s = self.p.order(i)
        here = self.at(s, self.p.yx)
        remote(here, here, self.z_send.at[0, s], self.z_recv.at[s], self.p.c_id).wait_recv()
        if self.name != "sv":
            self.z_copies(s, "start")
        for k in (0, 1):
            self.xy_copy(k, s).start()

    def second(self, i):
        s = self.p.order(i)
        for got, own, other in ((0, 2, 3), (1, 4, 5)):
            self.xy_copy(own, s, isinstance(i, int) and i == 0).start()
            self.xy_copy(got, s).wait_recv()
            self.xy_copy(other, s).start()

    def core_copy(self, s):
        c = self.p.c
        ref = self.whole.at[:, c, s] if self.name in BY_COLUMN else self.whole.at[s, :, c]
        return remote(ref, ref, self.c_send.at[s], self.c_recv.at[s], self.p.c_id)

    def last(self, i):
        s = self.p.order(i)
        for k in (2, 3, 4, 5):
            self.xy_copy(k, s).wait_recv()
        self.core_copy(s).start()

    def have(self, i):
        self.core_copy(self.p.order(i)).wait_recv()

    def finish(self):
        for s in range(4):
            if self.name != "sv":
                self.z_copies(s, "wait")
            elif s:
                self.straight(s).wait_send()
            for k in range(6):
                self.xy_copy(k, s).wait_send()
            self.core_copy(s).wait_send()


class Swap:
    SEMS = [pltpu.SemaphoreType.DMA((4,)), pltpu.SemaphoreType.DMA((4,))]

    def __init__(self, place, pieces, whole, sems):
        self.p, self.pieces, self.whole = place, pieces, whole
        self.send, self.recv = sems

    def copy(self, k):
        p = self.p
        to = lax.rem(p.t + k, 4)
        return remote(self.pieces.at[to], self.whole.at[p.t], self.send.at[k], self.recv.at[k], p.z_id(to))

    def start(self):
        for k in (1, 3, 2):
            self.copy(k).start()

    def done(self):
        for k in (1, 2, 3):
            self.copy(k).wait_recv()

    def finish(self):
        for k in (1, 2, 3):
            self.copy(k).wait_send()


class Mail:
    def __init__(self, place, buf, sem):
        self.p, self.buf, self.sem, self.depth = place, buf, sem, buf.shape[0]

    def copy(self, slot, dst, recv):
        return remote(self.buf.at[slot], dst, self.sem.at[slot], recv, self.p.c_id)

    def post(self, i, parts, dst, recv):
        slot = lax.rem(i, self.depth)

        @pl.when(i >= self.depth)
        def _():
            self.copy(slot, dst, recv).wait_send()

        for k, part in enumerate(parts):
            self.buf[slot, k] = part
        self.copy(slot, dst, recv).start()

    def finish(self):
        for slot in range(self.depth):
            self.copy(slot, self.buf.at[slot], self.sem.at[slot]).wait_send()


def column_pair(ref, q, c):
    return jnp.concatenate([ref[:, cols(q * 4 + c, 128)], ref[:, cols(q * 4 + 2 + c, 128)]], axis=1)


ACTS = ("sv", "wqkv", "wout", "w1", "w2", "XS", "CS", "LN1", "Q", "OUT", "F", "D", "END", "K1")
KINDS = ("", "O", "A", "S", "L")
SEQUENCE = (
    210, 110, 130, 10, 221, 410, 121, 310, 430, 222, 230, 21, 223, 30, 131, 330, 122, 22, 23, 231, 123, 500,
    132, 31, 32, 33, 140, 321, 232, 421, 240, 331, 133, 40, 41, 141, 322, 42, 43, 241, 233, 700, 323, 242,
    142, 800, 440, 431, 801, 143, 422, 332, 340, 341, 802, 243, 333, 803, 423, 432, 600, 900, 1000, 342, 433,
    343, 1001, 1002, 441, 442, 1003, 1300, 1100, 443, 1101, 1102, 1103, 1200,
)


def cut(raw, pieces):
    for i in range(4):
        pieces[i, 576:ROWS, :] = jnp.zeros((ROWS - 576, 256), BF16)
        for r in (*range(0, 576, CHUNK), 576):
            n = min(CHUNK, SEQ - r)
            pieces[i, r : r + n, :] = raw[SEQ * i + r : SEQ * i + r + n, :]


def spread_kernel(slot_mask, x_raw, ct_raw, *rest):
    names, n, m = list(PARTS), len(PARTS), len(SAVED)
    small, (w_qkv, w_out, w_fc1, w_fc2), rest = rest[:8], rest[8:12], rest[12 - n :]
    x_h, ct_h, out_h, probs_h, vectors = rest[n : n + 5]
    rest = rest[n + 5 :]
    whole_h, saved_h = dict(zip(WEIGHTS, rest[:4])), dict(zip(SAVED, rest[4 : 4 + m]))
    rest = rest[4 + m :]
    x, ct, out, b1, mask, stack, raw, x_in, ct_in = rest[:9]
    whole = dict(zip(names, rest[9 : 9 + n]))
    rest = rest[9 + n :]
    local_sem, keep_sem = rest[0], rest[1]
    swap_sems, rest = rest[2:6], rest[6:]
    sems, refs = rest[: 6 * n], rest[6 * n :]
    p = Place()
    own = {a: block_of(a, whole[a], p.t, p.yx, p.c) for a in names}
    f = Forward(x, whole, vectors, b1, mask, out, out_h, probs_h, saved_h, refs)
    gathers = {a: Gather(p, a, own[a], whole[a], sems[6 * i : 6 * i + 6]) for i, a in enumerate(names)}
    swaps = dict(XS=Swap(p, x_in, x, swap_sems[0:2]), CS=Swap(p, ct_in, ct, swap_sems[2:4]))
    local = [
        pltpu.make_async_copy(x_in.at[p.t], x.at[p.t], local_sem.at[0]),
        pltpu.make_async_copy(ct_in.at[p.t], ct.at[p.t], local_sem.at[1]),
    ]
    raw_loads = [pltpu.make_async_copy(a, raw, local_sem.at[2 + i]) for i, a in enumerate((x_raw, ct_raw))]
    raw_loads[0].start()
    mask[...] = jnp.full((1, 256), slot_mask[p.t].astype(F32))
    for row, ref in enumerate((small[0], small[1], small[2].at[0], small[2].at[1], *small[3:7])):
        stack[row : row + 1, :] = ref[...]
    lane = lax.broadcasted_iota(jnp.int32, (32, 256), 1)
    row = lax.broadcasted_iota(jnp.int32, (32, 256), 0)
    place = jnp.where(lane == row + p.d * 32, 1.0, 0.0).astype(BF16)
    own["sv"][8:16, :] = jnp.zeros((8, 256), F32)
    own["sv"][0:8, :] = mm(stack[...].astype(BF16), place)
    own["sv"][8:9, 0:128] = small[7][...].astype(BF16).astype(F32)
    p.greet()
    pending = []
    resid_stored = f.stores(("resid",))

    def keep(src, dst):
        c = pltpu.make_async_copy(src, dst, keep_sem.at[len(pending)])
        c.start()
        pending.append(c)

    def ready(name):
        if name == "wqkv":
            for i in range(3):
                own[name][:, i * 256 : i * 256 + 256] = w_qkv[i].astype(BF16)
        elif name != "sv":
            own[name][...] = dict(wout=w_out, w1=w_fc1, w2=w_fc2)[name][...].astype(BF16)

    def do(code, step):
        name, kind = ACTS[code // 100], KINDS[code // 10 % 10]
        if name in gathers:
            g = gathers[name]
            if kind == "O":
                ready(name)
                g.open()
            elif kind == "A":
                g.arrive(step)
            elif kind == "S":
                g.second(step)
            else:
                g.last(step)
        elif name in swaps:
            if name == "XS":
                raw_loads[0].wait()
                cut(raw, x_in)
                raw_loads[1].start()
                local[0].start()
            else:
                raw_loads[1].wait()
                cut(raw, ct_in)
                local[1].start()
            swaps[name].start()
        elif name == "LN1":
            for i in range(4):
                gathers["sv"].have(i)
            sv = whole["sv"]
            for t in range(4):
                vectors[t] = jnp.sum(sv[t, :, :, 0:8].reshape(8, 8, 256), axis=0)
                for d in range(8):
                    b1[t, :, d * 128 : d * 128 + 128] = sv[t, d // 2, d % 2, 8:9, 0:128]
            swaps["XS"].done()
            local[0].wait()
            keep(x, x_h)
            f.start_norm()
        elif name == "Q":
            gathers["wqkv"].have(step)
            f.heads(p.order(step), step)
        elif name == "OUT":
            for i in range(4):
                gathers["wout"].have(i)
            keep(whole["wqkv"], whole_h["wqkv"])
            keep(whole["wout"], whole_h["wout"])
            f.middle()
            f.turn()
            for c in (*f.stores(("q", "k", "v", "ctx", "nin_t", "ctx_t", "nmid_t")), *resid_stored):
                c.start()
        elif name == "F":
            gathers["w1"].have(step)
            f.hidden(p.order(step))
        elif name == "K1":
            keep(whole["w1"], whole_h["w1"])
            for c in f.stores(("slope", "act")):
                c.start()
            for c in resid_stored:
                c.wait()
        elif name == "D":
            gathers["w2"].have(step)
            f.down(p.order(step))
        elif name == "END":
            keep(whole["w2"], whole_h["w2"])
            f.finish()
            f.store_out().start()
            swaps["CS"].done()
            local[1].wait()
            keep(ct, ct_h)
    for item in SEQUENCE:
        if isinstance(item, int):
            do(item, item % 10)
            continue

        @pl.loop(0, 4 + max(code % 10 for code in item))
        def _(m, item=item):
            for code in item:
                lag = code % 10

                @pl.when((m >= lag) & (m < lag + 4))
                def _():
                    do(code, m - lag)

    f.drain_last(p.order(3))
    for c in [*pending, *f.stores([a for a in SAVED if a != "resid"]), f.store_out()]:
        c.wait()
    for s in swaps.values():
        s.finish()
    for g in gathers.values():
        g.finish()


def spread(slot_mask, x_raw, ct_raw, small, big):
    names, n, m = list(PARTS), len(PARTS), len(SAVED)
    outs = pl.pallas_call(
        spread_kernel,
        out_shape=[IMAGE, IMAGE, IMAGE, PROBS, jax.ShapeDtypeStruct((4, 8, 256), F32)]
        + [part(a) for a in WEIGHTS]
        + list(SAVED.values()),
        in_specs=[pl.BlockSpec(memory_space=pltpu.SMEM), ANY, ANY] + [VM] * (len(small) + len(big)),
        out_specs=[ANY] * 4 + [VM] + [ANY] * (4 + m),
        scratch_shapes=[scratch(IMAGE), scratch(IMAGE), scratch(IMAGE), pltpu.VMEM((4, 1, 1024), F32)]
        + [pltpu.VMEM((1, 256), F32), pltpu.VMEM((8, 32), F32), scratch(x_raw), scratch(IMAGE), scratch(IMAGE)]
        + [scratch(part(a)) for a in names]
        + [pltpu.SemaphoreType.DMA((4,)), pltpu.SemaphoreType.DMA((7,))]
        + Swap.SEMS * 2
        + Gather.SEMS * n
        + Forward.SCRATCH,
        compiler_params=pltpu.CompilerParams(
            collective_id=0, has_side_effects=True, vmem_limit_bytes=VMEM_BYTES
        ),
        name="spread",
    )(slot_mask, x_raw, ct_raw, *small, *big)
    return outs[:5], dict(zip(WEIGHTS, outs[5:9])), dict(zip(SAVED, outs[9:]))


REDUCED = ("w2", "w1", "wout", "wqkv")


def turn_of(i):
    return (1 - i // 2) * (1 - i % 2) * 3 + i // 2 * (2 - i % 2)


class Reduce:
    def __init__(self, place, name, refs):
        self.p, self.name = place, name
        self.own, self.got1, self.got2, self.got3 = refs[:4]
        self.c_recv, self.send, self.recv, self.z_send, self.z_recv = refs[4:]

    @staticmethod
    def scratch(name):
        rows, width = PARTS[name][0][3:]
        return [
            pltpu.VMEM((4, 4, rows, width), BF16),
            pltpu.VMEM((4, 4, rows // 2, width), BF16),
            pltpu.VMEM((2, 4, rows // 2, width), BF16),
            pltpu.VMEM((5, rows, width), BF16),
            pltpu.SemaphoreType.DMA((4,)),
            pltpu.SemaphoreType.DMA((4, 6)),
            pltpu.SemaphoreType.DMA((4, 6)),
            pltpu.SemaphoreType.DMA((4,)),
            pltpu.SemaphoreType.DMA((5,)),
        ]

    def block(self, ref, t, yx):
        return ref.at[yx, t] if self.name in BY_COLUMN else ref.at[t, yx]

    def wait_bytes(self, ref, sem):
        remote(ref, ref, self.z_send.at[0], sem, self.p.c_id).wait_recv()

    def add(self, dst, *more):
        rows, width = dst.shape
        n = min(rows, 64 if width > 128 else 512)

        @pl.loop(0, rows // n)
        def _(i):
            r = pl.ds(pl.multiple_of(i * n, n), n)
            total = dst[r, :]
            for ref in more:
                total += ref[r, :]
            dst[r, :] = total

    def first_copy(self, by_y, j, t):
        p = self.p
        yx = (1 - p.y) * 2 + j if by_y else j * 2 + 1 - p.x
        src = half_of(self.block(self.own, t, yx), 0 if by_y else 1)
        k = (0 if by_y else 2) + j
        return remote(src, self.got1.at[k, t], self.send.at[t, k], self.recv.at[t, k], p.y_id if by_y else p.x_id)

    def second_copy(self, j, t):
        p = self.p
        by_x = j == 0
        src = half_of(self.block(self.own, t, p.x_yx if by_x else p.y_yx), j)
        return remote(src, self.got2.at[j, t], self.send.at[t, 4 + j], self.recv.at[t, 4 + j],
                      p.x_id if by_x else p.y_id)

    def other_core(self, t=None):
        ref = self.own if t is None else self.own.at[:, t] if self.name in BY_COLUMN else self.own.at[t]
        self.wait_bytes(ref, self.c_recv.at[0 if t is None else t])

    def begin(self, t):
        p = self.p
        self.first_copy(True, 1 - p.x, t).start()
        self.first_copy(False, 1 - p.y, t).start()
        self.first_copy(True, p.x, t).start()
        self.first_copy(False, p.y, t).start()

    def cross(self, i):
        p, t = self.p, turn_of(i)
        for j in range(2):
            self.first_copy(True, j, t).wait_recv()
            self.first_copy(False, j, t).wait_recv()
        self.add(half_of(self.block(self.own, t, p.x_yx), 0), self.got1.at[1 - p.x, t])
        self.second_copy(0, t).start()
        self.add(half_of(self.block(self.own, t, p.y_yx), 1), self.got1.at[2 + 1 - p.y, t])
        self.second_copy(1, t).start()
        self.add(half_of(self.block(self.own, t, p.yx), 0), self.got1.at[p.x, t])
        self.add(half_of(self.block(self.own, t, p.yx), 1), self.got1.at[2 + p.y, t])

    def along(self, i):
        p, t = self.p, turn_of(i)
        mine = self.block(self.own, t, p.yx)
        for j in (0, 1):
            self.second_copy(j, t).wait_recv()
            self.add(half_of(mine, j), self.got2.at[j, t])
        for up, ends in ((True, (p.t == 0) & (t > 0)), (False, (p.t == 3) & (t < 3))):

            @pl.when(ends)
            def _():
                self.send_z(t, up).start()

    def pass_on(self, i, hop):
        p, t = self.p, turn_of(i)
        mine = self.block(self.own, t, p.yx)
        for up, here in ((True, (p.t == hop) & (t > hop)), (False, (p.t == 3 - hop) & (t < 3 - hop))):

            @pl.when(here)
            def _():
                self.wait_bytes(self.got3.at[t], self.z_recv.at[t])
                self.add(mine, self.got3.at[t])
                self.send_z(t, up).start()

    def send_z(self, t, up):
        p = self.p
        slot = t if up else t + (4 - t) * ((3 + t - p.t) // 2)
        return remote(self.block(self.own, t, p.yx), self.got3.at[slot], self.z_send.at[t], self.z_recv.at[slot],
                      p.z_id(p.t + 1 if up else p.t - 1))

    def end(self, result):
        p = self.p
        mine = self.block(self.own, p.t, p.yx)
        rows, width = mine.shape
        n = min(rows, 32 if width > 128 else 256)

        pieces = [(result, slice(None))]
        if self.name == "wqkv":
            pieces = [(result.at[i], slice(i * 256, i * 256 + 256)) for i in range(3)]

        def through(ref):
            @pl.loop(0, rows // n)
            def _(i):
                r = pl.ds(pl.multiple_of(i * n, n), n)
                for to, lanes in pieces:
                    more = ref[r, lanes].astype(F32)
                    to[r, :] = more if ref is mine else to[r, :] + more

        through(mine)
        for slot, there in ((p.t, p.t > 0), (4, p.t < 3)):

            @pl.when(there)
            def _():
                self.wait_bytes(self.got3.at[slot], self.z_recv.at[slot])
                through(self.got3.at[slot])

    def finish(self):
        p = self.p
        for t in range(4):
            for j in range(2):
                self.first_copy(True, j, t).wait_send()
                self.first_copy(False, j, t).wait_send()
                self.second_copy(j, t).wait_send()

            @pl.when(p.t != t)
            def _():
                block = self.block(self.own, t, p.yx)
                remote(block, block, self.z_send.at[t], self.z_recv.at[t], p.c_id).wait_send()


class Total:
    SCRATCH = [
        pltpu.VMEM((4, 16, D), F32),
        pltpu.VMEM((6, 16, D), F32),
        pltpu.SemaphoreType.DMA((6,)),
        pltpu.SemaphoreType.DMA((6,)),
    ]

    def __init__(self, place, acc, refs):
        self.p, self.acc = place, acc
        self.sent, self.got, self.send, self.recv = refs

    def copies(self, i):
        p = self.p
        if i < 3:
            return [remote(self.sent.at[i], self.got.at[i], self.send.at[i], self.recv.at[i], (p.c_id, p.x_id, p.y_id)[i])]
        return [
            remote(self.sent.at[3], self.got.at[2 + k], self.send.at[2 + k], self.recv.at[2 + k], p.z_id(lax.rem(p.t + k, 4)))
            for k in (1, 2, 3)
        ]

    def start(self, i):
        self.sent[i] = self.acc[...]
        for c in self.copies(i):
            c.start()

    def end(self, i):
        for c in self.copies(i):
            c.wait()
        for k in (i,) if i < 3 else (3, 4, 5):
            self.acc[...] += self.got[k]


class Stream:
    def __init__(self, n, src, buf, sem):
        self.n, self.src, self.buf, self.sem = n, src, buf, sem
        self.depth = buf.shape[0]

    def copies(self, i):
        slot = lax.rem(i, self.depth)
        return [
            pltpu.make_async_copy(a, b, self.sem.at[slot, k])
            for k, (a, b) in enumerate(self.src(i, self.buf.at[slot]))
        ]

    def start(self):
        for i in range(min(self.depth - 1, self.n)):
            for c in self.copies(jnp.int32(i)):
                c.start()

    def next(self, i):
        for c in self.copies(i):
            c.wait()

        @pl.when(i + self.depth - 1 < self.n)
        def _():
            for c in self.copies(i + self.depth - 1):
                c.start()

        return self.buf.at[lax.rem(i, self.depth)]


def accumulate(ref, here, value, step):
    @pl.when(step == 0)
    def _():
        ref[:, here] = value

    @pl.when(step > 0)
    def _():
        ref[:, here] += value


BACK = ("w2", "w1", "wout", "wqkv", "T", "G0", "GS", "GM", "SHARE", "HG", "HS", "HM", "GN", "GR", "OA", "OM", "AT", "AM", "GI", "GT")
STEPS = ("", "X", "Z", "E", "Y", "W")
COLLECT = (
    500, (600, 701,), (900,), 1200, 800, 1300, 1400, 10, 13, 11, 12, 1500, (1600, 1701, 20,), 311, 1800, 211,
    312, 40, 43, 53, 42, 41, 210, 1900, 213, 313, 310, (1000, 1101,), 212, 220, 51, 110, 223, 323, 50, 111,
    322, 321, 343, 112, 342, 52, 320, 352, 113, 400, 221, 241, 341, 120, 222, 243, 240, 353, 250, 340, 350,
    121, 253, 122, 140, 351, 251, 242, 123, 30, 141, 142, 401, 151, 252, 152, 330, 402, 150, 143, 230, 153,
    403, 130,
)


class Backward:
    NAMES = (
        ("image", "gmlp", "slope", "gmix", "gn", "resid", "split", "ctx_t", "b1", "part_sums", "load_sem")
        + ("col_buf", "col_sem", "row_buf", "row_sem", "head_buf", "head_sem", "probs", "probs_sem")
        + ("up_mail", "up_mail_sem", "mix_mail", "mix_mail_sem", "out_mail", "out_mail_sem", "down_mail", "down_mail_sem")
    )
    SCRATCH = [
        scratch(IMAGE),
        scratch(ACT),
        pltpu.VMEM((ROWS, 4 * D), BF16),
        pltpu.VMEM((ROWS, 3 * D), BF16),
        pltpu.VMEM((ROWS, D), F32),
        pltpu.VMEM((ROWS, D), F32),
        pltpu.VMEM((2, 4, 128, ROWS), BF16),
        pltpu.VMEM((4, 2, 128, ROWS), BF16),
        pltpu.VMEM((4, 1, 1024), F32),
        pltpu.VMEM((6, 8, D), F32),
        pltpu.SemaphoreType.DMA((12,)),
        pltpu.VMEM((3, 4, 2, 2, 256, 128), BF16),
        pltpu.SemaphoreType.DMA((3, 2)),
        pltpu.VMEM((3, 2, 2, 128, 1024), BF16),
        pltpu.SemaphoreType.DMA((3, 1)),
        pltpu.VMEM((3, 4, ROWS, 128), BF16),
        pltpu.SemaphoreType.DMA((3, 4)),
        pltpu.VMEM((2, 2, ROWS, ROWS), BF16),
        pltpu.SemaphoreType.DMA((2, 1)),
        pltpu.VMEM((2, 4, 128, 512), BF16),
        pltpu.SemaphoreType.DMA((2,)),
        pltpu.VMEM((2, 4, 128, 768), BF16),
        pltpu.SemaphoreType.DMA((2,)),
        pltpu.VMEM((2, 2, 4, 256, 128), BF16),
        pltpu.SemaphoreType.DMA((2,)),
        pltpu.VMEM((1, 4, 1024, 128), BF16),
        pltpu.SemaphoreType.DMA((1,)),
    ]

    def __init__(self, p, reduces, swaps_of, total, hbm, vectors, sums, refs):
        for a, b in zip(self.NAMES, refs):
            setattr(self, a, b)
        self.p, self.reduces, self.total, self.vectors, self.sums = p, reduces, total, vectors, sums
        self.hbm = hbm
        self.out_swap, self.tok_swap = swaps_of(self.image)
        self.ups_mail = Mail(p, self.up_mail, self.up_mail_sem)
        self.mixes_mail = Mail(p, self.mix_mail, self.mix_mail_sem)
        self.downs_mail = Mail(p, self.down_mail, self.down_mail_sem)
        self.outs_mail = Mail(p, self.out_mail, self.out_mail_sem)
        h = hbm
        self.out_buf = self.probs.at[0, 0, :, pl.ds(0, 256)]
        self.loads = {
            a: self.load(i, *b)
            for i, (a, b) in enumerate(
                dict(
                    ct=(h["ct"], self.image),
                    slope=(h["slope"], self.slope),
                    nin0=(h["nin_t"].at[:, p.c], self.split.at[0]),
                    nin1=(h["nin_t"].at[:, 1 - p.c], self.split.at[1]),
                    out=(h["out"].at[p.t], self.out_buf),
                    resid=(h["resid"], self.resid),
                    ctx_t=(h["ctx_t"], self.ctx_t),
                    x=(h["x"], self.image),
                ).items()
            )
        }
        self.nmid = [
            self.load(2, h["nmid_t"].at[:, p.c], self.split.at[0]),
            self.load(3, h["nmid_t"].at[:, 1 - p.c], self.split.at[1]),
        ]
        self.out_done = self.load(4, self.out_buf, h["out_o"].at[p.t])
        self.tok_done = self.load(0, self.image.at[p.t], h["gtok_o"].at[p.t])

        def down_src(i, b):
            return [
                (h["w2"].at[:, :, turn_of(i // 2), pl.ds(i % 2 * 512 + k * 256, 256)], b.at[:, :, k]) for k in range(2)
            ]

        def out_src(i, b):
            return [(h["wout"].at[:, :, i * 2 + k], b.at[:, :, k]) for k in range(2)]

        def head_src(i, b):
            at = cols(turn_of(i // 2) * 2 + i % 2, 128)
            return [(h[a].at[:, at], b.at[k]) for k, a in enumerate(("q", "k", "v", "ctx"))]

        self.downs = Stream(8, down_src, self.col_buf, self.col_sem)
        self.outs = Stream(2, out_src, self.col_buf, self.col_sem)
        self.ups = Stream(
            8, lambda i, b: [(h["w1"].at[i % 4, pl.ds(i // 4 * 2, 2)], b)], self.row_buf, self.row_sem
        )
        self.mixes = Stream(
            8,
            lambda i, b: [(h["wqkv"].at[i % 4, pl.ds(i // 4 * 2, 2)], b.at[:, :, :, pl.ds(0, 768)])],
            self.row_buf,
            self.row_sem,
        )
        self.heads = Stream(8, head_src, self.head_buf, self.head_sem)
        self.heads_p = Stream(
            8, lambda i, b: [(h["probs"].at[turn_of(i // 2) * 2 + i % 2], b)], self.probs, self.probs_sem
        )

    def load(self, i, src, dst):
        return pltpu.make_async_copy(src, dst, self.load_sem.at[i])

    def act_load(self, i):
        return self.load(8 + i, self.hbm["act"].at[:, cols(turn_of(i), 1024)], self.gmix.at[:, cols(i % 3, 1024)])

    def begin(self):
        self.loads["ct"].start()
        for i in range(3):
            self.act_load(i).start()
        self.loads["slope"].start()
        self.downs.start()
        self.ups.start()
        for a in ("out", "resid", "ctx_t", "nin0", "nin1"):
            self.loads[a].start()
        self.heads.start()
        self.part_sums[...] = jnp.zeros_like(self.part_sums)
        self.sums[...] = jnp.zeros_like(self.sums)

    def mask_cotangent(self):
        self.loads["ct"].wait()
        mask = self.hbm["mask"]

        @over_rows
        def _(rows):
            g = wide(self.image, rows) * jnp.concatenate([mask[...]] * 4, axis=1)
            self.gmlp[rows, :] = g.astype(BF16)
            self.part_sums[0] += fold(g)

        self.loads["out"].wait()
        self.out_done.start()

    def four_columns(self, c):
        return jnp.concatenate([self.gmlp[:, cols(yx * 2 + c, 128)] for yx in range(4)], axis=1)

    def down_share(self, i):
        r, t = self.reduces["w2"], turn_of(i)
        self.act_load(i).wait()
        g = t_mm(self.gmix[:, cols(i % 3, 1024)], self.four_columns(1 - self.p.c)).astype(BF16)
        self.downs_mail.post(
            i, [g[:, k * 128 : k * 128 + 128] for k in range(4)], r.own.at[:, t], r.c_recv.at[t]
        )

    def down_own(self, i):
        r, t = self.reduces["w2"], turn_of(i)
        r.other_core(t)
        g = t_mm(self.gmix[:, cols(i % 3, 1024)], self.four_columns(self.p.c))
        for k in range(4):
            r.own[k, t] = (g[:, k * 128 : k * 128 + 128] + r.own[k, t].astype(F32)).astype(BF16)
        r.begin(t)

        @pl.when(i == 0)
        def _():
            self.act_load(3).start()

    def share(self):
        self.out_swap.start()

    def whole_rows(self, tile):
        return jnp.concatenate([tile[d // 2, d % 2].reshape(512, 128) for d in range(8)], axis=1)

    def post_rows(self, mail, n, g, r, t, here):
        g = g.astype(BF16).reshape(4, 128, -1)
        mail.post(n, [g[k] for k in range(4)], r.own.at[t, :, :, here], r.c_recv.at[t])

    def hidden(self, i):
        t = turn_of(i)

        @pl.when(i == 0)
        def _():
            self.loads["slope"].wait()

        @pl.loop(0, 2)
        def _(j):
            w = self.whole_rows(self.downs.next(2 * i + j))
            here = cols(t * 2 + j, 512)
            gpre = mm_t(self.gmlp[...], w) * self.slope[:, here].astype(F32)
            self.slope[:, here] = gpre.astype(BF16)
            self.b1[t, :, cols(j, 512)] = jnp.sum(gpre, axis=0, keepdims=True)

    def hidden_share(self, i):
        r, t = self.reduces["w1"], turn_of(i)

        @pl.loop(0, 2)
        def _(j):
            g = mm(self.split[1].reshape(512, ROWS), self.slope[:, cols(t * 2 + j, 512)])
            self.post_rows(self.ups_mail, 2 * i + j, g, r, t, cols(j, 512))

    def add_own(self, r, t, here, value):
        width = value.shape[1]
        had = r.own[t, :, :, here].astype(F32)
        r.own[t, :, :, here] = (value.reshape(4, 128, width) + had).astype(BF16)

    def hidden_own(self, i):
        r, t = self.reduces["w1"], turn_of(i)
        r.other_core(t)

        @pl.loop(0, 2)
        def _(j):
            g = mm(self.split[0].reshape(512, ROWS), self.slope[:, cols(t * 2 + j, 512)])
            self.add_own(r, t, cols(j, 512), g)

        r.begin(t)

    def through_up(self):
        self.outs.start()

        @pl.loop(0, 8)
        def _(i):
            w = self.ups.next(i)
            g = mm_t(self.slope[:, cols(i % 4, 1024)], w[...].reshape(512, D))
            accumulate(self.gn, cols(i // 4, 512), g, i % 4)

        self.mixes.start()

    def norm_mid(self):
        self.loads["resid"].wait()
        gain = vec(self.vectors, 5)

        @over_rows
        def _(rows):
            normed = self.gn[rows, :]
            g, scaled = grad_norm_rows(self.resid[rows, :], gain, normed)
            g = g + self.gmlp[rows, :].astype(F32)
            self.part_sums[1] += fold(normed)
            self.part_sums[2] += fold(scaled)
            self.part_sums[3] += fold(g)
            self.gn[rows, :] = g
            self.gmlp[rows, :] = g.astype(BF16)

    def attn_out(self):
        r, p = self.reduces["wout"], self.p
        self.loads["ctx_t"].wait()
        self.out_done.wait()
        self.heads_p.start()

        @pl.loop(0, 2)
        def _(q):
            g = mm(self.ctx_t[...].reshape(D, ROWS), column_pair(self.gmlp, q, 1 - p.c)).astype(BF16)
            self.outs_mail.post(
                q,
                [g[:, k * 128 : k * 128 + 128].reshape(4, 256, 128) for k in range(2)],
                r.own.at[pl.ds(q * 2, 2)],
                r.c_recv.at[0],
            )

        @pl.loop(0, 2)
        def _(i):
            g = mm_t(self.gmlp[...], self.whole_rows(self.outs.next(i))).astype(BF16)
            for k in range(2):
                self.image[i * 2 + k] = g[:, k * 256 : k * 256 + 256]

    def attn_out_own(self):
        r, p = self.reduces["wout"], self.p
        r.other_core()

        @pl.loop(0, 2)
        def _(q):
            g = mm(self.ctx_t[...].reshape(D, ROWS), column_pair(self.gmlp, q, p.c))
            for k in range(2):
                had = r.own[q * 2 + k].astype(F32)
                r.own[q * 2 + k] = (g[:, k * 128 : k * 128 + 128].reshape(4, 256, 128) + had).astype(BF16)

        for i in range(4):
            r.begin(turn_of(i))
        for a in ("nin0", "nin1"):
            self.loads[a].wait()

    def attend(self, i):
        r, t = self.reduces["wqkv"], turn_of(i)

        @pl.loop(0, 2)
        def _(h):
            ins = self.heads.next(2 * i + h)
            probs = self.heads_p.next(2 * i + h)
            got = attend_back_pair(*(ins[k] for k in range(4)), self.image[t, :, cols(h, 128)], probs)
            for c in range(3):
                self.gmix[:, pl.ds(pl.multiple_of(t * 768 + c * 256 + h * 128, 128), 128)] = got[c].astype(BF16)
            here = cols(t * 2 + h, 128)
            self.sums[2:3, here] = jnp.sum(got[0], axis=0, keepdims=True)
            self.sums[3:4, here] = jnp.sum(got[2], axis=0, keepdims=True)

        g = mm(self.split[1].reshape(512, ROWS), self.gmix[:, cols(t, 768)])
        self.post_rows(self.mixes_mail, i, g, r, t, pl.ds(0, 768))

    def attend_own(self, i):
        r, t = self.reduces["wqkv"], turn_of(i)
        r.other_core(t)
        self.add_own(r, t, slice(None), mm(self.split[0].reshape(512, ROWS), self.gmix[:, cols(t, 768)]))
        r.begin(t)

    def through_mix(self):
        self.loads["x"].start()
        for c in self.nmid:
            c.start()

        @pl.loop(0, 8)
        def _(i):
            w = self.mixes.next(i)
            g = mm_t(self.gmix[:, cols(i % 4, 768)], w[:, :, :, 0:768].reshape(512, 768))
            accumulate(self.resid, cols(i // 4, 512), g, i % 4)

    def norm_in(self):
        self.loads["x"].wait()
        gain = vec(self.vectors, 0)

        @over_rows
        def _(rows):
            normed = self.resid[rows, :]
            g, scaled = grad_norm_rows(wide(self.image, rows), gain, normed)
            g = g + self.gn[rows, :]
            self.part_sums[4] += fold(normed)
            self.part_sums[5] += fold(scaled)
            for t in range(4):
                self.image[t, rows, :] = g[:, t * 256 : t * 256 + 256].astype(BF16)

        self.tok_swap.start()
        self.tok_done.start()
        sums = self.sums
        for row, i in ((7, 0), (6, 1), (5, 2), (4, 3), (1, 4), (0, 5)):
            sums[row : row + 1, :] = jnp.sum(self.part_sums[i], axis=0, keepdims=True)
        for t in range(4):
            sums[8 + t : 9 + t, :] = self.b1[t]
        self.total.start(0)
        for c in self.nmid:
            c.wait()

    def finish(self):
        self.tok_done.wait()
        for m in (self.ups_mail, self.mixes_mail, self.outs_mail, self.downs_mail):
            m.finish()
        for s in (self.out_swap, self.tok_swap):
            s.done()
            s.finish()
        for r in self.reduces.values():
            r.finish()


HBM = ("x", "out", "ct", "probs") + WEIGHTS


def collect_kernel(slot_mask, vectors, *rest):
    names = HBM + tuple(SAVED)
    n = len(names)
    hbm = dict(zip(names, rest[:n]))
    out_o, gtok_o = rest[n : n + 2]
    hbm |= dict(out_o=out_o, gtok_o=gtok_o)
    results = dict(zip(REDUCED, rest[n + 2 : n + 6]))
    small, rest = rest[n + 6 : n + 14], rest[n + 14 :]
    mask, sums, rest = rest[0], rest[1], rest[2:]
    mask[...] = jnp.full((1, 256), slot_mask[lax.axis_index("tensor")].astype(F32))
    hbm["mask"] = mask
    m = len(Backward.SCRATCH)
    refs, rest = rest[:m], rest[m:]
    out_sems, tok_sems, total_refs, rest = rest[0:2], rest[2:4], rest[4:8], rest[8:]
    p = Place()
    reduces = {a: Reduce(p, a, rest[9 * i : 9 * i + 9]) for i, a in enumerate(REDUCED)}
    total = Total(p, sums, total_refs)

    def swaps_of(image):
        return Swap(p, hbm["out"], out_o, out_sems), Swap(p, image, gtok_o, tok_sems)

    b = Backward(p, reduces, swaps_of, total, hbm, vectors, sums, refs)
    acts = dict(
        G0=b.mask_cotangent, GS=b.down_share, GM=b.down_own, SHARE=b.share, HG=b.hidden, HS=b.hidden_share, HM=b.hidden_own, GN=b.through_up, GR=b.norm_mid, OA=b.attn_out,
        OM=b.attn_out_own, AT=b.attend, AM=b.attend_own, GI=b.through_mix, GT=b.norm_in,
    )
    counted = ("GS", "GM", "HG", "HS", "HM", "AT", "AM")

    def act(code, i):
        name, kind = BACK[code // 100], STEPS[code // 10 % 10]
        if name in reduces:
            r = reduces[name]
            if kind == "E":
                r.end(results[name])
            elif kind in ("Y", "W"):
                r.pass_on(i, 1 if kind == "Y" else 2)
            else:
                (r.cross if kind == "X" else r.along)(i)
        elif name == "T":
            total.end(i)
            if i < 3:
                total.start(i + 1)
        elif name in counted:
            acts[name](i)
        else:
            acts[name]()

    b.begin()
    p.greet()
    for step in COLLECT:
        if isinstance(step, int):
            act(step, step % 10)
            continue

        @pl.loop(0, 4 + max(code % 10 for code in step))
        def _(m, step=step):
            for code in step:
                lag = code % 10

                @pl.when((m >= lag) & (m < lag + 4))
                def _():
                    act(code, m - lag)

    here = pl.ds(pl.multiple_of(p.t * 256 + p.d // 4 * 128, 128), 128)
    four = sums[0:8, here]
    mine = sum(jnp.where(p.d % 4 == k, four[:, k * 32 : k * 32 + 32], 0.0) for k in range(4))
    for i, row in enumerate((0, 1, None, 4, 5, 6, 7)):
        if row is None:
            small[i][...] = mine[2:4]
        else:
            small[i][...] = mine[row : row + 1]
    hidden = sums[8:12, pl.ds(pl.multiple_of(p.d * 128, 128), 128)]
    small[7][...] = sum(jnp.where(p.t == k, hidden[k : k + 1], 0.0) for k in range(4))
    b.finish()


def collect(slot_mask, vectors, hbm):
    names = HBM + tuple(SAVED)
    outs = pl.pallas_call(
        collect_kernel,
        out_shape=[IMAGE, IMAGE]
        + [jax.ShapeDtypeStruct((3, 128, 256) if a == "wqkv" else PARTS[a][0][3:], F32) for a in REDUCED]
        + [jax.ShapeDtypeStruct((2 if i == 2 else 1, 128 if i == 7 else 32), F32) for i in range(8)],
        in_specs=[pl.BlockSpec(memory_space=pltpu.SMEM), VM] + [ANY] * len(names),
        out_specs=[ANY, ANY] + [VM] * 12,
        scratch_shapes=[pltpu.VMEM((1, 256), F32), pltpu.VMEM((16, D), F32)]
        + Backward.SCRATCH
        + Swap.SEMS * 2
        + Total.SCRATCH
        + sum((Reduce.scratch(a) for a in REDUCED), []),
        compiler_params=pltpu.CompilerParams(
            collective_id=1, has_side_effects=True, vmem_limit_bytes=VMEM_BYTES
        ),
        name="collect",
    )(slot_mask, vectors, *[hbm[a] for a in names])
    return outs[0], outs[1], dict(zip(REDUCED, outs[2:6])), outs[6:]


def gather_plain(w_qkv, w_out, w_fc1, w_fc2):
    def all_of(shard, axis):
        return lax.all_gather(
            lax.all_gather(shard.astype(BF16), "dp", axis=axis, tiled=True), "tensor", axis=0
        )

    wqkv = all_of(w_qkv.reshape(-1, 768), 0)
    wout = all_of(w_out, 1).reshape(D, 8, 128).transpose(1, 0, 2)
    w1 = all_of(w_fc1, 0)
    w2 = all_of(w_fc2, 1).reshape(4 * D, 8, 128).transpose(1, 0, 2)
    return wqkv, wout, w1, w2


def scatter_plain(grads):
    def mine(grad, axis):
        part = lax.psum_scatter(grad, "tensor", scatter_dimension=0, tiled=True)
        return lax.psum_scatter(part, "dp", scatter_dimension=axis, tiled=True).astype(F32)

    g_qkv = mine(grads["wqkv"], 1)[0]
    g_out = mine(grads["wout"].transpose(1, 0, 2).reshape(D, D), 1)
    g_fc1 = mine(grads["w1"], 1)[0]
    g_fc2 = mine(grads["w2"].transpose(1, 0, 2).reshape(4 * D, D), 1)
    return g_qkv, g_out, g_fc1, g_fc2


def on_device(
    dp,
    tokens_in,
    cotangent,
    slot_mask,
    norm1_gain,
    norm1_bias,
    w_qkv,
    b_qkv,
    w_out,
    b_out,
    norm2_gain,
    norm2_bias,
    w_fc1,
    b_fc1,
    w_fc2,
    b_fc2,
):
    def images(rows):
        return jnp.pad(rows.reshape(4, SEQ, 256), ((0, 0), (0, ROWS - SEQ), (0, 0)))

    def exchange(pieces):
        return lax.all_to_all(pieces, "tensor", split_axis=0, concat_axis=0, tiled=True)

    if dp == 8:
        small = (norm1_gain, norm1_bias, b_qkv, b_out, norm2_gain, norm2_bias, b_fc2, b_fc1)
        big = (w_qkv.transpose(1, 0, 2), w_out, w_fc1, w_fc2)
        first, weights, saved = spread(slot_mask, tokens_in, cotangent, small, big)
        x, ct, out, probs, vectors = first
        hbm = dict(x=x, out=out, ct=ct, probs=probs, **weights, **saved)
        out, gtok, got, g_small = collect(slot_mask, vectors, hbm)
    else:
        mask = jnp.broadcast_to(
            lax.dynamic_index_in_dim(slot_mask, lax.axis_index("tensor"), 0).astype(F32), (1, 256)
        )
        small = jnp.concatenate(
            (norm1_gain, norm1_bias, b_qkv[0], b_qkv[1], b_out, norm2_gain, norm2_bias, b_fc2)
        ).astype(BF16)
        vectors = lax.all_gather(
            lax.all_gather(small, "dp", axis=1, tiled=True), "tensor", axis=0
        ).astype(F32)
        hidden_bias = lax.all_gather(
            lax.all_gather(b_fc1.astype(BF16), "dp", axis=1, tiled=True), "tensor", axis=0
        ).astype(F32)
        x = exchange(images(tokens_in))
        ct = exchange(images(cotangent))
        plain = gather_plain(w_qkv, w_out, w_fc1, w_fc2)
        weights = {a: b.reshape(PARTS[a][0]) for a, b in zip(WEIGHTS, plain)}
        out, probs, saved = forward(x, weights, vectors, hidden_bias, mask)
    if dp == 8:
        g_qkv, g_out, g_fc1, g_fc2 = (got[a] for a in GRADS)
        g_qkv = g_qkv.transpose(1, 0, 2)
    else:
        flat = [weights[a].reshape(GRADS[a].shape) for a in GRADS]
        gtok, sums, grads = backward(x, ct, *flat, vectors, mask, probs, saved)
        g_qkv, g_out, g_fc1, g_fc2 = scatter_plain(grads)
        out, gtok = exchange(out), exchange(gtok)

        def total(part, axis):
            part = lax.psum_scatter(part, "tensor", scatter_dimension=0, tiled=True)
            return lax.psum_scatter(part, "dp", scatter_dimension=axis, tiled=True)

        s = total(sums[0:8].reshape(8, 4, 256).transpose(1, 0, 2), 2)[0]
        g_small = (s[0:1], s[1:2], s[2:4], s[4:5], s[5:6], s[6:7], s[7:8], total(sums[8:12], 1))

    def rows(pieces):
        return pieces[:, :SEQ].reshape(4 * SEQ, 256)

    return (
        rows(out),
        rows(gtok),
        g_small[0],
        g_small[1],
        g_qkv.reshape(w_qkv.shape),
        g_small[2][:, None],
        g_out,
        g_small[3],
        g_small[4],
        g_small[5],
        g_fc1,
        g_small[7],
        g_fc2,
        g_small[6],
    )


def solution(mesh):
    both, turned = P("dp", "tensor"), P("tensor", "dp")
    mixed, pair = P("dp", None, "tensor"), P(None, "tensor", "dp")
    params = (turned, turned, mixed, pair, turned, turned, turned, turned, both, turned, turned, turned)
    return jax.shard_map(
        functools.partial(on_device, mesh.shape["dp"]),
        mesh=mesh,
        in_specs=(both, both, P("dp"), *params),
        out_specs=(both, both, *params),
        check_vma=False,
    )
```
